32 devices in a mesh: dp: 8 (over z, x), tensor: 4 (over y, core).
Axes of the slice: x: 2, y: 2, z: 4, core: 2. Of those that a mesh axis runs over, the one named last changes fastest.
Arguments:
- tokens: bfloat16 [16, 512, 2048], P('dp'), may hold values from -6 to 6
- lengths: int32 [16], P('dp'), may hold values from 128 to 512, as said below
- out_grad: bfloat16 [16, 512, 2048], P('dp'), may hold values from -6 to 6
- input_gain: float32 [2048], replicated, may hold values from 0.5 to 1.5
- mamba_gate_weight: bfloat16 [2048, 3072], P(None, 'tensor'), may hold values from -0.125 to 0.125
- mamba_in_weight: bfloat16 [2048, 3072], P(None, 'tensor'), may hold values from -0.125 to 0.125
- state_weight: bfloat16 [2048, 512], replicated, may hold values from -0.125 to 0.125
- step_weight: bfloat16 [2048, 48], P(None, 'tensor'), may hold values from -0.125 to 0.125
- conv_weight: float32 [4, 3072], P(None, 'tensor'), may hold values from -3 to 3
- conv_bias: float32 [3072], P('tensor'), may hold values from -1.8 to 1.8
- conv_state_weight: float32 [4, 512], replicated, may hold values from -3 to 3
- conv_state_bias: float32 [512], replicated, may hold values from -1.8 to 1.8
- step_bias: float32 [48], P('tensor'), may hold values from -6 to -1
- decay_log: float32 [48], P('tensor'), may hold values from -1 to 2
- skip_scale: float32 [48], P('tensor'), may hold values from 0.5 to 1.5
- mamba_gain: float32 [3072], P('tensor'), may hold values from 0.5 to 1.5
- mamba_out_weight: bfloat16 [3072, 2048], P('tensor'), may hold values from -0.109375 to 0.109375
- query_weight: bfloat16 [2048, 1024], P(None, 'tensor'), may hold values from -0.125 to 0.125
- key_value_weight: bfloat16 [2048, 512], replicated, may hold values from -0.125 to 0.125
- attn_out_weight: bfloat16 [1024, 2048], P('tensor'), may hold values from -0.5 to 0.5
- ffn_gain: float32 [2048], replicated, may hold values from 0.5 to 1.5
- gate_weight: bfloat16 [2048, 4096], P(None, 'tensor'), may hold values from -0.125 to 0.125
- up_weight: bfloat16 [2048, 4096], P(None, 'tensor'), may hold values from -0.125 to 0.125
- down_weight: bfloat16 [4096, 2048], P('tensor'), may hold values from -0.09375 to 0.09375
Outputs:
- out: bfloat16 [16, 512, 2048], P('dp')
- in_grad: float32 [16, 512, 2048], P('dp')
- input_gain_grad: float32 [2048], P('dp')
- mamba_gate_weight_grad: float32 [2048, 3072], P('dp', 'tensor')
- mamba_in_weight_grad: float32 [2048, 3072], P('dp', 'tensor')
- state_weight_grad: float32 [2048, 512], P(('dp', 'tensor'))
- step_weight_grad: float32 [2048, 48], P('dp', 'tensor')
- conv_weight_grad: float32 [4, 3072], P(None, 'tensor')
- conv_bias_grad: float32 [3072], P('tensor')
- conv_state_weight_grad: float32 [4, 512], P(None, ('dp', 'tensor'))
- conv_state_bias_grad: float32 [512], P(('dp', 'tensor'))
- step_bias_grad: float32 [48], P('tensor')
- decay_log_grad: float32 [48], P('tensor')
- skip_scale_grad: float32 [48], P('tensor')
- mamba_gain_grad: float32 [3072], P('tensor')
- mamba_out_weight_grad: float32 [3072, 2048], P('tensor', 'dp')
- query_weight_grad: float32 [2048, 1024], P('dp', 'tensor')
- key_value_weight_grad: float32 [2048, 512], P(('dp', 'tensor'))
- attn_out_weight_grad: float32 [1024, 2048], P('tensor', 'dp')
- ffn_gain_grad: float32 [2048], P('dp')
- gate_weight_grad: float32 [2048, 4096], P('dp', 'tensor')
- up_weight_grad: float32 [2048, 4096], P('dp', 'tensor')
- down_weight_grad: float32 [4096, 2048], P('tensor', 'dp')
The draws below stay inside these ranges and needn't reach their ends.
Inputs may be any that keep to these rules, and one draw needn't show every extreme that they name: Positions 0 to lengths - 1 of a slot are its tokens, the rest padding. Some slot has length 512 and some other slot 128.
All inputs are finite; a program needn't handle non-finite values.
Results may differ from the reference program's by a relative error of at most 0.023.
Values sent between devices are 32-bit elements; how exact they have to be, the bound alone decides.
A program may use at most 320 MiB of HBM per device.

```python
import jax
import jax.numpy as jnp
from jax import lax

D = 2048
MHEADS = 48
MHDIM = 64
STATE = 256
CONV = 4
AHEADS = 8
KVHEADS = 2
AHDIM = 128
FF = 4096
LEN = 512
DSSM = 3072
SLOTS = 16
N_TENSOR = 4


def draw_lengths(key, part):
    first, second, third = jax.random.split(jax.random.fold_in(key, 17), 3)
    drawn = jax.random.randint(first, (SLOTS,), LEN // 4, LEN + 1)
    full_slot = jax.random.randint(second, (), 0, SLOTS)
    short_slot = (full_slot + 1 + jax.random.randint(third, (), 0, SLOTS - 1)) % SLOTS
    drawn = drawn.at[full_slot].set(LEN)
    drawn = drawn.at[short_slot].set(LEN // 4)
    return drawn.astype(jnp.int32)


def level_of(key, dims, cuts, low, largest):
    def one(axis_at, shards_of):
        steps = jax.random.uniform(jax.random.fold_in(jax.random.fold_in(key, 6), axis_at), (shards_of,), jnp.float32, low / len(cuts), largest / len(cuts))
        return jnp.repeat(jnp.exp(steps), dims[axis_at] // shards_of).reshape((-1,) + (1,) * (len(dims) - axis_at - 1))

    factor_of = one(*cuts[0])
    for cut in cuts[1:]:
        factor_of = factor_of * one(*cut)
    return factor_of


def gaussian(rng, dims, spread, limit, cuts=(), dtype=jnp.bfloat16):
    level = level_of(rng, dims, cuts, -0.22, 0.18) if cuts else 1.0
    values = jax.random.normal(rng, dims, jnp.float32) * spread * level
    return jnp.minimum(jnp.maximum(values, -limit), limit).astype(dtype)


def setup_inputs(seed: int = 0) -> dict:
    seeds = jax.random.split(jax.random.key(seed), 25)
    tokens = gaussian(seeds[0], (SLOTS, LEN, D), 1.0, 6.0, ((0, 8),))
    lengths = draw_lengths(jax.random.fold_in(seeds[24], 71), 0)
    out_grad = gaussian(seeds[2], (SLOTS, LEN, D), 1.0, 6.0, ((0, 8),))
    input_gain = jnp.clip(1.0 + 0.1 * jax.random.normal(seeds[3], (D,), jnp.float32), 0.5, 1.5)
    mamba_gate_weight = gaussian(seeds[4], (D, DSSM), D ** -0.5, 0.125, ((1, 4),))
    mamba_in_weight = gaussian(seeds[5], (D, DSSM), D ** -0.5, 0.125, ((1, 4),))
    state_weight = gaussian(seeds[6], (D, 2 * STATE), D ** -0.5, 0.125)
    step_weight = gaussian(seeds[7], (D, MHEADS), D ** -0.5, 0.125, ((1, 4),))
    conv_weight = gaussian(seeds[8], (CONV, DSSM), CONV ** -0.5, 3.0, ((1, 4),), jnp.float32)
    conv_bias = gaussian(seeds[9], (DSSM,), 0.3, 1.8, ((0, 4),), jnp.float32)
    conv_state_weight = gaussian(seeds[10], (CONV, 2 * STATE), CONV ** -0.5, 3.0, (), jnp.float32)
    conv_state_bias = gaussian(seeds[11], (2 * STATE,), 0.3, 1.8, (), jnp.float32)
    step_bias = jnp.clip(-6.0 + 5.0 * jax.random.uniform(seeds[12], (MHEADS,), jnp.float32) ** level_of(seeds[12], (MHEADS,), ((0, 4),), -0.2, 0.2), -6.0, -1.0)
    decay_log = jnp.clip(-1.0 + 3.0 * jax.random.uniform(seeds[13], (MHEADS,), jnp.float32) ** level_of(seeds[13], (MHEADS,), ((0, 4),), -0.2, 0.2), -1.0, 2.0)
    skip_scale = jnp.clip(0.5 + 1.0 * jax.random.uniform(seeds[14], (MHEADS,), jnp.float32) ** level_of(seeds[14], (MHEADS,), ((0, 4),), -0.2, 0.2), 0.5, 1.5)
    mamba_gain = jnp.clip(1.0 + 0.1 * jax.random.normal(seeds[15], (DSSM,), jnp.float32), 0.5, 1.5)
    mamba_out_weight = gaussian(seeds[16], (DSSM, D), DSSM ** -0.5, 0.109375, ((0, 4),))
    query_weight = gaussian(seeds[17], (D, AHEADS * AHDIM), D ** -0.5, 0.125, ((1, 4),))
    key_value_weight = gaussian(seeds[18], (D, 2 * KVHEADS * AHDIM), D ** -0.5, 0.125)
    attn_out_weight = gaussian(seeds[19], (AHEADS * AHDIM, D), (AHEADS * AHDIM // 8) ** -0.5, 0.5, ((0, 4),))
    ffn_gain = jnp.clip(1.0 + 0.1 * jax.random.normal(seeds[20], (D,), jnp.float32), 0.5, 1.5)
    gate_weight = gaussian(seeds[21], (D, FF), D ** -0.5, 0.125, ((1, 4),))
    up_weight = gaussian(seeds[22], (D, FF), D ** -0.5, 0.125, ((1, 4),))
    down_weight = gaussian(seeds[23], (FF, D), FF ** -0.5, 0.09375, ((0, 4),))
    return dict(tokens=tokens, lengths=lengths, out_grad=out_grad, input_gain=input_gain, mamba_gate_weight=mamba_gate_weight, mamba_in_weight=mamba_in_weight, state_weight=state_weight, step_weight=step_weight, conv_weight=conv_weight, conv_bias=conv_bias, conv_state_weight=conv_state_weight, conv_state_bias=conv_state_bias, step_bias=step_bias, decay_log=decay_log, skip_scale=skip_scale, mamba_gain=mamba_gain, mamba_out_weight=mamba_out_weight, query_weight=query_weight, key_value_weight=key_value_weight, attn_out_weight=attn_out_weight, ffn_gain=ffn_gain, gate_weight=gate_weight, up_weight=up_weight, down_weight=down_weight)


@jax.custom_vjp
def low(v):
    return lax.optimization_barrier(v.astype(jnp.bfloat16)).astype(jnp.float32)

@jax.custom_vjp
def low_back(v):
    return v

def low_keep(v):
    return (low(v), None)

def low_pass(kept, grad):
    return (grad,)

def back_keep(v):
    return (v, None)

def back_low(kept, grad):
    return (low(grad),)
low.defvjp(low_keep, low_pass)
low_back.defvjp(back_keep, back_low)
epsilon = 1e-05
rope_base = 100000000000.0

def matmul(left, right):
    return jnp.dot(left, right, precision=lax.Precision.HIGHEST)

def rms_norm(values, gain):
    return values * lax.rsqrt(lax.optimization_barrier(jnp.mean(values * values, axis=-1, keepdims=True)) + epsilon) * gain

def causal_conv(values, kernel, bias):
    width = kernel.shape[0]
    count = values.shape[0]
    padded = jnp.pad(values, ((width - 1, 0), (0, 0)))
    total = jnp.zeros_like(values) + bias
    for offset in range(width):
        total = total + padded[offset:offset + count] * kernel[offset]
    return total

def rotary(values, positions):
    half = values.shape[-1] // 2
    freqs = rope_base ** (-(jnp.arange(half).astype(jnp.float32) * 2.0) / values.shape[-1])
    angles = positions[:, None] * freqs[None, :]
    cosine = jnp.cos(angles)[:, None, :]
    sine = jnp.sin(angles)[:, None, :]
    first = values[..., :half]
    second = values[..., half:]
    return jnp.concatenate([first * cosine - second * sine, second * cosine + first * sine], axis=-1)

def layer(inputs, weights, length):
    input_gain, mamba_gate_weight, mamba_in_weight, state_weight, step_weight, conv_weight, conv_bias, conv_state_weight, conv_state_bias, step_bias, decay_log, skip_scale, mamba_gain, mamba_out_weight, query_weight, key_value_weight, attn_out_weight, ffn_gain, gate_weight, up_weight, down_weight = weights
    count = inputs.shape[0]
    rows = jnp.arange(count).astype(jnp.int32)
    causal = rows[:, None] >= rows[None, :]
    positions = rows.astype(jnp.float32)
    normed = low(rms_norm(inputs, input_gain))
    zgate = low_back(matmul(normed, mamba_gate_weight))
    xpre = low_back(matmul(normed, mamba_in_weight))
    steppre = low_back(matmul(normed, step_weight))
    xconv = low(jax.nn.silu(causal_conv(xpre, conv_weight, conv_bias)))
    stepsize = jax.nn.softplus(steppre + step_bias)
    cumul = jnp.cumsum(-stepsize * jnp.exp(decay_log), axis=0).T
    weighted = low(jnp.repeat(stepsize, MHDIM, axis=1) * xconv)
    heads_dev = MHEADS // N_TENSOR
    pieces = []
    for group in range(N_TENSOR):
        statepre = low_back(matmul(normed, state_weight))
        sconv = low(jax.nn.silu(causal_conv(statepre, conv_state_weight, conv_state_bias)))
        inner = low_back(matmul(sconv[:, STATE:], sconv[:, :STATE].T))
        part = cumul[group * heads_dev:(group + 1) * heads_dev]
        differ = part[:, :, None] - part[:, None, :]
        decay = jnp.where(causal, jnp.exp(jnp.where(causal, differ, 0.0)), 0.0)
        mixing = low(inner[None] * decay)
        block = weighted[:, group * heads_dev * MHDIM:(group + 1) * heads_dev * MHDIM].reshape(count, heads_dev, MHDIM)
        result = jnp.einsum('hts,shp->thp', mixing, block, precision=lax.Precision.HIGHEST)
        pieces.append(result.reshape(count, heads_dev * MHDIM))
    ssd = low_back(jnp.concatenate(pieces, axis=1) + jnp.repeat(skip_scale, MHDIM) * xconv)
    gated = ssd * jax.nn.silu(zgate)
    scaled = low(rms_norm(gated, mamba_gain))
    mamba_out = matmul(scaled, mamba_out_weight)
    query = low(rotary(low_back(matmul(normed, query_weight)).reshape(count, AHEADS, AHDIM), positions))
    kv_width = KVHEADS * AHDIM
    valid_keys = causal & (rows[None, :] < length)
    q_dev = AHEADS // N_TENSOR
    group_size = AHEADS // KVHEADS
    scale = AHDIM ** (-0.5)
    contexts = []
    for group in range(N_TENSOR):
        kv_head = group * q_dev // group_size
        key_pre = low_back(matmul(normed, key_value_weight[:, kv_head * AHDIM:(kv_head + 1) * AHDIM]))
        value_pre = low_back(matmul(normed, key_value_weight[:, kv_width + kv_head * AHDIM:kv_width + (kv_head + 1) * AHDIM]))
        keys = low(rotary(key_pre[:, None, :], positions)[:, 0])
        values = low(value_pre)
        group_query = query[:, group * q_dev:(group + 1) * q_dev]
        scores = low_back(jnp.einsum('thd,sd->hts', group_query, keys, precision=lax.Precision.HIGHEST) * scale)
        probs = low(jax.nn.softmax(jnp.where(valid_keys[None], scores, -1e+30), axis=-1))
        context = low(low_back(jnp.einsum('hts,sd->thd', probs, values, precision=lax.Precision.HIGHEST)))
        contexts.append(context.reshape(count, q_dev * AHDIM))
    attn_out = matmul(jnp.concatenate(contexts, axis=1), attn_out_weight)
    mixed = low_back(mamba_out + attn_out)
    hidden = inputs + mixed
    normed2 = low(rms_norm(hidden, ffn_gain))
    gate = low_back(matmul(normed2, gate_weight))
    upper = low_back(matmul(normed2, up_weight))
    inner_ffn = low(jax.nn.silu(gate) * upper)
    return hidden + matmul(inner_ffn, down_weight)

def reference(tokens, lengths, out_grad, input_gain, mamba_gate_weight, mamba_in_weight, state_weight, step_weight, conv_weight, conv_bias, conv_state_weight, conv_state_bias, step_bias, decay_log, skip_scale, mamba_gain, mamba_out_weight, query_weight, key_value_weight, attn_out_weight, ffn_gain, gate_weight, up_weight, down_weight):
    weights = tuple((item.astype(jnp.float32) for item in (input_gain, mamba_gate_weight, mamba_in_weight, state_weight, step_weight, conv_weight, conv_bias, conv_state_weight, conv_state_bias, step_bias, decay_log, skip_scale, mamba_gain, mamba_out_weight, query_weight, key_value_weight, attn_out_weight, ffn_gain, gate_weight, up_weight, down_weight)))

    def one_slot(totals, slot):
        inputs, length, cotangent = slot
        rows = jnp.arange(LEN).astype(jnp.int32)
        valid = (rows < length).astype(jnp.float32)[:, None]

        def forward(values, params):
            return layer(values, params, length)
        result, pullback = jax.vjp(forward, inputs.astype(jnp.float32), weights)
        grad_in, grad_weights = pullback(cotangent.astype(jnp.float32) * valid)
        totals = jax.tree.map(jnp.add, totals, grad_weights)
        return (totals, (result.astype(jnp.bfloat16), grad_in))
    zeros = jax.tree.map(jnp.zeros_like, weights)
    totals, stacked = lax.scan(one_slot, zeros, (tokens, lengths, out_grad))
    return (stacked[0], stacked[1], totals[0], totals[1], totals[2], totals[3], totals[4], totals[5], totals[6], totals[7], totals[8], totals[9], totals[10], totals[11], totals[12], totals[13], totals[14], totals[15], totals[16], totals[17], totals[18], totals[19], totals[20])
```

```python
import jax
import jax.numpy as jnp
from jax import lax
from jax.sharding import PartitionSpec as P

MHDIM = 64
STATE = 256
AHEADS = 8
KVHEADS = 2
AHDIM = 128
DSSM = 3072

epsilon = 1e-05
rope_base = 100000000000.0
f32 = jnp.float32
bf16 = jnp.bfloat16


def plain_dot(left, right):
    return jnp.dot(left, right, preferred_element_type=f32)


def right_trans(left, right):
    return lax.dot_general(left, right, (((1,), (1,)), ((), ())), preferred_element_type=f32)


def left_trans(left, right):
    return lax.dot_general(left, right, (((0,), (0,)), ((), ())), preferred_element_type=f32)


def silu_slope(values):
    sig = jax.nn.sigmoid(values)
    return sig * (1.0 + values * (1.0 - sig))


def causal_conv(values, kernel, bias):
    width = kernel.shape[0]
    count = values.shape[0]
    padded = jnp.pad(values, ((width - 1, 0), (0, 0)))
    total = jnp.zeros_like(values) + bias
    for offset in range(width):
        total = total + padded[offset : offset + count] * kernel[offset]
    return total


def conv_back(grads, values, kernel):
    width = kernel.shape[0]
    count = values.shape[0]
    padded = jnp.pad(values, ((width - 1, 0), (0, 0)))
    after = jnp.pad(grads, ((0, width - 1), (0, 0)))
    d_values = jnp.zeros_like(values)
    kernel_rows = []
    for offset in range(width):
        start = width - 1 - offset
        d_values = d_values + after[start : start + count] * kernel[offset]
        kernel_rows.append(jnp.sum(grads * padded[offset : offset + count], axis=0))
    return (d_values, jnp.stack(kernel_rows), jnp.sum(grads, axis=0))


def rotary(values, cosine, sine):
    half = values.shape[-1] // 2
    first = values[..., :half]
    second = values[..., half:]
    return jnp.concatenate(
        [first * cosine - second * sine, second * cosine + first * sine], axis=-1
    )


def rotary_back(grads, cosine, sine):
    half = grads.shape[-1] // 2
    first = grads[..., :half]
    second = grads[..., half:]
    return jnp.concatenate(
        [first * cosine + second * sine, second * cosine - first * sine], axis=-1
    )


def swap(values, axis, size, bit):
    return lax.ppermute(values, axis, [(i, i ^ bit) for i in range(size)])


def halving_order(members, bit, limit):
    if bit >= limit:
        return members
    low = halving_order([m for m in members if not m & bit], bit * 2, limit)
    high = halving_order([m for m in members if m & bit], bit * 2, limit)
    return low + high


class Scatter:
    def __init__(self, size):
        self.size = size
        self.flight = []

    def send(self, values, bit):
        if bit == 1:
            if len(self.flight) >= 2:
                values, _ = lax.optimization_barrier((values, self.flight[-2]))
            got = swap(values, "dp", self.size, bit)
            self.flight.append(got)
            return got
        return swap(values, "dp", self.size, bit)

    def run(self, product, axis):
        size = self.size
        if size < 4:
            held = product([0])
            if size == 2:
                held = held + self.send(product([1]), 1)
            return held
        first = halving_order([r for r in range(size) if not r & 1 and r & 2], 4, size)
        later = halving_order([r for r in range(size) if not r & 1 and not r & 2], 4, size)
        got_a = self.send(product([r ^ 1 for r in first]), 1)
        got_b = self.send(product([r ^ 1 for r in later]), 1)
        got_c = self.send(product(first) + got_a, 2)
        held = product(later) + got_b + got_c
        bit = 4
        while bit < size:
            half = held.shape[axis] // 2
            keep = lax.slice_in_dim(held, 0, half, axis=axis)
            away = lax.slice_in_dim(held, half, 2 * half, axis=axis)
            held = keep + self.send(away, bit)
            bit *= 2
        return held


def make_per_device(dp_size, t_size):
    def per_device(
        tokens,
        lengths,
        out_grad,
        input_gain,
        mamba_gate_weight,
        mamba_in_weight,
        state_weight,
        step_weight,
        conv_weight,
        conv_bias,
        conv_state_weight,
        conv_state_bias,
        step_bias,
        decay_log,
        skip_scale,
        mamba_gain,
        mamba_out_weight,
        query_weight,
        key_value_weight,
        attn_out_weight,
        ffn_gain,
        gate_weight,
        up_weight,
        down_weight,
    ):
        micro = tokens.shape[0]
        count = tokens.shape[1]
        width = tokens.shape[2]
        half = count // 2
        local_heads = step_weight.shape[1]
        q_local = query_weight.shape[1] // AHDIM
        kv_width = key_value_weight.shape[1] // 2
        group_size = AHEADS // KVHEADS
        me_dp = lax.axis_index("dp")
        me_t = lax.axis_index("tensor")
        core = lax.rem(me_t, 2)
        kv_head = me_t * q_local // group_size
        key_weight = lax.dynamic_slice_in_dim(key_value_weight, kv_head * AHDIM, AHDIM, 1)
        value_weight = lax.dynamic_slice_in_dim(
            key_value_weight, kv_width + kv_head * AHDIM, AHDIM, 1
        )
        scale = AHDIM ** (-0.5)
        rows = jnp.arange(count)
        causal = rows[:, None] >= rows[None, :]
        lower = causal.astype(f32)
        freqs = rope_base ** (-(jnp.arange(AHDIM // 2).astype(f32) * 2.0) / AHDIM)
        angles = rows.astype(f32)[:, None] * freqs[None, :]
        cosine = jnp.cos(angles)[:, None, :]
        sine = jnp.sin(angles)[:, None, :]
        skip_rep = jnp.repeat(skip_scale, MHDIM)
        rates = jnp.exp(decay_log)

        def t_swap(values, bit):
            return swap(values, "tensor", t_size, bit)

        def t_total(values):
            bit = 1
            while bit < t_size:
                values = values + t_swap(values, bit)
                bit *= 2
            return values

        def mine(values):
            return lax.dynamic_slice_in_dim(values, core * half, half, 0)

        def other(values):
            return lax.dynamic_slice_in_dim(values, (1 - core) * half, half, 0)

        def relative(values):
            return jnp.concatenate([mine(values), other(values)], axis=0)

        def in_order(own, far):
            return jnp.where(
                core == 0,
                jnp.concatenate([own, far], axis=0),
                jnp.concatenate([far, own], axis=0),
            )

        def summed(own, far):
            own = own + t_swap(far, 1)
            bit = 2
            while bit < t_size:
                own = own + t_swap(own, bit)
                bit *= 2
            return own

        block = width // dp_size

        def block_order(values):
            return [
                lax.dynamic_slice_in_dim(values, jnp.bitwise_xor(me_dp, r) * block, block, 1)
                for r in range(dp_size)
            ]

        def pick(blocks, members):
            return jnp.concatenate([blocks[r] for r in members], axis=1)

        scatter = Scatter(dp_size)

        slots = []
        for index in range(micro):
            keep = {}
            inputs = tokens[index].astype(f32)
            inv_one = lax.rsqrt(jnp.mean(inputs * inputs, axis=-1, keepdims=True) + epsilon)
            unit_one = inputs * inv_one
            normed = (unit_one * input_gain).astype(bf16)
            zgate = plain_dot(normed, mamba_gate_weight)
            xpre = plain_dot(normed, mamba_in_weight)
            statepre = plain_dot(normed, state_weight)
            steppre = plain_dot(normed, step_weight)
            xlin = causal_conv(xpre, conv_weight, conv_bias)
            xconv = jax.nn.silu(xlin).astype(bf16)
            xvals = xconv.astype(f32)
            slin = causal_conv(statepre, conv_state_weight, conv_state_bias)
            sconv = jax.nn.silu(slin).astype(bf16)
            binput = sconv[:, :STATE]
            cinput = sconv[:, STATE:]
            inner = right_trans(cinput, binput)
            stepsize = jax.nn.softplus(steppre + step_bias)
            cumul = lax.dot_general(
                -stepsize * rates,
                lower,
                (((0,), (1,)), ((), ())),
                precision=lax.Precision.HIGHEST,
                preferred_element_type=f32,
            )
            differ = cumul[:, :, None] - cumul[:, None, :]
            decay = jnp.where(causal, jnp.exp(jnp.where(causal, differ, 0.0)), 0.0)
            mixing = (inner[None] * decay).astype(bf16)
            step_rep = jnp.repeat(stepsize, MHDIM, axis=1)
            weighted = (step_rep * xvals).astype(bf16)
            wblock = weighted.reshape(count, local_heads, MHDIM)
            ssd = jnp.einsum("hts,shp->thp", mixing, wblock, preferred_element_type=f32).reshape(
                count, -1
            )
            ssd = ssd + skip_rep * xvals
            zsig = jax.nn.sigmoid(zgate)
            zsilu = zgate * zsig
            gated = ssd * zsilu
            total_square = t_total(jnp.sum(gated * gated, axis=-1))
            inv_mamba = lax.rsqrt(total_square / DSSM + epsilon)[:, None]
            scaled = (gated * inv_mamba * mamba_gain).astype(bf16)
            query_pre = plain_dot(normed, query_weight).reshape(count, q_local, AHDIM)
            query = rotary(query_pre, cosine, sine).astype(bf16)
            key_pre = plain_dot(normed, key_weight)
            keys = rotary(key_pre[:, None, :], cosine, sine)[:, 0].astype(bf16)
            values = plain_dot(normed, value_weight).astype(bf16)
            length = lengths[index]
            valid_keys = causal & (rows[None, :] < length)
            scores = jnp.einsum("thd,sd->hts", query, keys, preferred_element_type=f32) * scale
            masked = jnp.where(valid_keys[None], scores, -1e30)
            peak = jnp.max(masked, axis=-1, keepdims=True)
            expo = jnp.exp(masked - peak)
            total_exp = jnp.sum(expo, axis=-1, keepdims=True)
            log_total = peak + jnp.log(total_exp)
            probs = (expo / total_exp).astype(bf16)
            context = jnp.einsum("hts,sd->thd", probs, values, preferred_element_type=f32)
            context = context.reshape(count, -1).astype(bf16)
            far = plain_dot(other(scaled), mamba_out_weight) + plain_dot(
                other(context), attn_out_weight
            )
            own = plain_dot(mine(scaled), mamba_out_weight) + plain_dot(
                mine(context), attn_out_weight
            )
            keep["mixed"] = summed(own, far)
            keep.update(
                inputs=inputs, inv_one=inv_one, unit_one=unit_one, normed=normed, zgate=zgate,
                xpre=xpre, statepre=statepre, steppre=steppre, xlin=xlin, xvals=xvals, slin=slin,
                binput=binput, cinput=cinput, inner=inner, stepsize=stepsize, decay=decay,
                mixing=mixing, step_rep=step_rep, wblock=wblock, ssd=ssd, zsig=zsig, zsilu=zsilu,
                gated=gated, inv_mamba=inv_mamba, scaled=scaled, query=query, keys=keys,
                values=values, valid_keys=valid_keys, log_total=log_total, context=context,
            )
            slots.append(keep)

        for index in range(micro):
            keep = slots[index]
            hidden_own = mine(keep["inputs"]) + keep["mixed"]
            hidden = jnp.concatenate([hidden_own, t_swap(hidden_own, 1)], axis=0)
            inv_two = lax.rsqrt(jnp.mean(hidden * hidden, axis=-1, keepdims=True) + epsilon)
            unit_two = hidden * inv_two
            normed_two = (unit_two * ffn_gain).astype(bf16)
            gate = plain_dot(normed_two, gate_weight)
            upper = plain_dot(normed_two, up_weight)
            gsig = jax.nn.sigmoid(gate)
            gsilu = gate * gsig
            inner_ffn = (gsilu * upper).astype(bf16)
            valid = (rows < lengths[index]).astype(f32)[:, None]
            cotangent = relative(out_grad[index].astype(f32) * valid)
            cot_low = cotangent.astype(bf16)
            d_inner_ffn = right_trans(cot_low, down_weight)
            d_gate = (d_inner_ffn * upper * gsig * (1.0 + gate * (1.0 - gsig))).astype(bf16)
            d_up = (d_inner_ffn * gsilu).astype(bf16)
            far = right_trans(d_gate[half:], gate_weight) + right_trans(d_up[half:], up_weight)
            own = right_trans(d_gate[:half], gate_weight) + right_trans(d_up[:half], up_weight)
            keep["d_normed_two"] = summed(own, far)
            keep.update(
                hidden=hidden, inv_two=inv_two[:half], unit_two=unit_two[:half],
                normed_two=normed_two, inner_ffn=inner_ffn, cotangent=cotangent, cot_low=cot_low,
                d_gate=d_gate, d_up=d_up,
            )

        def joined(name):
            return jnp.concatenate([keep[name] for keep in slots], axis=0)

        cot_blocks = block_order(joined("cot_low"))
        inner_all = joined("inner_ffn")
        g_down = scatter.run(lambda m: left_trans(inner_all, pick(cot_blocks, m)), 1)
        two_blocks = block_order(joined("normed_two"))
        d_gate_all = joined("d_gate")
        g_gate = scatter.run(lambda m: left_trans(pick(two_blocks, m), d_gate_all), 0)
        d_up_all = joined("d_up")
        g_up = scatter.run(lambda m: left_trans(pick(two_blocks, m), d_up_all), 0)

        outputs_list = []
        for index in range(micro):
            keep = slots[index]
            inner_ffn = keep["inner_ffn"]
            ffn_own = summed(
                plain_dot(inner_ffn[:half], down_weight), plain_dot(inner_ffn[half:], down_weight)
            )
            out = keep["hidden"] + jnp.concatenate([ffn_own, t_swap(ffn_own, 1)], axis=0)
            outputs_list.append(in_order(out[:half], out[half:]).astype(bf16))

        pad_step = 128 - local_heads
        back_weight = jnp.concatenate(
            [
                mamba_gate_weight,
                mamba_in_weight,
                query_weight,
                state_weight,
                key_weight,
                value_weight,
                jnp.pad(step_weight, ((0, 0), (0, pad_step))),
            ],
            axis=1,
        )
        head_total = None
        for index in range(micro):
            keep = slots[index]
            k = keep
            d_normed_two = keep["d_normed_two"]
            unit_two = keep["unit_two"]
            g_ffn_gain = jnp.sum(d_normed_two * unit_two, axis=0)
            d_unit_two = d_normed_two * ffn_gain
            d_rest = keep["inv_two"] * (
                d_unit_two - unit_two * jnp.mean(d_unit_two * unit_two, axis=-1, keepdims=True)
            )
            d_hidden = keep["cotangent"][:half] + d_rest
            d_both = keep["cotangent"] + jnp.concatenate([d_rest, t_swap(d_rest, 1)], axis=0)
            d_mixed = in_order(d_both[:half], d_both[half:]).astype(bf16)
            keep["d_mixed"] = d_mixed
            d_context = (
                right_trans(d_mixed, attn_out_weight).astype(bf16).reshape(count, q_local, AHDIM)
            )
            again = (
                jnp.einsum("thd,sd->hts", k["query"], k["keys"], preferred_element_type=f32)
                * scale
            )
            probs_full = jnp.where(k["valid_keys"][None], jnp.exp(again - k["log_total"]), 0.0)
            probs_low = probs_full.astype(bf16)
            d_probs = jnp.einsum("thd,sd->hts", d_context, k["values"], preferred_element_type=f32)
            d_values = jnp.einsum("hts,thd->sd", probs_low, d_context, preferred_element_type=f32)
            delta = jnp.sum(probs_full * d_probs, axis=-1, keepdims=True)
            d_scores = (probs_full * (d_probs - delta)).astype(bf16)
            d_query = (
                jnp.einsum("hts,sd->thd", d_scores, k["keys"], preferred_element_type=f32) * scale
            )
            d_keys = (
                jnp.einsum("hts,thd->sd", d_scores, k["query"], preferred_element_type=f32) * scale
            )
            d_query_pre = rotary_back(d_query, cosine, sine).reshape(count, -1).astype(bf16)
            d_key_full = rotary_back(d_keys[:, None, :], cosine, sine)[:, 0]
            d_scaled = right_trans(d_mixed, mamba_out_weight)
            gated = k["gated"]
            inv_mamba = k["inv_mamba"]
            g_mamba_gain = jnp.sum(d_scaled * gated * inv_mamba, axis=0)
            d_norm_in = d_scaled * mamba_gain
            cross = t_total(jnp.sum(d_norm_in * gated, axis=-1))
            d_gated = inv_mamba * d_norm_in - gated * inv_mamba**3 * cross[:, None] / DSSM
            d_ssd = (d_gated * k["zsilu"]).astype(bf16)
            d_ssd_full = d_ssd.astype(f32)
            zgate, zsig = k["zgate"], k["zsig"]
            d_zgate = (d_gated * k["ssd"] * zsig * (1.0 + zgate * (1.0 - zsig))).astype(bf16)
            xvals, stepsize, decay = k["xvals"], k["stepsize"], k["decay"]
            g_skip = jnp.sum((d_ssd_full * xvals).reshape(count, local_heads, MHDIM), axis=(0, 2))
            dblock = d_ssd.reshape(count, local_heads, MHDIM)
            d_mixing = jnp.einsum("thp,shp->hts", dblock, k["wblock"], preferred_element_type=f32)
            d_weighted = jnp.einsum(
                "hts,thp->shp", k["mixing"], dblock, preferred_element_type=f32
            ).reshape(count, -1)
            d_xvals = d_ssd_full * skip_rep + d_weighted * k["step_rep"]
            d_step = jnp.sum((d_weighted * xvals).reshape(count, local_heads, MHDIM), axis=-1)
            d_inner = jnp.sum(d_mixing * decay, axis=0).astype(bf16)
            flow = d_mixing * k["inner"][None] * decay
            d_cumul = jnp.sum(flow, axis=2) - jnp.sum(flow, axis=1)
            d_logdecay = lax.dot_general(
                lower,
                d_cumul,
                (((0,), (1,)), ((), ())),
                precision=lax.Precision.HIGHEST,
                preferred_element_type=f32,
            )
            d_step = d_step - d_logdecay * rates
            g_decay_log = jnp.sum(-d_logdecay * stepsize * rates, axis=0)
            d_steppre_full = d_step * jax.nn.sigmoid(k["steppre"] + step_bias)
            g_step_bias = jnp.sum(d_steppre_full, axis=0)
            d_steppre = d_steppre_full.astype(bf16)
            d_cinput = plain_dot(d_inner, k["binput"])
            d_binput = left_trans(d_inner, k["cinput"])
            d_slin = jnp.concatenate([d_binput, d_cinput], axis=1) * silu_slope(k["slin"])
            d_statepre_full, g_conv_state_weight, g_conv_state_bias = conv_back(
                d_slin, k["statepre"], conv_state_weight
            )
            d_xlin = d_xvals * silu_slope(k["xlin"])
            d_xpre_full, g_conv_weight, g_conv_bias = conv_back(d_xlin, k["xpre"], conv_weight)
            d_xpre = d_xpre_full.astype(bf16)
            piece = d_statepre_full.shape[1] // t_size
            parts = [
                lax.dynamic_slice_in_dim(
                    d_statepre_full, jnp.bitwise_xor(me_t, q) * piece, piece, 1
                )
                for q in range(t_size)
            ]
            order = halving_order(list(range(0, t_size, 2)), 2, t_size)
            state_sum = jnp.concatenate([parts[q] for q in order], axis=1) + t_swap(
                jnp.concatenate([parts[q ^ 1] for q in order], axis=1), 1
            )
            bit = 2
            while bit < t_size:
                cut = state_sum.shape[1] // 2
                state_sum = state_sum[:, :cut] + t_swap(state_sum[:, cut:], bit)
                bit *= 2
            kv_far = jnp.where(core == 0, d_values, d_key_full)
            kv_own = jnp.where(core == 0, d_key_full, d_values)
            kv_sum = kv_own + t_swap(kv_far, 1)
            keep["shared"] = jnp.concatenate([state_sum, kv_sum], axis=1).astype(bf16)
            keep["d_early"] = jnp.concatenate([d_zgate, d_query_pre], axis=1)
            keep["d_xpre"] = d_xpre
            keep["d_steppre"] = d_steppre
            back = jnp.concatenate(
                [
                    d_zgate,
                    d_xpre,
                    d_query_pre,
                    d_statepre_full.astype(bf16),
                    d_key_full.astype(bf16),
                    d_values.astype(bf16),
                    jnp.pad(d_steppre, ((0, 0), (0, pad_step))),
                ],
                axis=1,
            )
            d_normed = summed(
                right_trans(mine(back), back_weight), right_trans(other(back), back_weight)
            )
            unit_own = mine(k["unit_one"])
            g_input_gain = jnp.sum(d_normed * unit_own, axis=0)
            d_unit_one = d_normed * input_gain
            keep["grad_own"] = d_hidden + mine(k["inv_one"]) * (
                d_unit_one - unit_own * jnp.mean(d_unit_one * unit_own, axis=-1, keepdims=True)
            )
            fresh = (
                g_conv_weight, g_conv_bias, g_step_bias, g_decay_log, g_skip, g_mamba_gain,
                g_conv_state_weight, g_conv_state_bias, g_input_gain, g_ffn_gain,
            )
            head_total = (
                fresh if head_total is None else tuple(a + b for a, b in zip(head_total, fresh))
            )

        mixed_blocks = block_order(joined("d_mixed"))
        mixer_all = jnp.concatenate([joined("scaled"), joined("context")], axis=1)
        g_outs = scatter.run(lambda m: left_trans(mixer_all, pick(mixed_blocks, m)), 1)
        one_blocks = block_order(joined("normed"))
        d_early = joined("d_early")
        g_early = scatter.run(lambda m: left_trans(pick(one_blocks, m), d_early), 0)
        d_late = jnp.concatenate([joined("d_xpre"), joined("shared")], axis=1)
        g_late = scatter.run(lambda m: left_trans(pick(one_blocks, m), d_late), 0)
        d_step_all = joined("d_steppre")
        g_step = scatter.run(lambda m: left_trans(d_step_all, pick(one_blocks, m)), 1).T

        grads_list = [
            in_order(keep["grad_own"], t_swap(keep["grad_own"], 1)) for keep in slots
        ]

        once = me_t < 2
        g_gains = [jnp.where(once, g, 0.0) for g in head_total[8:]]
        flat = lambda items: jnp.concatenate([g.reshape(-1) for g in items])
        heads = lax.psum(flat(head_total[:6]), "dp")
        wide = lax.psum(flat(list(head_total[6:8]) + g_gains), ("dp", "tensor"))

        def cut(vector, shapes):
            parts, start = [], 0
            for shape in shapes:
                size = 1
                for s in shape:
                    size *= s
                parts.append(vector[start : start + size].reshape(shape))
                start += size
            return parts

        heads = cut(heads, [g.shape for g in head_total[:6]])
        wide = cut(wide, [g.shape for g in head_total[6:]])
        place = me_dp * t_size + me_t
        share = conv_state_bias.shape[0] // (dp_size * t_size)
        g_conv_state_weight = lax.dynamic_slice_in_dim(wide[0], place * share, share, 1)
        g_conv_state_bias = lax.dynamic_slice_in_dim(wide[1], place * share, share, 0)
        g_input_gain = lax.dynamic_slice_in_dim(wide[2], me_dp * block, block, 0)
        g_ffn_gain = lax.dynamic_slice_in_dim(wide[3], me_dp * block, block, 0)

        mamba_cols = mamba_in_weight.shape[1]
        tail = g_late[:, mamba_cols:]
        sub = block // t_size
        rowsets = []
        for q in range(t_size):
            part = lax.dynamic_slice_in_dim(tail, jnp.bitwise_xor(me_t, q) * sub, sub, 0)
            rowsets.append(part if q == 0 else t_swap(part, q))
        stacked = jnp.stack(rowsets)
        piece = state_weight.shape[1] // t_size
        sources = [
            lax.dynamic_index_in_dim(stacked, jnp.bitwise_xor(me_t, j), 0, keepdims=False)
            for j in range(t_size)
        ]
        g_state = jnp.concatenate([s[:, :piece] for s in sources], axis=1)
        pairs = t_size // 2
        g_kv = jnp.concatenate(
            [sources[(b % pairs) * 2 + b // pairs][:, piece:] for b in range(t_size)], axis=1
        )
        gate_cols = mamba_gate_weight.shape[1]
        mamba_rows = mamba_out_weight.shape[0]
        return (
            jnp.stack(outputs_list),
            jnp.stack(grads_list),
            g_input_gain,
            g_early[:, :gate_cols],
            g_late[:, :mamba_cols],
            g_state,
            g_step,
            heads[0],
            heads[1],
            g_conv_state_weight,
            g_conv_state_bias,
            heads[2],
            heads[3],
            heads[4],
            heads[5],
            g_outs[:mamba_rows],
            g_early[:, gate_cols:],
            g_kv,
            g_outs[mamba_rows:],
            g_ffn_gain,
            g_gate,
            g_up,
            g_down,
        )

    return per_device


def solution(mesh):
    placed = (
        P("dp", None, None),
        P("dp"),
        P("dp", None, None),
        P(),
        P(None, "tensor"),
        P(None, "tensor"),
        P(),
        P(None, "tensor"),
        P(None, "tensor"),
        P("tensor"),
        P(),
        P(),
        P("tensor"),
        P("tensor"),
        P("tensor"),
        P("tensor"),
        P("tensor", None),
        P(None, "tensor"),
        P(),
        P("tensor", None),
        P(),
        P(None, "tensor"),
        P(None, "tensor"),
        P("tensor", None),
    )
    return jax.shard_map(
        make_per_device(mesh.shape["dp"], mesh.shape["tensor"]),
        mesh=mesh,
        in_specs=placed,
        out_specs=(
            P("dp", None, None),
            P("dp", None, None),
            P("dp"),
            P("dp", "tensor"),
            P("dp", "tensor"),
            P(("dp", "tensor"), None),
            P("dp", "tensor"),
            P(None, "tensor"),
            P("tensor"),
            P(None, ("dp", "tensor")),
            P(("dp", "tensor")),
            P("tensor"),
            P("tensor"),
            P("tensor"),
            P("tensor"),
            P("tensor", "dp"),
            P("dp", "tensor"),
            P(("dp", "tensor"), None),
            P("tensor", "dp"),
            P("dp"),
            P("dp", "tensor"),
            P("dp", "tensor"),
            P("tensor", "dp"),
        ),
        check_vma=False,
    )
```

```python
import jax
import jax.numpy as jnp
from jax import lax
from jax.sharding import PartitionSpec as P

MHDIM = 64
STATE = 256
AHEADS = 8
KVHEADS = 2
AHDIM = 128
DSSM = 3072

epsilon = 1e-05
rope_base = 100000000000.0
f32 = jnp.float32
bf16 = jnp.bfloat16


def plain_dot(left, right):
    return jnp.dot(left, right, preferred_element_type=f32)


def right_trans(left, right):
    return lax.dot_general(left, right, (((1,), (1,)), ((), ())), preferred_element_type=f32)


def left_trans(left, right):
    return lax.dot_general(left, right, (((0,), (0,)), ((), ())), preferred_element_type=f32)


def silu_slope(values):
    sig = jax.nn.sigmoid(values)
    return sig * (1.0 + values * (1.0 - sig))


def causal_conv(values, kernel, bias):
    width = kernel.shape[0]
    count = values.shape[0]
    padded = jnp.pad(values, ((width - 1, 0), (0, 0)))
    total = jnp.zeros_like(values) + bias
    for offset in range(width):
        total = total + padded[offset : offset + count] * kernel[offset]
    return total


def conv_back(grads, values, kernel):
    width = kernel.shape[0]
    count = values.shape[0]
    padded = jnp.pad(values, ((width - 1, 0), (0, 0)))
    after = jnp.pad(grads, ((0, width - 1), (0, 0)))
    d_values = jnp.zeros_like(values)
    kernel_rows = []
    for offset in range(width):
        start = width - 1 - offset
        d_values = d_values + after[start : start + count] * kernel[offset]
        kernel_rows.append(jnp.sum(grads * padded[offset : offset + count], axis=0))
    return (d_values, jnp.stack(kernel_rows), jnp.sum(grads, axis=0))


def rotary(values, cosine, sine):
    half = values.shape[-1] // 2
    first = values[..., :half]
    second = values[..., half:]
    return jnp.concatenate(
        [first * cosine - second * sine, second * cosine + first * sine], axis=-1
    )


def rotary_back(grads, cosine, sine):
    half = grads.shape[-1] // 2
    first = grads[..., :half]
    second = grads[..., half:]
    return jnp.concatenate(
        [first * cosine + second * sine, second * cosine - first * sine], axis=-1
    )


def swap(values, axis, size, bit):
    return lax.ppermute(values, axis, [(i, i ^ bit) for i in range(size)])


def halving_order(members, bit, limit):
    if bit >= limit:
        return members
    low = halving_order([m for m in members if not m & bit], bit * 2, limit)
    high = halving_order([m for m in members if m & bit], bit * 2, limit)
    return low + high


class Order:
    def __init__(self):
        self.last = ()

    def gate(self, *values):
        return lax.optimization_barrier((values, self.last))[0]

    def mark(self, *values):
        self.last = values


class Scatter:
    def __init__(self, order, size, blocks, whole, axis):
        self.order, self.size, self.axis = order, size, axis
        self.blocks, self.whole = blocks, whole
        evens = [r for r in range(size) if not r & 1]
        self.first = halving_order([r for r in evens if r & 2], 4, size)
        self.later = halving_order([r for r in evens if not r & 2], 4, size)

    def product(self, members, wait=None):
        picked = jnp.concatenate([self.blocks[r] for r in members], axis=1)
        if self.axis == 0:
            return left_trans(picked, self.whole)
        return left_trans(self.whole, picked)

    def send(self, values, bit):
        return swap(values, "dp", self.size, bit)

    def start_first(self):
        part = self.product([r ^ 1 for r in self.first])
        self.got_first = self.send(part, 1)
        return part

    def start_later(self):
        part = self.product([r ^ 1 for r in self.later])
        self.got_later = self.send(part, 1)
        return part

    def take_first(self):
        (got,) = self.order.gate(self.got_first)
        held = self.product(self.first) + got
        self.got_second = self.send(held, 2)
        self.order.mark(held)

    def take_later(self):
        got, second = self.order.gate(self.got_later, self.got_second)
        held = self.product(self.later) + got + second
        self.halve(held, 4)

    def halve(self, held, bit):
        if bit >= self.size:
            self.keep, self.got_last = held, None
            self.order.mark(held)
            return
        half = held.shape[self.axis] // 2
        self.keep = lax.slice_in_dim(held, 0, half, axis=self.axis)
        away = lax.slice_in_dim(held, half, 2 * half, axis=self.axis)
        self.got_last = self.send(away, bit)
        self.bit = bit
        self.order.mark(away)

    def finish(self):
        while self.got_last is not None:
            (got,) = self.order.gate(self.got_last)
            self.halve(self.keep + got, self.bit * 2)
        return self.keep


def make_per_device(dp_size, t_size):
    def per_device(
        tokens,
        lengths,
        out_grad,
        input_gain,
        mamba_gate_weight,
        mamba_in_weight,
        state_weight,
        step_weight,
        conv_weight,
        conv_bias,
        conv_state_weight,
        conv_state_bias,
        step_bias,
        decay_log,
        skip_scale,
        mamba_gain,
        mamba_out_weight,
        query_weight,
        key_value_weight,
        attn_out_weight,
        ffn_gain,
        gate_weight,
        up_weight,
        down_weight,
    ):
        micro = tokens.shape[0]
        count = tokens.shape[1]
        width = tokens.shape[2]
        half = count // 2
        local_heads = step_weight.shape[1]
        q_local = query_weight.shape[1] // AHDIM
        kv_width = key_value_weight.shape[1] // 2
        group_size = AHEADS // KVHEADS
        me_dp = lax.axis_index("dp")
        me_t = lax.axis_index("tensor")
        core = lax.rem(me_t, 2)
        kv_head = me_t * q_local // group_size
        key_weight = lax.dynamic_slice_in_dim(key_value_weight, kv_head * AHDIM, AHDIM, 1)
        value_weight = lax.dynamic_slice_in_dim(
            key_value_weight, kv_width + kv_head * AHDIM, AHDIM, 1
        )
        scale = AHDIM ** (-0.5)
        rows = jnp.arange(count)
        causal = rows[:, None] >= rows[None, :]
        lower = causal.astype(f32)
        freqs = rope_base ** (-(jnp.arange(AHDIM // 2).astype(f32) * 2.0) / AHDIM)
        angles = rows.astype(f32)[:, None] * freqs[None, :]
        cosine = jnp.cos(angles)[:, None, :]
        sine = jnp.sin(angles)[:, None, :]
        skip_rep = jnp.repeat(skip_scale, MHDIM)
        rates = jnp.exp(decay_log)

        def t_swap(values, bit):
            return swap(values, "tensor", t_size, bit)

        def t_total(values):
            bit = 1
            while bit < t_size:
                values = values + t_swap(values, bit)
                bit *= 2
            return values

        def mine(values):
            return lax.dynamic_slice_in_dim(values, core * half, half, 0)

        def other(values):
            return lax.dynamic_slice_in_dim(values, (1 - core) * half, half, 0)

        def relative(values):
            return jnp.concatenate([mine(values), other(values)], axis=0)

        def in_order(own, far):
            return jnp.where(
                core == 0,
                jnp.concatenate([own, far], axis=0),
                jnp.concatenate([far, own], axis=0),
            )

        def half_sum(own, far):
            own = own + t_swap(far, 1)
            bit = 2
            while bit < t_size // 2:
                own = own + t_swap(own, bit)
                bit *= 2
            return own, t_swap(own, bit)

        block = width // dp_size

        def block_order(values):
            return [
                lax.dynamic_slice_in_dim(values, jnp.bitwise_xor(me_dp, r) * block, block, 1)
                for r in range(dp_size)
            ]

        order = Order()

        def forward(index, slot):
            inputs = slot.astype(f32)
            inv_one = lax.rsqrt(jnp.mean(inputs * inputs, axis=-1, keepdims=True) + epsilon)
            unit_one = inputs * inv_one
            normed = (unit_one * input_gain).astype(bf16)
            zgate = plain_dot(normed, mamba_gate_weight)
            xpre = plain_dot(normed, mamba_in_weight)
            statepre = plain_dot(normed, state_weight)
            steppre = plain_dot(normed, step_weight)
            xlin = causal_conv(xpre, conv_weight, conv_bias)
            xconv = jax.nn.silu(xlin).astype(bf16)
            xvals = xconv.astype(f32)
            slin = causal_conv(statepre, conv_state_weight, conv_state_bias)
            sconv = jax.nn.silu(slin).astype(bf16)
            binput = sconv[:, :STATE]
            cinput = sconv[:, STATE:]
            inner = right_trans(cinput, binput)
            stepsize = jax.nn.softplus(steppre + step_bias)
            cumul = lax.dot_general(
                -stepsize * rates,
                lower,
                (((0,), (1,)), ((), ())),
                precision=lax.Precision.HIGHEST,
                preferred_element_type=f32,
            )
            differ = cumul[:, :, None] - cumul[:, None, :]
            decay = jnp.where(causal, jnp.exp(jnp.where(causal, differ, 0.0)), 0.0)
            mixing = (inner[None] * decay).astype(bf16)
            step_rep = jnp.repeat(stepsize, MHDIM, axis=1)
            weighted = (step_rep * xvals).astype(bf16)
            wblock = weighted.reshape(count, local_heads, MHDIM)
            ssd = jnp.einsum("hts,shp->thp", mixing, wblock, preferred_element_type=f32).reshape(
                count, -1
            )
            ssd = ssd + skip_rep * xvals
            zsig = jax.nn.sigmoid(zgate)
            zsilu = zgate * zsig
            gated = ssd * zsilu
            total_square = t_total(jnp.sum(gated * gated, axis=-1))
            inv_mamba = lax.rsqrt(total_square / DSSM + epsilon)[:, None]
            scaled = (gated * inv_mamba * mamba_gain).astype(bf16)
            query_pre = plain_dot(normed, query_weight).reshape(count, q_local, AHDIM)
            query = rotary(query_pre, cosine, sine).astype(bf16)
            key_pre = plain_dot(normed, key_weight)
            keys = rotary(key_pre[:, None, :], cosine, sine)[:, 0].astype(bf16)
            values = plain_dot(normed, value_weight).astype(bf16)
            valid_keys = causal & (rows[None, :] < lengths[index])
            scores = jnp.einsum("thd,sd->hts", query, keys, preferred_element_type=f32) * scale
            masked = jnp.where(valid_keys[None], scores, -1e30)
            peak = jnp.max(masked, axis=-1, keepdims=True)
            expo = jnp.exp(masked - peak)
            total_exp = jnp.sum(expo, axis=-1, keepdims=True)
            log_total = peak + jnp.log(total_exp)
            probs = (expo / total_exp).astype(bf16)
            context = jnp.einsum("hts,sd->thd", probs, values, preferred_element_type=f32)
            context = context.reshape(count, -1).astype(bf16)
            far = plain_dot(other(scaled), mamba_out_weight) + plain_dot(
                other(context), attn_out_weight
            )
            own = plain_dot(mine(scaled), mamba_out_weight) + plain_dot(
                mine(context), attn_out_weight
            )
            mixed_own, mixed_far = half_sum(own, far)
            order.mark(mixed_own)
            return dict(
                mixed_own=mixed_own, mixed_far=mixed_far,
                inputs=inputs, inv_one=inv_one, unit_one=unit_one, normed=normed, zgate=zgate,
                xpre=xpre, statepre=statepre, steppre=steppre, xlin=xlin, xvals=xvals, slin=slin,
                binput=binput, cinput=cinput, inner=inner, stepsize=stepsize, decay=decay,
                mixing=mixing, step_rep=step_rep, wblock=wblock, ssd=ssd, zsig=zsig, zsilu=zsilu,
                gated=gated, inv_mamba=inv_mamba, scaled=scaled, query=query, keys=keys,
                values=values, valid_keys=valid_keys, log_total=log_total, context=context,
            )

        def feed_forward(index, k):
            own, far = order.gate(k["mixed_own"], k["mixed_far"])
            hidden_own = mine(k["inputs"]) + own + far
            hidden = jnp.concatenate([hidden_own, t_swap(hidden_own, 1)], axis=0)
            inv_two = lax.rsqrt(jnp.mean(hidden * hidden, axis=-1, keepdims=True) + epsilon)
            unit_two = hidden * inv_two
            normed_two = (unit_two * ffn_gain).astype(bf16)
            gate = plain_dot(normed_two, gate_weight)
            upper = plain_dot(normed_two, up_weight)
            gsig = jax.nn.sigmoid(gate)
            gsilu = gate * gsig
            inner_ffn = (gsilu * upper).astype(bf16)
            valid = (rows < lengths[index]).astype(f32)[:, None]
            cotangent = relative(out_grad[index].astype(f32) * valid)
            cot_low = cotangent.astype(bf16)
            d_inner_ffn = right_trans(cot_low, down_weight)
            d_gate = (d_inner_ffn * upper * gsig * (1.0 + gate * (1.0 - gsig))).astype(bf16)
            d_up = (d_inner_ffn * gsilu).astype(bf16)
            far = right_trans(d_gate[half:], gate_weight) + right_trans(d_up[half:], up_weight)
            own = right_trans(d_gate[:half], gate_weight) + right_trans(d_up[:half], up_weight)
            back_own, back_far = half_sum(own, far)
            order.mark(back_own)
            k.update(
                back_own=back_own, back_far=back_far,
                hidden=hidden, inv_two=inv_two[:half], unit_two=unit_two[:half],
                normed_two=normed_two, inner_ffn=inner_ffn, cotangent=cotangent, cot_low=cot_low,
                d_gate=d_gate, d_up=d_up,
            )

        def output_sum(k):
            (inner_ffn,) = order.gate(k["inner_ffn"])
            k["ffn_own"], k["ffn_far"] = half_sum(
                plain_dot(inner_ffn[:half], down_weight), plain_dot(inner_ffn[half:], down_weight)
            )
            order.mark(k["ffn_own"])

        def output(k):
            own, far = order.gate(k["ffn_own"], k["ffn_far"])
            ffn_own = own + far
            out = k["hidden"] + jnp.concatenate([ffn_own, t_swap(ffn_own, 1)], axis=0)
            out = in_order(out[:half], out[half:]).astype(bf16)
            order.mark(out)
            return out

        def back_attention(k):
            own, far = order.gate(k["back_own"], k["back_far"])
            d_normed_two = own + far
            unit_two = k["unit_two"]
            g_ffn_gain = jnp.sum(d_normed_two * unit_two, axis=0)
            d_unit_two = d_normed_two * ffn_gain
            d_rest = k["inv_two"] * (
                d_unit_two - unit_two * jnp.mean(d_unit_two * unit_two, axis=-1, keepdims=True)
            )
            d_hidden = k["cotangent"][:half] + d_rest
            d_both = k["cotangent"] + jnp.concatenate([d_rest, t_swap(d_rest, 1)], axis=0)
            d_mixed = in_order(d_both[:half], d_both[half:]).astype(bf16)
            d_context = (
                right_trans(d_mixed, attn_out_weight).astype(bf16).reshape(count, q_local, AHDIM)
            )
            again = (
                jnp.einsum("thd,sd->hts", k["query"], k["keys"], preferred_element_type=f32)
                * scale
            )
            probs_full = jnp.where(k["valid_keys"][None], jnp.exp(again - k["log_total"]), 0.0)
            probs_low = probs_full.astype(bf16)
            d_probs = jnp.einsum("thd,sd->hts", d_context, k["values"], preferred_element_type=f32)
            d_values = jnp.einsum("hts,thd->sd", probs_low, d_context, preferred_element_type=f32)
            delta = jnp.sum(probs_full * d_probs, axis=-1, keepdims=True)
            d_scores = (probs_full * (d_probs - delta)).astype(bf16)
            d_query = (
                jnp.einsum("hts,sd->thd", d_scores, k["keys"], preferred_element_type=f32) * scale
            )
            d_keys = (
                jnp.einsum("hts,thd->sd", d_scores, k["query"], preferred_element_type=f32) * scale
            )
            d_query_pre = rotary_back(d_query, cosine, sine).reshape(count, -1).astype(bf16)
            d_key_full = rotary_back(d_keys[:, None, :], cosine, sine)[:, 0]
            kv_far = jnp.where(core == 0, d_values, d_key_full)
            kv_own = jnp.where(core == 0, d_key_full, d_values)
            d_scaled = right_trans(d_mixed, mamba_out_weight)
            gated = k["gated"]
            inv_mamba = k["inv_mamba"]
            g_mamba_gain = jnp.sum(d_scaled * gated * inv_mamba, axis=0)
            d_norm_in = d_scaled * mamba_gain
            cross = t_total(jnp.sum(d_norm_in * gated, axis=-1))
            d_gated = inv_mamba * d_norm_in - gated * inv_mamba**3 * cross[:, None] / DSSM
            d_ssd = (d_gated * k["zsilu"]).astype(bf16)
            zgate, zsig = k["zgate"], k["zsig"]
            d_zgate = (d_gated * k["ssd"] * zsig * (1.0 + zgate * (1.0 - zsig))).astype(bf16)
            k.update(
                d_mixed=d_mixed, d_hidden=d_hidden, g_ffn_gain=g_ffn_gain, d_ssd=d_ssd,
                g_mamba_gain=g_mamba_gain, d_query_pre=d_query_pre, d_key_full=d_key_full,
                d_values=d_values, d_zgate=d_zgate, kv_sum=kv_own + t_swap(kv_far, 1),
                d_early=jnp.concatenate([d_zgate, d_query_pre], axis=1),
            )
            order.mark(d_ssd, d_zgate, d_query_pre)

        def back_states(k):
            (d_ssd,) = order.gate(k["d_ssd"])
            d_ssd_full = d_ssd.astype(f32)
            xvals, stepsize, decay = k["xvals"], k["stepsize"], k["decay"]
            g_skip = jnp.sum((d_ssd_full * xvals).reshape(count, local_heads, MHDIM), axis=(0, 2))
            dblock = d_ssd.reshape(count, local_heads, MHDIM)
            d_mixing = jnp.einsum("thp,shp->hts", dblock, k["wblock"], preferred_element_type=f32)
            d_weighted = jnp.einsum(
                "hts,thp->shp", k["mixing"], dblock, preferred_element_type=f32
            ).reshape(count, -1)
            d_xvals = d_ssd_full * skip_rep + d_weighted * k["step_rep"]
            d_step = jnp.sum((d_weighted * xvals).reshape(count, local_heads, MHDIM), axis=-1)
            d_inner = jnp.sum(d_mixing * decay, axis=0).astype(bf16)
            flow = d_mixing * k["inner"][None] * decay
            d_cumul = jnp.sum(flow, axis=2) - jnp.sum(flow, axis=1)
            d_logdecay = lax.dot_general(
                lower,
                d_cumul,
                (((0,), (1,)), ((), ())),
                precision=lax.Precision.HIGHEST,
                preferred_element_type=f32,
            )
            d_step = d_step - d_logdecay * rates
            g_decay_log = jnp.sum(-d_logdecay * stepsize * rates, axis=0)
            d_steppre_full = d_step * jax.nn.sigmoid(k["steppre"] + step_bias)
            g_step_bias = jnp.sum(d_steppre_full, axis=0)
            d_steppre = d_steppre_full.astype(bf16)
            k.update(
                d_inner=d_inner, d_xvals=d_xvals, d_steppre=d_steppre, g_skip=g_skip,
                g_decay_log=g_decay_log, g_step_bias=g_step_bias,
            )
            order.mark(d_inner, d_xvals, d_steppre)

        pad_step = 128 - local_heads

        def back_inputs(k):
            d_inner, d_xvals = order.gate(k["d_inner"], k["d_xvals"])
            d_cinput = plain_dot(d_inner, k["binput"])
            d_binput = left_trans(d_inner, k["cinput"])
            d_slin = jnp.concatenate([d_binput, d_cinput], axis=1) * silu_slope(k["slin"])
            d_statepre_full, g_conv_state_weight, g_conv_state_bias = conv_back(
                d_slin, k["statepre"], conv_state_weight
            )
            d_xlin = d_xvals * silu_slope(k["xlin"])
            d_xpre_full, g_conv_weight, g_conv_bias = conv_back(d_xlin, k["xpre"], conv_weight)
            d_xpre = d_xpre_full.astype(bf16)
            piece = d_statepre_full.shape[1] // t_size
            parts = [
                lax.dynamic_slice_in_dim(
                    d_statepre_full, jnp.bitwise_xor(me_t, q) * piece, piece, 1
                )
                for q in range(t_size)
            ]
            pieces = halving_order(list(range(0, t_size, 2)), 2, t_size)
            state_sum = jnp.concatenate([parts[q] for q in pieces], axis=1) + t_swap(
                jnp.concatenate([parts[q ^ 1] for q in pieces], axis=1), 1
            )
            bit = 2
            while bit < t_size:
                cut = state_sum.shape[1] // 2
                state_sum = state_sum[:, :cut] + t_swap(state_sum[:, cut:], bit)
                bit *= 2
            k["shared"] = jnp.concatenate([state_sum, k["kv_sum"]], axis=1).astype(bf16)
            k["d_xpre"] = d_xpre
            back = jnp.concatenate(
                [
                    k["d_zgate"],
                    d_xpre,
                    k["d_query_pre"],
                    d_statepre_full.astype(bf16),
                    k["d_key_full"].astype(bf16),
                    k["d_values"].astype(bf16),
                    jnp.pad(k["d_steppre"], ((0, 0), (0, pad_step))),
                ],
                axis=1,
            )
            k["norm_own"], k["norm_far"] = half_sum(
                right_trans(mine(back), back_weight), right_trans(other(back), back_weight)
            )
            k.update(
                g_conv_weight=g_conv_weight, g_conv_bias=g_conv_bias,
                g_conv_state_weight=g_conv_state_weight, g_conv_state_bias=g_conv_state_bias,
            )
            order.mark(k["norm_own"], d_xpre)

        def input_grad(k):
            own, far = order.gate(k["norm_own"], k["norm_far"])
            d_normed = own + far
            unit_own = mine(k["unit_one"])
            k["g_input_gain"] = jnp.sum(d_normed * unit_own, axis=0)
            d_unit_one = d_normed * input_gain
            grad_own = k["d_hidden"] + mine(k["inv_one"]) * (
                d_unit_one - unit_own * jnp.mean(d_unit_one * unit_own, axis=-1, keepdims=True)
            )
            grad = in_order(grad_own, t_swap(grad_own, 1))
            order.mark(grad)
            return grad

        slots = []
        for index in range(micro):
            slot = tokens[index]
            if index:
                (slot,) = order.gate(slot)
            slots.append(forward(index, slot))
        for index in range(micro):
            feed_forward(index, slots[index])

        def joined(name):
            return jnp.concatenate([k[name] for k in slots], axis=0)

        def scatter(blocks, whole, axis):
            return Scatter(order, dp_size, blocks, whole, axis)

        def starts(work):
            (work.whole,) = order.gate(work.whole)
            order.mark(work.start_first())
            order.mark(work.start_later())

        two_blocks = block_order(joined("normed_two"))
        w_down = scatter(block_order(joined("cot_low")), joined("inner_ffn"), 1)
        w_gate = scatter(two_blocks, joined("d_gate"), 0)
        w_up = scatter(two_blocks, joined("d_up"), 0)
        for work in (w_down, w_gate, w_up):
            starts(work)
        for k in slots:
            output_sum(k)
        back_weight = jnp.concatenate(
            [
                mamba_gate_weight,
                mamba_in_weight,
                query_weight,
                state_weight,
                key_weight,
                value_weight,
                jnp.pad(step_weight, ((0, 0), (0, pad_step))),
            ],
            axis=1,
        )
        back_attention(slots[0])
        w_down.take_first()
        back_states(slots[0])
        back_inputs(slots[0])
        w_down.take_later()
        for k in slots[1:]:
            back_attention(k)
        w_outs = scatter(
            block_order(joined("d_mixed")),
            jnp.concatenate([joined("scaled"), joined("context")], axis=1),
            1,
        )
        starts(w_outs)
        w_gate.take_first()
        one_blocks = block_order(joined("normed"))
        w_early = scatter(one_blocks, joined("d_early"), 0)
        starts(w_early)
        for k in slots[1:]:
            back_states(k)
        w_gate.take_later()
        for k in slots[1:]:
            back_inputs(k)
        w_step = scatter(one_blocks, joined("d_steppre"), 1)
        w_late = scatter(
            one_blocks, jnp.concatenate([joined("d_xpre"), joined("shared")], axis=1), 0
        )
        starts(w_step)
        starts(w_late)
        outputs_list = [output(k) for k in slots]
        w_up.take_first()
        g_down = w_down.finish()
        w_up.take_later()
        g_gate = w_gate.finish()
        grads_list = [input_grad(k) for k in slots]

        def total(name):
            value = slots[0][name]
            for k in slots[1:]:
                value = value + k[name]
            return value

        once = me_t < 2
        names = [
            "g_conv_state_weight", "g_conv_state_bias", "g_input_gain", "g_ffn_gain",
            "g_conv_weight", "g_conv_bias", "g_step_bias", "g_decay_log", "g_skip",
            "g_mamba_gain",
        ]
        small = {name: total(name) for name in names}
        for name in ("g_input_gain", "g_ffn_gain"):
            small[name] = jnp.where(once, small[name], 0.0)
        vector = jnp.concatenate([small[name].reshape(-1) for name in names])
        (vector,) = order.gate(vector)
        bit = 1
        while bit < dp_size:
            vector = vector + swap(vector, "dp", dp_size, bit)
            bit *= 2
        order.mark(vector)
        shared_size = sum(small[name].size for name in names[:4])
        wide_vector = t_total(vector[:shared_size])
        start = 0
        for name in names:
            shape, size = small[name].shape, small[name].size
            source = wide_vector if start < shared_size else vector
            small[name] = source[start : start + size].reshape(shape)
            start += size
        place = me_dp * t_size + me_t
        share = conv_state_bias.shape[0] // (dp_size * t_size)
        g_conv_state_weight = lax.dynamic_slice_in_dim(
            small["g_conv_state_weight"], place * share, share, 1
        )
        g_conv_state_bias = lax.dynamic_slice_in_dim(
            small["g_conv_state_bias"], place * share, share, 0
        )
        g_input_gain = lax.dynamic_slice_in_dim(small["g_input_gain"], me_dp * block, block, 0)
        g_ffn_gain = lax.dynamic_slice_in_dim(small["g_ffn_gain"], me_dp * block, block, 0)
        heads = [small[name] for name in names[4:]]

        w_outs.take_first()
        g_up = w_up.finish()
        w_outs.take_later()
        w_early.take_first()
        g_outs = w_outs.finish()
        w_early.take_later()
        w_step.take_first()
        w_step.take_later()
        w_late.take_first()
        g_early = w_early.finish()
        w_late.take_later()
        g_step = w_step.finish().T
        g_late = w_late.finish()

        mamba_cols = mamba_in_weight.shape[1]
        tail = g_late[:, mamba_cols:]
        sub = block // t_size
        rowsets = []
        for q in range(t_size):
            part = lax.dynamic_slice_in_dim(tail, jnp.bitwise_xor(me_t, q) * sub, sub, 0)
            rowsets.append(part if q == 0 else t_swap(part, q))
        stacked = jnp.stack(rowsets)
        piece = state_weight.shape[1] // t_size
        sources = [
            lax.dynamic_index_in_dim(stacked, jnp.bitwise_xor(me_t, j), 0, keepdims=False)
            for j in range(t_size)
        ]
        g_state = jnp.concatenate([s[:, :piece] for s in sources], axis=1)
        pairs = t_size // 2
        g_kv = jnp.concatenate(
            [sources[(b % pairs) * 2 + b // pairs][:, piece:] for b in range(t_size)], axis=1
        )
        gate_cols = mamba_gate_weight.shape[1]
        mamba_rows = mamba_out_weight.shape[0]
        return (
            jnp.stack(outputs_list),
            jnp.stack(grads_list),
            g_input_gain,
            g_early[:, :gate_cols],
            g_late[:, :mamba_cols],
            g_state,
            g_step,
            heads[0],
            heads[1],
            g_conv_state_weight,
            g_conv_state_bias,
            heads[2],
            heads[3],
            heads[4],
            heads[5],
            g_outs[:mamba_rows],
            g_early[:, gate_cols:],
            g_kv,
            g_outs[mamba_rows:],
            g_ffn_gain,
            g_gate,
            g_up,
            g_down,
        )

    return per_device


def solution(mesh):
    placed = (
        P("dp", None, None),
        P("dp"),
        P("dp", None, None),
        P(),
        P(None, "tensor"),
        P(None, "tensor"),
        P(),
        P(None, "tensor"),
        P(None, "tensor"),
        P("tensor"),
        P(),
        P(),
        P("tensor"),
        P("tensor"),
        P("tensor"),
        P("tensor"),
        P("tensor", None),
        P(None, "tensor"),
        P(),
        P("tensor", None),
        P(),
        P(None, "tensor"),
        P(None, "tensor"),
        P("tensor", None),
    )
    return jax.shard_map(
        make_per_device(mesh.shape["dp"], mesh.shape["tensor"]),
        mesh=mesh,
        in_specs=placed,
        out_specs=(
            P("dp", None, None),
            P("dp", None, None),
            P("dp"),
            P("dp", "tensor"),
            P("dp", "tensor"),
            P(("dp", "tensor"), None),
            P("dp", "tensor"),
            P(None, "tensor"),
            P("tensor"),
            P(None, ("dp", "tensor")),
            P(("dp", "tensor")),
            P("tensor"),
            P("tensor"),
            P("tensor"),
            P("tensor"),
            P("tensor", "dp"),
            P("dp", "tensor"),
            P(("dp", "tensor"), None),
            P("tensor", "dp"),
            P("dp"),
            P("dp", "tensor"),
            P("dp", "tensor"),
            P("tensor", "dp"),
        ),
        check_vma=False,
    )
```

```python
import functools

import jax
import jax.numpy as jnp
from jax import lax
from jax.experimental import pallas as pl
from jax.experimental.pallas import tpu as pltpu
from jax.sharding import PartitionSpec as P

MHDIM = 64
STATE = 256
AHEADS = 8
KVHEADS = 2
AHDIM = 128
DSSM = 3072

epsilon = 1e-05
rope_base = 100000000000.0
f32 = jnp.float32
bf16 = jnp.bfloat16


def plain_dot(left, right):
    return jnp.dot(left, right, preferred_element_type=f32)


def right_trans(left, right):
    return lax.dot_general(left, right, (((1,), (1,)), ((), ())), preferred_element_type=f32)


def left_trans(left, right):
    return lax.dot_general(left, right, (((0,), (0,)), ((), ())), preferred_element_type=f32)


def silu_slope(values):
    sig = jax.nn.sigmoid(values)
    return sig * (1.0 + values * (1.0 - sig))


LANES = 128
BLOCK = 128


def shifted(values, steps, row):
    if steps == 0:
        return values
    count = values.shape[0]
    moved = pltpu.roll(values, steps % count, 0)
    if steps > 0:
        return jnp.where(row >= steps, moved, 0.0)
    return jnp.where(row < count + steps, moved, 0.0)


def tap_sum(values, taps, bias):
    row = lax.broadcasted_iota(jnp.int32, values.shape, 0)
    width = taps.shape[0]
    total = jnp.zeros_like(values) + bias
    for k in range(width):
        total = total + shifted(values, width - 1 - k, row) * taps[k : k + 1, :]
    return total


def tap_back(grads, values, taps):
    row = lax.broadcasted_iota(jnp.int32, values.shape, 0)
    width = taps.shape[0]
    back = jnp.zeros_like(values)
    tap_grads = []
    for k in range(width):
        steps = width - 1 - k
        back = back + shifted(grads, -steps, row) * taps[k : k + 1, :]
        tap_grads.append(jnp.sum(grads * shifted(values, steps, row), axis=0, keepdims=True))
    return back, jnp.concatenate(tap_grads, axis=0)


def column_of(values, lane, index):
    return jnp.sum(jnp.where(lane == index, values, 0.0), axis=1, keepdims=True)


def exact_dot(left, right):
    return jnp.dot(left, right, precision=lax.Precision.HIGHEST, preferred_element_type=f32)


def turned(values, cosine, sine):
    return values * cosine + pltpu.roll(values, AHDIM // 2, 1) * sine


def scores_of(query, keys, lo, hi, length):
    scores = right_trans(query[lo:hi], keys[:hi]) * AHDIM ** (-0.5)
    t = lax.broadcasted_iota(jnp.int32, (hi - lo, hi), 0) + lo
    s = lax.broadcasted_iota(jnp.int32, (hi - lo, hi), 1)
    return scores, (t >= s) & (s < length)


def attention_forward(query_pre, key_pre, value_pre, cosine, sine, length, query, keys, values, logs, context):
    count, width = query.shape
    keys[...] = turned(key_pre, cosine, sine).astype(bf16)
    values[...] = value_pre.astype(bf16)
    lane = lax.broadcasted_iota(jnp.int32, (count, LANES), 1)
    kept = jnp.zeros((count, LANES), f32)
    for h in range(width // AHDIM):
        lanes = slice(h * AHDIM, (h + 1) * AHDIM)
        query[:, lanes] = turned(query_pre[:, lanes], cosine, sine).astype(bf16)
        found = []
        for i in range(count // BLOCK):
            lo, hi = i * BLOCK, (i + 1) * BLOCK
            scores, valid = scores_of(query[:, lanes], keys[...], lo, hi, length)
            masked = jnp.where(valid, scores, -1e30)
            peak = jnp.max(masked, axis=1, keepdims=True)
            expo = jnp.exp(masked - peak)
            total = jnp.sum(expo, axis=1, keepdims=True)
            found.append(peak + jnp.log(total))
            probs = (expo / total).astype(bf16)
            context[lo:hi, lanes] = plain_dot(probs, values[:hi, :]).astype(bf16)
        kept = jnp.where(lane == h, jnp.concatenate(found, axis=0), kept)
    logs[...] = kept


def attention_backward(d_context, query, keys, values, logs, cosine, sine, length, d_query_pre, d_keys, d_values):
    count, width = query.shape
    lane = lax.broadcasted_iota(jnp.int32, (count, LANES), 1)
    scale = AHDIM ** (-0.5)
    key_total = jnp.zeros((count, AHDIM), f32)
    value_total = jnp.zeros((count, AHDIM), f32)
    for h in range(width // AHDIM):
        lanes = slice(h * AHDIM, (h + 1) * AHDIM)
        log = column_of(logs[...], lane, h)
        pieces = []
        for i in range(count // BLOCK):
            lo, hi = i * BLOCK, (i + 1) * BLOCK
            scores, valid = scores_of(query[:, lanes], keys[...], lo, hi, length)
            probs = jnp.where(valid, jnp.exp(scores - log[lo:hi]), 0.0)
            grads = d_context[lo:hi, lanes]
            d_probs = right_trans(grads, values[:hi, :])
            delta = jnp.sum(probs * d_probs, axis=1, keepdims=True)
            d_scores = (probs * (d_probs - delta)).astype(bf16)
            pieces.append(plain_dot(d_scores, keys[:hi, :]) * scale)
            d_key = left_trans(d_scores, query[lo:hi, lanes]) * scale
            d_value = left_trans(probs.astype(bf16), grads)
            if hi < count:
                rest = jnp.zeros((count - hi, AHDIM), f32)
                d_key = jnp.concatenate([d_key, rest], axis=0)
                d_value = jnp.concatenate([d_value, rest], axis=0)
            key_total = key_total + d_key
            value_total = value_total + d_value
        d_query_pre[:, lanes] = turned(jnp.concatenate(pieces, axis=0), cosine, -sine).astype(bf16)
    d_keys[...] = turned(key_total, cosine, -sine)
    d_values[...] = value_total


def columns_of(channels, heads_width):
    places, start = {}, 0
    for name, size in (
        ("zgate", channels), ("query", heads_width), ("xpre", channels), ("state", 2 * STATE),
        ("key", AHDIM), ("value", AHDIM), ("step", LANES),
    ):
        places[name] = slice(start, start + size)
        start += size
    return places, start


def forward_kernel(
    lengths, proj, cosine, sine, conv_weight, conv_bias, state_taps, state_bias, step_bias, rates,
    skip_rep, gated, ssd, square, xconv, sconv, stepsize, cumul, inner, query, keys, values, logs,
    context, cumul_rows, *, slot, places,
):
    xpre, zgate = proj.at[:, places["xpre"]], proj.at[:, places["zgate"]]
    statepre, steppre = proj.at[:, places["state"]], proj.at[:, places["step"]]
    attention_forward(
        proj.at[:, places["query"]], proj[:, places["key"]], proj[:, places["value"]],
        cosine[...], sine[...], lengths[slot], query, keys, values, logs, context,
    )
    count, channels = xpre.shape
    xlin = tap_sum(xpre[...], conv_weight[...], conv_bias[...])
    xconv[...] = (xlin * jax.nn.sigmoid(xlin)).astype(bf16)
    slin = tap_sum(statepre[...], state_taps[...], state_bias[...])
    sconv[...] = (slin * jax.nn.sigmoid(slin)).astype(bf16)
    inner[...] = right_trans(sconv[:, STATE:], sconv[:, :STATE])
    step = jax.nn.softplus(steppre[...] + step_bias[...])
    stepsize[...] = step
    row = lax.broadcasted_iota(jnp.int32, (count, count), 0)
    col = lax.broadcasted_iota(jnp.int32, (count, count), 1)
    total = exact_dot(jnp.where(row >= col, 1.0, 0.0), -step * rates[...])
    cumul[...] = total
    cumul_rows[...] = total.T
    square[...] = jnp.zeros_like(square)

    def pair(p):
        lanes = slice(p * LANES, (p + 1) * LANES)
        lane = lax.broadcasted_iota(jnp.int32, (count, LANES), 1)
        xvals = xconv[:, lanes].astype(f32)
        low_half = lane < MHDIM
        step_rep = jnp.where(
            low_half, column_of(stepsize[...], lane, 2 * p), column_of(stepsize[...], lane, 2 * p + 1)
        )
        weighted = (step_rep * xvals).astype(bf16)
        columns = [column_of(cumul[...], lane, 2 * p + h) for h in range(2)]
        for i in range(count // BLOCK):
            lo, hi = i * BLOCK, (i + 1) * BLOCK
            results = []
            for h in range(2):
                differ = columns[h][lo:hi] - cumul_rows[2 * p + h : 2 * p + h + 1, :hi]
                t = lax.broadcasted_iota(jnp.int32, (BLOCK, hi), 0) + lo
                s = lax.broadcasted_iota(jnp.int32, (BLOCK, hi), 1)
                decay = jnp.exp(jnp.where(t >= s, differ, -1e30))
                mixing = (inner[lo:hi, :hi] * decay).astype(bf16)
                results.append(plain_dot(mixing, weighted[:hi]))
            half = jnp.where(low_half[lo:hi], results[0], results[1])
            half = half + skip_rep[:, lanes] * xvals[lo:hi]
            ssd[lo:hi, lanes] = half
            z = zgate[lo:hi, lanes]
            value = half * (z * jax.nn.sigmoid(z))
            gated[lo:hi, lanes] = value
            square[lo:hi, :] += value * value

    for p in range(channels // LANES):
        pair(p)


def full(*shape):
    return jax.ShapeDtypeStruct(shape, f32)


def low(*shape):
    return jax.ShapeDtypeStruct(shape, bf16)


def in_vmem(count):
    return [pl.BlockSpec(memory_space=pltpu.VMEM)] * count


def mixers_forward(slot, channels, heads_width, lengths, proj, *rest):
    count = proj.shape[0]
    return pl.pallas_call(
        functools.partial(
            forward_kernel, slot=slot, places=columns_of(channels, heads_width)[0]
        ),
        out_shape=(
            full(count, channels), full(count, channels), full(count, LANES), low(count, channels),
            low(count, 2 * STATE), full(count, LANES), full(count, LANES), full(count, count),
            low(count, heads_width), low(count, AHDIM), low(count, AHDIM), full(count, LANES),
            low(count, heads_width),
        ),
        in_specs=[pl.BlockSpec(memory_space=pltpu.SMEM)] + in_vmem(1 + len(rest)),
        out_specs=tuple(in_vmem(13)),
        scratch_shapes=[pltpu.VMEM((LANES, count), f32)],
        compiler_params=pltpu.CompilerParams(vmem_limit_bytes=48 * 2**20),
        cost_estimate=pl.CostEstimate(
            flops=9 * 10**9, bytes_accessed=20 * 2**20, transcendentals=5 * 10**6
        ),
    )(lengths, proj, *rest)


def backward_kernel(
    lengths, d_mixer, gated_in, inv_cross, gain, proj, ssd, xconv, sconv, stepsize, cumul, inner,
    query, keys, values, logs, cosine, sine, conv_weight, conv_bias, state_taps, state_bias,
    step_bias, rates, skip_rep,
    back, d_statepre, d_keys, d_values, g_conv, g_state, g_heads, g_skip, g_gain,
    d_ssd, d_xvals, cumul_rows, d_inner, row_sums, col_sums, d_step, *, slot, places,
):
    count, channels = ssd.shape
    xpre, zgate = proj.at[:, places["xpre"]], proj.at[:, places["zgate"]]
    statepre, steppre = proj.at[:, places["state"]], proj.at[:, places["step"]]
    attention_backward(
        d_mixer[:, channels:].astype(bf16), query, keys, values, logs, cosine[...], sine[...],
        lengths[slot], back.at[:, places["query"]], d_keys, d_values,
    )
    back[:, places["key"]] = d_keys[...].astype(bf16)
    back[:, places["value"]] = d_values[...].astype(bf16)
    d_zgate, d_xpre = back.at[:, places["zgate"]], back.at[:, places["xpre"]]
    d_steppre = back.at[:, places["step"]]
    d_scaled = d_mixer[:, :channels]
    g_gain[...] = jnp.sum(d_scaled * gated_in[...] * inv_cross[:, 0:1], axis=0, keepdims=True)
    inv = inv_cross[:, 0:1]
    cross = inv_cross[:, 1:2]
    d_gated = inv * (d_scaled * gain[...]) - gated_in[...] * cross
    z = zgate[...]
    sig = jax.nn.sigmoid(z)
    d_low = (d_gated * (z * sig)).astype(bf16)
    d_ssd[...] = d_low
    d_zgate[...] = (d_gated * ssd[...] * sig * (1.0 + z * (1.0 - sig))).astype(bf16)
    g_skip[...] = jnp.sum(d_low.astype(f32) * xconv[...].astype(f32), axis=0, keepdims=True)
    cumul_rows[...] = cumul[...].T
    d_inner[...] = jnp.zeros_like(d_inner)
    row_sums[...] = jnp.zeros_like(row_sums)
    col_sums[...] = jnp.zeros_like(col_sums)
    d_step[...] = jnp.zeros_like(d_step)

    def pair(p):
        lanes = slice(p * LANES, (p + 1) * LANES)
        lane = lax.broadcasted_iota(jnp.int32, (count, LANES), 1)
        low_half = lane < MHDIM
        xvals = xconv[:, lanes].astype(f32)
        step_rep = jnp.where(
            low_half, column_of(stepsize[...], lane, 2 * p), column_of(stepsize[...], lane, 2 * p + 1)
        )
        weighted = (step_rep * xvals).astype(bf16)
        grads = d_ssd[:, lanes]
        columns = [column_of(cumul[...], lane, 2 * p + h) for h in range(2)]
        pieces = []
        for h in range(2):
            only = jnp.where(low_half == (h == 0), grads, jnp.zeros_like(grads))
            back_part = jnp.zeros((count, LANES), f32)
            sums = []
            col_total = jnp.zeros((1, count), f32)
            for i in range(count // BLOCK):
                lo, hi = i * BLOCK, (i + 1) * BLOCK
                differ = columns[h][lo:hi] - cumul_rows[2 * p + h : 2 * p + h + 1, :hi]
                t = lax.broadcasted_iota(jnp.int32, (BLOCK, hi), 0) + lo
                s = lax.broadcasted_iota(jnp.int32, (BLOCK, hi), 1)
                decay = jnp.exp(jnp.where(t >= s, differ, -1e30))
                mixing = inner[lo:hi, :hi] * decay
                part = left_trans(mixing.astype(bf16), only[lo:hi])
                d_mixing = right_trans(only[lo:hi], weighted[:hi])
                d_inner[lo:hi, :hi] += d_mixing * decay
                flow = d_mixing * mixing
                sums.append(jnp.sum(flow, axis=1, keepdims=True))
                down = jnp.sum(flow, axis=0, keepdims=True)
                if hi < count:
                    part = jnp.concatenate([part, jnp.zeros((count - hi, LANES), f32)], axis=0)
                    down = jnp.concatenate([down, jnp.zeros((1, count - hi), f32)], axis=1)
                back_part = back_part + part
                col_total = col_total + down
            here = lane == 2 * p + h
            row_sums[...] = jnp.where(here, jnp.concatenate(sums, axis=0), row_sums[...])
            col_sums[2 * p + h : 2 * p + h + 1, :] = col_total
            pieces.append(back_part)
        d_weighted = pieces[0] + pieces[1]
        d_xvals[:, lanes] = grads.astype(f32) * skip_rep[:, lanes] + d_weighted * step_rep
        product = d_weighted * xvals
        for h in range(2):
            value = jnp.sum(
                jnp.where(low_half == (h == 0), product, 0.0), axis=1, keepdims=True
            )
            d_step[...] = jnp.where(lane == 2 * p + h, value, d_step[...])

    for p in range(channels // LANES):
        pair(p)

    d_cumul = row_sums[...] - col_sums[...].T
    row = lax.broadcasted_iota(jnp.int32, (count, count), 0)
    col = lax.broadcasted_iota(jnp.int32, (count, count), 1)
    d_logdecay = exact_dot(jnp.where(row <= col, 1.0, 0.0), d_cumul)
    rate = rates[...]
    d_full = (d_step[...] - d_logdecay * rate) * jax.nn.sigmoid(steppre[...] + step_bias[...])
    d_steppre[...] = d_full.astype(bf16)
    g_heads[0:1, :] = jnp.sum(d_full, axis=0, keepdims=True)
    g_heads[1:2, :] = jnp.sum(-d_logdecay * stepsize[...] * rate, axis=0, keepdims=True)

    d_in = d_inner[...].astype(bf16)
    d_c = plain_dot(d_in, sconv[:, :STATE])
    d_b = left_trans(d_in, sconv[:, STATE:])
    slin = tap_sum(statepre[...], state_taps[...], state_bias[...])
    d_slin = jnp.concatenate([d_b, d_c], axis=1) * silu_slope(slin)
    back_state, tap_grads = tap_back(d_slin, statepre[...], state_taps[...])
    d_statepre[...] = back_state
    back[:, places["state"]] = back_state.astype(bf16)
    g_state[...] = jnp.concatenate([tap_grads, jnp.sum(d_slin, axis=0, keepdims=True)], axis=0)
    xlin = tap_sum(xpre[...], conv_weight[...], conv_bias[...])
    d_xlin = d_xvals[...] * silu_slope(xlin)
    back_x, tap_grads = tap_back(d_xlin, xpre[...], conv_weight[...])
    d_xpre[...] = back_x.astype(bf16)
    g_conv[...] = jnp.concatenate([tap_grads, jnp.sum(d_xlin, axis=0, keepdims=True)], axis=0)


def mixers_backward(slot, slots, held, lengths, d_mixer, gated, inv_cross, gain, proj, ssd, *rest):
    count, channels = ssd.shape
    width = proj.shape[1]
    heads_width = d_mixer.shape[1] - channels
    taps = rest[11].shape[0]
    operands = (d_mixer, gated, inv_cross, gain, proj, ssd) + rest
    kernel = functools.partial(
        backward_kernel, slot=slot, places=columns_of(channels, heads_width)[0]
    )
    aliases = {}
    extra_specs, extra = [], ()
    if held is not None:
        aliases = {0: 0}
        extra_specs, extra = [pl.BlockSpec(memory_space=pl.ANY)], (held,)
        inside = kernel
        kernel = lambda _, *refs: inside(*refs)
    return pl.pallas_call(
        kernel,
        grid=(1,),
        out_shape=(
            low(slots * count, width), full(count, 2 * STATE), full(count, AHDIM),
            full(count, AHDIM), full(taps + 1, channels), full(taps + 1, 2 * STATE),
            full(2, LANES), full(1, channels), full(1, channels),
        ),
        in_specs=extra_specs
        + [pl.BlockSpec(memory_space=pltpu.SMEM)]
        + in_vmem(len(operands)),
        out_specs=tuple([pl.BlockSpec((count, width), lambda i: (slot, 0))] + in_vmem(8)),
        scratch_shapes=[
            pltpu.VMEM((count, channels), bf16),
            pltpu.VMEM((count, channels), f32),
            pltpu.VMEM((LANES, count), f32),
            pltpu.VMEM((count, count), f32),
            pltpu.VMEM((count, LANES), f32),
            pltpu.VMEM((LANES, count), f32),
            pltpu.VMEM((count, LANES), f32),
        ],
        input_output_aliases=aliases,
        compiler_params=pltpu.CompilerParams(vmem_limit_bytes=56 * 2**20),
        cost_estimate=pl.CostEstimate(
            flops=20 * 10**9, bytes_accessed=30 * 2**20, transcendentals=7 * 10**6
        ),
    )(*extra, lengths, *operands)


def swap(values, axis, size, bit):
    return lax.ppermute(values, axis, [(i, i ^ bit) for i in range(size)])


def halving_order(members, bit, limit):
    if bit >= limit:
        return members
    low = halving_order([m for m in members if not m & bit], bit * 2, limit)
    high = halving_order([m for m in members if m & bit], bit * 2, limit)
    return low + high


class Order:
    def __init__(self):
        self.last = ()

    def gate(self, *values):
        return lax.optimization_barrier((values, self.last))[0]

    def mark(self, *values):
        self.last = values


class Scatter:
    def __init__(self, order, size, blocks, whole, axis):
        self.order, self.size, self.axis = order, size, axis
        self.blocks, self.whole = blocks, whole
        evens = [r for r in range(size) if not r & 1]
        self.first = halving_order([r for r in evens if r & 2], 4, size)
        self.later = halving_order([r for r in evens if not r & 2], 4, size)

    def product(self, members, wait=None):
        picked = jnp.concatenate([self.blocks[r] for r in members], axis=1)
        if self.axis == 0:
            return left_trans(picked, self.whole)
        return left_trans(self.whole, picked)

    def send(self, values, bit):
        return swap(values, "dp", self.size, bit)

    def start_first(self):
        part = self.product([r ^ 1 for r in self.first])
        self.got_first = self.send(part, 1)
        return part

    def start_later(self):
        part = self.product([r ^ 1 for r in self.later])
        self.got_later = self.send(part, 1)
        return part

    def take_first(self):
        (got,) = self.order.gate(self.got_first)
        held = self.product(self.first) + got
        self.got_second = self.send(held, 2)
        self.order.mark(held)

    def take_later(self):
        got, second = self.order.gate(self.got_later, self.got_second)
        held = self.product(self.later) + got + second
        self.halve(held, 4)

    def halve(self, held, bit):
        if bit >= self.size:
            self.keep, self.got_last = held, None
            self.order.mark(held)
            return
        half = held.shape[self.axis] // 2
        self.keep = lax.slice_in_dim(held, 0, half, axis=self.axis)
        away = lax.slice_in_dim(held, half, 2 * half, axis=self.axis)
        self.got_last = self.send(away, bit)
        self.bit = bit
        self.order.mark(away)

    def finish(self):
        while self.got_last is not None:
            (got,) = self.order.gate(self.got_last)
            self.halve(self.keep + got, self.bit * 2)
        return self.keep


def make_per_device(dp_size, t_size):
    def per_device(
        tokens,
        lengths,
        out_grad,
        input_gain,
        mamba_gate_weight,
        mamba_in_weight,
        state_weight,
        step_weight,
        conv_weight,
        conv_bias,
        conv_state_weight,
        conv_state_bias,
        step_bias,
        decay_log,
        skip_scale,
        mamba_gain,
        mamba_out_weight,
        query_weight,
        key_value_weight,
        attn_out_weight,
        ffn_gain,
        gate_weight,
        up_weight,
        down_weight,
    ):
        micro = tokens.shape[0]
        count = tokens.shape[1]
        width = tokens.shape[2]
        half = count // 2
        local_heads = step_weight.shape[1]
        q_local = query_weight.shape[1] // AHDIM
        kv_width = key_value_weight.shape[1] // 2
        group_size = AHEADS // KVHEADS
        me_dp = lax.axis_index("dp")
        me_t = lax.axis_index("tensor")
        core = lax.rem(me_t, 2)
        kv_head = me_t * q_local // group_size
        key_weight = lax.dynamic_slice_in_dim(key_value_weight, kv_head * AHDIM, AHDIM, 1)
        value_weight = lax.dynamic_slice_in_dim(
            key_value_weight, kv_width + kv_head * AHDIM, AHDIM, 1
        )
        rows = jnp.arange(count)
        freqs = rope_base ** (-(jnp.arange(AHDIM // 2).astype(f32) * 2.0) / AHDIM)
        angles = rows.astype(f32)[:, None] * freqs[None, :]
        cosine, sine = jnp.cos(angles), jnp.sin(angles)
        cosine = jnp.concatenate([cosine, cosine], axis=1)
        sine = jnp.concatenate([-sine, sine], axis=1)
        channels = mamba_in_weight.shape[1]
        heads_width = query_weight.shape[1]
        places, _ = columns_of(channels, heads_width)
        pad_step = LANES - local_heads

        def lane_row(vector):
            return jnp.pad(vector, (0, pad_step))[None]

        mixer_rows = (
            conv_weight, conv_bias[None], conv_state_weight, conv_state_bias[None],
            lane_row(step_bias), lane_row(jnp.exp(decay_log)), jnp.repeat(skip_scale, MHDIM)[None],
        )
        in_weight = jnp.concatenate(
            [
                mamba_gate_weight,
                query_weight,
                mamba_in_weight,
                state_weight,
                key_weight,
                value_weight,
                jnp.pad(step_weight, ((0, 0), (0, pad_step))),
            ],
            axis=1,
        )
        out_weight = jnp.concatenate([mamba_out_weight, attn_out_weight], axis=0)

        def t_swap(values, bit):
            return swap(values, "tensor", t_size, bit)

        def t_total(values):
            bit = 1
            while bit < t_size:
                values = values + t_swap(values, bit)
                bit *= 2
            return values

        def mine(values):
            return lax.dynamic_slice_in_dim(values, core * half, half, 0)

        def other(values):
            return lax.dynamic_slice_in_dim(values, (1 - core) * half, half, 0)

        def relative(values):
            return jnp.concatenate([mine(values), other(values)], axis=0)

        def in_order(own, far):
            return jnp.where(
                core == 0,
                jnp.concatenate([own, far], axis=0),
                jnp.concatenate([far, own], axis=0),
            )

        def half_sum(own, far):
            own = own + t_swap(far, 1)
            bit = 2
            while bit < t_size // 2:
                own = own + t_swap(own, bit)
                bit *= 2
            return own, t_swap(own, bit)

        block = width // dp_size

        def block_order(values):
            return [
                lax.dynamic_slice_in_dim(values, jnp.bitwise_xor(me_dp, r) * block, block, 1)
                for r in range(dp_size)
            ]

        order = Order()

        def forward(index, slot):
            inputs = slot.astype(f32)
            inv_one = lax.rsqrt(jnp.mean(inputs * inputs, axis=-1, keepdims=True) + epsilon)
            unit_one = inputs * inv_one
            normed = (unit_one * input_gain).astype(bf16)
            proj = plain_dot(normed, in_weight)
            gated, ssd, square, *kept, query, keys, values, logs, context = mixers_forward(
                index, channels, heads_width, lengths, proj, cosine, sine, *mixer_rows
            )
            total_square = t_total(jnp.sum(square, axis=-1))
            inv_mamba = lax.rsqrt(total_square / DSSM + epsilon)[:, None]
            scaled = (gated * inv_mamba * mamba_gain).astype(bf16)
            mixer = jnp.concatenate([scaled, context], axis=1)
            mixed_own, mixed_far = half_sum(
                plain_dot(mine(mixer), out_weight), plain_dot(other(mixer), out_weight)
            )
            order.mark(mixed_own)
            return dict(
                mixed_own=mixed_own, mixed_far=mixed_far, inputs=inputs, inv_one=inv_one,
                unit_one=unit_one, normed=normed, proj=proj, gated=gated, ssd=ssd, kept=kept,
                attention=(query, keys, values, logs), inv_mamba=inv_mamba, mixer=mixer,
            )

        def feed_forward(index, k):
            own, far = order.gate(k["mixed_own"], k["mixed_far"])
            hidden_own = mine(k["inputs"]) + own + far
            hidden = jnp.concatenate([hidden_own, t_swap(hidden_own, 1)], axis=0)
            inv_two = lax.rsqrt(jnp.mean(hidden * hidden, axis=-1, keepdims=True) + epsilon)
            unit_two = hidden * inv_two
            normed_two = (unit_two * ffn_gain).astype(bf16)
            gate = plain_dot(normed_two, gate_weight)
            upper = plain_dot(normed_two, up_weight)
            gsig = jax.nn.sigmoid(gate)
            gsilu = gate * gsig
            inner_ffn = (gsilu * upper).astype(bf16)
            valid = (rows < lengths[index]).astype(f32)[:, None]
            cotangent = relative(out_grad[index].astype(f32) * valid)
            cot_low = cotangent.astype(bf16)
            d_inner_ffn = right_trans(cot_low, down_weight)
            d_gate = (d_inner_ffn * upper * gsig * (1.0 + gate * (1.0 - gsig))).astype(bf16)
            d_up = (d_inner_ffn * gsilu).astype(bf16)
            far = right_trans(d_gate[half:], gate_weight) + right_trans(d_up[half:], up_weight)
            own = right_trans(d_gate[:half], gate_weight) + right_trans(d_up[:half], up_weight)
            back_own, back_far = half_sum(own, far)
            order.mark(back_own)
            k.update(
                back_own=back_own, back_far=back_far,
                hidden=hidden, inv_two=inv_two[:half], unit_two=unit_two[:half],
                normed_two=normed_two, inner_ffn=inner_ffn, cotangent=cotangent, cot_low=cot_low,
                d_gate=d_gate, d_up=d_up,
            )

        def output_sum(k):
            (inner_ffn,) = order.gate(k["inner_ffn"])
            k["ffn_own"], k["ffn_far"] = half_sum(
                plain_dot(inner_ffn[:half], down_weight), plain_dot(inner_ffn[half:], down_weight)
            )
            order.mark(k["ffn_own"])

        def output(k):
            own, far = order.gate(k["ffn_own"], k["ffn_far"])
            ffn_own = own + far
            out = k["hidden"] + jnp.concatenate([ffn_own, t_swap(ffn_own, 1)], axis=0)
            out = in_order(out[:half], out[half:]).astype(bf16)
            order.mark(out)
            return out

        def back_head(k):
            own, far = order.gate(k["back_own"], k["back_far"])
            d_normed_two = own + far
            unit_two = k["unit_two"]
            d_unit_two = d_normed_two * ffn_gain
            d_rest = k["inv_two"] * (
                d_unit_two - unit_two * jnp.mean(d_unit_two * unit_two, axis=-1, keepdims=True)
            )
            d_both = k["cotangent"] + jnp.concatenate([d_rest, t_swap(d_rest, 1)], axis=0)
            d_mixed = in_order(d_both[:half], d_both[half:]).astype(bf16)
            d_mixer = right_trans(d_mixed, out_weight)
            k["g_ffn_gain"] = jnp.sum(d_normed_two * unit_two, axis=0)
            k["d_hidden"] = k["cotangent"][:half] + d_rest
            k["d_mixed"], k["d_mixer"] = d_mixed, d_mixer
            k["cross"] = t_total(
                jnp.sum(d_mixer[:, :channels] * mamba_gain * k["gated"], axis=-1)
            )[:, None]
            order.mark(d_mixer)

        def back_mixers(index, k, held):
            d_mixer, cross = order.gate(k["d_mixer"], k["cross"])
            inv = k["inv_mamba"]
            inv_cross = jnp.concatenate([inv, inv**3 * cross / DSSM], axis=1)
            inv_cross = jnp.pad(inv_cross, ((0, 0), (0, LANES - 2)))
            back, d_statepre, d_keys, d_values, g_conv, g_state, g_heads, g_skip, g_gain = (
                mixers_backward(
                    index, micro, held, lengths, d_mixer, k["gated"], inv_cross, mamba_gain[None],
                    k["proj"], k["ssd"], *k["kept"], *k["attention"], cosine, sine, *mixer_rows,
                )
            )
            kv_far = jnp.where(core == 0, d_values, d_keys)
            kv_own = jnp.where(core == 0, d_keys, d_values)
            k["kv_sum"] = kv_own + t_swap(kv_far, 1)
            k["d_statepre"] = d_statepre
            k.update(
                g_conv_weight=g_conv[:-1], g_conv_bias=g_conv[-1],
                g_conv_state_weight=g_state[:-1], g_conv_state_bias=g_state[-1],
                g_step_bias=g_heads[0, :local_heads], g_decay_log=g_heads[1, :local_heads],
                g_skip=jnp.sum(g_skip.reshape(local_heads, MHDIM), axis=1),
                g_mamba_gain=g_gain[0],
            )
            order.mark(back)
            return back

        def back_inputs(index, k, back):
            back, d_statepre = order.gate(back, k["d_statepre"])
            piece = d_statepre.shape[1] // t_size
            parts = [
                lax.dynamic_slice_in_dim(d_statepre, jnp.bitwise_xor(me_t, q) * piece, piece, 1)
                for q in range(t_size)
            ]
            pieces = halving_order(list(range(0, t_size, 2)), 2, t_size)
            state_sum = jnp.concatenate([parts[q] for q in pieces], axis=1) + t_swap(
                jnp.concatenate([parts[q ^ 1] for q in pieces], axis=1), 1
            )
            bit = 2
            while bit < t_size:
                cut = state_sum.shape[1] // 2
                state_sum = state_sum[:, :cut] + t_swap(state_sum[:, cut:], bit)
                bit *= 2
            k["shared"] = jnp.concatenate([state_sum, k["kv_sum"]], axis=1).astype(bf16)
            rows_own = lax.dynamic_slice_in_dim(back, index * count + core * half, half, 0)
            rows_far = lax.dynamic_slice_in_dim(back, index * count + (1 - core) * half, half, 0)
            k["norm_own"], k["norm_far"] = half_sum(
                right_trans(rows_own, in_weight), right_trans(rows_far, in_weight)
            )
            order.mark(k["norm_own"])

        def input_grad(k):
            own, far = order.gate(k["norm_own"], k["norm_far"])
            d_normed = own + far
            unit_own = mine(k["unit_one"])
            k["g_input_gain"] = jnp.sum(d_normed * unit_own, axis=0)
            d_unit_one = d_normed * input_gain
            grad_own = k["d_hidden"] + mine(k["inv_one"]) * (
                d_unit_one - unit_own * jnp.mean(d_unit_one * unit_own, axis=-1, keepdims=True)
            )
            grad = in_order(grad_own, t_swap(grad_own, 1))
            order.mark(grad)
            return grad

        slots = []
        for index in range(micro):
            slot = tokens[index]
            if index:
                (slot,) = order.gate(slot)
            slots.append(forward(index, slot))
        for index in range(micro):
            feed_forward(index, slots[index])

        def joined(name):
            return jnp.concatenate([k[name] for k in slots], axis=0)

        def scatter(blocks, whole, axis):
            return Scatter(order, dp_size, blocks, whole, axis)

        def start_first(work):
            (work.whole,) = order.gate(work.whole)
            order.mark(work.start_first())

        def start_later(work):
            (work.whole,) = order.gate(work.whole)
            order.mark(work.start_later())

        two_blocks = block_order(joined("normed_two"))
        w_down = scatter(block_order(joined("cot_low")), joined("inner_ffn"), 1)
        w_gate = scatter(two_blocks, joined("d_gate"), 0)
        w_up = scatter(two_blocks, joined("d_up"), 0)
        first, last = slots
        start_first(w_down)
        start_later(w_down)
        back_head(first)
        w_down.take_first()
        start_first(w_gate)
        back = back_mixers(0, first, None)
        w_down.take_later()
        start_later(w_gate)
        back_inputs(0, first, back)
        w_gate.take_first()
        start_first(w_up)
        g_down = w_down.finish()
        back_head(last)
        w_gate.take_later()
        start_later(w_up)
        back = back_mixers(1, last, back)
        w_up.take_first()
        w_outs = scatter(block_order(joined("d_mixed")), joined("mixer"), 1)
        start_first(w_outs)
        g_gate = w_gate.finish()
        back_inputs(1, last, back)
        w_up.take_later()
        start_later(w_outs)
        for k in slots:
            output_sum(k)
        w_outs.take_first()
        one_blocks = block_order(joined("normed"))
        w_early = scatter(one_blocks, back[:, : channels + heads_width], 0)
        w_step = scatter(one_blocks, back[:, places["step"]][:, :local_heads], 1)
        w_late = scatter(
            one_blocks, jnp.concatenate([back[:, places["xpre"]], joined("shared")], axis=1), 0
        )
        start_first(w_early)
        g_up = w_up.finish()
        grads_list = [input_grad(first)]
        w_outs.take_later()
        start_later(w_early)
        outputs_list = [output(first)]
        w_early.take_first()
        start_first(w_late)
        start_first(w_step)
        start_later(w_step)
        g_outs = w_outs.finish()
        grads_list.append(input_grad(last))
        w_early.take_later()
        start_later(w_late)
        outputs_list.append(output(last))
        w_step.take_first()
        w_step.take_later()

        def total(name):
            value = slots[0][name]
            for k in slots[1:]:
                value = value + k[name]
            return value

        once = me_t < 2
        names = [
            "g_conv_state_weight", "g_conv_state_bias", "g_input_gain", "g_ffn_gain",
            "g_conv_weight", "g_conv_bias", "g_step_bias", "g_decay_log", "g_skip",
            "g_mamba_gain",
        ]
        small = {name: total(name) for name in names}
        for name in ("g_input_gain", "g_ffn_gain"):
            small[name] = jnp.where(once, small[name], 0.0)
        vector = jnp.concatenate([small[name].reshape(-1) for name in names])
        (vector,) = order.gate(vector)
        bit = 1
        while bit < dp_size:
            vector = vector + swap(vector, "dp", dp_size, bit)
            bit *= 2
        order.mark(vector)
        shared_size = sum(small[name].size for name in names[:4])
        wide_vector = t_total(vector[:shared_size])
        start = 0
        for name in names:
            shape, size = small[name].shape, small[name].size
            source = wide_vector if start < shared_size else vector
            small[name] = source[start : start + size].reshape(shape)
            start += size
        place = me_dp * t_size + me_t
        share = conv_state_bias.shape[0] // (dp_size * t_size)
        g_conv_state_weight = lax.dynamic_slice_in_dim(
            small["g_conv_state_weight"], place * share, share, 1
        )
        g_conv_state_bias = lax.dynamic_slice_in_dim(
            small["g_conv_state_bias"], place * share, share, 0
        )
        g_input_gain = lax.dynamic_slice_in_dim(small["g_input_gain"], me_dp * block, block, 0)
        g_ffn_gain = lax.dynamic_slice_in_dim(small["g_ffn_gain"], me_dp * block, block, 0)
        heads = [small[name] for name in names[4:]]

        w_late.take_first()
        g_early = w_early.finish()
        g_step = w_step.finish().T
        w_late.take_later()
        g_late = w_late.finish()

        mamba_cols = mamba_in_weight.shape[1]
        tail = g_late[:, mamba_cols:]
        sub = block // t_size
        rowsets = []
        for q in range(t_size):
            part = lax.dynamic_slice_in_dim(tail, jnp.bitwise_xor(me_t, q) * sub, sub, 0)
            rowsets.append(part if q == 0 else t_swap(part, q))
        stacked = jnp.stack(rowsets)
        piece = state_weight.shape[1] // t_size
        sources = [
            lax.dynamic_index_in_dim(stacked, jnp.bitwise_xor(me_t, j), 0, keepdims=False)
            for j in range(t_size)
        ]
        g_state = jnp.concatenate([s[:, :piece] for s in sources], axis=1)
        pairs = t_size // 2
        g_kv = jnp.concatenate(
            [sources[(b % pairs) * 2 + b // pairs][:, piece:] for b in range(t_size)], axis=1
        )
        gate_cols = mamba_gate_weight.shape[1]
        mamba_rows = mamba_out_weight.shape[0]
        return (
            jnp.stack(outputs_list),
            jnp.stack(grads_list),
            g_input_gain,
            g_early[:, :gate_cols],
            g_late[:, :mamba_cols],
            g_state,
            g_step,
            heads[0],
            heads[1],
            g_conv_state_weight,
            g_conv_state_bias,
            heads[2],
            heads[3],
            heads[4],
            heads[5],
            g_outs[:mamba_rows],
            g_early[:, gate_cols:],
            g_kv,
            g_outs[mamba_rows:],
            g_ffn_gain,
            g_gate,
            g_up,
            g_down,
        )

    return per_device


def solution(mesh):
    placed = (
        P("dp", None, None),
        P("dp"),
        P("dp", None, None),
        P(),
        P(None, "tensor"),
        P(None, "tensor"),
        P(),
        P(None, "tensor"),
        P(None, "tensor"),
        P("tensor"),
        P(),
        P(),
        P("tensor"),
        P("tensor"),
        P("tensor"),
        P("tensor"),
        P("tensor", None),
        P(None, "tensor"),
        P(),
        P("tensor", None),
        P(),
        P(None, "tensor"),
        P(None, "tensor"),
        P("tensor", None),
    )
    return jax.shard_map(
        make_per_device(mesh.shape["dp"], mesh.shape["tensor"]),
        mesh=mesh,
        in_specs=placed,
        out_specs=(
            P("dp", None, None),
            P("dp", None, None),
            P("dp"),
            P("dp", "tensor"),
            P("dp", "tensor"),
            P(("dp", "tensor"), None),
            P("dp", "tensor"),
            P(None, "tensor"),
            P("tensor"),
            P(None, ("dp", "tensor")),
            P(("dp", "tensor")),
            P("tensor"),
            P("tensor"),
            P("tensor"),
            P("tensor"),
            P("tensor", "dp"),
            P("dp", "tensor"),
            P(("dp", "tensor"), None),
            P("tensor", "dp"),
            P("dp"),
            P("dp", "tensor"),
            P("dp", "tensor"),
            P("tensor", "dp"),
        ),
        check_vma=False,
    )
```

```python
import functools

import jax
import jax.numpy as jnp
from jax import lax
from jax.experimental import pallas as pl
from jax.experimental.pallas import tpu as pltpu
from jax.sharding import PartitionSpec as P

MHDIM = 64
STATE = 256
AHEADS = 8
KVHEADS = 2
AHDIM = 128
DSSM = 3072

epsilon = 1e-05
rope_base = 100000000000.0
f32 = jnp.float32
bf16 = jnp.bfloat16


def plain_dot(left, right):
    return jnp.dot(left, right, preferred_element_type=f32)


def right_trans(left, right):
    return lax.dot_general(left, right, (((1,), (1,)), ((), ())), preferred_element_type=f32)


def left_trans(left, right):
    return lax.dot_general(left, right, (((0,), (0,)), ((), ())), preferred_element_type=f32)


def silu_slope(values):
    sig = jax.nn.sigmoid(values)
    return sig * (1.0 + values * (1.0 - sig))


MESH = pl.DeviceIdType.MESH
LANES = 128
BLOCK = 128


def shifted(values, steps, row):
    if steps == 0:
        return values
    count = values.shape[0]
    moved = pltpu.roll(values, steps % count, 0)
    if steps > 0:
        return jnp.where(row >= steps, moved, 0.0)
    return jnp.where(row < count + steps, moved, 0.0)


def tap_sum(values, taps, bias):
    row = lax.broadcasted_iota(jnp.int32, values.shape, 0)
    width = taps.shape[0]
    total = jnp.zeros_like(values) + bias
    for k in range(width):
        total = total + shifted(values, width - 1 - k, row) * taps[k : k + 1, :]
    return total


def tap_back(grads, values, taps):
    row = lax.broadcasted_iota(jnp.int32, values.shape, 0)
    width = taps.shape[0]
    back = jnp.zeros_like(values)
    tap_grads = []
    for k in range(width):
        steps = width - 1 - k
        back = back + shifted(grads, -steps, row) * taps[k : k + 1, :]
        tap_grads.append(jnp.sum(grads * shifted(values, steps, row), axis=0, keepdims=True))
    return back, jnp.concatenate(tap_grads, axis=0)


def column_of(values, lane, index):
    return jnp.sum(jnp.where(lane == index, values, 0.0), axis=1, keepdims=True)


def exact_dot(left, right):
    return jnp.dot(left, right, precision=lax.Precision.HIGHEST, preferred_element_type=f32)


def turned(values, cosine, sine):
    return values * cosine + pltpu.roll(values, AHDIM // 2, 1) * sine


def scores_of(query, keys, lo, hi, length):
    scores = right_trans(query[lo:hi], keys[:hi]) * AHDIM ** (-0.5)
    t = lax.broadcasted_iota(jnp.int32, (hi - lo, hi), 0) + lo
    s = lax.broadcasted_iota(jnp.int32, (hi - lo, hi), 1)
    return scores, (t >= s) & (s < length)


def attention_forward(query_pre, key_pre, value_pre, cosine, sine, length, query, keys, values, logs, context):
    count, width = query.shape
    keys[...] = turned(key_pre, cosine, sine).astype(bf16)
    values[...] = value_pre.astype(bf16)
    lane = lax.broadcasted_iota(jnp.int32, (count, LANES), 1)
    kept = jnp.zeros((count, LANES), f32)
    for h in range(width // AHDIM):
        lanes = slice(h * AHDIM, (h + 1) * AHDIM)
        query[:, lanes] = turned(query_pre[:, lanes], cosine, sine).astype(bf16)
        found = []
        for i in range(count // BLOCK):
            lo, hi = i * BLOCK, (i + 1) * BLOCK
            scores, valid = scores_of(query[:, lanes], keys[...], lo, hi, length)
            masked = jnp.where(valid, scores, -1e30)
            peak = jnp.max(masked, axis=1, keepdims=True)
            expo = jnp.exp(masked - peak)
            total = jnp.sum(expo, axis=1, keepdims=True)
            found.append(peak + jnp.log(total))
            probs = (expo / total).astype(bf16)
            context[lo:hi, lanes] = plain_dot(probs, values[:hi, :]).astype(bf16)
        kept = jnp.where(lane == h, jnp.concatenate(found, axis=0), kept)
    logs[...] = kept


def attention_backward(d_context, query, keys, values, logs, cosine, sine, length, d_query_pre, d_keys, d_values):
    count, width = query.shape
    lane = lax.broadcasted_iota(jnp.int32, (count, LANES), 1)
    scale = AHDIM ** (-0.5)
    key_total = jnp.zeros((count, AHDIM), f32)
    value_total = jnp.zeros((count, AHDIM), f32)
    for h in range(width // AHDIM):
        lanes = slice(h * AHDIM, (h + 1) * AHDIM)
        log = column_of(logs[...], lane, h)
        pieces = []
        for i in range(count // BLOCK):
            lo, hi = i * BLOCK, (i + 1) * BLOCK
            scores, valid = scores_of(query[:, lanes], keys[...], lo, hi, length)
            probs = jnp.where(valid, jnp.exp(scores - log[lo:hi]), 0.0)
            grads = d_context[lo:hi, lanes]
            d_probs = right_trans(grads, values[:hi, :])
            delta = jnp.sum(probs * d_probs, axis=1, keepdims=True)
            d_scores = (probs * (d_probs - delta)).astype(bf16)
            pieces.append(plain_dot(d_scores, keys[:hi, :]) * scale)
            d_key = left_trans(d_scores, query[lo:hi, lanes]) * scale
            d_value = left_trans(probs.astype(bf16), grads)
            if hi < count:
                rest = jnp.zeros((count - hi, AHDIM), f32)
                d_key = jnp.concatenate([d_key, rest], axis=0)
                d_value = jnp.concatenate([d_value, rest], axis=0)
            key_total = key_total + d_key
            value_total = value_total + d_value
        d_query_pre[:, lanes] = turned(jnp.concatenate(pieces, axis=0), cosine, -sine).astype(bf16)
    d_keys[...] = turned(key_total, cosine, -sine)
    d_values[...] = value_total


def columns_of(channels, heads_width):
    places, start = {}, 0
    for name, size in (
        ("zgate", channels), ("query", heads_width), ("xpre", channels), ("state", 2 * STATE),
        ("key", AHDIM), ("value", AHDIM), ("step", LANES),
    ):
        places[name] = slice(start, start + size)
        start += size
    return places, start


def forward_kernel(
    lengths, proj, cosine, sine, conv_weight, conv_bias, state_taps, state_bias, step_bias, rates,
    skip_rep, gated, ssd, square, xconv, sconv, stepsize, cumul, inner, query, keys, values, logs,
    context, cumul_rows, *, slot, places,
):
    xpre, zgate = proj.at[:, places["xpre"]], proj.at[:, places["zgate"]]
    statepre, steppre = proj.at[:, places["state"]], proj.at[:, places["step"]]
    attention_forward(
        proj.at[:, places["query"]], proj[:, places["key"]], proj[:, places["value"]],
        cosine[...], sine[...], lengths[slot], query, keys, values, logs, context,
    )
    count, channels = xpre.shape
    xlin = tap_sum(xpre[...], conv_weight[...], conv_bias[...])
    xconv[...] = (xlin * jax.nn.sigmoid(xlin)).astype(bf16)
    slin = tap_sum(statepre[...], state_taps[...], state_bias[...])
    sconv[...] = (slin * jax.nn.sigmoid(slin)).astype(bf16)
    inner[...] = right_trans(sconv[:, STATE:], sconv[:, :STATE])
    step = jax.nn.softplus(steppre[...] + step_bias[...])
    stepsize[...] = step
    row = lax.broadcasted_iota(jnp.int32, (count, count), 0)
    col = lax.broadcasted_iota(jnp.int32, (count, count), 1)
    total = exact_dot(jnp.where(row >= col, 1.0, 0.0), -step * rates[...])
    cumul[...] = total
    cumul_rows[...] = total.T
    square[...] = jnp.zeros_like(square)

    def pair(p):
        lanes = slice(p * LANES, (p + 1) * LANES)
        lane = lax.broadcasted_iota(jnp.int32, (count, LANES), 1)
        xvals = xconv[:, lanes].astype(f32)
        low_half = lane < MHDIM
        step_rep = jnp.where(
            low_half, column_of(stepsize[...], lane, 2 * p), column_of(stepsize[...], lane, 2 * p + 1)
        )
        weighted = (step_rep * xvals).astype(bf16)
        columns = [column_of(cumul[...], lane, 2 * p + h) for h in range(2)]
        for i in range(count // BLOCK):
            lo, hi = i * BLOCK, (i + 1) * BLOCK
            results = []
            for h in range(2):
                differ = columns[h][lo:hi] - cumul_rows[2 * p + h : 2 * p + h + 1, :hi]
                t = lax.broadcasted_iota(jnp.int32, (BLOCK, hi), 0) + lo
                s = lax.broadcasted_iota(jnp.int32, (BLOCK, hi), 1)
                decay = jnp.exp(jnp.where(t >= s, differ, -1e30))
                mixing = (inner[lo:hi, :hi] * decay).astype(bf16)
                results.append(plain_dot(mixing, weighted[:hi]))
            half = jnp.where(low_half[lo:hi], results[0], results[1])
            half = half + skip_rep[:, lanes] * xvals[lo:hi]
            ssd[lo:hi, lanes] = half
            z = zgate[lo:hi, lanes]
            value = half * (z * jax.nn.sigmoid(z))
            gated[lo:hi, lanes] = value
            square[lo:hi, :] += value * value

    for p in range(channels // LANES):
        pair(p)


def full(*shape):
    return jax.ShapeDtypeStruct(shape, f32)


def low(*shape):
    return jax.ShapeDtypeStruct(shape, bf16)


def in_vmem(count):
    return [pl.BlockSpec(memory_space=pltpu.VMEM)] * count


def mixers_forward(slot, channels, heads_width, lengths, proj, *rest):
    count = proj.shape[0]
    return pl.pallas_call(
        functools.partial(
            forward_kernel, slot=slot, places=columns_of(channels, heads_width)[0]
        ),
        out_shape=(
            full(count, channels), full(count, channels), full(count, LANES), low(count, channels),
            low(count, 2 * STATE), full(count, LANES), full(count, LANES), full(count, count),
            low(count, heads_width), low(count, AHDIM), low(count, AHDIM), full(count, LANES),
            low(count, heads_width),
        ),
        in_specs=[pl.BlockSpec(memory_space=pltpu.SMEM)] + in_vmem(1 + len(rest)),
        out_specs=tuple(in_vmem(13)),
        scratch_shapes=[pltpu.VMEM((LANES, count), f32)],
        compiler_params=pltpu.CompilerParams(vmem_limit_bytes=48 * 2**20),
        cost_estimate=pl.CostEstimate(
            flops=9 * 10**9, bytes_accessed=20 * 2**20, transcendentals=5 * 10**6
        ),
    )(lengths, proj, *rest)


def backward_kernel(
    lengths, d_mixer, gated_in, inv_cross, gain, proj, ssd, xconv, sconv, stepsize, cumul, inner,
    query, keys, values, logs, cosine, sine, conv_weight, conv_bias, state_taps, state_bias,
    step_bias, rates, skip_rep,
    back, d_statepre, d_keys, d_values, g_conv, g_state, g_heads, g_skip, g_gain,
    d_ssd, d_xvals, cumul_rows, d_inner, row_sums, col_sums, d_step, *, slot, places,
):
    count, channels = ssd.shape
    xpre, zgate = proj.at[:, places["xpre"]], proj.at[:, places["zgate"]]
    statepre, steppre = proj.at[:, places["state"]], proj.at[:, places["step"]]
    attention_backward(
        d_mixer[:, channels:].astype(bf16), query, keys, values, logs, cosine[...], sine[...],
        lengths[slot], back.at[:, places["query"]], d_keys, d_values,
    )
    back[:, places["key"]] = d_keys[...].astype(bf16)
    back[:, places["value"]] = d_values[...].astype(bf16)
    d_zgate, d_xpre = back.at[:, places["zgate"]], back.at[:, places["xpre"]]
    d_steppre = back.at[:, places["step"]]
    d_scaled = d_mixer[:, :channels]
    g_gain[...] = jnp.sum(d_scaled * gated_in[...] * inv_cross[:, 0:1], axis=0, keepdims=True)
    inv = inv_cross[:, 0:1]
    cross = inv_cross[:, 1:2]
    d_gated = inv * (d_scaled * gain[...]) - gated_in[...] * cross
    z = zgate[...]
    sig = jax.nn.sigmoid(z)
    d_low = (d_gated * (z * sig)).astype(bf16)
    d_ssd[...] = d_low
    d_zgate[...] = (d_gated * ssd[...] * sig * (1.0 + z * (1.0 - sig))).astype(bf16)
    g_skip[...] = jnp.sum(d_low.astype(f32) * xconv[...].astype(f32), axis=0, keepdims=True)
    cumul_rows[...] = cumul[...].T
    d_inner[...] = jnp.zeros_like(d_inner)
    row_sums[...] = jnp.zeros_like(row_sums)
    col_sums[...] = jnp.zeros_like(col_sums)
    d_step[...] = jnp.zeros_like(d_step)

    def pair(p):
        lanes = slice(p * LANES, (p + 1) * LANES)
        lane = lax.broadcasted_iota(jnp.int32, (count, LANES), 1)
        low_half = lane < MHDIM
        xvals = xconv[:, lanes].astype(f32)
        step_rep = jnp.where(
            low_half, column_of(stepsize[...], lane, 2 * p), column_of(stepsize[...], lane, 2 * p + 1)
        )
        weighted = (step_rep * xvals).astype(bf16)
        grads = d_ssd[:, lanes]
        columns = [column_of(cumul[...], lane, 2 * p + h) for h in range(2)]
        pieces = []
        for h in range(2):
            only = jnp.where(low_half == (h == 0), grads, jnp.zeros_like(grads))
            back_part = jnp.zeros((count, LANES), f32)
            sums = []
            col_total = jnp.zeros((1, count), f32)
            for i in range(count // BLOCK):
                lo, hi = i * BLOCK, (i + 1) * BLOCK
                differ = columns[h][lo:hi] - cumul_rows[2 * p + h : 2 * p + h + 1, :hi]
                t = lax.broadcasted_iota(jnp.int32, (BLOCK, hi), 0) + lo
                s = lax.broadcasted_iota(jnp.int32, (BLOCK, hi), 1)
                decay = jnp.exp(jnp.where(t >= s, differ, -1e30))
                mixing = inner[lo:hi, :hi] * decay
                part = left_trans(mixing.astype(bf16), only[lo:hi])
                d_mixing = right_trans(only[lo:hi], weighted[:hi])
                d_inner[lo:hi, :hi] += d_mixing * decay
                flow = d_mixing * mixing
                sums.append(jnp.sum(flow, axis=1, keepdims=True))
                down = jnp.sum(flow, axis=0, keepdims=True)
                if hi < count:
                    part = jnp.concatenate([part, jnp.zeros((count - hi, LANES), f32)], axis=0)
                    down = jnp.concatenate([down, jnp.zeros((1, count - hi), f32)], axis=1)
                back_part = back_part + part
                col_total = col_total + down
            here = lane == 2 * p + h
            row_sums[...] = jnp.where(here, jnp.concatenate(sums, axis=0), row_sums[...])
            col_sums[2 * p + h : 2 * p + h + 1, :] = col_total
            pieces.append(back_part)
        d_weighted = pieces[0] + pieces[1]
        d_xvals[:, lanes] = grads.astype(f32) * skip_rep[:, lanes] + d_weighted * step_rep
        product = d_weighted * xvals
        for h in range(2):
            value = jnp.sum(
                jnp.where(low_half == (h == 0), product, 0.0), axis=1, keepdims=True
            )
            d_step[...] = jnp.where(lane == 2 * p + h, value, d_step[...])

    for p in range(channels // LANES):
        pair(p)

    d_cumul = row_sums[...] - col_sums[...].T
    row = lax.broadcasted_iota(jnp.int32, (count, count), 0)
    col = lax.broadcasted_iota(jnp.int32, (count, count), 1)
    d_logdecay = exact_dot(jnp.where(row <= col, 1.0, 0.0), d_cumul)
    rate = rates[...]
    d_full = (d_step[...] - d_logdecay * rate) * jax.nn.sigmoid(steppre[...] + step_bias[...])
    d_steppre[...] = d_full.astype(bf16)
    g_heads[0:1, :] = jnp.sum(d_full, axis=0, keepdims=True)
    g_heads[1:2, :] = jnp.sum(-d_logdecay * stepsize[...] * rate, axis=0, keepdims=True)

    d_in = d_inner[...].astype(bf16)
    d_c = plain_dot(d_in, sconv[:, :STATE])
    d_b = left_trans(d_in, sconv[:, STATE:])
    slin = tap_sum(statepre[...], state_taps[...], state_bias[...])
    d_slin = jnp.concatenate([d_b, d_c], axis=1) * silu_slope(slin)
    back_state, tap_grads = tap_back(d_slin, statepre[...], state_taps[...])
    d_statepre[...] = back_state
    back[:, places["state"]] = back_state.astype(bf16)
    g_state[...] = jnp.concatenate([tap_grads, jnp.sum(d_slin, axis=0, keepdims=True)], axis=0)
    xlin = tap_sum(xpre[...], conv_weight[...], conv_bias[...])
    d_xlin = d_xvals[...] * silu_slope(xlin)
    back_x, tap_grads = tap_back(d_xlin, xpre[...], conv_weight[...])
    d_xpre[...] = back_x.astype(bf16)
    g_conv[...] = jnp.concatenate([tap_grads, jnp.sum(d_xlin, axis=0, keepdims=True)], axis=0)


def mixers_backward(slot, slots, held, lengths, d_mixer, gated, inv_cross, gain, proj, ssd, *rest):
    count, channels = ssd.shape
    width = proj.shape[1]
    heads_width = d_mixer.shape[1] - channels
    taps = rest[11].shape[0]
    operands = (d_mixer, gated, inv_cross, gain, proj, ssd) + rest
    kernel = functools.partial(
        backward_kernel, slot=slot, places=columns_of(channels, heads_width)[0]
    )
    aliases = {}
    extra_specs, extra = [], ()
    if held is not None:
        aliases = {0: 0}
        extra_specs, extra = [pl.BlockSpec(memory_space=pl.ANY)], (held,)
        inside = kernel
        kernel = lambda _, *refs: inside(*refs)
    return pl.pallas_call(
        kernel,
        grid=(1,),
        out_shape=(
            low(slots * count, width), full(count, 2 * STATE), full(count, AHDIM),
            full(count, AHDIM), full(taps + 1, channels), full(taps + 1, 2 * STATE),
            full(2, LANES), full(1, channels), full(1, channels),
        ),
        in_specs=extra_specs
        + [pl.BlockSpec(memory_space=pltpu.SMEM)]
        + in_vmem(len(operands)),
        out_specs=tuple([pl.BlockSpec((count, width), lambda i: (slot, 0))] + in_vmem(8)),
        scratch_shapes=[
            pltpu.VMEM((count, channels), bf16),
            pltpu.VMEM((count, channels), f32),
            pltpu.VMEM((LANES, count), f32),
            pltpu.VMEM((count, count), f32),
            pltpu.VMEM((count, LANES), f32),
            pltpu.VMEM((LANES, count), f32),
            pltpu.VMEM((count, LANES), f32),
        ],
        input_output_aliases=aliases,
        compiler_params=pltpu.CompilerParams(vmem_limit_bytes=56 * 2**20),
        cost_estimate=pl.CostEstimate(
            flops=20 * 10**9, bytes_accessed=30 * 2**20, transcendentals=7 * 10**6
        ),
    )(*extra, lengths, *operands)


def swap(values, axis, size, bit):
    return lax.ppermute(values, axis, [(i, i ^ bit) for i in range(size)])


def halving_order(members, bit, limit):
    if bit >= limit:
        return members
    low = halving_order([m for m in members if not m & bit], bit * 2, limit)
    high = halving_order([m for m in members if m & bit], bit * 2, limit)
    return low + high


class Order:
    def __init__(self):
        self.last = ()

    def gate(self, *values):
        return lax.optimization_barrier((values, self.last))[0]

    def mark(self, *values):
        self.last = values


def scatter_all(size, parts):
    rows = parts[0].shape[0]
    works = len(parts)
    share = rows // size
    chunk = min(256, rows // 4)
    levels = size.bit_length() - 1
    spans = []
    for level in range(1, levels):
        lo, hi = rows >> (level + 1), rows >> level
        step = min(chunk, hi - lo)
        spans += [(level, start, step) for start in range(hi - step, lo - 1, -step)]
    spans.append((levels, 0, share))
    pieces = [(w,) + span for w in range(works) for span in spans]
    per_work = len(spans)
    widths = [p.shape[1] for p in parts]
    wide = max(widths)

    def kernel(*refs):
        held_in, outs = refs[:works], refs[works : 2 * works]
        loads, refs = refs[2 * works], refs[2 * works + 1 :]
        landed, refs = refs[:works], refs[works:]
        later, refs = refs[: works * (levels - 1)], refs[works * (levels - 1) :]
        load_sems, out_sems, x_send, x_recv, z_send, z_recv = refs
        me = lax.axis_index("dp")

        def partner(level):
            bit = 1 << level
            return me + bit - 2 * bit * lax.rem(me // bit, 2)

        barrier = pltpu.get_barrier_semaphore()
        for level in range(levels):
            pl.semaphore_signal(
                barrier, inc=1, device_id={"dp": partner(level)}, device_id_type=MESH
            )
        pl.semaphore_wait(barrier, levels)

        def first_copy(number):
            w, _, start, step = pieces[number]
            return pltpu.make_async_remote_copy(
                src_ref=held_in[w].at[pl.ds(rows // 2 + start, step), :],
                dst_ref=landed[w].at[pl.ds(start, step), :],
                send_sem=x_send.at[number],
                recv_sem=x_recv.at[number],
                device_id={"dp": partner(0)},
                device_id_type=MESH,
            )

        def load(number):
            w, _, start, step = pieces[number]
            return pltpu.make_async_copy(
                held_in[w].at[pl.ds(start, step), :],
                loads.at[number % 2, pl.ds(0, step), pl.ds(0, widths[w])],
                load_sems.at[number % 2],
            )

        def later_copy(number):
            w, level, start, step = pieces[number]
            return pltpu.make_async_remote_copy(
                src_ref=landed[w].at[pl.ds(start, step), :],
                dst_ref=later[w * (levels - 1) + level - 1].at[pl.ds(start - (rows >> (level + 1)), step), :],
                send_sem=z_send.at[number],
                recv_sem=z_recv.at[number],
                device_id={"dp": partner(level)},
                device_id_type=MESH,
            )

        def store(w):
            return pltpu.make_async_copy(
                landed[w].at[pl.ds(0, share), :], outs[w], out_sems.at[w]
            )

        for number in range(len(pieces)):
            first_copy(number).start()
        load(0).start()
        arrived = set()

        def need(w, level, start, step):
            base = rows >> (level + 1)
            for other in range(w * per_work, (w + 1) * per_work):
                _, its_level, its_start, its_step = pieces[other]
                if its_level != level or other in arrived:
                    continue
                if its_start - base < start + step and start < its_start - base + its_step:
                    later_copy(other).wait_recv()
                    arrived.add(other)

        def finish(w):
            level = levels - 1
            need(w, level, 0, share)
            landed[w][:share, :] += later[w * (levels - 1) + level - 1][:share, :]
            store(w).start()

        for number, (w, level, start, step) in enumerate(pieces):
            load(number).wait()
            if number + 1 < len(pieces):
                load(number + 1).start()
            first_copy(number).wait_recv()
            value = loads[number % 2, :step, : widths[w]] + landed[w][start : start + step, :]
            for before in range(1, min(level, levels - 1)):
                need(w, before, start, step)
                value = value + later[w * (levels - 1) + before - 1][start : start + step, :]
            landed[w][start : start + step, :] = value
            if level < levels:
                later_copy(number).start()
            if w and number == w * per_work + min(2, per_work - 1):
                finish(w - 1)
        finish(works - 1)
        for number, (w, level, start, step) in enumerate(pieces):
            first_copy(number).wait_send()
            if level < levels:
                later_copy(number).wait_send()
        for w in range(works):
            store(w).wait()

    scratch = [pltpu.VMEM((2, chunk, wide), f32)]
    scratch += [pltpu.VMEM((rows // 2, n), f32) for n in widths]
    scratch += [
        pltpu.VMEM((rows >> (level + 1), n), f32) for n in widths for level in range(1, levels)
    ]
    scratch += [
        pltpu.SemaphoreType.DMA((2,)),
        pltpu.SemaphoreType.DMA((works,)),
    ] + [pltpu.SemaphoreType.DMA((len(pieces),))] * 4
    total = sum(rows * n * 4 for n in widths)
    return pl.pallas_call(
        kernel,
        out_shape=tuple(jax.ShapeDtypeStruct((share, n), f32) for n in widths),
        in_specs=[pl.BlockSpec(memory_space=pl.ANY)] * works,
        out_specs=tuple([pl.BlockSpec(memory_space=pl.ANY)] * works),
        scratch_shapes=scratch,
        compiler_params=pltpu.CompilerParams(
            collective_id=0, has_side_effects=True, vmem_limit_bytes=60 * 2**20
        ),
        cost_estimate=pl.CostEstimate(
            flops=total // 2, bytes_accessed=20 * total, transcendentals=0
        ),
    )(*parts)


def make_per_device(dp_size, t_size):
    def per_device(
        tokens,
        lengths,
        out_grad,
        input_gain,
        mamba_gate_weight,
        mamba_in_weight,
        state_weight,
        step_weight,
        conv_weight,
        conv_bias,
        conv_state_weight,
        conv_state_bias,
        step_bias,
        decay_log,
        skip_scale,
        mamba_gain,
        mamba_out_weight,
        query_weight,
        key_value_weight,
        attn_out_weight,
        ffn_gain,
        gate_weight,
        up_weight,
        down_weight,
    ):
        micro = tokens.shape[0]
        count = tokens.shape[1]
        width = tokens.shape[2]
        half = count // 2
        local_heads = step_weight.shape[1]
        q_local = query_weight.shape[1] // AHDIM
        kv_width = key_value_weight.shape[1] // 2
        group_size = AHEADS // KVHEADS
        me_dp = lax.axis_index("dp")
        me_t = lax.axis_index("tensor")
        core = lax.rem(me_t, 2)
        kv_head = me_t * q_local // group_size
        key_weight = lax.dynamic_slice_in_dim(key_value_weight, kv_head * AHDIM, AHDIM, 1)
        value_weight = lax.dynamic_slice_in_dim(
            key_value_weight, kv_width + kv_head * AHDIM, AHDIM, 1
        )
        rows = jnp.arange(count)
        freqs = rope_base ** (-(jnp.arange(AHDIM // 2).astype(f32) * 2.0) / AHDIM)
        angles = rows.astype(f32)[:, None] * freqs[None, :]
        cosine, sine = jnp.cos(angles), jnp.sin(angles)
        cosine = jnp.concatenate([cosine, cosine], axis=1)
        sine = jnp.concatenate([-sine, sine], axis=1)
        channels = mamba_in_weight.shape[1]
        heads_width = query_weight.shape[1]
        places, _ = columns_of(channels, heads_width)
        pad_step = LANES - local_heads

        def lane_row(vector):
            return jnp.pad(vector, (0, pad_step))[None]

        mixer_rows = (
            conv_weight, conv_bias[None], conv_state_weight, conv_state_bias[None],
            lane_row(step_bias), lane_row(jnp.exp(decay_log)), jnp.repeat(skip_scale, MHDIM)[None],
        )
        in_weight = jnp.concatenate(
            [
                mamba_gate_weight,
                query_weight,
                mamba_in_weight,
                state_weight,
                key_weight,
                value_weight,
                jnp.pad(step_weight, ((0, 0), (0, pad_step))),
            ],
            axis=1,
        )
        out_weight = jnp.concatenate([mamba_out_weight, attn_out_weight], axis=0)

        def t_swap(values, bit):
            return swap(values, "tensor", t_size, bit)

        def t_total(values):
            bit = 1
            while bit < t_size:
                values = values + t_swap(values, bit)
                bit *= 2
            return values

        def mine(values):
            return lax.dynamic_slice_in_dim(values, core * half, half, 0)

        def other(values):
            return lax.dynamic_slice_in_dim(values, (1 - core) * half, half, 0)

        def relative(values):
            return jnp.concatenate([mine(values), other(values)], axis=0)

        def in_order(own, far):
            return jnp.where(
                core == 0,
                jnp.concatenate([own, far], axis=0),
                jnp.concatenate([far, own], axis=0),
            )

        def half_sum(own, far):
            own = own + t_swap(far, 1)
            bit = 2
            while bit < t_size // 2:
                own = own + t_swap(own, bit)
                bit *= 2
            return own, t_swap(own, bit)

        block = width // dp_size

        order = Order()

        def forward(index, slot):
            inputs = slot.astype(f32)
            inv_one = lax.rsqrt(jnp.mean(inputs * inputs, axis=-1, keepdims=True) + epsilon)
            unit_one = inputs * inv_one
            normed = (unit_one * input_gain).astype(bf16)
            proj = plain_dot(normed, in_weight)
            gated, ssd, square, *kept, query, keys, values, logs, context = mixers_forward(
                index, channels, heads_width, lengths, proj, cosine, sine, *mixer_rows
            )
            total_square = t_total(jnp.sum(square, axis=-1))
            inv_mamba = lax.rsqrt(total_square / DSSM + epsilon)[:, None]
            scaled = (gated * inv_mamba * mamba_gain).astype(bf16)
            mixer = jnp.concatenate([scaled, context], axis=1)
            mixed_own, mixed_far = half_sum(
                plain_dot(mine(mixer), out_weight), plain_dot(other(mixer), out_weight)
            )
            order.mark(mixed_own)
            return dict(
                mixed_own=mixed_own, mixed_far=mixed_far, inputs=inputs, inv_one=inv_one,
                unit_one=unit_one, normed=normed, proj=proj, gated=gated, ssd=ssd, kept=kept,
                attention=(query, keys, values, logs), inv_mamba=inv_mamba, mixer=mixer,
            )

        def feed_forward(index, k):
            own, far = order.gate(k["mixed_own"], k["mixed_far"])
            hidden_own = mine(k["inputs"]) + own + far
            hidden = jnp.concatenate([hidden_own, t_swap(hidden_own, 1)], axis=0)
            inv_two = lax.rsqrt(jnp.mean(hidden * hidden, axis=-1, keepdims=True) + epsilon)
            unit_two = hidden * inv_two
            normed_two = (unit_two * ffn_gain).astype(bf16)
            gate = plain_dot(normed_two, gate_weight)
            upper = plain_dot(normed_two, up_weight)
            gsig = jax.nn.sigmoid(gate)
            gsilu = gate * gsig
            inner_ffn = (gsilu * upper).astype(bf16)
            valid = (rows < lengths[index]).astype(f32)[:, None]
            cotangent = relative(out_grad[index].astype(f32) * valid)
            cot_low = cotangent.astype(bf16)
            d_inner_ffn = right_trans(cot_low, down_weight)
            d_gate = (d_inner_ffn * upper * gsig * (1.0 + gate * (1.0 - gsig))).astype(bf16)
            d_up = (d_inner_ffn * gsilu).astype(bf16)
            far = right_trans(d_gate[half:], gate_weight) + right_trans(d_up[half:], up_weight)
            own = right_trans(d_gate[:half], gate_weight) + right_trans(d_up[:half], up_weight)
            back_own, back_far = half_sum(own, far)
            order.mark(back_own)
            k.update(
                back_own=back_own, back_far=back_far,
                hidden=hidden, inv_two=inv_two[:half], unit_two=unit_two[:half],
                normed_two=normed_two, inner_ffn=inner_ffn, cotangent=cotangent, cot_low=cot_low,
                d_gate=d_gate, d_up=d_up,
            )

        def output_sum(k):
            (inner_ffn,) = order.gate(k["inner_ffn"])
            k["ffn_own"], k["ffn_far"] = half_sum(
                plain_dot(inner_ffn[:half], down_weight), plain_dot(inner_ffn[half:], down_weight)
            )
            order.mark(k["ffn_own"])

        def output(k):
            own, far = order.gate(k["ffn_own"], k["ffn_far"])
            ffn_own = own + far
            out = k["hidden"] + jnp.concatenate([ffn_own, t_swap(ffn_own, 1)], axis=0)
            out = in_order(out[:half], out[half:]).astype(bf16)
            order.mark(out)
            return out

        def back_head(k):
            own, far = order.gate(k["back_own"], k["back_far"])
            d_normed_two = own + far
            unit_two = k["unit_two"]
            d_unit_two = d_normed_two * ffn_gain
            d_rest = k["inv_two"] * (
                d_unit_two - unit_two * jnp.mean(d_unit_two * unit_two, axis=-1, keepdims=True)
            )
            d_both = k["cotangent"] + jnp.concatenate([d_rest, t_swap(d_rest, 1)], axis=0)
            d_mixed = in_order(d_both[:half], d_both[half:]).astype(bf16)
            d_mixer = right_trans(d_mixed, out_weight)
            k["g_ffn_gain"] = jnp.sum(d_normed_two * unit_two, axis=0)
            k["d_hidden"] = k["cotangent"][:half] + d_rest
            k["d_mixed"], k["d_mixer"] = d_mixed, d_mixer
            k["cross"] = t_total(
                jnp.sum(d_mixer[:, :channels] * mamba_gain * k["gated"], axis=-1)
            )[:, None]
            order.mark(d_mixer)

        def back_mixers(index, k, held):
            d_mixer, cross = order.gate(k["d_mixer"], k["cross"])
            inv = k["inv_mamba"]
            inv_cross = jnp.concatenate([inv, inv**3 * cross / DSSM], axis=1)
            inv_cross = jnp.pad(inv_cross, ((0, 0), (0, LANES - 2)))
            back, d_statepre, d_keys, d_values, g_conv, g_state, g_heads, g_skip, g_gain = (
                mixers_backward(
                    index, micro, held, lengths, d_mixer, k["gated"], inv_cross, mamba_gain[None],
                    k["proj"], k["ssd"], *k["kept"], *k["attention"], cosine, sine, *mixer_rows,
                )
            )
            kv_far = jnp.where(core == 0, d_values, d_keys)
            kv_own = jnp.where(core == 0, d_keys, d_values)
            k["kv_sum"] = kv_own + t_swap(kv_far, 1)
            k["d_statepre"] = d_statepre
            k.update(
                g_conv_weight=g_conv[:-1], g_conv_bias=g_conv[-1],
                g_conv_state_weight=g_state[:-1], g_conv_state_bias=g_state[-1],
                g_step_bias=g_heads[0, :local_heads], g_decay_log=g_heads[1, :local_heads],
                g_skip=jnp.sum(g_skip.reshape(local_heads, MHDIM), axis=1),
                g_mamba_gain=g_gain[0],
            )
            order.mark(back)
            return back

        def back_inputs(index, k, back):
            back, d_statepre = order.gate(back, k["d_statepre"])
            piece = d_statepre.shape[1] // t_size
            parts = [
                lax.dynamic_slice_in_dim(d_statepre, jnp.bitwise_xor(me_t, q) * piece, piece, 1)
                for q in range(t_size)
            ]
            pieces = halving_order(list(range(0, t_size, 2)), 2, t_size)
            state_sum = jnp.concatenate([parts[q] for q in pieces], axis=1) + t_swap(
                jnp.concatenate([parts[q ^ 1] for q in pieces], axis=1), 1
            )
            bit = 2
            while bit < t_size:
                cut = state_sum.shape[1] // 2
                state_sum = state_sum[:, :cut] + t_swap(state_sum[:, cut:], bit)
                bit *= 2
            k["shared"] = jnp.concatenate([state_sum, k["kv_sum"]], axis=1).astype(bf16)
            rows_own = lax.dynamic_slice_in_dim(back, index * count + core * half, half, 0)
            rows_far = lax.dynamic_slice_in_dim(back, index * count + (1 - core) * half, half, 0)
            k["norm_own"], k["norm_far"] = half_sum(
                right_trans(rows_own, in_weight), right_trans(rows_far, in_weight)
            )
            order.mark(k["norm_own"])

        def input_grad(k):
            own, far = order.gate(k["norm_own"], k["norm_far"])
            d_normed = own + far
            unit_own = mine(k["unit_one"])
            k["g_input_gain"] = jnp.sum(d_normed * unit_own, axis=0)
            d_unit_one = d_normed * input_gain
            grad_own = k["d_hidden"] + mine(k["inv_one"]) * (
                d_unit_one - unit_own * jnp.mean(d_unit_one * unit_own, axis=-1, keepdims=True)
            )
            grad = in_order(grad_own, t_swap(grad_own, 1))
            order.mark(grad)
            return grad

        slots = []
        for index in range(micro):
            slot = tokens[index]
            if index:
                (slot,) = order.gate(slot)
            slots.append(forward(index, slot))
        for index in range(micro):
            feed_forward(index, slots[index])

        def joined(name):
            return jnp.concatenate([k[name] for k in slots], axis=0)

        def relative_columns(values):
            blocks = halving_order(list(range(dp_size)), 1, dp_size)
            return jnp.concatenate(
                [
                    lax.dynamic_slice_in_dim(values, jnp.bitwise_xor(me_dp, r) * block, block, 1)
                    for r in blocks
                ],
                axis=1,
            )

        two_columns = relative_columns(joined("normed_two"))
        cot_columns = relative_columns(joined("cot_low"))
        part_down = left_trans(cot_columns, joined("inner_ffn"))
        part_gate = left_trans(two_columns, joined("d_gate"))
        part_up = left_trans(two_columns, joined("d_up"))
        back = None
        for index, k in enumerate(slots):
            back_head(k)
            back = back_mixers(index, k, back)
            back_inputs(index, k, back)
        part_outs = left_trans(relative_columns(joined("d_mixed")), joined("mixer"))
        one_columns = relative_columns(joined("normed"))
        part_early = left_trans(one_columns, back[:, : channels + heads_width])
        part_late = left_trans(
            one_columns,
            jnp.concatenate(
                [back[:, places["xpre"]], joined("shared"), back[:, places["step"]]], axis=1
            ),
        )
        for k in slots:
            output_sum(k)
        g_down, g_gate, g_up, g_outs, g_early, g_late = scatter_all(
            dp_size, [part_down, part_gate, part_up, part_outs, part_early, part_late]
        )
        order.mark(g_late)
        g_down, g_outs = g_down.T, g_outs.T
        shared_end = channels + joined("shared").shape[1]
        g_step = g_late[:, shared_end : shared_end + local_heads]
        g_late = g_late[:, :shared_end]
        grads_list = [input_grad(k) for k in slots]
        outputs_list = [output(k) for k in slots]

        def total(name):
            value = slots[0][name]
            for k in slots[1:]:
                value = value + k[name]
            return value

        once = me_t < 2
        names = [
            "g_conv_state_weight", "g_conv_state_bias", "g_input_gain", "g_ffn_gain",
            "g_conv_weight", "g_conv_bias", "g_step_bias", "g_decay_log", "g_skip",
            "g_mamba_gain",
        ]
        small = {name: total(name) for name in names}
        for name in ("g_input_gain", "g_ffn_gain"):
            small[name] = jnp.where(once, small[name], 0.0)
        vector = jnp.concatenate([small[name].reshape(-1) for name in names])
        (vector,) = order.gate(vector)
        bit = 1
        while bit < dp_size:
            vector = vector + swap(vector, "dp", dp_size, bit)
            bit *= 2
        order.mark(vector)
        shared_size = sum(small[name].size for name in names[:4])
        wide_vector = t_total(vector[:shared_size])
        start = 0
        for name in names:
            shape, size = small[name].shape, small[name].size
            source = wide_vector if start < shared_size else vector
            small[name] = source[start : start + size].reshape(shape)
            start += size
        place = me_dp * t_size + me_t
        share = conv_state_bias.shape[0] // (dp_size * t_size)
        g_conv_state_weight = lax.dynamic_slice_in_dim(
            small["g_conv_state_weight"], place * share, share, 1
        )
        g_conv_state_bias = lax.dynamic_slice_in_dim(
            small["g_conv_state_bias"], place * share, share, 0
        )
        g_input_gain = lax.dynamic_slice_in_dim(small["g_input_gain"], me_dp * block, block, 0)
        g_ffn_gain = lax.dynamic_slice_in_dim(small["g_ffn_gain"], me_dp * block, block, 0)
        heads = [small[name] for name in names[4:]]

        mamba_cols = mamba_in_weight.shape[1]
        tail = g_late[:, mamba_cols:]
        sub = block // t_size
        rowsets = []
        for q in range(t_size):
            part = lax.dynamic_slice_in_dim(tail, jnp.bitwise_xor(me_t, q) * sub, sub, 0)
            rowsets.append(part if q == 0 else t_swap(part, q))
        stacked = jnp.stack(rowsets)
        piece = state_weight.shape[1] // t_size
        sources = [
            lax.dynamic_index_in_dim(stacked, jnp.bitwise_xor(me_t, j), 0, keepdims=False)
            for j in range(t_size)
        ]
        g_state = jnp.concatenate([s[:, :piece] for s in sources], axis=1)
        pairs = t_size // 2
        g_kv = jnp.concatenate(
            [sources[(b % pairs) * 2 + b // pairs][:, piece:] for b in range(t_size)], axis=1
        )
        gate_cols = mamba_gate_weight.shape[1]
        mamba_rows = mamba_out_weight.shape[0]
        return (
            jnp.stack(outputs_list),
            jnp.stack(grads_list),
            g_input_gain,
            g_early[:, :gate_cols],
            g_late[:, :mamba_cols],
            g_state,
            g_step,
            heads[0],
            heads[1],
            g_conv_state_weight,
            g_conv_state_bias,
            heads[2],
            heads[3],
            heads[4],
            heads[5],
            g_outs[:mamba_rows],
            g_early[:, gate_cols:],
            g_kv,
            g_outs[mamba_rows:],
            g_ffn_gain,
            g_gate,
            g_up,
            g_down,
        )

    return per_device


def solution(mesh):
    placed = (
        P("dp", None, None),
        P("dp"),
        P("dp", None, None),
        P(),
        P(None, "tensor"),
        P(None, "tensor"),
        P(),
        P(None, "tensor"),
        P(None, "tensor"),
        P("tensor"),
        P(),
        P(),
        P("tensor"),
        P("tensor"),
        P("tensor"),
        P("tensor"),
        P("tensor", None),
        P(None, "tensor"),
        P(),
        P("tensor", None),
        P(),
        P(None, "tensor"),
        P(None, "tensor"),
        P("tensor", None),
    )
    return jax.shard_map(
        make_per_device(mesh.shape["dp"], mesh.shape["tensor"]),
        mesh=mesh,
        in_specs=placed,
        out_specs=(
            P("dp", None, None),
            P("dp", None, None),
            P("dp"),
            P("dp", "tensor"),
            P("dp", "tensor"),
            P(("dp", "tensor"), None),
            P("dp", "tensor"),
            P(None, "tensor"),
            P("tensor"),
            P(None, ("dp", "tensor")),
            P(("dp", "tensor")),
            P("tensor"),
            P("tensor"),
            P("tensor"),
            P("tensor"),
            P("tensor", "dp"),
            P("dp", "tensor"),
            P(("dp", "tensor"), None),
            P("tensor", "dp"),
            P("dp"),
            P("dp", "tensor"),
            P("dp", "tensor"),
            P("tensor", "dp"),
        ),
        check_vma=False,
    )
```

```python
import functools

import jax
import jax.numpy as jnp
from jax import lax
from jax.experimental import pallas as pl
from jax.experimental.pallas import tpu as pltpu
from jax.sharding import PartitionSpec as P

MHDIM = 64
STATE = 256
AHEADS = 8
KVHEADS = 2
AHDIM = 128
DSSM = 3072

epsilon = 1e-05
rope_base = 100000000000.0
f32 = jnp.float32
bf16 = jnp.bfloat16


def plain_dot(left, right):
    return jnp.dot(left, right, preferred_element_type=f32)


def right_trans(left, right):
    return lax.dot_general(left, right, (((1,), (1,)), ((), ())), preferred_element_type=f32)


def left_trans(left, right):
    return lax.dot_general(left, right, (((0,), (0,)), ((), ())), preferred_element_type=f32)


def silu_slope(values):
    sig = jax.nn.sigmoid(values)
    return sig * (1.0 + values * (1.0 - sig))


MESH = pl.DeviceIdType.MESH
LANES = 128
BLOCK = 128


def shifted(values, steps, row):
    if steps == 0:
        return values
    count = values.shape[0]
    moved = pltpu.roll(values, steps % count, 0)
    if steps > 0:
        return jnp.where(row >= steps, moved, 0.0)
    return jnp.where(row < count + steps, moved, 0.0)


def tap_sum(values, taps, bias):
    row = lax.broadcasted_iota(jnp.int32, values.shape, 0)
    width = taps.shape[0]
    total = jnp.zeros_like(values) + bias
    for k in range(width):
        total = total + shifted(values, width - 1 - k, row) * taps[k : k + 1, :]
    return total


def tap_back(grads, values, taps):
    row = lax.broadcasted_iota(jnp.int32, values.shape, 0)
    width = taps.shape[0]
    back = jnp.zeros_like(values)
    tap_grads = []
    for k in range(width):
        steps = width - 1 - k
        back = back + shifted(grads, -steps, row) * taps[k : k + 1, :]
        tap_grads.append(jnp.sum(grads * shifted(values, steps, row), axis=0, keepdims=True))
    return back, jnp.concatenate(tap_grads, axis=0)


def column_of(values, lane, index):
    return jnp.sum(jnp.where(lane == index, values, 0.0), axis=1, keepdims=True)


def exact_dot(left, right):
    return jnp.dot(left, right, precision=lax.Precision.HIGHEST, preferred_element_type=f32)


def turned(values, cosine, sine):
    return values * cosine + pltpu.roll(values, AHDIM // 2, 1) * sine


def scores_of(query, keys, lo, hi, length):
    scores = right_trans(query[lo:hi], keys[:hi]) * AHDIM ** (-0.5)
    t = lax.broadcasted_iota(jnp.int32, (hi - lo, hi), 0) + lo
    s = lax.broadcasted_iota(jnp.int32, (hi - lo, hi), 1)
    return scores, (t >= s) & (s < length)


def attention_forward(query_pre, key_pre, value_pre, cosine, sine, length, query, keys, values, logs, context):
    count, width = query.shape
    keys[...] = turned(key_pre, cosine, sine).astype(bf16)
    values[...] = value_pre.astype(bf16)
    lane = lax.broadcasted_iota(jnp.int32, (count, LANES), 1)
    kept = jnp.zeros((count, LANES), f32)
    for h in range(width // AHDIM):
        lanes = slice(h * AHDIM, (h + 1) * AHDIM)
        query[:, lanes] = turned(query_pre[:, lanes], cosine, sine).astype(bf16)
        found = []
        for i in range(count // BLOCK):
            lo, hi = i * BLOCK, (i + 1) * BLOCK
            scores, valid = scores_of(query[:, lanes], keys[...], lo, hi, length)
            masked = jnp.where(valid, scores, -1e30)
            peak = jnp.max(masked, axis=1, keepdims=True)
            expo = jnp.exp(masked - peak)
            total = jnp.sum(expo, axis=1, keepdims=True)
            found.append(peak + jnp.log(total))
            probs = (expo / total).astype(bf16)
            context[lo:hi, lanes] = plain_dot(probs, values[:hi, :]).astype(bf16)
        kept = jnp.where(lane == h, jnp.concatenate(found, axis=0), kept)
    logs[...] = kept


def attention_backward(d_context, query, keys, values, logs, cosine, sine, length, d_query_pre, d_keys, d_values):
    count, width = query.shape
    lane = lax.broadcasted_iota(jnp.int32, (count, LANES), 1)
    scale = AHDIM ** (-0.5)
    key_total = jnp.zeros((count, AHDIM), f32)
    value_total = jnp.zeros((count, AHDIM), f32)
    for h in range(width // AHDIM):
        lanes = slice(h * AHDIM, (h + 1) * AHDIM)
        log = column_of(logs[...], lane, h)
        pieces = []
        for i in range(count // BLOCK):
            lo, hi = i * BLOCK, (i + 1) * BLOCK
            scores, valid = scores_of(query[:, lanes], keys[...], lo, hi, length)
            probs = jnp.where(valid, jnp.exp(scores - log[lo:hi]), 0.0)
            grads = d_context[lo:hi, lanes]
            d_probs = right_trans(grads, values[:hi, :])
            delta = jnp.sum(probs * d_probs, axis=1, keepdims=True)
            d_scores = (probs * (d_probs - delta)).astype(bf16)
            pieces.append(plain_dot(d_scores, keys[:hi, :]) * scale)
            d_key = left_trans(d_scores, query[lo:hi, lanes]) * scale
            d_value = left_trans(probs.astype(bf16), grads)
            if hi < count:
                rest = jnp.zeros((count - hi, AHDIM), f32)
                d_key = jnp.concatenate([d_key, rest], axis=0)
                d_value = jnp.concatenate([d_value, rest], axis=0)
            key_total = key_total + d_key
            value_total = value_total + d_value
        d_query_pre[:, lanes] = turned(jnp.concatenate(pieces, axis=0), cosine, -sine).astype(bf16)
    d_keys[...] = turned(key_total, cosine, -sine)
    d_values[...] = value_total


def columns_of(channels, heads_width):
    places, start = {}, 0
    for name, size in (
        ("zgate", channels), ("query", heads_width), ("xpre", channels), ("state", 2 * STATE),
        ("key", AHDIM), ("value", AHDIM), ("step", LANES),
    ):
        places[name] = slice(start, start + size)
        start += size
    return places, start


def forward_kernel(
    lengths, proj, cosine, sine, conv_weight, conv_bias, state_taps, state_bias, step_bias, rates,
    skip_rep, gated, ssd, square, xconv, sconv, stepsize, cumul, inner, query, keys, values, logs,
    context, cumul_rows, *, slot, places,
):
    xpre, zgate = proj.at[:, places["xpre"]], proj.at[:, places["zgate"]]
    statepre, steppre = proj.at[:, places["state"]], proj.at[:, places["step"]]
    attention_forward(
        proj.at[:, places["query"]], proj[:, places["key"]], proj[:, places["value"]],
        cosine[...], sine[...], lengths[slot], query, keys, values, logs, context,
    )
    count, channels = xpre.shape
    xlin = tap_sum(xpre[...], conv_weight[...], conv_bias[...])
    xconv[...] = (xlin * jax.nn.sigmoid(xlin)).astype(bf16)
    slin = tap_sum(statepre[...], state_taps[...], state_bias[...])
    sconv[...] = (slin * jax.nn.sigmoid(slin)).astype(bf16)
    inner[...] = right_trans(sconv[:, STATE:], sconv[:, :STATE])
    step = jax.nn.softplus(steppre[...] + step_bias[...])
    stepsize[...] = step
    row = lax.broadcasted_iota(jnp.int32, (count, count), 0)
    col = lax.broadcasted_iota(jnp.int32, (count, count), 1)
    total = exact_dot(jnp.where(row >= col, 1.0, 0.0), -step * rates[...])
    cumul[...] = total
    cumul_rows[...] = total.T
    square[...] = jnp.zeros_like(square)

    def pair(p):
        lanes = slice(p * LANES, (p + 1) * LANES)
        lane = lax.broadcasted_iota(jnp.int32, (count, LANES), 1)
        xvals = xconv[:, lanes].astype(f32)
        low_half = lane < MHDIM
        step_rep = jnp.where(
            low_half, column_of(stepsize[...], lane, 2 * p), column_of(stepsize[...], lane, 2 * p + 1)
        )
        weighted = (step_rep * xvals).astype(bf16)
        columns = [column_of(cumul[...], lane, 2 * p + h) for h in range(2)]
        for i in range(count // BLOCK):
            lo, hi = i * BLOCK, (i + 1) * BLOCK
            results = []
            for h in range(2):
                differ = columns[h][lo:hi] - cumul_rows[2 * p + h : 2 * p + h + 1, :hi]
                t = lax.broadcasted_iota(jnp.int32, (BLOCK, hi), 0) + lo
                s = lax.broadcasted_iota(jnp.int32, (BLOCK, hi), 1)
                decay = jnp.exp(jnp.where(t >= s, differ, -1e30))
                mixing = (inner[lo:hi, :hi] * decay).astype(bf16)
                results.append(plain_dot(mixing, weighted[:hi]))
            half = jnp.where(low_half[lo:hi], results[0], results[1])
            half = half + skip_rep[:, lanes] * xvals[lo:hi]
            ssd[lo:hi, lanes] = half
            z = zgate[lo:hi, lanes]
            value = half * (z * jax.nn.sigmoid(z))
            gated[lo:hi, lanes] = value
            square[lo:hi, :] += value * value

    for p in range(channels // LANES):
        pair(p)


def full(*shape):
    return jax.ShapeDtypeStruct(shape, f32)


def low(*shape):
    return jax.ShapeDtypeStruct(shape, bf16)


def in_vmem(count):
    return [pl.BlockSpec(memory_space=pltpu.VMEM)] * count


def mixers_forward(slot, channels, heads_width, lengths, proj, *rest):
    count = proj.shape[0]
    return pl.pallas_call(
        functools.partial(
            forward_kernel, slot=slot, places=columns_of(channels, heads_width)[0]
        ),
        out_shape=(
            full(count, channels), full(count, channels), full(count, LANES), low(count, channels),
            low(count, 2 * STATE), full(count, LANES), full(count, LANES), full(count, count),
            low(count, heads_width), low(count, AHDIM), low(count, AHDIM), full(count, LANES),
            low(count, heads_width),
        ),
        in_specs=[pl.BlockSpec(memory_space=pltpu.SMEM)] + in_vmem(1 + len(rest)),
        out_specs=tuple(in_vmem(13)),
        scratch_shapes=[pltpu.VMEM((LANES, count), f32)],
        compiler_params=pltpu.CompilerParams(vmem_limit_bytes=48 * 2**20),
        cost_estimate=pl.CostEstimate(
            flops=9 * 10**9, bytes_accessed=20 * 2**20, transcendentals=5 * 10**6
        ),
    )(lengths, proj, *rest)


def backward_kernel(
    lengths, d_mixer, gated_in, inv_cross, gain, proj, ssd, xconv, sconv, stepsize, cumul, inner,
    query, keys, values, logs, cosine, sine, conv_weight, conv_bias, state_taps, state_bias,
    step_bias, rates, skip_rep,
    back, d_statepre, d_keys, d_values, g_conv, g_state, g_heads, g_skip, g_gain,
    d_ssd, d_xvals, cumul_rows, d_inner, row_sums, col_sums, d_step, *, slot, places,
):
    count, channels = ssd.shape
    xpre, zgate = proj.at[:, places["xpre"]], proj.at[:, places["zgate"]]
    statepre, steppre = proj.at[:, places["state"]], proj.at[:, places["step"]]
    attention_backward(
        d_mixer[:, channels:].astype(bf16), query, keys, values, logs, cosine[...], sine[...],
        lengths[slot], back.at[:, places["query"]], d_keys, d_values,
    )
    back[:, places["key"]] = d_keys[...].astype(bf16)
    back[:, places["value"]] = d_values[...].astype(bf16)
    d_zgate, d_xpre = back.at[:, places["zgate"]], back.at[:, places["xpre"]]
    d_steppre = back.at[:, places["step"]]
    d_scaled = d_mixer[:, :channels]
    g_gain[...] = jnp.sum(d_scaled * gated_in[...] * inv_cross[:, 0:1], axis=0, keepdims=True)
    inv = inv_cross[:, 0:1]
    cross = inv_cross[:, 1:2]
    d_gated = inv * (d_scaled * gain[...]) - gated_in[...] * cross
    z = zgate[...]
    sig = jax.nn.sigmoid(z)
    d_low = (d_gated * (z * sig)).astype(bf16)
    d_ssd[...] = d_low
    d_zgate[...] = (d_gated * ssd[...] * sig * (1.0 + z * (1.0 - sig))).astype(bf16)
    g_skip[...] = jnp.sum(d_low.astype(f32) * xconv[...].astype(f32), axis=0, keepdims=True)
    cumul_rows[...] = cumul[...].T
    d_inner[...] = jnp.zeros_like(d_inner)
    row_sums[...] = jnp.zeros_like(row_sums)
    col_sums[...] = jnp.zeros_like(col_sums)
    d_step[...] = jnp.zeros_like(d_step)

    def pair(p):
        lanes = slice(p * LANES, (p + 1) * LANES)
        lane = lax.broadcasted_iota(jnp.int32, (count, LANES), 1)
        low_half = lane < MHDIM
        xvals = xconv[:, lanes].astype(f32)
        step_rep = jnp.where(
            low_half, column_of(stepsize[...], lane, 2 * p), column_of(stepsize[...], lane, 2 * p + 1)
        )
        weighted = (step_rep * xvals).astype(bf16)
        grads = d_ssd[:, lanes]
        columns = [column_of(cumul[...], lane, 2 * p + h) for h in range(2)]
        pieces = []
        for h in range(2):
            only = jnp.where(low_half == (h == 0), grads, jnp.zeros_like(grads))
            back_part = jnp.zeros((count, LANES), f32)
            sums = []
            col_total = jnp.zeros((1, count), f32)
            for i in range(count // BLOCK):
                lo, hi = i * BLOCK, (i + 1) * BLOCK
                differ = columns[h][lo:hi] - cumul_rows[2 * p + h : 2 * p + h + 1, :hi]
                t = lax.broadcasted_iota(jnp.int32, (BLOCK, hi), 0) + lo
                s = lax.broadcasted_iota(jnp.int32, (BLOCK, hi), 1)
                decay = jnp.exp(jnp.where(t >= s, differ, -1e30))
                mixing = inner[lo:hi, :hi] * decay
                part = left_trans(mixing.astype(bf16), only[lo:hi])
                d_mixing = right_trans(only[lo:hi], weighted[:hi])
                d_inner[lo:hi, :hi] += d_mixing * decay
                flow = d_mixing * mixing
                sums.append(jnp.sum(flow, axis=1, keepdims=True))
                down = jnp.sum(flow, axis=0, keepdims=True)
                if hi < count:
                    part = jnp.concatenate([part, jnp.zeros((count - hi, LANES), f32)], axis=0)
                    down = jnp.concatenate([down, jnp.zeros((1, count - hi), f32)], axis=1)
                back_part = back_part + part
                col_total = col_total + down
            here = lane == 2 * p + h
            row_sums[...] = jnp.where(here, jnp.concatenate(sums, axis=0), row_sums[...])
            col_sums[2 * p + h : 2 * p + h + 1, :] = col_total
            pieces.append(back_part)
        d_weighted = pieces[0] + pieces[1]
        d_xvals[:, lanes] = grads.astype(f32) * skip_rep[:, lanes] + d_weighted * step_rep
        product = d_weighted * xvals
        for h in range(2):
            value = jnp.sum(
                jnp.where(low_half == (h == 0), product, 0.0), axis=1, keepdims=True
            )
            d_step[...] = jnp.where(lane == 2 * p + h, value, d_step[...])

    for p in range(channels // LANES):
        pair(p)

    d_cumul = row_sums[...] - col_sums[...].T
    row = lax.broadcasted_iota(jnp.int32, (count, count), 0)
    col = lax.broadcasted_iota(jnp.int32, (count, count), 1)
    d_logdecay = exact_dot(jnp.where(row <= col, 1.0, 0.0), d_cumul)
    rate = rates[...]
    d_full = (d_step[...] - d_logdecay * rate) * jax.nn.sigmoid(steppre[...] + step_bias[...])
    d_steppre[...] = d_full.astype(bf16)
    g_heads[0:1, :] = jnp.sum(d_full, axis=0, keepdims=True)
    g_heads[1:2, :] = jnp.sum(-d_logdecay * stepsize[...] * rate, axis=0, keepdims=True)

    d_in = d_inner[...].astype(bf16)
    d_c = plain_dot(d_in, sconv[:, :STATE])
    d_b = left_trans(d_in, sconv[:, STATE:])
    slin = tap_sum(statepre[...], state_taps[...], state_bias[...])
    d_slin = jnp.concatenate([d_b, d_c], axis=1) * silu_slope(slin)
    back_state, tap_grads = tap_back(d_slin, statepre[...], state_taps[...])
    d_statepre[...] = back_state
    back[:, places["state"]] = back_state.astype(bf16)
    g_state[...] = jnp.concatenate([tap_grads, jnp.sum(d_slin, axis=0, keepdims=True)], axis=0)
    xlin = tap_sum(xpre[...], conv_weight[...], conv_bias[...])
    d_xlin = d_xvals[...] * silu_slope(xlin)
    back_x, tap_grads = tap_back(d_xlin, xpre[...], conv_weight[...])
    d_xpre[...] = back_x.astype(bf16)
    g_conv[...] = jnp.concatenate([tap_grads, jnp.sum(d_xlin, axis=0, keepdims=True)], axis=0)


def mixers_backward(slot, slots, held, lengths, d_mixer, gated, inv_cross, gain, proj, ssd, *rest):
    count, channels = ssd.shape
    width = proj.shape[1]
    heads_width = d_mixer.shape[1] - channels
    taps = rest[11].shape[0]
    operands = (d_mixer, gated, inv_cross, gain, proj, ssd) + rest
    kernel = functools.partial(
        backward_kernel, slot=slot, places=columns_of(channels, heads_width)[0]
    )
    aliases = {}
    extra_specs, extra = [], ()
    if held is not None:
        aliases = {0: 0}
        extra_specs, extra = [pl.BlockSpec(memory_space=pl.ANY)], (held,)
        inside = kernel
        kernel = lambda _, *refs: inside(*refs)
    return pl.pallas_call(
        kernel,
        grid=(1,),
        out_shape=(
            low(slots * count, width), full(count, 2 * STATE), full(count, AHDIM),
            full(count, AHDIM), full(taps + 1, channels), full(taps + 1, 2 * STATE),
            full(2, LANES), full(1, channels), full(1, channels),
        ),
        in_specs=extra_specs
        + [pl.BlockSpec(memory_space=pltpu.SMEM)]
        + in_vmem(len(operands)),
        out_specs=tuple([pl.BlockSpec((count, width), lambda i: (slot, 0))] + in_vmem(8)),
        scratch_shapes=[
            pltpu.VMEM((count, channels), bf16),
            pltpu.VMEM((count, channels), f32),
            pltpu.VMEM((LANES, count), f32),
            pltpu.VMEM((count, count), f32),
            pltpu.VMEM((count, LANES), f32),
            pltpu.VMEM((LANES, count), f32),
            pltpu.VMEM((count, LANES), f32),
        ],
        input_output_aliases=aliases,
        compiler_params=pltpu.CompilerParams(vmem_limit_bytes=56 * 2**20),
        cost_estimate=pl.CostEstimate(
            flops=20 * 10**9, bytes_accessed=30 * 2**20, transcendentals=7 * 10**6
        ),
    )(*extra, lengths, *operands)


def swap(values, axis, size, bit):
    return lax.ppermute(values, axis, [(i, i ^ bit) for i in range(size)])


def halving_order(members, bit, limit):
    if bit >= limit:
        return members
    low = halving_order([m for m in members if not m & bit], bit * 2, limit)
    high = halving_order([m for m in members if m & bit], bit * 2, limit)
    return low + high


class Order:
    def __init__(self):
        self.last = ()
        self.queue = []

    def point(self, value):
        if not self.queue:
            return value
        return lax.optimization_barrier((value, self.queue.pop(0)))[0]

    def gate(self, *values):
        return lax.optimization_barrier((values, self.last))[0]

    def mark(self, *values):
        self.last = values


def scatter_all(size, parts):
    rows = parts[0].shape[0]
    works = len(parts)
    share = rows // size
    chunk = min(256, rows // 4)
    levels = size.bit_length() - 1
    spans = []
    for level in range(1, levels):
        lo, hi = rows >> (level + 1), rows >> level
        step = min(chunk, hi - lo)
        spans += [(level, start, step) for start in range(hi - step, lo - 1, -step)]
    spans.append((levels, 0, share))
    pieces = [(w,) + span for w in range(works) for span in spans]
    per_work = len(spans)
    widths = [p.shape[1] for p in parts]
    wide = max(widths)

    def kernel(*refs):
        held_in, outs = refs[:works], refs[works : 2 * works]
        loads, refs = refs[2 * works], refs[2 * works + 1 :]
        landed, refs = refs[:works], refs[works:]
        later, refs = refs[: works * (levels - 1)], refs[works * (levels - 1) :]
        load_sems, out_sems, x_send, x_recv, z_send, z_recv = refs
        me = lax.axis_index("dp")

        def partner(level):
            bit = 1 << level
            return me + bit - 2 * bit * lax.rem(me // bit, 2)

        barrier = pltpu.get_barrier_semaphore()
        for level in range(levels):
            pl.semaphore_signal(
                barrier, inc=1, device_id={"dp": partner(level)}, device_id_type=MESH
            )
        pl.semaphore_wait(barrier, levels)

        def first_copy(number):
            w, _, start, step = pieces[number]
            return pltpu.make_async_remote_copy(
                src_ref=held_in[w].at[pl.ds(rows // 2 + start, step), :],
                dst_ref=landed[w].at[pl.ds(start, step), :],
                send_sem=x_send.at[number],
                recv_sem=x_recv.at[number],
                device_id={"dp": partner(0)},
                device_id_type=MESH,
            )

        def load(number):
            w, _, start, step = pieces[number]
            return pltpu.make_async_copy(
                held_in[w].at[pl.ds(start, step), :],
                loads.at[number % 2, pl.ds(0, step), pl.ds(0, widths[w])],
                load_sems.at[number % 2],
            )

        def later_copy(number):
            w, level, start, step = pieces[number]
            return pltpu.make_async_remote_copy(
                src_ref=landed[w].at[pl.ds(start, step), :],
                dst_ref=later[w * (levels - 1) + level - 1].at[pl.ds(start - (rows >> (level + 1)), step), :],
                send_sem=z_send.at[number],
                recv_sem=z_recv.at[number],
                device_id={"dp": partner(level)},
                device_id_type=MESH,
            )

        def store(w):
            return pltpu.make_async_copy(
                landed[w].at[pl.ds(0, share), :], outs[w], out_sems.at[w]
            )

        for number in range(len(pieces)):
            first_copy(number).start()
        load(0).start()
        arrived = set()

        def need(w, level, start, step):
            base = rows >> (level + 1)
            for other in range(w * per_work, (w + 1) * per_work):
                _, its_level, its_start, its_step = pieces[other]
                if its_level != level or other in arrived:
                    continue
                if its_start - base < start + step and start < its_start - base + its_step:
                    later_copy(other).wait_recv()
                    arrived.add(other)

        def finish(w):
            level = levels - 1
            need(w, level, 0, share)
            landed[w][:share, :] += later[w * (levels - 1) + level - 1][:share, :]
            store(w).start()

        for number, (w, level, start, step) in enumerate(pieces):
            load(number).wait()
            if number + 1 < len(pieces):
                load(number + 1).start()
            first_copy(number).wait_recv()
            value = loads[number % 2, :step, : widths[w]] + landed[w][start : start + step, :]
            for before in range(1, min(level, levels - 1)):
                need(w, before, start, step)
                value = value + later[w * (levels - 1) + before - 1][start : start + step, :]
            landed[w][start : start + step, :] = value
            if level < levels:
                later_copy(number).start()
            if w and number == w * per_work + min(2, per_work - 1):
                finish(w - 1)
        finish(works - 1)
        for number, (w, level, start, step) in enumerate(pieces):
            first_copy(number).wait_send()
            if level < levels:
                later_copy(number).wait_send()
        for w in range(works):
            store(w).wait()

    scratch = [pltpu.VMEM((2, chunk, wide), f32)]
    scratch += [pltpu.VMEM((rows // 2, n), f32) for n in widths]
    scratch += [
        pltpu.VMEM((rows >> (level + 1), n), f32) for n in widths for level in range(1, levels)
    ]
    scratch += [
        pltpu.SemaphoreType.DMA((2,)),
        pltpu.SemaphoreType.DMA((works,)),
    ] + [pltpu.SemaphoreType.DMA((len(pieces),))] * 4
    total = sum(rows * n * 4 for n in widths)
    return pl.pallas_call(
        kernel,
        out_shape=tuple(jax.ShapeDtypeStruct((share, n), f32) for n in widths),
        in_specs=[pl.BlockSpec(memory_space=pl.ANY)] * works,
        out_specs=tuple([pl.BlockSpec(memory_space=pl.ANY)] * works),
        scratch_shapes=scratch,
        compiler_params=pltpu.CompilerParams(
            collective_id=0, has_side_effects=True, vmem_limit_bytes=60 * 2**20
        ),
        cost_estimate=pl.CostEstimate(
            flops=total // 2, bytes_accessed=total // 4, transcendentals=0
        ),
    )(*parts)


def make_per_device(dp_size, t_size):
    def per_device(
        tokens,
        lengths,
        out_grad,
        input_gain,
        mamba_gate_weight,
        mamba_in_weight,
        state_weight,
        step_weight,
        conv_weight,
        conv_bias,
        conv_state_weight,
        conv_state_bias,
        step_bias,
        decay_log,
        skip_scale,
        mamba_gain,
        mamba_out_weight,
        query_weight,
        key_value_weight,
        attn_out_weight,
        ffn_gain,
        gate_weight,
        up_weight,
        down_weight,
    ):
        micro = tokens.shape[0]
        count = tokens.shape[1]
        width = tokens.shape[2]
        half = count // 2
        local_heads = step_weight.shape[1]
        q_local = query_weight.shape[1] // AHDIM
        kv_width = key_value_weight.shape[1] // 2
        group_size = AHEADS // KVHEADS
        me_dp = lax.axis_index("dp")
        me_t = lax.axis_index("tensor")
        core = lax.rem(me_t, 2)
        kv_head = me_t * q_local // group_size
        key_weight = lax.dynamic_slice_in_dim(key_value_weight, kv_head * AHDIM, AHDIM, 1)
        value_weight = lax.dynamic_slice_in_dim(
            key_value_weight, kv_width + kv_head * AHDIM, AHDIM, 1
        )
        rows = jnp.arange(count)
        freqs = rope_base ** (-(jnp.arange(AHDIM // 2).astype(f32) * 2.0) / AHDIM)
        angles = rows.astype(f32)[:, None] * freqs[None, :]
        cosine, sine = jnp.cos(angles), jnp.sin(angles)
        cosine = jnp.concatenate([cosine, cosine], axis=1)
        sine = jnp.concatenate([-sine, sine], axis=1)
        channels = mamba_in_weight.shape[1]
        heads_width = query_weight.shape[1]
        places, _ = columns_of(channels, heads_width)
        pad_step = LANES - local_heads

        def lane_row(vector):
            return jnp.pad(vector, (0, pad_step))[None]

        mixer_rows = (
            conv_weight, conv_bias[None], conv_state_weight, conv_state_bias[None],
            lane_row(step_bias), lane_row(jnp.exp(decay_log)), jnp.repeat(skip_scale, MHDIM)[None],
        )
        in_weight = jnp.concatenate(
            [
                mamba_gate_weight,
                query_weight,
                mamba_in_weight,
                state_weight,
                key_weight,
                value_weight,
                jnp.pad(step_weight, ((0, 0), (0, pad_step))),
            ],
            axis=1,
        )
        out_weight = jnp.concatenate([mamba_out_weight, attn_out_weight], axis=0)

        def t_swap(values, bit):
            return swap(values, "tensor", t_size, bit)

        def t_total(values):
            bit = 1
            while bit < t_size:
                values = values + t_swap(values, bit)
                bit *= 2
            return values

        def mine(values):
            return lax.dynamic_slice_in_dim(values, core * half, half, 0)

        def other(values):
            return lax.dynamic_slice_in_dim(values, (1 - core) * half, half, 0)

        def relative(values):
            return jnp.concatenate([mine(values), other(values)], axis=0)

        def in_order(own, far):
            return jnp.where(
                core == 0,
                jnp.concatenate([own, far], axis=0),
                jnp.concatenate([far, own], axis=0),
            )

        def half_sum(own, far, pieces):
            own = own + t_swap(far, 1)
            bit = 2
            while bit < t_size // 2:
                own = own + t_swap(own, bit)
                bit *= 2
            step = -(-own.shape[0] // (8 * pieces)) * 8
            parts = []
            for start in range(0, own.shape[0], step):
                parts.append(t_swap(own[start : start + step], bit))
            order.queue += parts
            return own, parts

        def add_up(own, parts):
            for part in parts:
                order.queue = [p for p in order.queue if p is not part]
            own, *parts = order.gate(own, *parts)
            return own + jnp.concatenate(parts, axis=0)

        block = width // dp_size

        order = Order()

        def forward(index, slot):
            inputs = slot.astype(f32)
            inv_one = lax.rsqrt(jnp.mean(inputs * inputs, axis=-1, keepdims=True) + epsilon)
            unit_one = inputs * inv_one
            normed = (unit_one * input_gain).astype(bf16)
            proj = order.point(plain_dot(normed, in_weight))
            gated, ssd, square, *kept, query, keys, values, logs, context = mixers_forward(
                index, channels, heads_width, lengths, proj, cosine, sine, *mixer_rows
            )
            gated = order.point(gated)
            total_square = t_total(jnp.sum(square, axis=-1))
            inv_mamba = lax.rsqrt(total_square / DSSM + epsilon)[:, None]
            scaled = (gated * inv_mamba * mamba_gain).astype(bf16)
            mixer = jnp.concatenate([scaled, context], axis=1)
            mixed_own, mixed_far = half_sum(
                plain_dot(mine(mixer), out_weight), plain_dot(other(mixer), out_weight), 3
            )
            order.mark(mixed_own)
            return dict(
                mixed_own=mixed_own, mixed_far=mixed_far, inputs=inputs, inv_one=inv_one,
                unit_one=unit_one, normed=normed, proj=proj, gated=gated, ssd=ssd, kept=kept,
                attention=(query, keys, values, logs), inv_mamba=inv_mamba, mixer=mixer,
            )

        def feed_forward(index, k):
            hidden_own = mine(k["inputs"]) + add_up(k["mixed_own"], k["mixed_far"])
            hidden = jnp.concatenate([hidden_own, t_swap(hidden_own, 1)], axis=0)
            inv_two = lax.rsqrt(jnp.mean(hidden * hidden, axis=-1, keepdims=True) + epsilon)
            unit_two = hidden * inv_two
            normed_two = (unit_two * ffn_gain).astype(bf16)
            gate = order.point(plain_dot(normed_two, gate_weight))
            upper = plain_dot(normed_two, up_weight)
            gsig = jax.nn.sigmoid(gate)
            gsilu = gate * gsig
            inner_ffn = (gsilu * upper).astype(bf16)
            valid = (rows < lengths[index]).astype(f32)[:, None]
            cotangent = relative(out_grad[index].astype(f32) * valid)
            cot_low = cotangent.astype(bf16)
            d_inner_ffn = order.point(right_trans(cot_low, down_weight))
            d_gate = (d_inner_ffn * upper * gsig * (1.0 + gate * (1.0 - gsig))).astype(bf16)
            d_up = (d_inner_ffn * gsilu).astype(bf16)
            far = right_trans(d_gate[half:], gate_weight) + right_trans(d_up[half:], up_weight)
            own = right_trans(d_gate[:half], gate_weight) + right_trans(d_up[:half], up_weight)
            back_own, back_far = half_sum(own, far, 3)
            order.mark(back_own)
            k.update(
                back_own=back_own, back_far=back_far,
                hidden=hidden, inv_two=inv_two[:half], unit_two=unit_two[:half],
                normed_two=normed_two, inner_ffn=inner_ffn, cotangent=cotangent, cot_low=cot_low,
                d_gate=d_gate, d_up=d_up,
            )

        def output_sum(k):
            (inner_ffn,) = order.gate(k["inner_ffn"])
            k["ffn_own"], k["ffn_far"] = half_sum(
                plain_dot(inner_ffn[:half], down_weight),
                plain_dot(inner_ffn[half:], down_weight),
                1,
            )
            order.mark(k["ffn_own"])

        def output(k):
            ffn_own = add_up(k["ffn_own"], k["ffn_far"])
            out = k["hidden"] + jnp.concatenate([ffn_own, t_swap(ffn_own, 1)], axis=0)
            out = in_order(out[:half], out[half:]).astype(bf16)
            order.mark(out)
            return out

        def back_head(k):
            unit_two = k["unit_two"]
            g_ffn_gain = jnp.sum(k["back_own"] * unit_two, axis=0)
            d_normed_two = add_up(k["back_own"], k["back_far"])
            d_unit_two = d_normed_two * ffn_gain
            d_rest = k["inv_two"] * (
                d_unit_two - unit_two * jnp.mean(d_unit_two * unit_two, axis=-1, keepdims=True)
            )
            d_both = k["cotangent"] + jnp.concatenate([d_rest, t_swap(d_rest, 1)], axis=0)
            d_mixed = in_order(d_both[:half], d_both[half:]).astype(bf16)
            d_mixer = right_trans(d_mixed, out_weight)
            k["g_ffn_gain"] = g_ffn_gain
            k["d_hidden"] = k["cotangent"][:half] + d_rest
            k["d_mixed"], k["d_mixer"] = d_mixed, d_mixer
            k["cross"] = t_total(
                jnp.sum(d_mixer[:, :channels] * mamba_gain * k["gated"], axis=-1)
            )[:, None]
            order.mark(d_mixer)

        def back_mixers(index, k, held):
            d_mixer, cross = order.gate(k["d_mixer"], k["cross"])
            inv = k["inv_mamba"]
            inv_cross = jnp.concatenate([inv, inv**3 * cross / DSSM], axis=1)
            inv_cross = jnp.pad(inv_cross, ((0, 0), (0, LANES - 2)))
            back, d_statepre, d_keys, d_values, g_conv, g_state, g_heads, g_skip, g_gain = (
                mixers_backward(
                    index, micro, held, lengths, d_mixer, k["gated"], inv_cross, mamba_gain[None],
                    k["proj"], k["ssd"], *k["kept"], *k["attention"], cosine, sine, *mixer_rows,
                )
            )
            kv_far = jnp.where(core == 0, d_values, d_keys)
            kv_own = jnp.where(core == 0, d_keys, d_values)
            k["kv_sum"] = kv_own + t_swap(kv_far, 1)
            k["d_statepre"] = d_statepre
            k.update(
                g_conv_weight=g_conv[:-1], g_conv_bias=g_conv[-1],
                g_conv_state_weight=g_state[:-1], g_conv_state_bias=g_state[-1],
                g_step_bias=g_heads[0, :local_heads], g_decay_log=g_heads[1, :local_heads],
                g_skip=jnp.sum(g_skip.reshape(local_heads, MHDIM), axis=1),
                g_mamba_gain=g_gain[0],
            )
            order.mark(back)
            return back

        def back_inputs(index, k, back):
            back, d_statepre = order.gate(back, k["d_statepre"])
            piece = d_statepre.shape[1] // t_size
            parts = [
                lax.dynamic_slice_in_dim(d_statepre, jnp.bitwise_xor(me_t, q) * piece, piece, 1)
                for q in range(t_size)
            ]
            pieces = halving_order(list(range(0, t_size, 2)), 2, t_size)
            state_sum = jnp.concatenate([parts[q] for q in pieces], axis=1) + t_swap(
                jnp.concatenate([parts[q ^ 1] for q in pieces], axis=1), 1
            )
            bit = 2
            while bit < t_size:
                cut = state_sum.shape[1] // 2
                state_sum = state_sum[:, :cut] + t_swap(state_sum[:, cut:], bit)
                bit *= 2
            k["shared"] = jnp.concatenate([state_sum, k["kv_sum"]], axis=1).astype(bf16)
            rows_own = lax.dynamic_slice_in_dim(back, index * count + core * half, half, 0)
            rows_far = lax.dynamic_slice_in_dim(back, index * count + (1 - core) * half, half, 0)
            k["norm_own"], k["norm_far"] = half_sum(
                right_trans(rows_own, in_weight), right_trans(rows_far, in_weight), 1
            )
            unit_own = mine(k["unit_one"])
            k["g_input_gain"] = jnp.sum(k["norm_own"] * unit_own, axis=0)
            order.mark(k["norm_own"])

        def input_grad(k):
            d_normed = add_up(k["norm_own"], k["norm_far"])
            unit_own = mine(k["unit_one"])
            d_unit_one = d_normed * input_gain
            grad_own = k["d_hidden"] + mine(k["inv_one"]) * (
                d_unit_one - unit_own * jnp.mean(d_unit_one * unit_own, axis=-1, keepdims=True)
            )
            grad = in_order(grad_own, t_swap(grad_own, 1))
            order.mark(grad)
            return grad

        slots = []
        for index in range(micro):
            slot = tokens[index]
            if index:
                (slot,) = order.gate(slot)
            slots.append(forward(index, slot))
        for index in range(micro):
            feed_forward(index, slots[index])

        def joined(name):
            return jnp.concatenate([k[name] for k in slots], axis=0)

        def relative_columns(values):
            blocks = halving_order(list(range(dp_size)), 1, dp_size)
            return jnp.concatenate(
                [
                    lax.dynamic_slice_in_dim(values, jnp.bitwise_xor(me_dp, r) * block, block, 1)
                    for r in blocks
                ],
                axis=1,
            )

        def scattered(part, dimension):
            return lax.psum_scatter(part, "dp", scatter_dimension=dimension, tiled=True)

        inner_all, cot_all = order.gate(joined("inner_ffn"), joined("cot_low"))
        part_down = left_trans(inner_all, cot_all)
        order.mark(part_down)
        g_down = scattered(part_down, 1)
        two_all = order.point(order.gate(joined("normed_two"))[0])
        part_gate = left_trans(two_all, joined("d_gate"))
        order.mark(part_gate)
        g_gate = scattered(part_gate, 0)
        two_all = order.point(order.gate(two_all)[0])
        part_up = left_trans(two_all, joined("d_up"))
        order.mark(part_up)
        g_up = scattered(part_up, 0)
        back = None
        for index, k in enumerate(slots):
            back_head(k)
            back = back_mixers(index, k, back)
            back_inputs(index, k, back)
            output_sum(k)
        (mixed_all,) = order.gate(joined("d_mixed"))
        part_outs = left_trans(relative_columns(mixed_all), joined("mixer"))
        one_columns = relative_columns(joined("normed"))
        part_early = left_trans(one_columns, back[:, : channels + heads_width])
        part_late = left_trans(
            one_columns,
            jnp.concatenate(
                [back[:, places["xpre"]], joined("shared"), back[:, places["step"]]], axis=1
            ),
        )
        order.mark(part_outs, part_early, part_late)

        def total(name):
            value = slots[0][name]
            for k in slots[1:]:
                value = value + k[name]
            return value

        names = [
            "g_conv_state_weight", "g_conv_state_bias", "g_input_gain", "g_ffn_gain",
            "g_conv_weight", "g_conv_bias", "g_step_bias", "g_decay_log", "g_skip",
            "g_mamba_gain",
        ]
        small = {name: total(name) for name in names}
        vector = jnp.concatenate([small[name].reshape(-1) for name in names])
        (vector,) = order.gate(vector)
        bit = 1
        while bit < dp_size:
            vector = vector + swap(vector, "dp", dp_size, bit)
            bit *= 2
        order.mark(vector)
        shared_size = sum(small[name].size for name in names[:4])
        wide_vector = t_total(vector[:shared_size])
        start = 0
        for name in names:
            shape, size = small[name].shape, small[name].size
            source = wide_vector if start < shared_size else vector
            small[name] = source[start : start + size].reshape(shape)
            start += size
        place = me_dp * t_size + me_t
        share = conv_state_bias.shape[0] // (dp_size * t_size)
        g_conv_state_weight = lax.dynamic_slice_in_dim(
            small["g_conv_state_weight"], place * share, share, 1
        )
        g_conv_state_bias = lax.dynamic_slice_in_dim(
            small["g_conv_state_bias"], place * share, share, 0
        )
        g_input_gain = lax.dynamic_slice_in_dim(small["g_input_gain"], me_dp * block, block, 0)
        g_ffn_gain = lax.dynamic_slice_in_dim(small["g_ffn_gain"], me_dp * block, block, 0)
        heads = [small[name] for name in names[4:]]

        outputs_list = [output(k) for k in slots]
        part_outs, part_early, part_late = order.gate(part_outs, part_early, part_late)
        g_outs, g_early, g_late = scatter_all(dp_size, [part_outs, part_early, part_late])
        order.mark(g_late)
        g_outs = g_outs.T
        shared_end = channels + joined("shared").shape[1]
        g_step = g_late[:, shared_end : shared_end + local_heads]
        g_late = g_late[:, :shared_end]
        grads_list = [input_grad(k) for k in slots]

        mamba_cols = mamba_in_weight.shape[1]
        tail = g_late[:, mamba_cols:]
        sub = block // t_size
        rowsets = []
        for q in range(t_size):
            part = lax.dynamic_slice_in_dim(tail, jnp.bitwise_xor(me_t, q) * sub, sub, 0)
            rowsets.append(part if q == 0 else t_swap(part, q))
        stacked = jnp.stack(rowsets)
        piece = state_weight.shape[1] // t_size
        sources = [
            lax.dynamic_index_in_dim(stacked, jnp.bitwise_xor(me_t, j), 0, keepdims=False)
            for j in range(t_size)
        ]
        g_state = jnp.concatenate([s[:, :piece] for s in sources], axis=1)
        pairs = t_size // 2
        g_kv = jnp.concatenate(
            [sources[(b % pairs) * 2 + b // pairs][:, piece:] for b in range(t_size)], axis=1
        )
        gate_cols = mamba_gate_weight.shape[1]
        mamba_rows = mamba_out_weight.shape[0]
        return (
            jnp.stack(outputs_list),
            jnp.stack(grads_list),
            g_input_gain,
            g_early[:, :gate_cols],
            g_late[:, :mamba_cols],
            g_state,
            g_step,
            heads[0],
            heads[1],
            g_conv_state_weight,
            g_conv_state_bias,
            heads[2],
            heads[3],
            heads[4],
            heads[5],
            g_outs[:mamba_rows],
            g_early[:, gate_cols:],
            g_kv,
            g_outs[mamba_rows:],
            g_ffn_gain,
            g_gate,
            g_up,
            g_down,
        )

    return per_device


def solution(mesh):
    placed = (
        P("dp", None, None),
        P("dp"),
        P("dp", None, None),
        P(),
        P(None, "tensor"),
        P(None, "tensor"),
        P(),
        P(None, "tensor"),
        P(None, "tensor"),
        P("tensor"),
        P(),
        P(),
        P("tensor"),
        P("tensor"),
        P("tensor"),
        P("tensor"),
        P("tensor", None),
        P(None, "tensor"),
        P(),
        P("tensor", None),
        P(),
        P(None, "tensor"),
        P(None, "tensor"),
        P("tensor", None),
    )
    return jax.shard_map(
        make_per_device(mesh.shape["dp"], mesh.shape["tensor"]),
        mesh=mesh,
        in_specs=placed,
        out_specs=(
            P("dp", None, None),
            P("dp", None, None),
            P("dp"),
            P("dp", "tensor"),
            P("dp", "tensor"),
            P(("dp", "tensor"), None),
            P("dp", "tensor"),
            P(None, "tensor"),
            P("tensor"),
            P(None, ("dp", "tensor")),
            P(("dp", "tensor")),
            P("tensor"),
            P("tensor"),
            P("tensor"),
            P("tensor"),
            P("tensor", "dp"),
            P("dp", "tensor"),
            P(("dp", "tensor"), None),
            P("tensor", "dp"),
            P("dp"),
            P("dp", "tensor"),
            P("dp", "tensor"),
            P("tensor", "dp"),
        ),
        check_vma=False,
    )
```

```python
import functools

import jax
import jax.numpy as jnp
from jax import lax
from jax.experimental import pallas as pl
from jax.experimental.pallas import tpu as pltpu
from jax.sharding import PartitionSpec as P

MHDIM = 64
STATE = 256
AHEADS = 8
KVHEADS = 2
AHDIM = 128
DSSM = 3072

epsilon = 1e-05
rope_base = 100000000000.0
f32 = jnp.float32
bf16 = jnp.bfloat16


def plain_dot(left, right):
    return jnp.dot(left, right, preferred_element_type=f32)


def right_trans(left, right):
    return lax.dot_general(left, right, (((1,), (1,)), ((), ())), preferred_element_type=f32)


def left_trans(left, right):
    return lax.dot_general(left, right, (((0,), (0,)), ((), ())), preferred_element_type=f32)


def silu_slope(values):
    sig = jax.nn.sigmoid(values)
    return sig * (1.0 + values * (1.0 - sig))


MESH = pl.DeviceIdType.MESH
LANES = 128
BLOCK = 128


def shifted(values, steps, row):
    if steps == 0:
        return values
    count = values.shape[0]
    moved = pltpu.roll(values, steps % count, 0)
    if steps > 0:
        return jnp.where(row >= steps, moved, 0.0)
    return jnp.where(row < count + steps, moved, 0.0)


def tap_sum(values, taps, bias):
    row = lax.broadcasted_iota(jnp.int32, values.shape, 0)
    width = taps.shape[0]
    total = jnp.zeros_like(values) + bias
    for k in range(width):
        total = total + shifted(values, width - 1 - k, row) * taps[k : k + 1, :]
    return total


def tap_back(grads, values, taps):
    row = lax.broadcasted_iota(jnp.int32, values.shape, 0)
    width = taps.shape[0]
    back = jnp.zeros_like(values)
    tap_grads = []
    for k in range(width):
        steps = width - 1 - k
        back = back + shifted(grads, -steps, row) * taps[k : k + 1, :]
        tap_grads.append(jnp.sum(grads * shifted(values, steps, row), axis=0, keepdims=True))
    return back, jnp.concatenate(tap_grads, axis=0)


def column_of(values, lane, index):
    return jnp.sum(jnp.where(lane == index, values, 0.0), axis=1, keepdims=True)


def exact_dot(left, right):
    return jnp.dot(left, right, precision=lax.Precision.HIGHEST, preferred_element_type=f32)


def turned(values, cosine, sine):
    return values * cosine + pltpu.roll(values, AHDIM // 2, 1) * sine


def scores_of(query, keys, lo, hi, length):
    scores = right_trans(query[lo:hi], keys[:hi]) * AHDIM ** (-0.5)
    t = lax.broadcasted_iota(jnp.int32, (hi - lo, hi), 0) + lo
    s = lax.broadcasted_iota(jnp.int32, (hi - lo, hi), 1)
    return scores, (t >= s) & (s < length)


def attention_forward(query_pre, key_pre, value_pre, cosine, sine, length, query, keys, values, logs, context):
    count, width = query.shape
    keys[...] = turned(key_pre, cosine, sine).astype(bf16)
    values[...] = value_pre.astype(bf16)
    lane = lax.broadcasted_iota(jnp.int32, (count, LANES), 1)
    kept = jnp.zeros((count, LANES), f32)
    for h in range(width // AHDIM):
        lanes = slice(h * AHDIM, (h + 1) * AHDIM)
        query[:, lanes] = turned(query_pre[:, lanes], cosine, sine).astype(bf16)
        found = []
        for i in range(count // BLOCK):
            lo, hi = i * BLOCK, (i + 1) * BLOCK
            scores, valid = scores_of(query[:, lanes], keys[...], lo, hi, length)
            masked = jnp.where(valid, scores, -1e30)
            peak = jnp.max(masked, axis=1, keepdims=True)
            expo = jnp.exp(masked - peak)
            total = jnp.sum(expo, axis=1, keepdims=True)
            found.append(peak + jnp.log(total))
            probs = (expo / total).astype(bf16)
            context[lo:hi, lanes] = plain_dot(probs, values[:hi, :]).astype(bf16)
        kept = jnp.where(lane == h, jnp.concatenate(found, axis=0), kept)
    logs[...] = kept


def attention_backward(d_context, query, keys, values, logs, cosine, sine, length, d_query_pre, d_keys, d_values):
    count, width = query.shape
    lane = lax.broadcasted_iota(jnp.int32, (count, LANES), 1)
    scale = AHDIM ** (-0.5)
    key_total = jnp.zeros((count, AHDIM), f32)
    value_total = jnp.zeros((count, AHDIM), f32)
    for h in range(width // AHDIM):
        lanes = slice(h * AHDIM, (h + 1) * AHDIM)
        log = column_of(logs[...], lane, h)
        pieces = []
        for i in range(count // BLOCK):
            lo, hi = i * BLOCK, (i + 1) * BLOCK
            scores, valid = scores_of(query[:, lanes], keys[...], lo, hi, length)
            probs = jnp.where(valid, jnp.exp(scores - log[lo:hi]), 0.0)
            grads = d_context[lo:hi, lanes]
            d_probs = right_trans(grads, values[:hi, :])
            delta = jnp.sum(probs * d_probs, axis=1, keepdims=True)
            d_scores = (probs * (d_probs - delta)).astype(bf16)
            pieces.append(plain_dot(d_scores, keys[:hi, :]) * scale)
            d_key = left_trans(d_scores, query[lo:hi, lanes]) * scale
            d_value = left_trans(probs.astype(bf16), grads)
            if hi < count:
                rest = jnp.zeros((count - hi, AHDIM), f32)
                d_key = jnp.concatenate([d_key, rest], axis=0)
                d_value = jnp.concatenate([d_value, rest], axis=0)
            key_total = key_total + d_key
            value_total = value_total + d_value
        d_query_pre[:, lanes] = turned(jnp.concatenate(pieces, axis=0), cosine, -sine).astype(bf16)
    d_keys[...] = turned(key_total, cosine, -sine)
    d_values[...] = value_total


def columns_of(channels, heads_width):
    places, start = {}, 0
    for name, size in (
        ("zgate", channels), ("query", heads_width), ("xpre", channels), ("state", 2 * STATE),
        ("key", AHDIM), ("value", AHDIM), ("step", LANES),
    ):
        places[name] = slice(start, start + size)
        start += size
    return places, start


def forward_kernel(
    lengths, proj, cosine, sine, conv_weight, conv_bias, state_taps, state_bias, step_bias, rates,
    skip_rep, gated, ssd, square, xconv, sconv, stepsize, cumul, inner, query, keys, values, logs,
    context, cumul_rows, *, slot, places,
):
    xpre, zgate = proj.at[:, places["xpre"]], proj.at[:, places["zgate"]]
    statepre, steppre = proj.at[:, places["state"]], proj.at[:, places["step"]]
    attention_forward(
        proj.at[:, places["query"]], proj[:, places["key"]], proj[:, places["value"]],
        cosine[...], sine[...], lengths[slot], query, keys, values, logs, context,
    )
    count, channels = xpre.shape
    xlin = tap_sum(xpre[...], conv_weight[...], conv_bias[...])
    xconv[...] = (xlin * jax.nn.sigmoid(xlin)).astype(bf16)
    slin = tap_sum(statepre[...], state_taps[...], state_bias[...])
    sconv[...] = (slin * jax.nn.sigmoid(slin)).astype(bf16)
    inner[...] = right_trans(sconv[:, STATE:], sconv[:, :STATE])
    step = jax.nn.softplus(steppre[...] + step_bias[...])
    stepsize[...] = step
    row = lax.broadcasted_iota(jnp.int32, (count, count), 0)
    col = lax.broadcasted_iota(jnp.int32, (count, count), 1)
    total = exact_dot(jnp.where(row >= col, 1.0, 0.0), -step * rates[...])
    cumul[...] = total
    cumul_rows[...] = total.T
    square[...] = jnp.zeros_like(square)

    def pair(p):
        lanes = slice(p * LANES, (p + 1) * LANES)
        lane = lax.broadcasted_iota(jnp.int32, (count, LANES), 1)
        xvals = xconv[:, lanes].astype(f32)
        low_half = lane < MHDIM
        step_rep = jnp.where(
            low_half, column_of(stepsize[...], lane, 2 * p), column_of(stepsize[...], lane, 2 * p + 1)
        )
        weighted = (step_rep * xvals).astype(bf16)
        columns = [column_of(cumul[...], lane, 2 * p + h) for h in range(2)]
        for i in range(count // BLOCK):
            lo, hi = i * BLOCK, (i + 1) * BLOCK
            results = []
            for h in range(2):
                differ = columns[h][lo:hi] - cumul_rows[2 * p + h : 2 * p + h + 1, :hi]
                t = lax.broadcasted_iota(jnp.int32, (BLOCK, hi), 0) + lo
                s = lax.broadcasted_iota(jnp.int32, (BLOCK, hi), 1)
                decay = jnp.exp(jnp.where(t >= s, differ, -1e30))
                mixing = (inner[lo:hi, :hi] * decay).astype(bf16)
                results.append(plain_dot(mixing, weighted[:hi]))
            half = jnp.where(low_half[lo:hi], results[0], results[1])
            half = half + skip_rep[:, lanes] * xvals[lo:hi]
            ssd[lo:hi, lanes] = half
            z = zgate[lo:hi, lanes]
            value = half * (z * jax.nn.sigmoid(z))
            gated[lo:hi, lanes] = value
            square[lo:hi, :] += value * value

    for p in range(channels // LANES):
        pair(p)


def full(*shape):
    return jax.ShapeDtypeStruct(shape, f32)


def low(*shape):
    return jax.ShapeDtypeStruct(shape, bf16)


def in_vmem(count):
    return [pl.BlockSpec(memory_space=pltpu.VMEM)] * count


def mixers_forward(slot, channels, heads_width, lengths, proj, *rest):
    count = proj.shape[0]
    return pl.pallas_call(
        functools.partial(
            forward_kernel, slot=slot, places=columns_of(channels, heads_width)[0]
        ),
        out_shape=(
            full(count, channels), full(count, channels), full(count, LANES), low(count, channels),
            low(count, 2 * STATE), full(count, LANES), full(count, LANES), full(count, count),
            low(count, heads_width), low(count, AHDIM), low(count, AHDIM), full(count, LANES),
            low(count, heads_width),
        ),
        in_specs=[pl.BlockSpec(memory_space=pltpu.SMEM)] + in_vmem(1 + len(rest)),
        out_specs=tuple(in_vmem(13)),
        scratch_shapes=[pltpu.VMEM((LANES, count), f32)],
        compiler_params=pltpu.CompilerParams(vmem_limit_bytes=48 * 2**20),
        cost_estimate=pl.CostEstimate(
            flops=10**6, bytes_accessed=10**6, transcendentals=10**3
        ),
    )(lengths, proj, *rest)


def backward_kernel(
    lengths, d_mixer, gated_in, inv_cross, gain, proj, ssd, xconv, sconv, stepsize, cumul, inner,
    query, keys, values, logs, cosine, sine, conv_weight, conv_bias, state_taps, state_bias,
    step_bias, rates, skip_rep,
    back, d_statepre, d_keys, d_values, g_conv, g_state, g_heads, g_skip, g_gain,
    d_ssd, d_xvals, cumul_rows, d_inner, row_sums, col_sums, d_step, *, slot, places,
):
    count, channels = ssd.shape
    xpre, zgate = proj.at[:, places["xpre"]], proj.at[:, places["zgate"]]
    statepre, steppre = proj.at[:, places["state"]], proj.at[:, places["step"]]
    attention_backward(
        d_mixer[:, channels:].astype(bf16), query, keys, values, logs, cosine[...], sine[...],
        lengths[slot], back.at[:, places["query"]], d_keys, d_values,
    )
    back[:, places["key"]] = d_keys[...].astype(bf16)
    back[:, places["value"]] = d_values[...].astype(bf16)
    d_zgate, d_xpre = back.at[:, places["zgate"]], back.at[:, places["xpre"]]
    d_steppre = back.at[:, places["step"]]
    d_scaled = d_mixer[:, :channels]
    g_gain[...] = jnp.sum(d_scaled * gated_in[...] * inv_cross[:, 0:1], axis=0, keepdims=True)
    inv = inv_cross[:, 0:1]
    cross = inv_cross[:, 1:2]
    d_gated = inv * (d_scaled * gain[...]) - gated_in[...] * cross
    z = zgate[...]
    sig = jax.nn.sigmoid(z)
    d_low = (d_gated * (z * sig)).astype(bf16)
    d_ssd[...] = d_low
    d_zgate[...] = (d_gated * ssd[...] * sig * (1.0 + z * (1.0 - sig))).astype(bf16)
    g_skip[...] = jnp.sum(d_low.astype(f32) * xconv[...].astype(f32), axis=0, keepdims=True)
    cumul_rows[...] = cumul[...].T
    d_inner[...] = jnp.zeros_like(d_inner)
    row_sums[...] = jnp.zeros_like(row_sums)
    col_sums[...] = jnp.zeros_like(col_sums)
    d_step[...] = jnp.zeros_like(d_step)

    def pair(p):
        lanes = slice(p * LANES, (p + 1) * LANES)
        lane = lax.broadcasted_iota(jnp.int32, (count, LANES), 1)
        low_half = lane < MHDIM
        xvals = xconv[:, lanes].astype(f32)
        step_rep = jnp.where(
            low_half, column_of(stepsize[...], lane, 2 * p), column_of(stepsize[...], lane, 2 * p + 1)
        )
        weighted = (step_rep * xvals).astype(bf16)
        grads = d_ssd[:, lanes]
        columns = [column_of(cumul[...], lane, 2 * p + h) for h in range(2)]
        pieces = []
        for h in range(2):
            only = jnp.where(low_half == (h == 0), grads, jnp.zeros_like(grads))
            back_part = jnp.zeros((count, LANES), f32)
            sums = []
            col_total = jnp.zeros((1, count), f32)
            for i in range(count // BLOCK):
                lo, hi = i * BLOCK, (i + 1) * BLOCK
                differ = columns[h][lo:hi] - cumul_rows[2 * p + h : 2 * p + h + 1, :hi]
                t = lax.broadcasted_iota(jnp.int32, (BLOCK, hi), 0) + lo
                s = lax.broadcasted_iota(jnp.int32, (BLOCK, hi), 1)
                decay = jnp.exp(jnp.where(t >= s, differ, -1e30))
                mixing = inner[lo:hi, :hi] * decay
                part = left_trans(mixing.astype(bf16), only[lo:hi])
                d_mixing = right_trans(only[lo:hi], weighted[:hi])
                d_inner[lo:hi, :hi] += d_mixing * decay
                flow = d_mixing * mixing
                sums.append(jnp.sum(flow, axis=1, keepdims=True))
                down = jnp.sum(flow, axis=0, keepdims=True)
                if hi < count:
                    part = jnp.concatenate([part, jnp.zeros((count - hi, LANES), f32)], axis=0)
                    down = jnp.concatenate([down, jnp.zeros((1, count - hi), f32)], axis=1)
                back_part = back_part + part
                col_total = col_total + down
            here = lane == 2 * p + h
            row_sums[...] = jnp.where(here, jnp.concatenate(sums, axis=0), row_sums[...])
            col_sums[2 * p + h : 2 * p + h + 1, :] = col_total
            pieces.append(back_part)
        d_weighted = pieces[0] + pieces[1]
        d_xvals[:, lanes] = grads.astype(f32) * skip_rep[:, lanes] + d_weighted * step_rep
        product = d_weighted * xvals
        for h in range(2):
            value = jnp.sum(
                jnp.where(low_half == (h == 0), product, 0.0), axis=1, keepdims=True
            )
            d_step[...] = jnp.where(lane == 2 * p + h, value, d_step[...])

    for p in range(channels // LANES):
        pair(p)

    d_cumul = row_sums[...] - col_sums[...].T
    row = lax.broadcasted_iota(jnp.int32, (count, count), 0)
    col = lax.broadcasted_iota(jnp.int32, (count, count), 1)
    d_logdecay = exact_dot(jnp.where(row <= col, 1.0, 0.0), d_cumul)
    rate = rates[...]
    d_full = (d_step[...] - d_logdecay * rate) * jax.nn.sigmoid(steppre[...] + step_bias[...])
    d_steppre[...] = d_full.astype(bf16)
    g_heads[0:1, :] = jnp.sum(d_full, axis=0, keepdims=True)
    g_heads[1:2, :] = jnp.sum(-d_logdecay * stepsize[...] * rate, axis=0, keepdims=True)

    d_in = d_inner[...].astype(bf16)
    d_c = plain_dot(d_in, sconv[:, :STATE])
    d_b = left_trans(d_in, sconv[:, STATE:])
    slin = tap_sum(statepre[...], state_taps[...], state_bias[...])
    d_slin = jnp.concatenate([d_b, d_c], axis=1) * silu_slope(slin)
    back_state, tap_grads = tap_back(d_slin, statepre[...], state_taps[...])
    d_statepre[...] = back_state
    back[:, places["state"]] = back_state.astype(bf16)
    g_state[...] = jnp.concatenate([tap_grads, jnp.sum(d_slin, axis=0, keepdims=True)], axis=0)
    xlin = tap_sum(xpre[...], conv_weight[...], conv_bias[...])
    d_xlin = d_xvals[...] * silu_slope(xlin)
    back_x, tap_grads = tap_back(d_xlin, xpre[...], conv_weight[...])
    d_xpre[...] = back_x.astype(bf16)
    g_conv[...] = jnp.concatenate([tap_grads, jnp.sum(d_xlin, axis=0, keepdims=True)], axis=0)


def mixers_backward(slot, slots, held, lengths, d_mixer, gated, inv_cross, gain, proj, ssd, *rest):
    count, channels = ssd.shape
    width = proj.shape[1]
    heads_width = d_mixer.shape[1] - channels
    taps = rest[11].shape[0]
    operands = (d_mixer, gated, inv_cross, gain, proj, ssd) + rest
    kernel = functools.partial(
        backward_kernel, slot=slot, places=columns_of(channels, heads_width)[0]
    )
    aliases = {}
    extra_specs, extra = [], ()
    if held is not None:
        aliases = {0: 0}
        extra_specs, extra = [pl.BlockSpec(memory_space=pl.ANY)], (held,)
        inside = kernel
        kernel = lambda _, *refs: inside(*refs)
    return pl.pallas_call(
        kernel,
        grid=(1,),
        out_shape=(
            low(slots * count, width), full(count, 2 * STATE), full(count, AHDIM),
            full(count, AHDIM), full(taps + 1, channels), full(taps + 1, 2 * STATE),
            full(2, LANES), full(1, channels), full(1, channels),
        ),
        in_specs=extra_specs
        + [pl.BlockSpec(memory_space=pltpu.SMEM)]
        + in_vmem(len(operands)),
        out_specs=tuple([pl.BlockSpec((count, width), lambda i: (slot, 0))] + in_vmem(8)),
        scratch_shapes=[
            pltpu.VMEM((count, channels), bf16),
            pltpu.VMEM((count, channels), f32),
            pltpu.VMEM((LANES, count), f32),
            pltpu.VMEM((count, count), f32),
            pltpu.VMEM((count, LANES), f32),
            pltpu.VMEM((LANES, count), f32),
            pltpu.VMEM((count, LANES), f32),
        ],
        input_output_aliases=aliases,
        compiler_params=pltpu.CompilerParams(vmem_limit_bytes=56 * 2**20),
        cost_estimate=pl.CostEstimate(
            flops=10**6, bytes_accessed=10**6, transcendentals=10**3
        ),
    )(*extra, lengths, *operands)


def swap(values, axis, size, bit):
    return lax.ppermute(values, axis, [(i, i ^ bit) for i in range(size)])


def halving_order(members, bit, limit):
    if bit >= limit:
        return members
    low = halving_order([m for m in members if not m & bit], bit * 2, limit)
    high = halving_order([m for m in members if m & bit], bit * 2, limit)
    return low + high


class Order:
    def __init__(self):
        self.last = ()
        self.queue = []

    def point(self, value):
        if not self.queue:
            return value
        return lax.optimization_barrier((value, self.queue.pop(0)))[0]

    def gate(self, *values):
        return lax.optimization_barrier((values, self.last))[0]

    def mark(self, *values):
        self.last = values


def scatter_all(size, parts, halves):
    rows = parts[0].shape[0]
    works = len(parts)
    share = rows // size
    chunk = min(256, rows // 4)
    levels = size.bit_length() - 1
    spans = []
    for level in range(1, levels):
        lo, hi = rows >> (level + 1), rows >> level
        step = min(chunk, hi - lo)
        spans += [(level, start, step) for start in range(hi - step, lo - 1, -step)]
    spans.append((levels, 0, share))
    pieces = [(w,) + span for w in range(works) for span in spans]
    per_work = len(spans)
    widths = [p.shape[1] for p in parts]
    wide = max(widths)
    extra = len(halves)
    half_shape = halves[0].shape

    def kernel(*refs):
        held_in, refs = refs[:works], refs[works:]
        own, refs = refs[:extra], refs[extra:]
        outs, refs = refs[:works], refs[works:]
        mine, theirs, far, refs = (
            refs[:extra], refs[extra : 2 * extra], refs[2 * extra : 3 * extra], refs[3 * extra :]
        )
        loads, pair_loads, totals, refs = refs[0], refs[1], refs[2], refs[3:]
        landed, refs = refs[:works], refs[works:]
        later, refs = refs[: works * (levels - 1)], refs[works * (levels - 1) :]
        load_sems, out_sems, x_send, x_recv, z_send, z_recv, y_sems, c_sems, pair_sems = refs
        me = lax.axis_index("dp")
        spot = lax.axis_index("tensor")

        def neighbour(bit):
            return spot + bit - 2 * bit * lax.rem(spot // bit, 2)


        def partner(level):
            bit = 1 << level
            return me + bit - 2 * bit * lax.rem(me // bit, 2)

        barrier = pltpu.get_barrier_semaphore()
        for level in range(levels):
            pl.semaphore_signal(
                barrier, inc=1, device_id={"dp": partner(level)}, device_id_type=MESH
            )
        for bit in (1, 2):
            pl.semaphore_signal(
                barrier, inc=1, device_id={"tensor": neighbour(bit)}, device_id_type=MESH
            )
        pl.semaphore_wait(barrier, levels + 2)

        def y_copy(e):
            return pltpu.make_async_remote_copy(
                src_ref=own[e], dst_ref=far[e], send_sem=y_sems.at[0, e], recv_sem=y_sems.at[1, e],
                device_id={"tensor": neighbour(2)}, device_id_type=MESH,
            )

        def c_copy(e):
            return pltpu.make_async_remote_copy(
                src_ref=totals.at[e], dst_ref=theirs[e], send_sem=c_sems.at[0, e],
                recv_sem=c_sems.at[1, e], device_id={"tensor": neighbour(1)}, device_id_type=MESH,
            )

        def pair_copy(e, which):
            if which == 2:
                return pltpu.make_async_copy(totals.at[e], mine[e], pair_sems.at[2, e])
            source = own[e] if which == 0 else far[e]
            return pltpu.make_async_copy(source, pair_loads.at[which], pair_sems.at[which, e])

        def exchange(e):
            y_copy(e).wait_recv()
            pair_copy(e, 0).start()
            pair_copy(e, 1).start()
            pair_copy(e, 0).wait()
            pair_copy(e, 1).wait()
            totals[e] = pair_loads[0] + pair_loads[1]
            pair_copy(e, 2).start()
            c_copy(e).start()


        def first_copy(number):
            w, _, start, step = pieces[number]
            return pltpu.make_async_remote_copy(
                src_ref=held_in[w].at[pl.ds(rows // 2 + start, step), :],
                dst_ref=landed[w].at[pl.ds(start, step), :],
                send_sem=x_send.at[number],
                recv_sem=x_recv.at[number],
                device_id={"dp": partner(0)},
                device_id_type=MESH,
            )

        def load(number):
            w, _, start, step = pieces[number]
            return pltpu.make_async_copy(
                held_in[w].at[pl.ds(start, step), :],
                loads.at[number % 2, pl.ds(0, step), pl.ds(0, widths[w])],
                load_sems.at[number % 2],
            )

        def later_copy(number):
            w, level, start, step = pieces[number]
            return pltpu.make_async_remote_copy(
                src_ref=landed[w].at[pl.ds(start, step), :],
                dst_ref=later[w * (levels - 1) + level - 1].at[pl.ds(start - (rows >> (level + 1)), step), :],
                send_sem=z_send.at[number],
                recv_sem=z_recv.at[number],
                device_id={"dp": partner(level)},
                device_id_type=MESH,
            )

        def store(w):
            return pltpu.make_async_copy(
                landed[w].at[pl.ds(0, share), :], outs[w], out_sems.at[w]
            )

        for e in range(extra):
            y_copy(e).start()
        for number in range(len(pieces)):
            first_copy(number).start()
        load(0).start()
        arrived = set()

        def need(w, level, start, step):
            base = rows >> (level + 1)
            for other in range(w * per_work, (w + 1) * per_work):
                _, its_level, its_start, its_step = pieces[other]
                if its_level != level or other in arrived:
                    continue
                if its_start - base < start + step and start < its_start - base + its_step:
                    later_copy(other).wait_recv()
                    arrived.add(other)

        def finish(w):
            level = levels - 1
            need(w, level, 0, share)
            landed[w][:share, :] += later[w * (levels - 1) + level - 1][:share, :]
            store(w).start()

        for number, (w, level, start, step) in enumerate(pieces):
            load(number).wait()
            if number + 1 < len(pieces):
                load(number + 1).start()
            first_copy(number).wait_recv()
            value = loads[number % 2, :step, : widths[w]] + landed[w][start : start + step, :]
            for before in range(1, min(level, levels - 1)):
                need(w, before, start, step)
                value = value + later[w * (levels - 1) + before - 1][start : start + step, :]
            landed[w][start : start + step, :] = value
            if level < levels:
                later_copy(number).start()
            if w and number == w * per_work + min(2, per_work - 1):
                finish(w - 1)
            if number % 2 and number // 2 <= extra and number > 1:
                exchange(number // 2 - 1)
        for e in range((len(pieces) - 1) // 2, extra):
            exchange(e)
        finish(works - 1)
        for e in range(extra):
            y_copy(e).wait_send()
            c_copy(e).wait()
            pair_copy(e, 2).wait()
        for number, (w, level, start, step) in enumerate(pieces):
            first_copy(number).wait_send()
            if level < levels:
                later_copy(number).wait_send()
        for w in range(works):
            store(w).wait()

    scratch = [
        pltpu.VMEM((2, chunk, wide), f32),
        pltpu.VMEM((2,) + half_shape, f32),
        pltpu.VMEM((extra,) + half_shape, f32),
    ]
    scratch += [pltpu.VMEM((rows // 2, n), f32) for n in widths]
    scratch += [
        pltpu.VMEM((rows >> (level + 1), n), f32) for n in widths for level in range(1, levels)
    ]
    scratch += [
        pltpu.SemaphoreType.DMA((2,)),
        pltpu.SemaphoreType.DMA((works,)),
    ] + [pltpu.SemaphoreType.DMA((len(pieces),))] * 4
    scratch += [pltpu.SemaphoreType.DMA((n, extra)) for n in (2, 2, 3)]
    results = pl.pallas_call(
        kernel,
        out_shape=tuple([full(share, n) for n in widths] + [full(*half_shape)] * (3 * extra)),
        in_specs=[pl.BlockSpec(memory_space=pl.ANY)] * (works + extra),
        out_specs=tuple([pl.BlockSpec(memory_space=pl.ANY)] * (works + 3 * extra)),
        scratch_shapes=scratch,
        compiler_params=pltpu.CompilerParams(
            collective_id=0, has_side_effects=True, vmem_limit_bytes=60 * 2**20
        ),
        cost_estimate=pl.CostEstimate(
            flops=10**6, bytes_accessed=10**6, transcendentals=0
        ),
    )(*parts, *halves)
    return results[:works], results[works : works + extra], results[works + extra : works + 2 * extra]


def make_per_device(dp_size, t_size):
    def per_device(
        tokens,
        lengths,
        out_grad,
        input_gain,
        mamba_gate_weight,
        mamba_in_weight,
        state_weight,
        step_weight,
        conv_weight,
        conv_bias,
        conv_state_weight,
        conv_state_bias,
        step_bias,
        decay_log,
        skip_scale,
        mamba_gain,
        mamba_out_weight,
        query_weight,
        key_value_weight,
        attn_out_weight,
        ffn_gain,
        gate_weight,
        up_weight,
        down_weight,
    ):
        micro = tokens.shape[0]
        count = tokens.shape[1]
        width = tokens.shape[2]
        half = count // 2
        local_heads = step_weight.shape[1]
        q_local = query_weight.shape[1] // AHDIM
        kv_width = key_value_weight.shape[1] // 2
        group_size = AHEADS // KVHEADS
        me_dp = lax.axis_index("dp")
        me_t = lax.axis_index("tensor")
        core = lax.rem(me_t, 2)
        kv_head = me_t * q_local // group_size
        key_weight = lax.dynamic_slice_in_dim(key_value_weight, kv_head * AHDIM, AHDIM, 1)
        value_weight = lax.dynamic_slice_in_dim(
            key_value_weight, kv_width + kv_head * AHDIM, AHDIM, 1
        )
        rows = jnp.arange(count)
        freqs = rope_base ** (-(jnp.arange(AHDIM // 2).astype(f32) * 2.0) / AHDIM)
        angles = rows.astype(f32)[:, None] * freqs[None, :]
        cosine, sine = jnp.cos(angles), jnp.sin(angles)
        cosine = jnp.concatenate([cosine, cosine], axis=1)
        sine = jnp.concatenate([-sine, sine], axis=1)
        channels = mamba_in_weight.shape[1]
        heads_width = query_weight.shape[1]
        places, _ = columns_of(channels, heads_width)
        pad_step = LANES - local_heads

        def lane_row(vector):
            return jnp.pad(vector, (0, pad_step))[None]

        mixer_rows = (
            conv_weight, conv_bias[None], conv_state_weight, conv_state_bias[None],
            lane_row(step_bias), lane_row(jnp.exp(decay_log)), jnp.repeat(skip_scale, MHDIM)[None],
        )
        in_weight = jnp.concatenate(
            [
                mamba_gate_weight,
                query_weight,
                mamba_in_weight,
                state_weight,
                key_weight,
                value_weight,
                jnp.pad(step_weight, ((0, 0), (0, pad_step))),
            ],
            axis=1,
        )
        out_weight = jnp.concatenate([mamba_out_weight, attn_out_weight], axis=0)

        def t_swap(values, bit):
            return swap(values, "tensor", t_size, bit)

        def t_total(values):
            bit = 1
            while bit < t_size:
                values = values + t_swap(values, bit)
                bit *= 2
            return values

        def mine(values):
            return lax.dynamic_slice_in_dim(values, core * half, half, 0)

        def other(values):
            return lax.dynamic_slice_in_dim(values, (1 - core) * half, half, 0)

        def halves(values):
            values = lax.optimization_barrier(values)
            return mine(values), other(values)

        def relative(values):
            return jnp.concatenate([mine(values), other(values)], axis=0)

        def in_order(own, far):
            return jnp.where(
                core == 0,
                jnp.concatenate([own, far], axis=0),
                jnp.concatenate([far, own], axis=0),
            )

        def half_sum(own, far, pieces):
            own = own + t_swap(far, 1)
            bit = 2
            while bit < t_size // 2:
                own = own + t_swap(own, bit)
                bit *= 2
            step = -(-own.shape[0] // (8 * pieces)) * 8
            parts = []
            for start in range(0, own.shape[0], step):
                parts.append(t_swap(own[start : start + step], bit))
            order.queue += parts
            return own, parts

        def add_up(own, parts):
            for part in parts:
                order.queue = [p for p in order.queue if p is not part]
            own, *parts = order.gate(own, *parts)
            return own + jnp.concatenate(parts, axis=0)

        block = width // dp_size

        order = Order()

        def forward(index, slot):
            inputs = slot.astype(f32)
            inv_one = lax.rsqrt(jnp.mean(inputs * inputs, axis=-1, keepdims=True) + epsilon)
            unit_one = inputs * inv_one
            normed = (unit_one * input_gain).astype(bf16)
            proj = order.point(plain_dot(normed, in_weight))
            gated, ssd, square, *kept, query, keys, values, logs, context = mixers_forward(
                index, channels, heads_width, lengths, proj, cosine, sine, *mixer_rows
            )
            gated = order.point(gated)
            total_square = t_total(jnp.sum(square, axis=-1))
            inv_mamba = lax.rsqrt(total_square / DSSM + epsilon)[:, None]
            scaled = (gated * inv_mamba * mamba_gain).astype(bf16)
            mixer = jnp.concatenate([scaled, context], axis=1)
            mixed_own, mixed_far = half_sum(
                *halves(plain_dot(mixer, out_weight)), 3
            )
            order.mark(mixed_own)
            return dict(
                mixed_own=mixed_own, mixed_far=mixed_far, inputs=inputs, inv_one=inv_one,
                unit_one=unit_one, normed=normed, proj=proj, gated=gated, ssd=ssd, kept=kept,
                attention=(query, keys, values, logs), inv_mamba=inv_mamba, mixer=mixer,
            )

        def feed_forward(index, k):
            hidden_own = mine(k["inputs"]) + add_up(k["mixed_own"], k["mixed_far"])
            hidden = jnp.concatenate([hidden_own, t_swap(hidden_own, 1)], axis=0)
            inv_two = lax.rsqrt(jnp.mean(hidden * hidden, axis=-1, keepdims=True) + epsilon)
            unit_two = hidden * inv_two
            normed_two = (unit_two * ffn_gain).astype(bf16)
            gate = order.point(plain_dot(normed_two, gate_weight))
            upper = plain_dot(normed_two, up_weight)
            gsig = jax.nn.sigmoid(gate)
            gsilu = gate * gsig
            inner_ffn = (gsilu * upper).astype(bf16)
            valid = (rows < lengths[index]).astype(f32)[:, None]
            cotangent = relative(out_grad[index].astype(f32) * valid)
            cot_low = cotangent.astype(bf16)
            d_inner_ffn = order.point(right_trans(cot_low, down_weight))
            d_gate = (d_inner_ffn * upper * gsig * (1.0 + gate * (1.0 - gsig))).astype(bf16)
            d_up = (d_inner_ffn * gsilu).astype(bf16)
            back = right_trans(d_gate, gate_weight) + right_trans(d_up, up_weight)
            back_own, back_far = half_sum(back[:half], back[half:], 3)
            order.mark(back_own)
            k.update(
                back_own=back_own, back_far=back_far,
                hidden=hidden, inv_two=inv_two[:half], unit_two=unit_two[:half],
                normed_two=normed_two, inner_ffn=inner_ffn, cotangent=cotangent, cot_low=cot_low,
                d_gate=d_gate, d_up=d_up,
            )

        def output_sum(k):
            (inner_ffn,) = order.gate(k["inner_ffn"])
            ffn = plain_dot(inner_ffn, down_weight)
            k["ffn_own"] = ffn[:half] + t_swap(ffn[half:], 1)
            order.mark(k["ffn_own"])

        def output(k, own, theirs):
            out = k["hidden"] + jnp.concatenate([own, theirs], axis=0)
            return in_order(out[:half], out[half:]).astype(bf16)

        def back_head(k):
            unit_two = k["unit_two"]
            g_ffn_gain = jnp.sum(k["back_own"] * unit_two, axis=0)
            d_normed_two = add_up(k["back_own"], k["back_far"])
            d_unit_two = d_normed_two * ffn_gain
            d_rest = k["inv_two"] * (
                d_unit_two - unit_two * jnp.mean(d_unit_two * unit_two, axis=-1, keepdims=True)
            )
            d_both = k["cotangent"] + jnp.concatenate([d_rest, t_swap(d_rest, 1)], axis=0)
            d_hidden = in_order(d_both[:half], d_both[half:])
            d_mixed = d_hidden.astype(bf16)
            d_mixer = right_trans(d_mixed, out_weight)
            k["g_ffn_gain"] = g_ffn_gain
            k["d_hidden"] = d_hidden
            k["d_mixed"], k["d_mixer"] = d_mixed, d_mixer
            k["cross"] = t_total(
                jnp.sum(d_mixer[:, :channels] * mamba_gain * k["gated"], axis=-1)
            )[:, None]
            order.mark(d_mixer)

        def back_mixers(index, k, held):
            d_mixer, cross = order.gate(k["d_mixer"], k["cross"])
            inv = k["inv_mamba"]
            inv_cross = jnp.concatenate([inv, inv**3 * cross / DSSM], axis=1)
            inv_cross = jnp.pad(inv_cross, ((0, 0), (0, LANES - 2)))
            back, d_statepre, d_keys, d_values, g_conv, g_state, g_heads, g_skip, g_gain = (
                mixers_backward(
                    index, micro, held, lengths, d_mixer, k["gated"], inv_cross, mamba_gain[None],
                    k["proj"], k["ssd"], *k["kept"], *k["attention"], cosine, sine, *mixer_rows,
                )
            )
            kv_far = jnp.where(core == 0, d_values, d_keys)
            kv_own = jnp.where(core == 0, d_keys, d_values)
            k["kv_sum"] = kv_own + t_swap(kv_far, 1)
            k["d_statepre"] = d_statepre
            k.update(
                g_conv_weight=g_conv[:-1], g_conv_bias=g_conv[-1],
                g_conv_state_weight=g_state[:-1], g_conv_state_bias=g_state[-1],
                g_step_bias=g_heads[0, :local_heads], g_decay_log=g_heads[1, :local_heads],
                g_skip=jnp.sum(g_skip.reshape(local_heads, MHDIM), axis=1),
                g_mamba_gain=g_gain[0],
            )
            order.mark(back)
            return back

        def back_inputs(index, k, back):
            back, d_statepre = order.gate(back, k["d_statepre"])
            piece = d_statepre.shape[1] // t_size
            parts = [
                lax.dynamic_slice_in_dim(d_statepre, jnp.bitwise_xor(me_t, q) * piece, piece, 1)
                for q in range(t_size)
            ]
            pieces = halving_order(list(range(0, t_size, 2)), 2, t_size)
            state_sum = jnp.concatenate([parts[q] for q in pieces], axis=1) + t_swap(
                jnp.concatenate([parts[q ^ 1] for q in pieces], axis=1), 1
            )
            bit = 2
            while bit < t_size:
                cut = state_sum.shape[1] // 2
                state_sum = state_sum[:, :cut] + t_swap(state_sum[:, cut:], bit)
                bit *= 2
            k["shared"] = jnp.concatenate([state_sum, k["kv_sum"]], axis=1).astype(bf16)
            rows_back = lax.slice_in_dim(back, index * count, (index + 1) * count, axis=0)
            norm_own, norm_other = halves(right_trans(rows_back, in_weight))
            k["norm_own"] = norm_own + t_swap(norm_other, 1)
            unit_own = mine(k["unit_one"])
            k["g_input_gain"] = jnp.sum(k["norm_own"] * unit_own, axis=0)
            order.mark(k["norm_own"])

        def input_grad(k, own, theirs):
            d_normed = in_order(own, theirs)
            unit_one = k["unit_one"]
            d_unit_one = d_normed * input_gain
            return k["d_hidden"] + k["inv_one"] * (
                d_unit_one - unit_one * jnp.mean(d_unit_one * unit_one, axis=-1, keepdims=True)
            )

        slots = []
        for index in range(micro):
            slot = tokens[index]
            if index:
                (slot,) = order.gate(slot)
            slots.append(forward(index, slot))
        for index in range(micro):
            feed_forward(index, slots[index])

        def joined(name):
            return jnp.concatenate([k[name] for k in slots], axis=0)

        def relative_columns(values):
            blocks = halving_order(list(range(dp_size)), 1, dp_size)
            return jnp.concatenate(
                [
                    lax.dynamic_slice_in_dim(values, jnp.bitwise_xor(me_dp, r) * block, block, 1)
                    for r in blocks
                ],
                axis=1,
            )

        def scattered(part, dimension):
            return lax.psum_scatter(part, "dp", scatter_dimension=dimension, tiled=True)

        inner_all, cot_all = order.gate(joined("inner_ffn"), joined("cot_low"))
        part_down = left_trans(inner_all, cot_all)
        order.mark(part_down)
        g_down = scattered(part_down, 1)
        two_all = order.point(order.gate(joined("normed_two"))[0])
        part_gate = left_trans(two_all, joined("d_gate"))
        order.mark(part_gate)
        g_gate = scattered(part_gate, 0)
        first, last = slots
        back_head(first)
        two_all = order.gate(two_all)[0]
        part_up = left_trans(two_all, joined("d_up"))
        order.mark(part_up)
        g_up = scattered(part_up, 0)
        back_first = back_mixers(0, first, None)
        back_head(last)
        back_inputs(0, first, back_first)
        back = back_mixers(1, last, back_first)
        back_inputs(1, last, back)
        for k in slots:
            output_sum(k)
        (mixed_all,) = order.gate(joined("d_mixed"))
        part_outs = left_trans(relative_columns(mixed_all), joined("mixer"))
        one_columns = relative_columns(joined("normed"))
        part_early = left_trans(one_columns, back[:, : channels + heads_width])
        part_late = left_trans(
            one_columns,
            jnp.concatenate(
                [back[:, places["xpre"]], joined("shared"), back[:, places["step"]]], axis=1
            ),
        )
        sums = [first["norm_own"], first["ffn_own"], last["ffn_own"], last["norm_own"]]
        (g_outs, g_early, g_late), own, theirs = scatter_all(
            dp_size, [part_outs, part_early, part_late], sums
        )
        order.mark(g_late)

        def total(name):
            value = slots[0][name]
            for k in slots[1:]:
                value = value + k[name]
            return value

        names = [
            "g_conv_state_weight", "g_conv_state_bias", "g_input_gain", "g_ffn_gain",
            "g_conv_weight", "g_conv_bias", "g_step_bias", "g_decay_log", "g_skip",
            "g_mamba_gain",
        ]
        small = {name: total(name) for name in names}
        vector = jnp.concatenate([small[name].reshape(-1) for name in names])
        (vector,) = order.gate(vector)
        bit = 1
        while bit < dp_size:
            vector = vector + swap(vector, "dp", dp_size, bit)
            bit *= 2
        order.mark(vector)
        shared_size = sum(small[name].size for name in names[:4])
        wide_vector = t_total(vector[:shared_size])
        start = 0
        for name in names:
            shape, size = small[name].shape, small[name].size
            source = wide_vector if start < shared_size else vector
            small[name] = source[start : start + size].reshape(shape)
            start += size
        place = me_dp * t_size + me_t
        share = conv_state_bias.shape[0] // (dp_size * t_size)
        g_conv_state_weight = lax.dynamic_slice_in_dim(
            small["g_conv_state_weight"], place * share, share, 1
        )
        g_conv_state_bias = lax.dynamic_slice_in_dim(
            small["g_conv_state_bias"], place * share, share, 0
        )
        g_input_gain = lax.dynamic_slice_in_dim(small["g_input_gain"], me_dp * block, block, 0)
        g_ffn_gain = lax.dynamic_slice_in_dim(small["g_ffn_gain"], me_dp * block, block, 0)
        heads = [small[name] for name in names[4:]]

        g_outs = g_outs.T
        shared_end = channels + joined("shared").shape[1]
        g_step = g_late[:, shared_end : shared_end + local_heads]
        g_late = g_late[:, :shared_end]
        grads_list = [input_grad(first, own[0], theirs[0]), input_grad(last, own[3], theirs[3])]
        outputs_list = [output(first, own[1], theirs[1]), output(last, own[2], theirs[2])]

        mamba_cols = mamba_in_weight.shape[1]
        tail = g_late[:, mamba_cols:]
        sub = block // t_size
        rowsets = []
        for q in range(t_size):
            part = lax.dynamic_slice_in_dim(tail, jnp.bitwise_xor(me_t, q) * sub, sub, 0)
            rowsets.append(part if q == 0 else t_swap(part, q))
        stacked = jnp.stack(rowsets)
        piece = state_weight.shape[1] // t_size
        sources = [
            lax.dynamic_index_in_dim(stacked, jnp.bitwise_xor(me_t, j), 0, keepdims=False)
            for j in range(t_size)
        ]
        g_state = jnp.concatenate([s[:, :piece] for s in sources], axis=1)
        pairs = t_size // 2
        g_kv = jnp.concatenate(
            [sources[(b % pairs) * 2 + b // pairs][:, piece:] for b in range(t_size)], axis=1
        )
        gate_cols = mamba_gate_weight.shape[1]
        mamba_rows = mamba_out_weight.shape[0]
        return (
            jnp.stack(outputs_list),
            jnp.stack(grads_list),
            g_input_gain,
            g_early[:, :gate_cols],
            g_late[:, :mamba_cols],
            g_state,
            g_step,
            heads[0],
            heads[1],
            g_conv_state_weight,
            g_conv_state_bias,
            heads[2],
            heads[3],
            heads[4],
            heads[5],
            g_outs[:mamba_rows],
            g_early[:, gate_cols:],
            g_kv,
            g_outs[mamba_rows:],
            g_ffn_gain,
            g_gate,
            g_up,
            g_down,
        )

    return per_device


def solution(mesh):
    placed = (
        P("dp", None, None),
        P("dp"),
        P("dp", None, None),
        P(),
        P(None, "tensor"),
        P(None, "tensor"),
        P(),
        P(None, "tensor"),
        P(None, "tensor"),
        P("tensor"),
        P(),
        P(),
        P("tensor"),
        P("tensor"),
        P("tensor"),
        P("tensor"),
        P("tensor", None),
        P(None, "tensor"),
        P(),
        P("tensor", None),
        P(),
        P(None, "tensor"),
        P(None, "tensor"),
        P("tensor", None),
    )
    return jax.shard_map(
        make_per_device(mesh.shape["dp"], mesh.shape["tensor"]),
        mesh=mesh,
        in_specs=placed,
        out_specs=(
            P("dp", None, None),
            P("dp", None, None),
            P("dp"),
            P("dp", "tensor"),
            P("dp", "tensor"),
            P(("dp", "tensor"), None),
            P("dp", "tensor"),
            P(None, "tensor"),
            P("tensor"),
            P(None, ("dp", "tensor")),
            P(("dp", "tensor")),
            P("tensor"),
            P("tensor"),
            P("tensor"),
            P("tensor"),
            P("tensor", "dp"),
            P("dp", "tensor"),
            P(("dp", "tensor"), None),
            P("tensor", "dp"),
            P("dp"),
            P("dp", "tensor"),
            P("dp", "tensor"),
            P("tensor", "dp"),
        ),
        check_vma=False,
    )
```

```python
import functools

import jax
import jax.numpy as jnp
from jax import lax
from jax.experimental import pallas as pl
from jax.experimental.pallas import tpu as pltpu
from jax.sharding import PartitionSpec as P

MHDIM = 64
STATE = 256
AHEADS = 8
KVHEADS = 2
AHDIM = 128
DSSM = 3072

epsilon = 1e-05
rope_base = 100000000000.0
f32 = jnp.float32
bf16 = jnp.bfloat16


def plain_dot(left, right):
    return jnp.dot(left, right, preferred_element_type=f32)


def right_trans(left, right):
    return lax.dot_general(left, right, (((1,), (1,)), ((), ())), preferred_element_type=f32)


def left_trans(left, right):
    return lax.dot_general(left, right, (((0,), (0,)), ((), ())), preferred_element_type=f32)


def silu_slope(values):
    sig = jax.nn.sigmoid(values)
    return sig * (1.0 + values * (1.0 - sig))


MESH = pl.DeviceIdType.MESH
LANES = 128
BLOCK = 128


def shifted(values, steps, row):
    if steps == 0:
        return values
    count = values.shape[0]
    moved = pltpu.roll(values, steps % count, 0)
    if steps > 0:
        return jnp.where(row >= steps, moved, 0.0)
    return jnp.where(row < count + steps, moved, 0.0)


def tap_sum(values, taps, bias):
    row = lax.broadcasted_iota(jnp.int32, values.shape, 0)
    width = taps.shape[0]
    total = jnp.zeros_like(values) + bias
    for k in range(width):
        total = total + shifted(values, width - 1 - k, row) * taps[k : k + 1, :]
    return total


def tap_back(grads, values, taps):
    row = lax.broadcasted_iota(jnp.int32, values.shape, 0)
    width = taps.shape[0]
    back = jnp.zeros_like(values)
    tap_grads = []
    for k in range(width):
        steps = width - 1 - k
        back = back + shifted(grads, -steps, row) * taps[k : k + 1, :]
        tap_grads.append(jnp.sum(grads * shifted(values, steps, row), axis=0, keepdims=True))
    return back, jnp.concatenate(tap_grads, axis=0)


def column_of(values, lane, index):
    return jnp.sum(jnp.where(lane == index, values, 0.0), axis=1, keepdims=True)


def exact_dot(left, right):
    return jnp.dot(left, right, precision=lax.Precision.HIGHEST, preferred_element_type=f32)


def turned(values, cosine, sine):
    return values * cosine + pltpu.roll(values, AHDIM // 2, 1) * sine


def scores_of(query, keys, lo, hi, length):
    scores = right_trans(query[lo:hi], keys[:hi]) * AHDIM ** (-0.5)
    t = lax.broadcasted_iota(jnp.int32, (hi - lo, hi), 0) + lo
    s = lax.broadcasted_iota(jnp.int32, (hi - lo, hi), 1)
    return scores, (t >= s) & (s < length)


def attention_forward(query_pre, key_pre, value_pre, cosine, sine, length, query, keys, values, logs, context):
    count, width = query.shape
    keys[...] = turned(key_pre, cosine, sine).astype(bf16)
    values[...] = value_pre.astype(bf16)
    lane = lax.broadcasted_iota(jnp.int32, (count, LANES), 1)
    kept = jnp.zeros((count, LANES), f32)
    for h in range(width // AHDIM):
        lanes = slice(h * AHDIM, (h + 1) * AHDIM)
        query[:, lanes] = turned(query_pre[:, lanes], cosine, sine).astype(bf16)
        found = []
        for i in range(count // BLOCK):
            lo, hi = i * BLOCK, (i + 1) * BLOCK
            scores, valid = scores_of(query[:, lanes], keys[...], lo, hi, length)
            masked = jnp.where(valid, scores, -1e30)
            peak = jnp.max(masked, axis=1, keepdims=True)
            expo = jnp.exp(masked - peak)
            total = jnp.sum(expo, axis=1, keepdims=True)
            found.append(peak + jnp.log(total))
            probs = (expo / total).astype(bf16)
            context[lo:hi, lanes] = plain_dot(probs, values[:hi, :]).astype(bf16)
        kept = jnp.where(lane == h, jnp.concatenate(found, axis=0), kept)
    logs[...] = kept


def attention_backward(d_context, query, keys, values, logs, cosine, sine, length, d_query_pre, d_keys, d_values):
    count, width = query.shape
    lane = lax.broadcasted_iota(jnp.int32, (count, LANES), 1)
    scale = AHDIM ** (-0.5)
    key_total = jnp.zeros((count, AHDIM), f32)
    value_total = jnp.zeros((count, AHDIM), f32)
    for h in range(width // AHDIM):
        lanes = slice(h * AHDIM, (h + 1) * AHDIM)
        log = column_of(logs[...], lane, h)
        pieces = []
        for i in range(count // BLOCK):
            lo, hi = i * BLOCK, (i + 1) * BLOCK
            scores, valid = scores_of(query[:, lanes], keys[...], lo, hi, length)
            probs = jnp.where(valid, jnp.exp(scores - log[lo:hi]), 0.0)
            grads = d_context[lo:hi, lanes]
            d_probs = right_trans(grads, values[:hi, :])
            delta = jnp.sum(probs * d_probs, axis=1, keepdims=True)
            d_scores = (probs * (d_probs - delta)).astype(bf16)
            pieces.append(plain_dot(d_scores, keys[:hi, :]) * scale)
            d_key = left_trans(d_scores, query[lo:hi, lanes]) * scale
            d_value = left_trans(probs.astype(bf16), grads)
            if hi < count:
                rest = jnp.zeros((count - hi, AHDIM), f32)
                d_key = jnp.concatenate([d_key, rest], axis=0)
                d_value = jnp.concatenate([d_value, rest], axis=0)
            key_total = key_total + d_key
            value_total = value_total + d_value
        d_query_pre[:, lanes] = turned(jnp.concatenate(pieces, axis=0), cosine, -sine).astype(bf16)
    d_keys[...] = turned(key_total, cosine, -sine)
    d_values[...] = value_total


def columns_of(channels, heads_width):
    places, start = {}, 0
    for name, size in (
        ("zgate", channels), ("query", heads_width), ("xpre", channels), ("state", 2 * STATE),
        ("key", AHDIM), ("value", AHDIM), ("step", LANES),
    ):
        places[name] = slice(start, start + size)
        start += size
    return places, start


def forward_kernel(
    lengths, zgate, query_pre, xpre, statepre, key_pre, value_pre, steppre, cosine, sine, conv_weight, conv_bias, state_taps, state_bias, step_bias, rates,
    skip_rep, gated, ssd, square, xconv, sconv, stepsize, cumul, inner, query, keys, values, logs,
    context, cumul_rows, *, slot,
):
    attention_forward(
        query_pre, key_pre[...], value_pre[...],
        cosine[...], sine[...], lengths[slot], query, keys, values, logs, context,
    )
    count, channels = xpre.shape
    xlin = tap_sum(xpre[...], conv_weight[...], conv_bias[...])
    xconv[...] = (xlin * jax.nn.sigmoid(xlin)).astype(bf16)
    slin = tap_sum(statepre[...], state_taps[...], state_bias[...])
    sconv[...] = (slin * jax.nn.sigmoid(slin)).astype(bf16)
    inner[...] = right_trans(sconv[:, STATE:], sconv[:, :STATE])
    step = jax.nn.softplus(steppre[...] + step_bias[...])
    stepsize[...] = step
    row = lax.broadcasted_iota(jnp.int32, (count, count), 0)
    col = lax.broadcasted_iota(jnp.int32, (count, count), 1)
    total = exact_dot(jnp.where(row >= col, 1.0, 0.0), -step * rates[...])
    cumul[...] = total
    cumul_rows[...] = total.T
    square[...] = jnp.zeros_like(square)

    def pair(p):
        lanes = slice(p * LANES, (p + 1) * LANES)
        lane = lax.broadcasted_iota(jnp.int32, (count, LANES), 1)
        xvals = xconv[:, lanes].astype(f32)
        low_half = lane < MHDIM
        step_rep = jnp.where(
            low_half, column_of(stepsize[...], lane, 2 * p), column_of(stepsize[...], lane, 2 * p + 1)
        )
        weighted = (step_rep * xvals).astype(bf16)
        columns = [column_of(cumul[...], lane, 2 * p + h) for h in range(2)]
        for i in range(count // BLOCK):
            lo, hi = i * BLOCK, (i + 1) * BLOCK
            results = []
            for h in range(2):
                differ = columns[h][lo:hi] - cumul_rows[2 * p + h : 2 * p + h + 1, :hi]
                t = lax.broadcasted_iota(jnp.int32, (BLOCK, hi), 0) + lo
                s = lax.broadcasted_iota(jnp.int32, (BLOCK, hi), 1)
                decay = jnp.exp(jnp.where(t >= s, differ, -1e30))
                mixing = (inner[lo:hi, :hi] * decay).astype(bf16)
                results.append(plain_dot(mixing, weighted[:hi]))
            half = jnp.where(low_half[lo:hi], results[0], results[1])
            half = half + skip_rep[:, lanes] * xvals[lo:hi]
            ssd[lo:hi, lanes] = half
            z = zgate[lo:hi, lanes]
            value = half * (z * jax.nn.sigmoid(z))
            gated[lo:hi, lanes] = value
            square[lo:hi, :] += value * value

    for p in range(channels // LANES):
        pair(p)


def full(*shape):
    return jax.ShapeDtypeStruct(shape, f32)


def low(*shape):
    return jax.ShapeDtypeStruct(shape, bf16)


def in_vmem(count):
    return [pl.BlockSpec(memory_space=pltpu.VMEM)] * count


def whole_blocks(shapes):
    return [pl.BlockSpec(s.shape, lambda i, n=len(s.shape): (0,) * n) for s in shapes]


def mixers_forward(slot, lengths, *operands):
    count, channels = operands[0].shape
    heads_width = operands[1].shape[1]
    shapes = (
        full(count, channels), full(count, channels), full(count, LANES), low(count, channels),
        low(count, 2 * STATE), full(count, LANES), full(count, LANES), full(count, count),
        low(count, heads_width), low(count, AHDIM), low(count, AHDIM), full(count, LANES),
        low(count, heads_width),
    )
    return pl.pallas_call(
        functools.partial(forward_kernel, slot=slot),
        grid=(1,),
        out_shape=shapes,
        in_specs=[pl.BlockSpec(memory_space=pltpu.SMEM)] + in_vmem(len(operands)),
        out_specs=tuple(whole_blocks(shapes)),
        scratch_shapes=[pltpu.VMEM((LANES, count), f32)],
        compiler_params=pltpu.CompilerParams(vmem_limit_bytes=48 * 2**20),
        cost_estimate=pl.CostEstimate(
            flops=10**6, bytes_accessed=10**6, transcendentals=10**3
        ),
    )(lengths, *operands)


def backward_kernel(
    lengths, d_scaled_in, d_context_in, gated_in, inv_cross, gain, zgate, xpre, statepre, steppre,
    ssd, xconv, sconv, stepsize, cumul, inner,
    query, keys, values, logs, cosine, sine, conv_weight, conv_bias, state_taps, state_bias,
    step_bias, rates, skip_rep,
    back, d_statepre, d_keys, d_values, g_conv, g_state, g_heads, g_skip, g_gain,
    d_ssd, d_xvals, cumul_rows, d_inner, row_sums, col_sums, d_step, *, slot, places,
):
    count, channels = ssd.shape
    attention_backward(
        d_context_in[...].astype(bf16), query, keys, values, logs, cosine[...], sine[...],
        lengths[slot], back.at[:, places["query"]], d_keys, d_values,
    )
    back[:, places["key"]] = d_keys[...].astype(bf16)
    back[:, places["value"]] = d_values[...].astype(bf16)
    d_zgate, d_xpre = back.at[:, places["zgate"]], back.at[:, places["xpre"]]
    d_steppre = back.at[:, places["step"]]
    d_scaled = d_scaled_in[...]
    g_gain[...] = jnp.sum(d_scaled * gated_in[...] * inv_cross[:, 0:1], axis=0, keepdims=True)
    inv = inv_cross[:, 0:1]
    cross = inv_cross[:, 1:2]
    d_gated = inv * (d_scaled * gain[...]) - gated_in[...] * cross
    z = zgate[...]
    sig = jax.nn.sigmoid(z)
    d_low = (d_gated * (z * sig)).astype(bf16)
    d_ssd[...] = d_low
    d_zgate[...] = (d_gated * ssd[...] * sig * (1.0 + z * (1.0 - sig))).astype(bf16)
    g_skip[...] = jnp.sum(d_low.astype(f32) * xconv[...].astype(f32), axis=0, keepdims=True)
    cumul_rows[...] = cumul[...].T
    d_inner[...] = jnp.zeros_like(d_inner)
    row_sums[...] = jnp.zeros_like(row_sums)
    col_sums[...] = jnp.zeros_like(col_sums)
    d_step[...] = jnp.zeros_like(d_step)

    def pair(p):
        lanes = slice(p * LANES, (p + 1) * LANES)
        lane = lax.broadcasted_iota(jnp.int32, (count, LANES), 1)
        low_half = lane < MHDIM
        xvals = xconv[:, lanes].astype(f32)
        step_rep = jnp.where(
            low_half, column_of(stepsize[...], lane, 2 * p), column_of(stepsize[...], lane, 2 * p + 1)
        )
        weighted = (step_rep * xvals).astype(bf16)
        grads = d_ssd[:, lanes]
        columns = [column_of(cumul[...], lane, 2 * p + h) for h in range(2)]
        pieces = []
        for h in range(2):
            only = jnp.where(low_half == (h == 0), grads, jnp.zeros_like(grads))
            back_part = jnp.zeros((count, LANES), f32)
            sums = []
            col_total = jnp.zeros((1, count), f32)
            for i in range(count // BLOCK):
                lo, hi = i * BLOCK, (i + 1) * BLOCK
                differ = columns[h][lo:hi] - cumul_rows[2 * p + h : 2 * p + h + 1, :hi]
                t = lax.broadcasted_iota(jnp.int32, (BLOCK, hi), 0) + lo
                s = lax.broadcasted_iota(jnp.int32, (BLOCK, hi), 1)
                decay = jnp.exp(jnp.where(t >= s, differ, -1e30))
                mixing = inner[lo:hi, :hi] * decay
                part = left_trans(mixing.astype(bf16), only[lo:hi])
                d_mixing = right_trans(only[lo:hi], weighted[:hi])
                d_inner[lo:hi, :hi] += d_mixing * decay
                flow = d_mixing * mixing
                sums.append(jnp.sum(flow, axis=1, keepdims=True))
                down = jnp.sum(flow, axis=0, keepdims=True)
                if hi < count:
                    part = jnp.concatenate([part, jnp.zeros((count - hi, LANES), f32)], axis=0)
                    down = jnp.concatenate([down, jnp.zeros((1, count - hi), f32)], axis=1)
                back_part = back_part + part
                col_total = col_total + down
            here = lane == 2 * p + h
            row_sums[...] = jnp.where(here, jnp.concatenate(sums, axis=0), row_sums[...])
            col_sums[2 * p + h : 2 * p + h + 1, :] = col_total
            pieces.append(back_part)
        d_weighted = pieces[0] + pieces[1]
        d_xvals[:, lanes] = grads.astype(f32) * skip_rep[:, lanes] + d_weighted * step_rep
        product = d_weighted * xvals
        for h in range(2):
            value = jnp.sum(
                jnp.where(low_half == (h == 0), product, 0.0), axis=1, keepdims=True
            )
            d_step[...] = jnp.where(lane == 2 * p + h, value, d_step[...])

    for p in range(channels // LANES):
        pair(p)

    d_cumul = row_sums[...] - col_sums[...].T
    row = lax.broadcasted_iota(jnp.int32, (count, count), 0)
    col = lax.broadcasted_iota(jnp.int32, (count, count), 1)
    d_logdecay = exact_dot(jnp.where(row <= col, 1.0, 0.0), d_cumul)
    rate = rates[...]
    d_full = (d_step[...] - d_logdecay * rate) * jax.nn.sigmoid(steppre[...] + step_bias[...])
    d_steppre[...] = d_full.astype(bf16)
    g_heads[0:1, :] = jnp.sum(d_full, axis=0, keepdims=True)
    g_heads[1:2, :] = jnp.sum(-d_logdecay * stepsize[...] * rate, axis=0, keepdims=True)

    d_in = d_inner[...].astype(bf16)
    d_c = plain_dot(d_in, sconv[:, :STATE])
    d_b = left_trans(d_in, sconv[:, STATE:])
    slin = tap_sum(statepre[...], state_taps[...], state_bias[...])
    d_slin = jnp.concatenate([d_b, d_c], axis=1) * silu_slope(slin)
    back_state, tap_grads = tap_back(d_slin, statepre[...], state_taps[...])
    d_statepre[...] = back_state
    back[:, places["state"]] = back_state.astype(bf16)
    g_state[...] = jnp.concatenate([tap_grads, jnp.sum(d_slin, axis=0, keepdims=True)], axis=0)
    xlin = tap_sum(xpre[...], conv_weight[...], conv_bias[...])
    d_xlin = d_xvals[...] * silu_slope(xlin)
    back_x, tap_grads = tap_back(d_xlin, xpre[...], conv_weight[...])
    d_xpre[...] = back_x.astype(bf16)
    g_conv[...] = jnp.concatenate([tap_grads, jnp.sum(d_xlin, axis=0, keepdims=True)], axis=0)


def mixers_backward(slot, slots, held, lengths, *operands):
    count, channels = operands[0].shape
    heads_width = operands[1].shape[1]
    taps = operands[-7].shape[0]
    width = columns_of(channels, heads_width)[1]
    kernel = functools.partial(
        backward_kernel, slot=slot, places=columns_of(channels, heads_width)[0]
    )
    aliases = {}
    extra_specs, extra = [], ()
    if held is not None:
        aliases = {0: 0}
        extra_specs, extra = [pl.BlockSpec(memory_space=pl.ANY)], (held,)
        inside = kernel
        kernel = lambda _, *refs: inside(*refs)
    shapes = (
        full(count, 2 * STATE), full(count, AHDIM), full(count, AHDIM), full(taps + 1, channels),
        full(taps + 1, 2 * STATE), full(2, LANES), full(1, channels), full(1, channels),
    )
    return pl.pallas_call(
        kernel,
        grid=(1,),
        out_shape=(low(slots * count, width),) + shapes,
        in_specs=extra_specs
        + [pl.BlockSpec(memory_space=pltpu.SMEM)]
        + in_vmem(len(operands)),
        out_specs=tuple(
            [pl.BlockSpec((count, width), lambda i: (slot, 0))] + whole_blocks(shapes)
        ),
        scratch_shapes=[
            pltpu.VMEM((count, channels), bf16),
            pltpu.VMEM((count, channels), f32),
            pltpu.VMEM((LANES, count), f32),
            pltpu.VMEM((count, count), f32),
            pltpu.VMEM((count, LANES), f32),
            pltpu.VMEM((LANES, count), f32),
            pltpu.VMEM((count, LANES), f32),
        ],
        input_output_aliases=aliases,
        compiler_params=pltpu.CompilerParams(vmem_limit_bytes=56 * 2**20),
        cost_estimate=pl.CostEstimate(
            flops=10**6, bytes_accessed=10**6, transcendentals=10**3
        ),
    )(*extra, lengths, *operands)


def swap(values, axis, size, bit):
    return lax.ppermute(values, axis, [(i, i ^ bit) for i in range(size)])


def halving_order(members, bit, limit):
    if bit >= limit:
        return members
    low = halving_order([m for m in members if not m & bit], bit * 2, limit)
    high = halving_order([m for m in members if m & bit], bit * 2, limit)
    return low + high


class Order:
    def __init__(self):
        self.last = ()
        self.queue = []

    def point(self, value, skip=0):
        if len(self.queue) <= skip:
            return value
        return lax.optimization_barrier((value, self.queue.pop(skip)))[0]

    def gate(self, *values):
        return lax.optimization_barrier((values, self.last))[0]

    def mark(self, *values):
        self.last = values


def scatter_all(size, parts, halves):
    rows = parts[0].shape[0]
    works = len(parts)
    share = rows // size
    chunk = min(256, rows // 4)
    levels = size.bit_length() - 1
    spans = []
    for level in range(1, levels):
        lo, hi = rows >> (level + 1), rows >> level
        step = min(chunk, hi - lo)
        spans += [(level, start, step) for start in range(hi - step, lo - 1, -step)]
    spans.append((levels, 0, share))
    pieces = [(w,) + span for w in range(works) for span in spans]
    per_work = len(spans)
    widths = [p.shape[1] for p in parts]
    wide = max(widths)
    extra = len(halves)
    half_shape = halves[0].shape

    def kernel(*refs):
        held_in, refs = refs[:works], refs[works:]
        own, refs = refs[:extra], refs[extra:]
        outs, refs = refs[:works], refs[works:]
        mine, theirs, far, refs = (
            refs[:extra], refs[extra : 2 * extra], refs[2 * extra : 3 * extra], refs[3 * extra :]
        )
        loads, pair_loads, totals, refs = refs[0], refs[1], refs[2], refs[3:]
        landed, refs = refs[:works], refs[works:]
        later, refs = refs[: works * (levels - 1)], refs[works * (levels - 1) :]
        load_sems, out_sems, x_send, x_recv, z_send, z_recv, y_sems, c_sems, pair_sems = refs
        me = lax.axis_index("dp")
        spot = lax.axis_index("tensor")

        def neighbour(bit):
            return spot + bit - 2 * bit * lax.rem(spot // bit, 2)


        def partner(level):
            bit = 1 << level
            return me + bit - 2 * bit * lax.rem(me // bit, 2)

        barrier = pltpu.get_barrier_semaphore()
        for level in range(levels):
            pl.semaphore_signal(
                barrier, inc=1, device_id={"dp": partner(level)}, device_id_type=MESH
            )
        for bit in (1, 2):
            pl.semaphore_signal(
                barrier, inc=1, device_id={"tensor": neighbour(bit)}, device_id_type=MESH
            )
        pl.semaphore_wait(barrier, levels + 2)

        def y_copy(e):
            return pltpu.make_async_remote_copy(
                src_ref=own[e], dst_ref=far[e], send_sem=y_sems.at[0, e], recv_sem=y_sems.at[1, e],
                device_id={"tensor": neighbour(2)}, device_id_type=MESH,
            )

        def c_copy(e):
            return pltpu.make_async_remote_copy(
                src_ref=totals.at[e], dst_ref=theirs[e], send_sem=c_sems.at[0, e],
                recv_sem=c_sems.at[1, e], device_id={"tensor": neighbour(1)}, device_id_type=MESH,
            )

        def pair_copy(e, which):
            if which == 2:
                return pltpu.make_async_copy(totals.at[e], mine[e], pair_sems.at[2, e])
            source = own[e] if which == 0 else far[e]
            return pltpu.make_async_copy(source, pair_loads.at[which], pair_sems.at[which, e])

        def exchange(e):
            y_copy(e).wait_recv()
            pair_copy(e, 0).start()
            pair_copy(e, 1).start()
            pair_copy(e, 0).wait()
            pair_copy(e, 1).wait()
            totals[e] = pair_loads[0] + pair_loads[1]
            pair_copy(e, 2).start()
            c_copy(e).start()


        def first_copy(number):
            w, _, start, step = pieces[number]
            return pltpu.make_async_remote_copy(
                src_ref=held_in[w].at[pl.ds(rows // 2 + start, step), :],
                dst_ref=landed[w].at[pl.ds(start, step), :],
                send_sem=x_send.at[number],
                recv_sem=x_recv.at[number],
                device_id={"dp": partner(0)},
                device_id_type=MESH,
            )

        def load(number):
            w, _, start, step = pieces[number]
            return pltpu.make_async_copy(
                held_in[w].at[pl.ds(start, step), :],
                loads.at[number % 2, pl.ds(0, step), pl.ds(0, widths[w])],
                load_sems.at[number % 2],
            )

        def later_copy(number):
            w, level, start, step = pieces[number]
            return pltpu.make_async_remote_copy(
                src_ref=landed[w].at[pl.ds(start, step), :],
                dst_ref=later[w * (levels - 1) + level - 1].at[pl.ds(start - (rows >> (level + 1)), step), :],
                send_sem=z_send.at[number],
                recv_sem=z_recv.at[number],
                device_id={"dp": partner(level)},
                device_id_type=MESH,
            )

        def store(w):
            return pltpu.make_async_copy(
                landed[w].at[pl.ds(0, share), :], outs[w], out_sems.at[w]
            )

        for e in range(extra):
            y_copy(e).start()
        for number in range(len(pieces)):
            first_copy(number).start()
        load(0).start()
        arrived = set()

        def need(w, level, start, step):
            base = rows >> (level + 1)
            for other in range(w * per_work, (w + 1) * per_work):
                _, its_level, its_start, its_step = pieces[other]
                if its_level != level or other in arrived:
                    continue
                if its_start - base < start + step and start < its_start - base + its_step:
                    later_copy(other).wait_recv()
                    arrived.add(other)

        def finish(w):
            level = levels - 1
            need(w, level, 0, share)
            landed[w][:share, :] += later[w * (levels - 1) + level - 1][:share, :]
            store(w).start()

        for number, (w, level, start, step) in enumerate(pieces):
            load(number).wait()
            if number + 1 < len(pieces):
                load(number + 1).start()
            first_copy(number).wait_recv()
            value = loads[number % 2, :step, : widths[w]] + landed[w][start : start + step, :]
            for before in range(1, min(level, levels - 1)):
                need(w, before, start, step)
                value = value + later[w * (levels - 1) + before - 1][start : start + step, :]
            landed[w][start : start + step, :] = value
            if level < levels:
                later_copy(number).start()
            if w and number == w * per_work + min(2, per_work - 1):
                finish(w - 1)
            if number % 2 and number // 2 <= extra and number > 1:
                exchange(number // 2 - 1)
        for e in range((len(pieces) - 1) // 2, extra):
            exchange(e)
        finish(works - 1)
        for e in range(extra):
            y_copy(e).wait_send()
            c_copy(e).wait()
            pair_copy(e, 2).wait()
        for number, (w, level, start, step) in enumerate(pieces):
            first_copy(number).wait_send()
            if level < levels:
                later_copy(number).wait_send()
        for w in range(works):
            store(w).wait()

    scratch = [
        pltpu.VMEM((2, chunk, wide), f32),
        pltpu.VMEM((2,) + half_shape, f32),
        pltpu.VMEM((extra,) + half_shape, f32),
    ]
    scratch += [pltpu.VMEM((rows // 2, n), f32) for n in widths]
    scratch += [
        pltpu.VMEM((rows >> (level + 1), n), f32) for n in widths for level in range(1, levels)
    ]
    scratch += [
        pltpu.SemaphoreType.DMA((2,)),
        pltpu.SemaphoreType.DMA((works,)),
    ] + [pltpu.SemaphoreType.DMA((len(pieces),))] * 4
    scratch += [pltpu.SemaphoreType.DMA((n, extra)) for n in (2, 2, 3)]
    results = pl.pallas_call(
        kernel,
        out_shape=tuple([full(share, n) for n in widths] + [full(*half_shape)] * (3 * extra)),
        in_specs=[pl.BlockSpec(memory_space=pl.ANY)] * (works + extra),
        out_specs=tuple([pl.BlockSpec(memory_space=pl.ANY)] * (works + 3 * extra)),
        scratch_shapes=scratch,
        compiler_params=pltpu.CompilerParams(
            collective_id=0, has_side_effects=True, vmem_limit_bytes=60 * 2**20
        ),
        cost_estimate=pl.CostEstimate(
            flops=10**6, bytes_accessed=10**6, transcendentals=0
        ),
    )(*parts, *halves)
    return results[:works], results[works : works + extra], results[works + extra : works + 2 * extra]


def make_per_device(dp_size, t_size):
    def per_device(
        tokens,
        lengths,
        out_grad,
        input_gain,
        mamba_gate_weight,
        mamba_in_weight,
        state_weight,
        step_weight,
        conv_weight,
        conv_bias,
        conv_state_weight,
        conv_state_bias,
        step_bias,
        decay_log,
        skip_scale,
        mamba_gain,
        mamba_out_weight,
        query_weight,
        key_value_weight,
        attn_out_weight,
        ffn_gain,
        gate_weight,
        up_weight,
        down_weight,
    ):
        micro = tokens.shape[0]
        count = tokens.shape[1]
        width = tokens.shape[2]
        half = count // 2
        local_heads = step_weight.shape[1]
        q_local = query_weight.shape[1] // AHDIM
        kv_width = key_value_weight.shape[1] // 2
        group_size = AHEADS // KVHEADS
        me_dp = lax.axis_index("dp")
        me_t = lax.axis_index("tensor")
        core = lax.rem(me_t, 2)
        kv_head = me_t * q_local // group_size
        key_weight = lax.dynamic_slice_in_dim(key_value_weight, kv_head * AHDIM, AHDIM, 1)
        value_weight = lax.dynamic_slice_in_dim(
            key_value_weight, kv_width + kv_head * AHDIM, AHDIM, 1
        )
        rows = jnp.arange(count)
        freqs = rope_base ** (-(jnp.arange(AHDIM // 2).astype(f32) * 2.0) / AHDIM)
        angles = rows.astype(f32)[:, None] * freqs[None, :]
        cosine, sine = jnp.cos(angles), jnp.sin(angles)
        cosine = jnp.concatenate([cosine, cosine], axis=1)
        sine = jnp.concatenate([-sine, sine], axis=1)
        channels = mamba_in_weight.shape[1]
        heads_width = query_weight.shape[1]
        places, _ = columns_of(channels, heads_width)
        pad_step = LANES - local_heads

        def lane_row(vector):
            return jnp.pad(vector, (0, pad_step))[None]

        mixer_rows = (
            conv_weight, conv_bias[None], conv_state_weight, conv_state_bias[None],
            lane_row(step_bias), lane_row(jnp.exp(decay_log)), jnp.repeat(skip_scale, MHDIM)[None],
        )
        step_lanes = jnp.pad(step_weight, ((0, 0), (0, pad_step)))
        in_weights = (
            mamba_gate_weight, query_weight, mamba_in_weight, state_weight, key_weight,
            value_weight, step_lanes,
        )

        def t_swap(values, bit):
            return swap(values, "tensor", t_size, bit)

        def t_total(values):
            bit = 1
            while bit < t_size:
                values = values + t_swap(values, bit)
                bit *= 2
            return values

        def mine(values):
            return lax.dynamic_slice_in_dim(values, core * half, half, 0)

        def other(values):
            return lax.dynamic_slice_in_dim(values, (1 - core) * half, half, 0)

        def halves(values):
            values = lax.optimization_barrier(values)
            return mine(values), other(values)

        def relative(values):
            return jnp.concatenate([mine(values), other(values)], axis=0)

        def in_order(own, far):
            return jnp.where(
                core == 0,
                jnp.concatenate([own, far], axis=0),
                jnp.concatenate([far, own], axis=0),
            )

        def half_sum(own, far, pieces):
            own = own + t_swap(far, 1)
            bit = 2
            while bit < t_size // 2:
                own = own + t_swap(own, bit)
                bit *= 2
            step = -(-own.shape[0] // (8 * pieces)) * 8
            parts = []
            for start in range(0, own.shape[0], step):
                parts.append(t_swap(own[start : start + step], bit))
            order.queue += parts
            return own, parts

        def add_up(own, parts):
            for part in parts:
                order.queue = [p for p in order.queue if p is not part]
            own = order.point(own)
            own, *parts = order.gate(own, *parts)
            return own + jnp.concatenate(parts, axis=0)

        block = width // dp_size

        order = Order()

        def forward(index, slot):
            inputs = slot.astype(f32)
            inv_one = lax.rsqrt(jnp.mean(inputs * inputs, axis=-1, keepdims=True) + epsilon)
            unit_one = inputs * inv_one
            normed = (unit_one * input_gain).astype(bf16)
            pre = [plain_dot(normed, w) for w in in_weights]
            pre[0] = order.point(pre[0])
            gated, ssd, square, *kept, query, keys, values, logs, context = mixers_forward(
                index, lengths, *pre, cosine, sine, *mixer_rows
            )
            gated = order.point(gated)
            total_square = t_total(jnp.sum(square, axis=-1))
            inv_mamba = lax.rsqrt(total_square / DSSM + epsilon)[:, None]
            scaled = order.point((gated * inv_mamba * mamba_gain).astype(bf16))
            mixer = jnp.concatenate([scaled, context], axis=1)
            mixed_own, mixed_far = half_sum(
                *halves(plain_dot(scaled, mamba_out_weight) + plain_dot(context, attn_out_weight)),
                3,
            )
            order.mark(mixed_own)
            return dict(
                mixed_own=mixed_own, mixed_far=mixed_far, inputs=inputs, inv_one=inv_one,
                unit_one=unit_one, normed=normed, pre=pre, gated=gated, ssd=ssd, kept=kept,
                attention=(query, keys, values, logs), inv_mamba=inv_mamba, mixer=mixer,
            )

        def feed_forward(index, k):
            hidden_own = mine(k["inputs"]) + add_up(k["mixed_own"], k["mixed_far"])
            hidden = jnp.concatenate([hidden_own, t_swap(hidden_own, 1)], axis=0)
            inv_two = lax.rsqrt(jnp.mean(hidden * hidden, axis=-1, keepdims=True) + epsilon)
            unit_two = hidden * inv_two
            unit_two = order.point(unit_two)
            normed_two = (unit_two * ffn_gain).astype(bf16)
            gate = order.point(plain_dot(normed_two, gate_weight))
            upper = plain_dot(normed_two, up_weight)
            gsig = jax.nn.sigmoid(gate)
            gsilu = gate * gsig
            inner_ffn = (gsilu * upper).astype(bf16)
            valid = (rows < lengths[index]).astype(f32)[:, None]
            cotangent = relative(out_grad[index].astype(f32) * valid)
            cot_low = cotangent.astype(bf16)
            d_inner_ffn = order.point(right_trans(cot_low, down_weight))
            d_gate = (d_inner_ffn * upper * gsig * (1.0 + gate * (1.0 - gsig))).astype(bf16)
            d_up = (d_inner_ffn * gsilu).astype(bf16)
            back = right_trans(d_gate, gate_weight) + right_trans(d_up, up_weight)
            back_own, back_far = half_sum(back[:half], back[half:], 3)
            order.mark(back_own)
            k.update(
                back_own=back_own, back_far=back_far,
                hidden=hidden, inv_two=inv_two[:half], unit_two=unit_two[:half],
                normed_two=normed_two, inner_ffn=inner_ffn, cotangent=cotangent, cot_low=cot_low,
                d_gate=d_gate, d_up=d_up,
            )

        def output_sum(k):
            (inner_ffn,) = order.gate(k["inner_ffn"])
            ffn = plain_dot(inner_ffn, down_weight)
            k["ffn_own"] = ffn[:half] + t_swap(ffn[half:], 1)
            order.mark(k["ffn_own"])

        def output(k, own, theirs):
            out = k["hidden"] + jnp.concatenate([own, theirs], axis=0)
            return in_order(out[:half], out[half:]).astype(bf16)

        def back_head(k):
            unit_two = k["unit_two"]
            g_ffn_gain = jnp.sum(k["back_own"] * unit_two, axis=0)
            d_normed_two = add_up(k["back_own"], k["back_far"])
            d_unit_two = d_normed_two * ffn_gain
            d_rest = k["inv_two"] * (
                d_unit_two - unit_two * jnp.mean(d_unit_two * unit_two, axis=-1, keepdims=True)
            )
            d_both = k["cotangent"] + jnp.concatenate([d_rest, t_swap(d_rest, 1)], axis=0)
            d_hidden = in_order(d_both[:half], d_both[half:])
            d_mixed = d_hidden.astype(bf16)
            d_scaled = right_trans(d_mixed, mamba_out_weight)
            d_context = right_trans(d_mixed, attn_out_weight)
            k["g_ffn_gain"] = g_ffn_gain
            k["d_hidden"] = d_hidden
            k["d_mixed"], k["d_scaled"], k["d_context"] = d_mixed, d_scaled, d_context
            k["cross"] = t_total(jnp.sum(d_scaled * mamba_gain * k["gated"], axis=-1))[:, None]
            order.mark(d_scaled, d_context)

        def back_mixers(index, k, held):
            d_scaled, cross = order.gate(k["d_scaled"], k["cross"])
            inv = k["inv_mamba"]
            inv_cross = jnp.concatenate([inv, inv**3 * cross / DSSM], axis=1)
            inv_cross = jnp.pad(inv_cross, ((0, 0), (0, LANES - 2)))
            back, d_statepre, d_keys, d_values, g_conv, g_state, g_heads, g_skip, g_gain = (
                mixers_backward(
                    index, micro, held, lengths, d_scaled, k["d_context"], k["gated"], inv_cross,
                    mamba_gain[None], k["pre"][0], k["pre"][2], k["pre"][3], k["pre"][6], k["ssd"],
                    *k["kept"], *k["attention"], cosine, sine, *mixer_rows,
                )
            )
            kv_far = jnp.where(core == 0, d_values, d_keys)
            kv_own = jnp.where(core == 0, d_keys, d_values)
            k["kv_sum"] = kv_own + t_swap(kv_far, 1)
            k["d_statepre"] = d_statepre
            k.update(
                g_conv_weight=g_conv[:-1], g_conv_bias=g_conv[-1],
                g_conv_state_weight=g_state[:-1], g_conv_state_bias=g_state[-1],
                g_step_bias=g_heads[0, :local_heads], g_decay_log=g_heads[1, :local_heads],
                g_skip=jnp.sum(g_skip.reshape(local_heads, MHDIM), axis=1),
                g_mamba_gain=g_gain[0],
            )
            order.mark(back)
            return back

        def back_inputs(index, k, back):
            back, d_statepre = order.gate(back, k["d_statepre"])
            piece = d_statepre.shape[1] // t_size
            parts = [
                lax.dynamic_slice_in_dim(d_statepre, jnp.bitwise_xor(me_t, q) * piece, piece, 1)
                for q in range(t_size)
            ]
            pieces = halving_order(list(range(0, t_size, 2)), 2, t_size)
            state_sum = jnp.concatenate([parts[q] for q in pieces], axis=1) + t_swap(
                jnp.concatenate([parts[q ^ 1] for q in pieces], axis=1), 1
            )
            bit = 2
            while bit < t_size:
                cut = state_sum.shape[1] // 2
                state_sum = state_sum[:, :cut] + t_swap(state_sum[:, cut:], bit)
                bit *= 2
            k["shared"] = jnp.concatenate([state_sum, k["kv_sum"]], axis=1).astype(bf16)
            rows_back = lax.slice_in_dim(back, index * count, (index + 1) * count, axis=0)
            norm_own, norm_other = halves(right_trans(rows_back, in_weight))
            k["norm_own"] = norm_own + t_swap(norm_other, 1)
            unit_own = mine(k["unit_one"])
            k["g_input_gain"] = jnp.sum(k["norm_own"] * unit_own, axis=0)
            order.mark(k["norm_own"])

        def input_grad(k, own, theirs):
            d_normed = in_order(own, theirs)
            unit_one = k["unit_one"]
            d_unit_one = d_normed * input_gain
            return k["d_hidden"] + k["inv_one"] * (
                d_unit_one - unit_one * jnp.mean(d_unit_one * unit_one, axis=-1, keepdims=True)
            )

        slots = []
        for index in range(micro):
            slot = tokens[index]
            if index:
                (slot,) = order.gate(slot)
            slots.append(forward(index, slot))
        for index in range(micro):
            feed_forward(index, slots[index])

        def joined(name):
            return jnp.concatenate([k[name] for k in slots], axis=0)

        def relative_columns(values):
            blocks = halving_order(list(range(dp_size)), 1, dp_size)
            return jnp.concatenate(
                [
                    lax.dynamic_slice_in_dim(values, jnp.bitwise_xor(me_dp, r) * block, block, 1)
                    for r in blocks
                ],
                axis=1,
            )

        def scattered(part, dimension):
            return lax.psum_scatter(part, "dp", scatter_dimension=dimension, tiled=True)

        inner_all, cot_all = order.gate(joined("inner_ffn"), joined("cot_low"))
        part_down = left_trans(inner_all, cot_all)
        order.mark(part_down)
        g_down = scattered(part_down, 1)
        first, last = slots
        back_head(first)
        in_weight = jnp.concatenate(order.gate(*in_weights), axis=1)
        (two_all,) = order.gate(joined("normed_two"))
        part_gate = order.point(left_trans(two_all, joined("d_gate")))
        order.mark(part_gate)
        g_gate = scattered(part_gate, 0)
        (two_all,) = order.gate(two_all)
        part_up = order.point(left_trans(two_all, joined("d_up")))
        order.mark(part_up)
        g_up = scattered(part_up, 0)
        back_head(last)
        back_first = back_mixers(0, first, None)
        back_inputs(0, first, back_first)
        back = back_mixers(1, last, back_first)
        back_inputs(1, last, back)
        for k in slots:
            output_sum(k)
        def total(name):
            value = slots[0][name]
            for k in slots[1:]:
                value = value + k[name]
            return value

        names = [
            "g_conv_state_weight", "g_conv_state_bias", "g_input_gain", "g_ffn_gain",
            "g_conv_weight", "g_conv_bias", "g_step_bias", "g_decay_log", "g_skip",
            "g_mamba_gain",
        ]
        small = {name: total(name) for name in names}
        vector = jnp.concatenate([small[name].reshape(-1) for name in names])
        shared_size = sum(small[name].size for name in names[:4])

        def after(value, other):
            return lax.optimization_barrier((value, other))[0]

        hops = [1 << n for n in range(dp_size.bit_length() - 1)]
        mixed_all, normed_all = order.gate(joined("d_mixed"), joined("normed"))
        vector = vector + swap(vector, "dp", dp_size, hops[0])
        part_outs = left_trans(relative_columns(after(mixed_all, vector)), joined("mixer"))
        vector = vector + swap(vector, "dp", dp_size, hops[1])
        one_columns = relative_columns(normed_all)
        part_early = left_trans(after(one_columns, vector), back[:, : channels + heads_width])
        for hop in hops[2:]:
            vector = vector + swap(vector, "dp", dp_size, hop)
        part_late = left_trans(
            after(one_columns, vector),
            jnp.concatenate(
                [back[:, places["xpre"]], joined("shared"), back[:, places["step"]]], axis=1
            ),
        )
        wide_vector = t_total(vector[:shared_size])
        part_outs, part_early, part_late = lax.optimization_barrier(
            (part_outs, part_early, part_late, wide_vector)
        )[:3]
        sums = [first["norm_own"], first["ffn_own"], last["ffn_own"], last["norm_own"]]
        (g_outs, g_early, g_late), own, theirs = scatter_all(
            dp_size, [part_outs, part_early, part_late], sums
        )
        order.mark(g_late)

        start = 0
        for name in names:
            shape, size = small[name].shape, small[name].size
            source = wide_vector if start < shared_size else vector
            small[name] = source[start : start + size].reshape(shape)
            start += size
        place = me_dp * t_size + me_t
        share = conv_state_bias.shape[0] // (dp_size * t_size)
        g_conv_state_weight = lax.dynamic_slice_in_dim(
            small["g_conv_state_weight"], place * share, share, 1
        )
        g_conv_state_bias = lax.dynamic_slice_in_dim(
            small["g_conv_state_bias"], place * share, share, 0
        )
        g_input_gain = lax.dynamic_slice_in_dim(small["g_input_gain"], me_dp * block, block, 0)
        g_ffn_gain = lax.dynamic_slice_in_dim(small["g_ffn_gain"], me_dp * block, block, 0)
        heads = [small[name] for name in names[4:]]

        g_outs = g_outs.T
        shared_end = channels + joined("shared").shape[1]
        g_step = g_late[:, shared_end : shared_end + local_heads]
        g_late = g_late[:, :shared_end]
        grads_list = [input_grad(first, own[0], theirs[0]), input_grad(last, own[3], theirs[3])]
        outputs_list = [output(first, own[1], theirs[1]), output(last, own[2], theirs[2])]

        mamba_cols = mamba_in_weight.shape[1]
        tail = g_late[:, mamba_cols:]
        sub = block // t_size
        rowsets = []
        for q in range(t_size):
            part = lax.dynamic_slice_in_dim(tail, jnp.bitwise_xor(me_t, q) * sub, sub, 0)
            rowsets.append(part if q == 0 else t_swap(part, q))
        stacked = jnp.stack(rowsets)
        piece = state_weight.shape[1] // t_size
        sources = [
            lax.dynamic_index_in_dim(stacked, jnp.bitwise_xor(me_t, j), 0, keepdims=False)
            for j in range(t_size)
        ]
        g_state = jnp.concatenate([s[:, :piece] for s in sources], axis=1)
        pairs = t_size // 2
        g_kv = jnp.concatenate(
            [sources[(b % pairs) * 2 + b // pairs][:, piece:] for b in range(t_size)], axis=1
        )
        gate_cols = mamba_gate_weight.shape[1]
        mamba_rows = mamba_out_weight.shape[0]
        return (
            jnp.stack(outputs_list),
            jnp.stack(grads_list),
            g_input_gain,
            g_early[:, :gate_cols],
            g_late[:, :mamba_cols],
            g_state,
            g_step,
            heads[0],
            heads[1],
            g_conv_state_weight,
            g_conv_state_bias,
            heads[2],
            heads[3],
            heads[4],
            heads[5],
            g_outs[:mamba_rows],
            g_early[:, gate_cols:],
            g_kv,
            g_outs[mamba_rows:],
            g_ffn_gain,
            g_gate,
            g_up,
            g_down,
        )

    return per_device


def solution(mesh):
    placed = (
        P("dp", None, None),
        P("dp"),
        P("dp", None, None),
        P(),
        P(None, "tensor"),
        P(None, "tensor"),
        P(),
        P(None, "tensor"),
        P(None, "tensor"),
        P("tensor"),
        P(),
        P(),
        P("tensor"),
        P("tensor"),
        P("tensor"),
        P("tensor"),
        P("tensor", None),
        P(None, "tensor"),
        P(),
        P("tensor", None),
        P(),
        P(None, "tensor"),
        P(None, "tensor"),
        P("tensor", None),
    )
    return jax.shard_map(
        make_per_device(mesh.shape["dp"], mesh.shape["tensor"]),
        mesh=mesh,
        in_specs=placed,
        out_specs=(
            P("dp", None, None),
            P("dp", None, None),
            P("dp"),
            P("dp", "tensor"),
            P("dp", "tensor"),
            P(("dp", "tensor"), None),
            P("dp", "tensor"),
            P(None, "tensor"),
            P("tensor"),
            P(None, ("dp", "tensor")),
            P(("dp", "tensor")),
            P("tensor"),
            P("tensor"),
            P("tensor"),
            P("tensor"),
            P("tensor", "dp"),
            P("dp", "tensor"),
            P(("dp", "tensor"), None),
            P("tensor", "dp"),
            P("dp"),
            P("dp", "tensor"),
            P("dp", "tensor"),
            P("tensor", "dp"),
        ),
        check_vma=False,
    )
```

```python
import functools

import jax
import jax.numpy as jnp
from jax import lax
from jax.experimental import pallas as pl
from jax.experimental.pallas import tpu as pltpu
from jax.sharding import PartitionSpec as P

MHDIM = 64
STATE = 256
AHEADS = 8
KVHEADS = 2
AHDIM = 128
DSSM = 3072

epsilon = 1e-05
rope_base = 100000000000.0
f32 = jnp.float32
bf16 = jnp.bfloat16


def plain_dot(left, right):
    return jnp.dot(left, right, preferred_element_type=f32)


def right_trans(left, right):
    return lax.dot_general(left, right, (((1,), (1,)), ((), ())), preferred_element_type=f32)


def left_trans(left, right):
    return lax.dot_general(left, right, (((0,), (0,)), ((), ())), preferred_element_type=f32)


def silu_slope(values):
    sig = jax.nn.sigmoid(values)
    return sig * (1.0 + values * (1.0 - sig))


MESH = pl.DeviceIdType.MESH
LANES = 128
BLOCK = 128


def shifted(values, steps, row):
    if steps == 0:
        return values
    count = values.shape[0]
    moved = pltpu.roll(values, steps % count, 0)
    if steps > 0:
        return jnp.where(row >= steps, moved, 0.0)
    return jnp.where(row < count + steps, moved, 0.0)


def tap_sum(values, taps, bias):
    row = lax.broadcasted_iota(jnp.int32, values.shape, 0)
    width = taps.shape[0]
    total = jnp.zeros_like(values) + bias
    for k in range(width):
        total = total + shifted(values, width - 1 - k, row) * taps[k : k + 1, :]
    return total


def tap_back(grads, values, taps):
    row = lax.broadcasted_iota(jnp.int32, values.shape, 0)
    width = taps.shape[0]
    back = jnp.zeros_like(values)
    tap_grads = []
    for k in range(width):
        steps = width - 1 - k
        back = back + shifted(grads, -steps, row) * taps[k : k + 1, :]
        tap_grads.append(jnp.sum(grads * shifted(values, steps, row), axis=0, keepdims=True))
    return back, jnp.concatenate(tap_grads, axis=0)


def column_of(values, lane, index):
    return jnp.sum(jnp.where(lane == index, values, 0.0), axis=1, keepdims=True)


def exact_dot(left, right):
    return jnp.dot(left, right, precision=lax.Precision.HIGHEST, preferred_element_type=f32)


def turned(values, cosine, sine):
    return values * cosine + pltpu.roll(values, AHDIM // 2, 1) * sine


def scores_of(query, keys, lo, hi, length):
    scores = right_trans(query[lo:hi], keys[:hi]) * AHDIM ** (-0.5)
    t = lax.broadcasted_iota(jnp.int32, (hi - lo, hi), 0) + lo
    s = lax.broadcasted_iota(jnp.int32, (hi - lo, hi), 1)
    return scores, (t >= s) & (s < length)


def attention_forward(query_pre, key_pre, value_pre, cosine, sine, length, query, keys, values, logs, context):
    count, width = query.shape
    keys[...] = turned(key_pre, cosine, sine).astype(bf16)
    values[...] = value_pre.astype(bf16)
    lane = lax.broadcasted_iota(jnp.int32, (count, LANES), 1)
    kept = jnp.zeros((count, LANES), f32)
    for h in range(width // AHDIM):
        lanes = slice(h * AHDIM, (h + 1) * AHDIM)
        query[:, lanes] = turned(query_pre[:, lanes], cosine, sine).astype(bf16)
        found = []
        for i in range(count // BLOCK):
            lo, hi = i * BLOCK, (i + 1) * BLOCK
            scores, valid = scores_of(query[:, lanes], keys[...], lo, hi, length)
            masked = jnp.where(valid, scores, -1e30)
            peak = jnp.max(masked, axis=1, keepdims=True)
            expo = jnp.exp(masked - peak)
            total = jnp.sum(expo, axis=1, keepdims=True)
            found.append(peak + jnp.log(total))
            probs = (expo / total).astype(bf16)
            context[lo:hi, lanes] = plain_dot(probs, values[:hi, :]).astype(bf16)
        kept = jnp.where(lane == h, jnp.concatenate(found, axis=0), kept)
    logs[...] = kept


def attention_backward(d_context, query, keys, values, logs, cosine, sine, length, d_query_pre, d_keys, d_values):
    count, width = query.shape
    lane = lax.broadcasted_iota(jnp.int32, (count, LANES), 1)
    scale = AHDIM ** (-0.5)
    key_total = jnp.zeros((count, AHDIM), f32)
    value_total = jnp.zeros((count, AHDIM), f32)
    for h in range(width // AHDIM):
        lanes = slice(h * AHDIM, (h + 1) * AHDIM)
        log = column_of(logs[...], lane, h)
        pieces = []
        for i in range(count // BLOCK):
            lo, hi = i * BLOCK, (i + 1) * BLOCK
            scores, valid = scores_of(query[:, lanes], keys[...], lo, hi, length)
            probs = jnp.where(valid, jnp.exp(scores - log[lo:hi]), 0.0)
            grads = d_context[lo:hi, lanes]
            d_probs = right_trans(grads, values[:hi, :])
            delta = jnp.sum(probs * d_probs, axis=1, keepdims=True)
            d_scores = (probs * (d_probs - delta)).astype(bf16)
            pieces.append(plain_dot(d_scores, keys[:hi, :]) * scale)
            d_key = left_trans(d_scores, query[lo:hi, lanes]) * scale
            d_value = left_trans(probs.astype(bf16), grads)
            if hi < count:
                rest = jnp.zeros((count - hi, AHDIM), f32)
                d_key = jnp.concatenate([d_key, rest], axis=0)
                d_value = jnp.concatenate([d_value, rest], axis=0)
            key_total = key_total + d_key
            value_total = value_total + d_value
        d_query_pre[:, lanes] = turned(jnp.concatenate(pieces, axis=0), cosine, -sine).astype(bf16)
    d_keys[...] = turned(key_total, cosine, -sine)
    d_values[...] = value_total


def columns_of(channels, heads_width):
    places, start = {}, 0
    for name, size in (
        ("zgate", channels), ("query", heads_width), ("xpre", channels), ("state", 2 * STATE),
        ("key", AHDIM), ("value", AHDIM), ("step", LANES),
    ):
        places[name] = slice(start, start + size)
        start += size
    return places, start


def forward_kernel(
    lengths, zgate, query_pre, xpre, statepre, key_pre, value_pre, steppre, cosine, sine, conv_weight, conv_bias, state_taps, state_bias, step_bias, rates,
    skip_rep, gated, ssd, square, xconv, sconv, stepsize, cumul, inner, query, keys, values, logs,
    context, cumul_rows, *, slot,
):
    attention_forward(
        query_pre, key_pre[...], value_pre[...],
        cosine[...], sine[...], lengths[slot], query, keys, values, logs, context,
    )
    count, channels = xpre.shape
    xlin = tap_sum(xpre[...], conv_weight[...], conv_bias[...])
    xconv[...] = (xlin * jax.nn.sigmoid(xlin)).astype(bf16)
    slin = tap_sum(statepre[...], state_taps[...], state_bias[...])
    sconv[...] = (slin * jax.nn.sigmoid(slin)).astype(bf16)
    inner[...] = right_trans(sconv[:, STATE:], sconv[:, :STATE])
    step = jax.nn.softplus(steppre[...] + step_bias[...])
    stepsize[...] = step
    row = lax.broadcasted_iota(jnp.int32, (count, count), 0)
    col = lax.broadcasted_iota(jnp.int32, (count, count), 1)
    total = exact_dot(jnp.where(row >= col, 1.0, 0.0), -step * rates[...])
    cumul[...] = total
    cumul_rows[...] = total.T
    square[...] = jnp.zeros_like(square)

    def pair(p):
        lanes = slice(p * LANES, (p + 1) * LANES)
        lane = lax.broadcasted_iota(jnp.int32, (count, LANES), 1)
        xvals = xconv[:, lanes].astype(f32)
        low_half = lane < MHDIM
        step_rep = jnp.where(
            low_half, column_of(stepsize[...], lane, 2 * p), column_of(stepsize[...], lane, 2 * p + 1)
        )
        weighted = (step_rep * xvals).astype(bf16)
        columns = [column_of(cumul[...], lane, 2 * p + h) for h in range(2)]
        for i in range(count // BLOCK):
            lo, hi = i * BLOCK, (i + 1) * BLOCK
            results = []
            for h in range(2):
                differ = columns[h][lo:hi] - cumul_rows[2 * p + h : 2 * p + h + 1, :hi]
                t = lax.broadcasted_iota(jnp.int32, (BLOCK, hi), 0) + lo
                s = lax.broadcasted_iota(jnp.int32, (BLOCK, hi), 1)
                decay = jnp.exp(jnp.where(t >= s, differ, -1e30))
                mixing = (inner[lo:hi, :hi] * decay).astype(bf16)
                results.append(plain_dot(mixing, weighted[:hi]))
            half = jnp.where(low_half[lo:hi], results[0], results[1])
            half = half + skip_rep[:, lanes] * xvals[lo:hi]
            ssd[lo:hi, lanes] = half
            z = zgate[lo:hi, lanes]
            value = half * (z * jax.nn.sigmoid(z))
            gated[lo:hi, lanes] = value
            square[lo:hi, :] += value * value

    for p in range(channels // LANES):
        pair(p)


def full(*shape):
    return jax.ShapeDtypeStruct(shape, f32)


def low(*shape):
    return jax.ShapeDtypeStruct(shape, bf16)


def in_vmem(count):
    return [pl.BlockSpec(memory_space=pltpu.VMEM)] * count


def whole_blocks(shapes):
    return [pl.BlockSpec(s.shape, lambda i, n=len(s.shape): (0,) * n) for s in shapes]


def mixers_forward(slot, lengths, *operands):
    count, channels = operands[0].shape
    heads_width = operands[1].shape[1]
    shapes = (
        full(count, channels), full(count, channels), full(count, LANES), low(count, channels),
        low(count, 2 * STATE), full(count, LANES), full(count, LANES), full(count, count),
        low(count, heads_width), low(count, AHDIM), low(count, AHDIM), full(count, LANES),
        low(count, heads_width),
    )
    return pl.pallas_call(
        functools.partial(forward_kernel, slot=slot),
        grid=(1,),
        out_shape=shapes,
        in_specs=[pl.BlockSpec(memory_space=pltpu.SMEM)] + in_vmem(len(operands)),
        out_specs=tuple(whole_blocks(shapes)),
        scratch_shapes=[pltpu.VMEM((LANES, count), f32)],
        compiler_params=pltpu.CompilerParams(vmem_limit_bytes=48 * 2**20),
        cost_estimate=pl.CostEstimate(
            flops=10**6, bytes_accessed=10**6, transcendentals=10**3
        ),
    )(lengths, *operands)


def backward_kernel(
    lengths, d_scaled_in, d_context_in, gated_in, inv_cross, gain, zgate, xpre, statepre, steppre,
    ssd, xconv, sconv, stepsize, cumul, inner,
    query, keys, values, logs, cosine, sine, conv_weight, conv_bias, state_taps, state_bias,
    step_bias, rates, skip_rep,
    back, d_statepre, d_keys, d_values, g_conv, g_state, g_heads, g_skip, g_gain,
    d_ssd, d_xvals, cumul_rows, d_inner, row_sums, col_sums, d_step, *, slot, places,
):
    count, channels = ssd.shape
    attention_backward(
        d_context_in[...].astype(bf16), query, keys, values, logs, cosine[...], sine[...],
        lengths[slot], back.at[:, places["query"]], d_keys, d_values,
    )
    back[:, places["key"]] = d_keys[...].astype(bf16)
    back[:, places["value"]] = d_values[...].astype(bf16)
    d_zgate, d_xpre = back.at[:, places["zgate"]], back.at[:, places["xpre"]]
    d_steppre = back.at[:, places["step"]]
    d_scaled = d_scaled_in[...]
    g_gain[...] = jnp.sum(d_scaled * gated_in[...] * inv_cross[:, 0:1], axis=0, keepdims=True)
    inv = inv_cross[:, 0:1]
    cross = inv_cross[:, 1:2]
    d_gated = inv * (d_scaled * gain[...]) - gated_in[...] * cross
    z = zgate[...]
    sig = jax.nn.sigmoid(z)
    d_low = (d_gated * (z * sig)).astype(bf16)
    d_ssd[...] = d_low
    d_zgate[...] = (d_gated * ssd[...] * sig * (1.0 + z * (1.0 - sig))).astype(bf16)
    g_skip[...] = jnp.sum(d_low.astype(f32) * xconv[...].astype(f32), axis=0, keepdims=True)
    cumul_rows[...] = cumul[...].T
    d_inner[...] = jnp.zeros_like(d_inner)
    row_sums[...] = jnp.zeros_like(row_sums)
    col_sums[...] = jnp.zeros_like(col_sums)
    d_step[...] = jnp.zeros_like(d_step)

    def pair(p):
        lanes = slice(p * LANES, (p + 1) * LANES)
        lane = lax.broadcasted_iota(jnp.int32, (count, LANES), 1)
        low_half = lane < MHDIM
        xvals = xconv[:, lanes].astype(f32)
        step_rep = jnp.where(
            low_half, column_of(stepsize[...], lane, 2 * p), column_of(stepsize[...], lane, 2 * p + 1)
        )
        weighted = (step_rep * xvals).astype(bf16)
        grads = d_ssd[:, lanes]
        columns = [column_of(cumul[...], lane, 2 * p + h) for h in range(2)]
        pieces = []
        for h in range(2):
            only = jnp.where(low_half == (h == 0), grads, jnp.zeros_like(grads))
            back_part = jnp.zeros((count, LANES), f32)
            sums = []
            col_total = jnp.zeros((1, count), f32)
            for i in range(count // BLOCK):
                lo, hi = i * BLOCK, (i + 1) * BLOCK
                differ = columns[h][lo:hi] - cumul_rows[2 * p + h : 2 * p + h + 1, :hi]
                t = lax.broadcasted_iota(jnp.int32, (BLOCK, hi), 0) + lo
                s = lax.broadcasted_iota(jnp.int32, (BLOCK, hi), 1)
                decay = jnp.exp(jnp.where(t >= s, differ, -1e30))
                mixing = inner[lo:hi, :hi] * decay
                part = left_trans(mixing.astype(bf16), only[lo:hi])
                d_mixing = right_trans(only[lo:hi], weighted[:hi])
                d_inner[lo:hi, :hi] += d_mixing * decay
                flow = d_mixing * mixing
                sums.append(jnp.sum(flow, axis=1, keepdims=True))
                down = jnp.sum(flow, axis=0, keepdims=True)
                if hi < count:
                    part = jnp.concatenate([part, jnp.zeros((count - hi, LANES), f32)], axis=0)
                    down = jnp.concatenate([down, jnp.zeros((1, count - hi), f32)], axis=1)
                back_part = back_part + part
                col_total = col_total + down
            here = lane == 2 * p + h
            row_sums[...] = jnp.where(here, jnp.concatenate(sums, axis=0), row_sums[...])
            col_sums[2 * p + h : 2 * p + h + 1, :] = col_total
            pieces.append(back_part)
        d_weighted = pieces[0] + pieces[1]
        d_xvals[:, lanes] = grads.astype(f32) * skip_rep[:, lanes] + d_weighted * step_rep
        product = d_weighted * xvals
        for h in range(2):
            value = jnp.sum(
                jnp.where(low_half == (h == 0), product, 0.0), axis=1, keepdims=True
            )
            d_step[...] = jnp.where(lane == 2 * p + h, value, d_step[...])

    for p in range(channels // LANES):
        pair(p)

    d_cumul = row_sums[...] - col_sums[...].T
    row = lax.broadcasted_iota(jnp.int32, (count, count), 0)
    col = lax.broadcasted_iota(jnp.int32, (count, count), 1)
    d_logdecay = exact_dot(jnp.where(row <= col, 1.0, 0.0), d_cumul)
    rate = rates[...]
    d_full = (d_step[...] - d_logdecay * rate) * jax.nn.sigmoid(steppre[...] + step_bias[...])
    d_steppre[...] = d_full.astype(bf16)
    g_heads[0:1, :] = jnp.sum(d_full, axis=0, keepdims=True)
    g_heads[1:2, :] = jnp.sum(-d_logdecay * stepsize[...] * rate, axis=0, keepdims=True)

    d_in = d_inner[...].astype(bf16)
    d_c = plain_dot(d_in, sconv[:, :STATE])
    d_b = left_trans(d_in, sconv[:, STATE:])
    slin = tap_sum(statepre[...], state_taps[...], state_bias[...])
    d_slin = jnp.concatenate([d_b, d_c], axis=1) * silu_slope(slin)
    back_state, tap_grads = tap_back(d_slin, statepre[...], state_taps[...])
    d_statepre[...] = back_state
    back[:, places["state"]] = back_state.astype(bf16)
    g_state[...] = jnp.concatenate([tap_grads, jnp.sum(d_slin, axis=0, keepdims=True)], axis=0)
    xlin = tap_sum(xpre[...], conv_weight[...], conv_bias[...])
    d_xlin = d_xvals[...] * silu_slope(xlin)
    back_x, tap_grads = tap_back(d_xlin, xpre[...], conv_weight[...])
    d_xpre[...] = back_x.astype(bf16)
    g_conv[...] = jnp.concatenate([tap_grads, jnp.sum(d_xlin, axis=0, keepdims=True)], axis=0)


def mixers_backward(slot, slots, held, lengths, *operands):
    count, channels = operands[0].shape
    heads_width = operands[1].shape[1]
    taps = operands[-7].shape[0]
    width = columns_of(channels, heads_width)[1]
    kernel = functools.partial(
        backward_kernel, slot=slot, places=columns_of(channels, heads_width)[0]
    )
    aliases = {}
    extra_specs, extra = [], ()
    if held is not None:
        aliases = {0: 0}
        extra_specs, extra = [pl.BlockSpec(memory_space=pl.ANY)], (held,)
        inside = kernel
        kernel = lambda _, *refs: inside(*refs)
    shapes = (
        full(count, 2 * STATE), full(count, AHDIM), full(count, AHDIM), full(taps + 1, channels),
        full(taps + 1, 2 * STATE), full(2, LANES), full(1, channels), full(1, channels),
    )
    return pl.pallas_call(
        kernel,
        grid=(1,),
        out_shape=(low(slots * count, width),) + shapes,
        in_specs=extra_specs
        + [pl.BlockSpec(memory_space=pltpu.SMEM)]
        + in_vmem(len(operands)),
        out_specs=tuple(
            [pl.BlockSpec((count, width), lambda i: (slot, 0))] + whole_blocks(shapes)
        ),
        scratch_shapes=[
            pltpu.VMEM((count, channels), bf16),
            pltpu.VMEM((count, channels), f32),
            pltpu.VMEM((LANES, count), f32),
            pltpu.VMEM((count, count), f32),
            pltpu.VMEM((count, LANES), f32),
            pltpu.VMEM((LANES, count), f32),
            pltpu.VMEM((count, LANES), f32),
        ],
        input_output_aliases=aliases,
        compiler_params=pltpu.CompilerParams(vmem_limit_bytes=56 * 2**20),
        cost_estimate=pl.CostEstimate(
            flops=10**6, bytes_accessed=10**6, transcendentals=10**3
        ),
    )(*extra, lengths, *operands)


def swap(values, axis, size, bit):
    return lax.ppermute(values, axis, [(i, i ^ bit) for i in range(size)])


def halving_order(members, bit, limit):
    if bit >= limit:
        return members
    low = halving_order([m for m in members if not m & bit], bit * 2, limit)
    high = halving_order([m for m in members if m & bit], bit * 2, limit)
    return low + high


class Order:
    def __init__(self):
        self.last = ()
        self.queue = []

    def point(self, value, skip=0):
        if len(self.queue) <= skip:
            return value
        return lax.optimization_barrier((value, self.queue.pop(skip)))[0]

    def gate(self, *values):
        return lax.optimization_barrier((values, self.last))[0]

    def mark(self, *values):
        self.last = values


class Scatter:
    def __init__(self, order, size, blocks, whole, axis):
        self.order, self.size, self.axis = order, size, axis
        self.bit = 4
        self.blocks, self.whole = blocks, whole
        evens = [r for r in range(size) if not r & 1]
        self.first = halving_order([r for r in evens if r & 2], 4, size)
        self.later = halving_order([r for r in evens if not r & 2], 4, size)

    def product(self, members, wait=None):
        picked = jnp.concatenate([self.blocks[r] for r in members], axis=1)
        if self.axis == 0:
            return left_trans(picked, self.whole)
        return left_trans(self.whole, picked)

    def send(self, values, bit):
        return swap(values, "dp", self.size, bit)

    def start_first(self):
        part = self.product([r ^ 1 for r in self.first])
        self.got_first = self.send(part, 1)
        return part

    def start_later(self):
        part = self.product([r ^ 1 for r in self.later])
        self.got_later = self.send(part, 1)
        return part

    def take_first(self):
        (got,) = self.order.gate(self.got_first)
        held = self.product(self.first) + got
        self.got_second = self.send(held, 2)
        self.order.mark(held)

    def take_later(self):
        got, second = self.order.gate(self.got_later, self.got_second)
        held = self.product(self.later) + got + second
        self.halve(held, 4)

    def halve(self, held, bit):
        if bit >= self.size:
            self.keep, self.got_last = held, None
            self.order.mark(held)
            return
        half = held.shape[self.axis] // 2
        self.keep = lax.slice_in_dim(held, 0, half, axis=self.axis)
        away = lax.slice_in_dim(held, half, 2 * half, axis=self.axis)
        self.got_last = self.send(away, bit)
        self.bit = bit
        self.order.mark(away)

    def finish(self):
        while self.got_last is not None:
            (got,) = self.order.gate(self.got_last)
            self.halve(self.keep + got, self.bit * 2)
        return self.keep


def scatter_all(size, t_size, parts, halves, vector, shared_rows):
    rows = parts[0].shape[0]
    works = len(parts)
    share = rows // size
    chunk = min(256, rows // 4)
    levels = size.bit_length() - 1
    spans = []
    for level in range(1, levels):
        lo, hi = rows >> (level + 1), rows >> level
        step = min(chunk, hi - lo)
        spans += [(level, start, step) for start in range(hi - step, lo - 1, -step)]
    spans.append((levels, 0, share))
    pieces = [(w,) + span for w in range(works) for span in spans]
    per_work = len(spans)
    widths = [p.shape[1] for p in parts]
    wide = max(widths)
    extra = len(halves)
    half_shape = halves[0].shape

    def kernel(*refs):
        held_in, refs = refs[:works], refs[works:]
        own, refs = refs[:extra], refs[extra:]
        small, refs = refs[0], refs[1:]
        outs, refs = refs[:works], refs[works:]
        mine, theirs, far, refs = (
            refs[:extra], refs[extra : 2 * extra], refs[2 * extra : 3 * extra], refs[3 * extra :]
        )
        small_out, wide_out, refs = refs[0], refs[1], refs[2:]
        loads, pair_loads, totals, refs = refs[0], refs[1], refs[2], refs[3:]
        boxes, wide_boxes, refs = refs[0], refs[1], refs[2:]
        landed, refs = refs[:works], refs[works:]
        later, refs = refs[: works * (levels - 1)], refs[works * (levels - 1) :]
        load_sems, out_sems, x_send, x_recv, z_send, z_recv, y_sems, c_sems, pair_sems, v_sems, w_sems = refs
        me = lax.axis_index("dp")
        spot = lax.axis_index("tensor")

        def neighbour(bit):
            return spot + bit - 2 * bit * lax.rem(spot // bit, 2)


        def partner(level):
            bit = 1 << level
            return me + bit - 2 * bit * lax.rem(me // bit, 2)

        barrier = pltpu.get_barrier_semaphore()
        for other in range(1, size):
            pl.semaphore_signal(
                barrier, inc=1, device_id={"dp": lax.rem(me + other, size)}, device_id_type=MESH
            )
        for other in range(1, t_size):
            pl.semaphore_signal(
                barrier, inc=1, device_id={"tensor": lax.rem(spot + other, t_size)},
                device_id_type=MESH,
            )
        pl.semaphore_wait(barrier, size + t_size - 2)

        def small_copy(other):
            return pltpu.make_async_remote_copy(
                src_ref=small, dst_ref=boxes.at[size - other], send_sem=v_sems.at[0, other],
                recv_sem=v_sems.at[1, size - other],
                device_id={"dp": lax.rem(me + other, size)}, device_id_type=MESH,
            )

        def wide_copy(other):
            return pltpu.make_async_remote_copy(
                src_ref=small_out.at[pl.ds(0, shared_rows), :], dst_ref=wide_boxes.at[t_size - other],
                send_sem=w_sems.at[0, other], recv_sem=w_sems.at[1, t_size - other],
                device_id={"tensor": lax.rem(spot + other, t_size)}, device_id_type=MESH,
            )

        def in_turn(kept, count, place, rows):
            total = jnp.zeros((rows, LANES), f32)
            for number in range(count):
                offset = lax.rem(number - place + count, count)
                total = total + kept[offset]
            return total

        def small_sums(stage):
            if stage == 0:
                boxes[0] = small[...]
                for other in range(1, size):
                    small_copy(other).wait_recv()
                small_out[...] = in_turn(boxes, size, me, small.shape[0])
                for other in range(1, t_size):
                    wide_copy(other).start()
            else:
                wide_boxes[0] = small_out[:shared_rows, :]
                for other in range(1, t_size):
                    wide_copy(other).wait_recv()
                wide_out[...] = in_turn(wide_boxes, t_size, spot, shared_rows)


        def y_copy(e):
            return pltpu.make_async_remote_copy(
                src_ref=own[e], dst_ref=far[e], send_sem=y_sems.at[0, e], recv_sem=y_sems.at[1, e],
                device_id={"tensor": neighbour(2)}, device_id_type=MESH,
            )

        def c_copy(e):
            return pltpu.make_async_remote_copy(
                src_ref=totals.at[e], dst_ref=theirs[e], send_sem=c_sems.at[0, e],
                recv_sem=c_sems.at[1, e], device_id={"tensor": neighbour(1)}, device_id_type=MESH,
            )

        def pair_copy(e, which):
            if which == 2:
                return pltpu.make_async_copy(totals.at[e], mine[e], pair_sems.at[2, e])
            source = own[e] if which == 0 else far[e]
            return pltpu.make_async_copy(source, pair_loads.at[which], pair_sems.at[which, e])

        def exchange(e):
            y_copy(e).wait_recv()
            pair_copy(e, 0).start()
            pair_copy(e, 1).start()
            pair_copy(e, 0).wait()
            pair_copy(e, 1).wait()
            totals[e] = pair_loads[0] + pair_loads[1]
            pair_copy(e, 2).start()
            c_copy(e).start()


        def first_copy(number):
            w, _, start, step = pieces[number]
            return pltpu.make_async_remote_copy(
                src_ref=held_in[w].at[pl.ds(rows // 2 + start, step), :],
                dst_ref=landed[w].at[pl.ds(start, step), :],
                send_sem=x_send.at[number],
                recv_sem=x_recv.at[number],
                device_id={"dp": partner(0)},
                device_id_type=MESH,
            )

        def load(number):
            w, _, start, step = pieces[number]
            return pltpu.make_async_copy(
                held_in[w].at[pl.ds(start, step), :],
                loads.at[number % 2, pl.ds(0, step), pl.ds(0, widths[w])],
                load_sems.at[number % 2],
            )

        def later_copy(number):
            w, level, start, step = pieces[number]
            return pltpu.make_async_remote_copy(
                src_ref=landed[w].at[pl.ds(start, step), :],
                dst_ref=later[w * (levels - 1) + level - 1].at[pl.ds(start - (rows >> (level + 1)), step), :],
                send_sem=z_send.at[number],
                recv_sem=z_recv.at[number],
                device_id={"dp": partner(level)},
                device_id_type=MESH,
            )

        def store(w):
            return pltpu.make_async_copy(
                landed[w].at[pl.ds(0, share), :], outs[w], out_sems.at[w]
            )

        for other in range(1, size):
            small_copy(other).start()
        for e in range(extra):
            y_copy(e).start()
        for number in range(len(pieces)):
            first_copy(number).start()
        load(0).start()
        arrived = set()

        def need(w, level, start, step):
            base = rows >> (level + 1)
            for other in range(w * per_work, (w + 1) * per_work):
                _, its_level, its_start, its_step = pieces[other]
                if its_level != level or other in arrived:
                    continue
                if its_start - base < start + step and start < its_start - base + its_step:
                    later_copy(other).wait_recv()
                    arrived.add(other)

        def finish(w):
            level = levels - 1
            need(w, level, 0, share)
            landed[w][:share, :] += later[w * (levels - 1) + level - 1][:share, :]
            store(w).start()

        for number, (w, level, start, step) in enumerate(pieces):
            load(number).wait()
            if number + 1 < len(pieces):
                load(number + 1).start()
            first_copy(number).wait_recv()
            value = loads[number % 2, :step, : widths[w]] + landed[w][start : start + step, :]
            for before in range(1, min(level, levels - 1)):
                need(w, before, start, step)
                value = value + later[w * (levels - 1) + before - 1][start : start + step, :]
            landed[w][start : start + step, :] = value
            if level < levels:
                later_copy(number).start()
            if w and number == w * per_work + min(2, per_work - 1):
                finish(w - 1)
            if number in (0, 2):
                small_sums(number // 2)
            if number % 2 and number // 2 < extra:
                exchange(number // 2)
        for e in range(len(pieces) // 2, extra):
            exchange(e)
        finish(works - 1)
        for other in range(1, size):
            small_copy(other).wait_send()
        for other in range(1, t_size):
            wide_copy(other).wait_send()
        for e in range(extra):
            y_copy(e).wait_send()
            c_copy(e).wait()
            pair_copy(e, 2).wait()
        for number, (w, level, start, step) in enumerate(pieces):
            first_copy(number).wait_send()
            if level < levels:
                later_copy(number).wait_send()
        for w in range(works):
            store(w).wait()

    scratch = [
        pltpu.VMEM((2, chunk, wide), f32),
        pltpu.VMEM((2,) + half_shape, f32),
        pltpu.VMEM((extra,) + half_shape, f32),
        pltpu.VMEM((size,) + vector.shape, f32),
        pltpu.VMEM((t_size, shared_rows, LANES), f32),
    ]
    scratch += [pltpu.VMEM((rows // 2, n), f32) for n in widths]
    scratch += [
        pltpu.VMEM((rows >> (level + 1), n), f32) for n in widths for level in range(1, levels)
    ]
    scratch += [
        pltpu.SemaphoreType.DMA((2,)),
        pltpu.SemaphoreType.DMA((works,)),
    ] + [pltpu.SemaphoreType.DMA((len(pieces),))] * 4
    scratch += [pltpu.SemaphoreType.DMA((n, extra)) for n in (2, 2, 3)]
    scratch += [pltpu.SemaphoreType.DMA((2, size)), pltpu.SemaphoreType.DMA((2, t_size))]
    results = pl.pallas_call(
        kernel,
        out_shape=tuple(
            [full(share, n) for n in widths]
            + [full(*half_shape)] * (3 * extra)
            + [full(*vector.shape), full(shared_rows, LANES)]
        ),
        in_specs=[pl.BlockSpec(memory_space=pl.ANY)] * (works + extra) + in_vmem(1),
        out_specs=tuple([pl.BlockSpec(memory_space=pl.ANY)] * (works + 3 * extra) + in_vmem(2)),
        scratch_shapes=scratch,
        compiler_params=pltpu.CompilerParams(
            collective_id=0, has_side_effects=True, vmem_limit_bytes=60 * 2**20
        ),
        cost_estimate=pl.CostEstimate(
            flops=10**6, bytes_accessed=10**6, transcendentals=0
        ),
    )(*parts, *halves, vector)
    own = results[works : works + extra]
    theirs = results[works + extra : works + 2 * extra]
    return results[:works], own, theirs, results[-2], results[-1]


def make_per_device(dp_size, t_size):
    def per_device(
        tokens,
        lengths,
        out_grad,
        input_gain,
        mamba_gate_weight,
        mamba_in_weight,
        state_weight,
        step_weight,
        conv_weight,
        conv_bias,
        conv_state_weight,
        conv_state_bias,
        step_bias,
        decay_log,
        skip_scale,
        mamba_gain,
        mamba_out_weight,
        query_weight,
        key_value_weight,
        attn_out_weight,
        ffn_gain,
        gate_weight,
        up_weight,
        down_weight,
    ):
        micro = tokens.shape[0]
        count = tokens.shape[1]
        width = tokens.shape[2]
        half = count // 2
        local_heads = step_weight.shape[1]
        q_local = query_weight.shape[1] // AHDIM
        kv_width = key_value_weight.shape[1] // 2
        group_size = AHEADS // KVHEADS
        me_dp = lax.axis_index("dp")
        me_t = lax.axis_index("tensor")
        core = lax.rem(me_t, 2)
        kv_head = me_t * q_local // group_size
        key_weight = lax.dynamic_slice_in_dim(key_value_weight, kv_head * AHDIM, AHDIM, 1)
        value_weight = lax.dynamic_slice_in_dim(
            key_value_weight, kv_width + kv_head * AHDIM, AHDIM, 1
        )
        rows = jnp.arange(count)
        freqs = rope_base ** (-(jnp.arange(AHDIM // 2).astype(f32) * 2.0) / AHDIM)
        angles = rows.astype(f32)[:, None] * freqs[None, :]
        cosine, sine = jnp.cos(angles), jnp.sin(angles)
        cosine = jnp.concatenate([cosine, cosine], axis=1)
        sine = jnp.concatenate([-sine, sine], axis=1)
        channels = mamba_in_weight.shape[1]
        heads_width = query_weight.shape[1]
        places, _ = columns_of(channels, heads_width)
        pad_step = LANES - local_heads

        def lane_row(vector):
            return jnp.pad(vector, (0, pad_step))[None]

        mixer_rows = (
            conv_weight, conv_bias[None], conv_state_weight, conv_state_bias[None],
            lane_row(step_bias), lane_row(jnp.exp(decay_log)), jnp.repeat(skip_scale, MHDIM)[None],
        )
        step_lanes = jnp.pad(step_weight, ((0, 0), (0, pad_step)))
        in_weights = (
            mamba_gate_weight, query_weight, mamba_in_weight, state_weight, key_weight,
            value_weight, step_lanes,
        )

        def t_swap(values, bit):
            return swap(values, "tensor", t_size, bit)

        def t_total(values):
            bit = 1
            while bit < t_size:
                values = values + t_swap(values, bit)
                bit *= 2
            return values

        def mine(values):
            return lax.dynamic_slice_in_dim(values, core * half, half, 0)

        def other(values):
            return lax.dynamic_slice_in_dim(values, (1 - core) * half, half, 0)

        def halves(values):
            values = lax.optimization_barrier(values)
            return mine(values), other(values)

        def relative(values):
            return jnp.concatenate([mine(values), other(values)], axis=0)

        def in_order(own, far):
            return jnp.where(
                core == 0,
                jnp.concatenate([own, far], axis=0),
                jnp.concatenate([far, own], axis=0),
            )

        def half_sum(own, far, pieces):
            own = own + t_swap(far, 1)
            bit = 2
            while bit < t_size // 2:
                own = own + t_swap(own, bit)
                bit *= 2
            step = -(-own.shape[0] // (8 * pieces)) * 8
            parts = []
            for start in range(0, own.shape[0], step):
                parts.append(t_swap(own[start : start + step], bit))
            order.queue += parts
            return own, parts

        def add_up(own, parts):
            for part in parts:
                order.queue = [p for p in order.queue if p is not part]
            own = order.point(own)
            own, *parts = order.gate(own, *parts)
            return own + jnp.concatenate(parts, axis=0)

        block = width // dp_size

        order = Order()

        def forward(index, slot):
            inputs = slot.astype(f32)
            inv_one = lax.rsqrt(jnp.mean(inputs * inputs, axis=-1, keepdims=True) + epsilon)
            unit_one = inputs * inv_one
            normed = (unit_one * input_gain).astype(bf16)
            pre = [plain_dot(normed, w) for w in in_weights]
            pre[0] = order.point(pre[0])
            gated, ssd, square, *kept, query, keys, values, logs, context = mixers_forward(
                index, lengths, *pre, cosine, sine, *mixer_rows
            )
            gated = order.point(gated)
            total_square = t_total(jnp.sum(square, axis=-1))
            inv_mamba = lax.rsqrt(total_square / DSSM + epsilon)[:, None]
            scaled = order.point((gated * inv_mamba * mamba_gain).astype(bf16))
            mixer = jnp.concatenate([scaled, context], axis=1)
            mixed_own, mixed_far = half_sum(
                *halves(plain_dot(scaled, mamba_out_weight) + plain_dot(context, attn_out_weight)),
                3,
            )
            order.mark(mixed_own)
            return dict(
                mixed_own=mixed_own, mixed_far=mixed_far, inputs=inputs, inv_one=inv_one,
                unit_one=unit_one, normed=normed, pre=pre, gated=gated, ssd=ssd, kept=kept,
                attention=(query, keys, values, logs), inv_mamba=inv_mamba, mixer=mixer,
            )

        def feed_forward(index, k):
            hidden_own = mine(k["inputs"]) + add_up(k["mixed_own"], k["mixed_far"])
            hidden = jnp.concatenate([hidden_own, t_swap(hidden_own, 1)], axis=0)
            inv_two = lax.rsqrt(jnp.mean(hidden * hidden, axis=-1, keepdims=True) + epsilon)
            unit_two = hidden * inv_two
            unit_two = order.point(unit_two)
            normed_two = (unit_two * ffn_gain).astype(bf16)
            gate = order.point(plain_dot(normed_two, gate_weight))
            upper = plain_dot(normed_two, up_weight)
            gsig = jax.nn.sigmoid(gate)
            gsilu = gate * gsig
            inner_ffn = (gsilu * upper).astype(bf16)
            valid = (rows < lengths[index]).astype(f32)[:, None]
            cotangent = relative(out_grad[index].astype(f32) * valid)
            cot_low = cotangent.astype(bf16)
            d_inner_ffn = order.point(right_trans(cot_low, down_weight))
            d_gate = (d_inner_ffn * upper * gsig * (1.0 + gate * (1.0 - gsig))).astype(bf16)
            d_up = (d_inner_ffn * gsilu).astype(bf16)
            back = right_trans(d_gate, gate_weight) + right_trans(d_up, up_weight)
            back_own, back_far = half_sum(back[:half], back[half:], 3)
            order.mark(back_own)
            k.update(
                back_own=back_own, back_far=back_far,
                hidden=hidden, inv_two=inv_two[:half], unit_two=unit_two[:half],
                normed_two=normed_two, inner_ffn=inner_ffn, cotangent=cotangent, cot_low=cot_low,
                d_gate=d_gate, d_up=d_up,
            )

        def output_sum(k):
            (inner_ffn,) = order.gate(k["inner_ffn"])
            ffn = plain_dot(inner_ffn, down_weight)
            k["ffn_own"] = ffn[:half] + t_swap(ffn[half:], 1)
            order.mark(k["ffn_own"])

        def output(k, own, theirs):
            out = k["hidden"] + jnp.concatenate([own, theirs], axis=0)
            return in_order(out[:half], out[half:]).astype(bf16)

        def back_head(k):
            unit_two = k["unit_two"]
            g_ffn_gain = jnp.sum(k["back_own"] * unit_two, axis=0)
            d_normed_two = add_up(k["back_own"], k["back_far"])
            d_unit_two = d_normed_two * ffn_gain
            d_rest = k["inv_two"] * (
                d_unit_two - unit_two * jnp.mean(d_unit_two * unit_two, axis=-1, keepdims=True)
            )
            d_both = k["cotangent"] + jnp.concatenate([d_rest, t_swap(d_rest, 1)], axis=0)
            d_hidden = in_order(d_both[:half], d_both[half:])
            d_mixed = d_hidden.astype(bf16)
            d_scaled = right_trans(d_mixed, mamba_out_weight)
            d_context = right_trans(d_mixed, attn_out_weight)
            k["g_ffn_gain"] = g_ffn_gain
            k["d_hidden"] = d_hidden
            k["d_mixed"], k["d_scaled"], k["d_context"] = d_mixed, d_scaled, d_context
            k["cross"] = t_total(jnp.sum(d_scaled * mamba_gain * k["gated"], axis=-1))[:, None]
            order.mark(d_scaled, d_context)

        def back_mixers(index, k, held):
            d_scaled, cross = order.gate(k["d_scaled"], k["cross"])
            inv = k["inv_mamba"]
            inv_cross = jnp.concatenate([inv, inv**3 * cross / DSSM], axis=1)
            inv_cross = jnp.pad(inv_cross, ((0, 0), (0, LANES - 2)))
            back, d_statepre, d_keys, d_values, g_conv, g_state, g_heads, g_skip, g_gain = (
                mixers_backward(
                    index, micro, held, lengths, d_scaled, k["d_context"], k["gated"], inv_cross,
                    mamba_gain[None], k["pre"][0], k["pre"][2], k["pre"][3], k["pre"][6], k["ssd"],
                    *k["kept"], *k["attention"], cosine, sine, *mixer_rows,
                )
            )
            kv_far = jnp.where(core == 0, d_values, d_keys)
            kv_own = jnp.where(core == 0, d_keys, d_values)
            k["kv_sum"] = kv_own + t_swap(kv_far, 1)
            k["d_statepre"] = d_statepre
            k.update(
                g_conv_weight=g_conv[:-1], g_conv_bias=g_conv[-1],
                g_conv_state_weight=g_state[:-1], g_conv_state_bias=g_state[-1],
                g_step_bias=g_heads[0, :local_heads], g_decay_log=g_heads[1, :local_heads],
                g_skip=jnp.sum(g_skip.reshape(local_heads, MHDIM), axis=1),
                g_mamba_gain=g_gain[0],
            )
            order.mark(back)
            return back

        def back_inputs(index, k, back):
            back, d_statepre = order.gate(back, k["d_statepre"])
            piece = d_statepre.shape[1] // t_size
            parts = [
                lax.dynamic_slice_in_dim(d_statepre, jnp.bitwise_xor(me_t, q) * piece, piece, 1)
                for q in range(t_size)
            ]
            pieces = halving_order(list(range(0, t_size, 2)), 2, t_size)
            state_sum = jnp.concatenate([parts[q] for q in pieces], axis=1) + t_swap(
                jnp.concatenate([parts[q ^ 1] for q in pieces], axis=1), 1
            )
            bit = 2
            while bit < t_size:
                cut = state_sum.shape[1] // 2
                state_sum = state_sum[:, :cut] + t_swap(state_sum[:, cut:], bit)
                bit *= 2
            k["shared"] = jnp.concatenate([state_sum, k["kv_sum"]], axis=1).astype(bf16)
            rows_back = lax.slice_in_dim(back, index * count, (index + 1) * count, axis=0)
            norm_own, norm_other = halves(right_trans(rows_back, in_weight))
            k["norm_own"] = norm_own + t_swap(norm_other, 1)
            unit_own = mine(k["unit_one"])
            k["g_input_gain"] = jnp.sum(k["norm_own"] * unit_own, axis=0)
            order.mark(k["norm_own"])

        def input_grad(k, own, theirs):
            d_normed = in_order(own, theirs)
            unit_one = k["unit_one"]
            d_unit_one = d_normed * input_gain
            return k["d_hidden"] + k["inv_one"] * (
                d_unit_one - unit_one * jnp.mean(d_unit_one * unit_one, axis=-1, keepdims=True)
            )

        slots = []
        for index in range(micro):
            slot = tokens[index]
            if index:
                (slot,) = order.gate(slot)
            slots.append(forward(index, slot))
        for index in range(micro):
            feed_forward(index, slots[index])

        def joined(name):
            return jnp.concatenate([k[name] for k in slots], axis=0)

        def relative_columns(values):
            blocks = halving_order(list(range(dp_size)), 1, dp_size)
            return jnp.concatenate(
                [
                    lax.dynamic_slice_in_dim(values, jnp.bitwise_xor(me_dp, r) * block, block, 1)
                    for r in blocks
                ],
                axis=1,
            )

        def scattered(part, dimension):
            return lax.psum_scatter(part, "dp", scatter_dimension=dimension, tiled=True)

        inner_all, cot_all = order.gate(joined("inner_ffn"), joined("cot_low"))
        part_down = left_trans(inner_all, cot_all)
        order.mark(part_down)
        g_down = scattered(part_down, 1)
        def block_order(values):
            return [
                lax.dynamic_slice_in_dim(values, jnp.bitwise_xor(me_dp, r) * block, block, 1)
                for r in range(dp_size)
            ]

        def begin(work, send):
            (work.whole,) = order.gate(work.whole)
            order.mark(send())

        first, last = slots
        w_up = Scatter(order, dp_size, block_order(joined("normed_two")), joined("d_up"), 0)
        begin(w_up, w_up.start_first)
        back_head(first)
        in_weight = jnp.concatenate(order.gate(*in_weights), axis=1)
        (two_all,) = order.gate(joined("normed_two"))
        part_gate = order.point(left_trans(two_all, joined("d_gate")))
        order.mark(part_gate)
        g_gate = scattered(part_gate, 0)
        w_up.whole = order.point(w_up.whole)
        begin(w_up, w_up.start_later)
        back_head(last)
        w_outs = Scatter(order, dp_size, block_order(joined("d_mixed")), joined("mixer"), 1)
        begin(w_outs, w_outs.start_first)
        back_first = back_mixers(0, first, None)
        w_up.take_first()
        begin(w_outs, w_outs.start_later)
        back_inputs(0, first, back_first)
        back = back_mixers(1, last, back_first)
        w_up.take_later()
        w_outs.take_first()
        back_inputs(1, last, back)
        for k in slots:
            output_sum(k)
        one_columns = relative_columns(order.gate(joined("normed"))[0])
        part_early = left_trans(one_columns, back[:, : channels + heads_width])
        part_late = left_trans(
            one_columns,
            jnp.concatenate(
                [back[:, places["xpre"]], joined("shared"), back[:, places["step"]]], axis=1
            ),
        )
        def total(name):
            value = slots[0][name]
            for k in slots[1:]:
                value = value + k[name]
            return value

        names = [
            "g_conv_state_weight", "g_conv_state_bias", "g_input_gain", "g_ffn_gain",
            "g_conv_weight", "g_conv_bias", "g_step_bias", "g_decay_log", "g_skip",
            "g_mamba_gain",
        ]
        small = {name: total(name) for name in names}
        vector = jnp.concatenate([small[name].reshape(-1) for name in names])
        vector_rows = -(-vector.size // (8 * LANES)) * 8
        vector = jnp.pad(vector, (0, vector_rows * LANES - vector.size)).reshape(-1, LANES)
        shared_size = sum(small[name].size for name in names[:4])
        shared_rows = -(-shared_size // (8 * LANES)) * 8

        w_outs.take_later()
        part_early, part_late = order.gate(part_early, part_late)
        sums = [first["norm_own"], first["ffn_own"], last["ffn_own"], last["norm_own"]]
        (g_early, g_late), own, theirs, vector, wide_vector = scatter_all(
            dp_size, t_size, [part_early, part_late], sums, vector, shared_rows
        )
        vector, wide_vector = vector.reshape(-1), wide_vector.reshape(-1)
        order.mark(g_late)
        g_up = w_up.finish()
        g_outs = w_outs.finish()

        start = 0
        for name in names:
            shape, size = small[name].shape, small[name].size
            source = wide_vector if start < shared_size else vector
            small[name] = source[start : start + size].reshape(shape)
            start += size
        place = me_dp * t_size + me_t
        share = conv_state_bias.shape[0] // (dp_size * t_size)
        g_conv_state_weight = lax.dynamic_slice_in_dim(
            small["g_conv_state_weight"], place * share, share, 1
        )
        g_conv_state_bias = lax.dynamic_slice_in_dim(
            small["g_conv_state_bias"], place * share, share, 0
        )
        g_input_gain = lax.dynamic_slice_in_dim(small["g_input_gain"], me_dp * block, block, 0)
        g_ffn_gain = lax.dynamic_slice_in_dim(small["g_ffn_gain"], me_dp * block, block, 0)
        heads = [small[name] for name in names[4:]]

        shared_end = channels + joined("shared").shape[1]
        g_step = g_late[:, shared_end : shared_end + local_heads]
        g_late = g_late[:, :shared_end]
        grads_list = [input_grad(first, own[0], theirs[0]), input_grad(last, own[3], theirs[3])]
        outputs_list = [output(first, own[1], theirs[1]), output(last, own[2], theirs[2])]

        mamba_cols = mamba_in_weight.shape[1]
        tail = g_late[:, mamba_cols:]
        sub = block // t_size
        rowsets = []
        for q in range(t_size):
            part = lax.dynamic_slice_in_dim(tail, jnp.bitwise_xor(me_t, q) * sub, sub, 0)
            rowsets.append(part if q == 0 else t_swap(part, q))
        stacked = jnp.stack(rowsets)
        piece = state_weight.shape[1] // t_size
        sources = [
            lax.dynamic_index_in_dim(stacked, jnp.bitwise_xor(me_t, j), 0, keepdims=False)
            for j in range(t_size)
        ]
        g_state = jnp.concatenate([s[:, :piece] for s in sources], axis=1)
        pairs = t_size // 2
        g_kv = jnp.concatenate(
            [sources[(b % pairs) * 2 + b // pairs][:, piece:] for b in range(t_size)], axis=1
        )
        gate_cols = mamba_gate_weight.shape[1]
        mamba_rows = mamba_out_weight.shape[0]
        return (
            jnp.stack(outputs_list),
            jnp.stack(grads_list),
            g_input_gain,
            g_early[:, :gate_cols],
            g_late[:, :mamba_cols],
            g_state,
            g_step,
            heads[0],
            heads[1],
            g_conv_state_weight,
            g_conv_state_bias,
            heads[2],
            heads[3],
            heads[4],
            heads[5],
            g_outs[:mamba_rows],
            g_early[:, gate_cols:],
            g_kv,
            g_outs[mamba_rows:],
            g_ffn_gain,
            g_gate,
            g_up,
            g_down,
        )

    return per_device


def solution(mesh):
    placed = (
        P("dp", None, None),
        P("dp"),
        P("dp", None, None),
        P(),
        P(None, "tensor"),
        P(None, "tensor"),
        P(),
        P(None, "tensor"),
        P(None, "tensor"),
        P("tensor"),
        P(),
        P(),
        P("tensor"),
        P("tensor"),
        P("tensor"),
        P("tensor"),
        P("tensor", None),
        P(None, "tensor"),
        P(),
        P("tensor", None),
        P(),
        P(None, "tensor"),
        P(None, "tensor"),
        P("tensor", None),
    )
    return jax.shard_map(
        make_per_device(mesh.shape["dp"], mesh.shape["tensor"]),
        mesh=mesh,
        in_specs=placed,
        out_specs=(
            P("dp", None, None),
            P("dp", None, None),
            P("dp"),
            P("dp", "tensor"),
            P("dp", "tensor"),
            P(("dp", "tensor"), None),
            P("dp", "tensor"),
            P(None, "tensor"),
            P("tensor"),
            P(None, ("dp", "tensor")),
            P(("dp", "tensor")),
            P("tensor"),
            P("tensor"),
            P("tensor"),
            P("tensor"),
            P("tensor", "dp"),
            P("dp", "tensor"),
            P(("dp", "tensor"), None),
            P("tensor", "dp"),
            P("dp"),
            P("dp", "tensor"),
            P("dp", "tensor"),
            P("tensor", "dp"),
        ),
        check_vma=False,
    )
```

```python
import functools

import jax
import jax.numpy as jnp
from jax import lax
from jax.experimental import pallas as pl
from jax.experimental.pallas import tpu as pltpu
from jax.sharding import PartitionSpec as P

MHDIM = 64
STATE = 256
AHEADS = 8
KVHEADS = 2
AHDIM = 128
DSSM = 3072

epsilon = 1e-05
rope_base = 100000000000.0
f32 = jnp.float32
bf16 = jnp.bfloat16


def plain_dot(left, right):
    return jnp.dot(left, right, preferred_element_type=f32)


def right_trans(left, right):
    return lax.dot_general(left, right, (((1,), (1,)), ((), ())), preferred_element_type=f32)


def left_trans(left, right):
    return lax.dot_general(left, right, (((0,), (0,)), ((), ())), preferred_element_type=f32)


def silu_slope(values):
    sig = jax.nn.sigmoid(values)
    return sig * (1.0 + values * (1.0 - sig))


MESH = pl.DeviceIdType.MESH
LANES = 128
BLOCK = 128


def shifted(values, steps, row):
    if steps == 0:
        return values
    count = values.shape[0]
    moved = pltpu.roll(values, steps % count, 0)
    if steps > 0:
        return jnp.where(row >= steps, moved, 0.0)
    return jnp.where(row < count + steps, moved, 0.0)


def tap_sum(values, taps, bias):
    row = lax.broadcasted_iota(jnp.int32, values.shape, 0)
    width = taps.shape[0]
    total = jnp.zeros_like(values) + bias
    for k in range(width):
        total = total + shifted(values, width - 1 - k, row) * taps[k : k + 1, :]
    return total


def tap_back(grads, values, taps):
    row = lax.broadcasted_iota(jnp.int32, values.shape, 0)
    width = taps.shape[0]
    back = jnp.zeros_like(values)
    tap_grads = []
    for k in range(width):
        steps = width - 1 - k
        back = back + shifted(grads, -steps, row) * taps[k : k + 1, :]
        tap_grads.append(jnp.sum(grads * shifted(values, steps, row), axis=0, keepdims=True))
    return back, jnp.concatenate(tap_grads, axis=0)


def column_of(values, lane, index):
    return jnp.sum(jnp.where(lane == index, values, 0.0), axis=1, keepdims=True)


def exact_dot(left, right):
    return jnp.dot(left, right, precision=lax.Precision.HIGHEST, preferred_element_type=f32)


def turned(values, cosine, sine):
    return values * cosine + pltpu.roll(values, AHDIM // 2, 1) * sine


def scores_of(query, keys, lo, hi, length):
    scores = right_trans(query[lo:hi], keys[:hi]) * AHDIM ** (-0.5)
    t = lax.broadcasted_iota(jnp.int32, (hi - lo, hi), 0) + lo
    s = lax.broadcasted_iota(jnp.int32, (hi - lo, hi), 1)
    return scores, (t >= s) & (s < length)


def attention_forward(query_pre, key_pre, value_pre, cosine, sine, length, query, keys, values, logs, context):
    count, width = query.shape
    keys[...] = turned(key_pre, cosine, sine).astype(bf16)
    values[...] = value_pre.astype(bf16)
    lane = lax.broadcasted_iota(jnp.int32, (count, LANES), 1)
    kept = jnp.zeros((count, LANES), f32)
    for h in range(width // AHDIM):
        lanes = slice(h * AHDIM, (h + 1) * AHDIM)
        query[:, lanes] = turned(query_pre[:, lanes], cosine, sine).astype(bf16)
        found = []
        for i in range(count // BLOCK):
            lo, hi = i * BLOCK, (i + 1) * BLOCK
            scores, valid = scores_of(query[:, lanes], keys[...], lo, hi, length)
            masked = jnp.where(valid, scores, -1e30)
            peak = jnp.max(masked, axis=1, keepdims=True)
            expo = jnp.exp(masked - peak)
            total = jnp.sum(expo, axis=1, keepdims=True)
            found.append(peak + jnp.log(total))
            probs = (expo / total).astype(bf16)
            context[lo:hi, lanes] = plain_dot(probs, values[:hi, :]).astype(bf16)
        kept = jnp.where(lane == h, jnp.concatenate(found, axis=0), kept)
    logs[...] = kept


def attention_backward(d_context, query, keys, values, logs, cosine, sine, length, d_query_pre, d_keys, d_values):
    count, width = query.shape
    lane = lax.broadcasted_iota(jnp.int32, (count, LANES), 1)
    scale = AHDIM ** (-0.5)
    key_total = jnp.zeros((count, AHDIM), f32)
    value_total = jnp.zeros((count, AHDIM), f32)
    for h in range(width // AHDIM):
        lanes = slice(h * AHDIM, (h + 1) * AHDIM)
        log = column_of(logs[...], lane, h)
        pieces = []
        for i in range(count // BLOCK):
            lo, hi = i * BLOCK, (i + 1) * BLOCK
            scores, valid = scores_of(query[:, lanes], keys[...], lo, hi, length)
            probs = jnp.where(valid, jnp.exp(scores - log[lo:hi]), 0.0)
            grads = d_context[lo:hi, lanes]
            d_probs = right_trans(grads, values[:hi, :])
            delta = jnp.sum(probs * d_probs, axis=1, keepdims=True)
            d_scores = (probs * (d_probs - delta)).astype(bf16)
            pieces.append(plain_dot(d_scores, keys[:hi, :]) * scale)
            d_key = left_trans(d_scores, query[lo:hi, lanes]) * scale
            d_value = left_trans(probs.astype(bf16), grads)
            if hi < count:
                rest = jnp.zeros((count - hi, AHDIM), f32)
                d_key = jnp.concatenate([d_key, rest], axis=0)
                d_value = jnp.concatenate([d_value, rest], axis=0)
            key_total = key_total + d_key
            value_total = value_total + d_value
        d_query_pre[:, lanes] = turned(jnp.concatenate(pieces, axis=0), cosine, -sine).astype(bf16)
    d_keys[...] = turned(key_total, cosine, -sine)
    d_values[...] = value_total


def columns_of(channels, heads_width):
    places, start = {}, 0
    for name, size in (
        ("zgate", channels), ("query", heads_width), ("xpre", channels), ("state", 2 * STATE),
        ("key", AHDIM), ("value", AHDIM), ("step", LANES),
    ):
        places[name] = slice(start, start + size)
        start += size
    return places, start


def forward_kernel(
    lengths, zgate, query_pre, xpre, statepre, key_pre, value_pre, steppre, cosine, sine, conv_weight, conv_bias, state_taps, state_bias, step_bias, rates,
    skip_rep, gated, ssd, square, xconv, sconv, stepsize, cumul, inner, query, keys, values, logs,
    context, cumul_rows, *, slot,
):
    attention_forward(
        query_pre, key_pre[...], value_pre[...],
        cosine[...], sine[...], lengths[slot], query, keys, values, logs, context,
    )
    count, channels = xpre.shape
    xlin = tap_sum(xpre[...], conv_weight[...], conv_bias[...])
    xconv[...] = (xlin * jax.nn.sigmoid(xlin)).astype(bf16)
    slin = tap_sum(statepre[...], state_taps[...], state_bias[...])
    sconv[...] = (slin * jax.nn.sigmoid(slin)).astype(bf16)
    inner[...] = right_trans(sconv[:, STATE:], sconv[:, :STATE])
    step = jax.nn.softplus(steppre[...] + step_bias[...])
    stepsize[...] = step
    row = lax.broadcasted_iota(jnp.int32, (count, count), 0)
    col = lax.broadcasted_iota(jnp.int32, (count, count), 1)
    total = exact_dot(jnp.where(row >= col, 1.0, 0.0), -step * rates[...])
    cumul[...] = total
    cumul_rows[...] = total.T
    square[...] = jnp.zeros_like(square)

    def pair(p):
        lanes = slice(p * LANES, (p + 1) * LANES)
        lane = lax.broadcasted_iota(jnp.int32, (count, LANES), 1)
        xvals = xconv[:, lanes].astype(f32)
        low_half = lane < MHDIM
        step_rep = jnp.where(
            low_half, column_of(stepsize[...], lane, 2 * p), column_of(stepsize[...], lane, 2 * p + 1)
        )
        weighted = (step_rep * xvals).astype(bf16)
        columns = [column_of(cumul[...], lane, 2 * p + h) for h in range(2)]
        for i in range(count // BLOCK):
            lo, hi = i * BLOCK, (i + 1) * BLOCK
            results = []
            for h in range(2):
                differ = columns[h][lo:hi] - cumul_rows[2 * p + h : 2 * p + h + 1, :hi]
                t = lax.broadcasted_iota(jnp.int32, (BLOCK, hi), 0) + lo
                s = lax.broadcasted_iota(jnp.int32, (BLOCK, hi), 1)
                decay = jnp.exp(jnp.where(t >= s, differ, -1e30))
                mixing = (inner[lo:hi, :hi] * decay).astype(bf16)
                results.append(plain_dot(mixing, weighted[:hi]))
            half = jnp.where(low_half[lo:hi], results[0], results[1])
            half = half + skip_rep[:, lanes] * xvals[lo:hi]
            ssd[lo:hi, lanes] = half
            z = zgate[lo:hi, lanes]
            value = half * (z * jax.nn.sigmoid(z))
            gated[lo:hi, lanes] = value
            square[lo:hi, :] += value * value

    for p in range(channels // LANES):
        pair(p)


def full(*shape):
    return jax.ShapeDtypeStruct(shape, f32)


def low(*shape):
    return jax.ShapeDtypeStruct(shape, bf16)


def in_vmem(count):
    return [pl.BlockSpec(memory_space=pltpu.VMEM)] * count


def whole_blocks(shapes):
    return [pl.BlockSpec(s.shape, lambda i, n=len(s.shape): (0,) * n) for s in shapes]


def mixers_forward(slot, lengths, *operands):
    count, channels = operands[0].shape
    heads_width = operands[1].shape[1]
    shapes = (
        full(count, channels), full(count, channels), full(count, LANES), low(count, channels),
        low(count, 2 * STATE), full(count, LANES), full(count, LANES), full(count, count),
        low(count, heads_width), low(count, AHDIM), low(count, AHDIM), full(count, LANES),
        low(count, heads_width),
    )
    return pl.pallas_call(
        functools.partial(forward_kernel, slot=slot),
        grid=(1,),
        out_shape=shapes,
        in_specs=[pl.BlockSpec(memory_space=pltpu.SMEM)] + in_vmem(len(operands)),
        out_specs=tuple(whole_blocks(shapes)),
        scratch_shapes=[pltpu.VMEM((LANES, count), f32)],
        compiler_params=pltpu.CompilerParams(vmem_limit_bytes=48 * 2**20),
        cost_estimate=pl.CostEstimate(
            flops=10**6, bytes_accessed=10**6, transcendentals=10**3
        ),
    )(lengths, *operands)


def backward_kernel(
    lengths, d_scaled_in, d_context_in, gated_in, inv_cross, gain, zgate, xpre, statepre, steppre,
    ssd, xconv, sconv, stepsize, cumul, inner,
    query, keys, values, logs, cosine, sine, conv_weight, conv_bias, state_taps, state_bias,
    step_bias, rates, skip_rep,
    back, d_statepre, d_keys, d_values, g_conv, g_state, g_heads, g_skip, g_gain,
    d_ssd, d_xvals, cumul_rows, d_inner, row_sums, col_sums, d_step, *, slot, places,
):
    count, channels = ssd.shape
    attention_backward(
        d_context_in[...].astype(bf16), query, keys, values, logs, cosine[...], sine[...],
        lengths[slot], back.at[:, places["query"]], d_keys, d_values,
    )
    back[:, places["key"]] = d_keys[...].astype(bf16)
    back[:, places["value"]] = d_values[...].astype(bf16)
    d_zgate, d_xpre = back.at[:, places["zgate"]], back.at[:, places["xpre"]]
    d_steppre = back.at[:, places["step"]]
    d_scaled = d_scaled_in[...]
    g_gain[...] = jnp.sum(d_scaled * gated_in[...] * inv_cross[:, 0:1], axis=0, keepdims=True)
    inv = inv_cross[:, 0:1]
    cross = inv_cross[:, 1:2]
    d_gated = inv * (d_scaled * gain[...]) - gated_in[...] * cross
    z = zgate[...]
    sig = jax.nn.sigmoid(z)
    d_low = (d_gated * (z * sig)).astype(bf16)
    d_ssd[...] = d_low
    d_zgate[...] = (d_gated * ssd[...] * sig * (1.0 + z * (1.0 - sig))).astype(bf16)
    g_skip[...] = jnp.sum(d_low.astype(f32) * xconv[...].astype(f32), axis=0, keepdims=True)
    cumul_rows[...] = cumul[...].T
    d_inner[...] = jnp.zeros_like(d_inner)
    row_sums[...] = jnp.zeros_like(row_sums)
    col_sums[...] = jnp.zeros_like(col_sums)
    d_step[...] = jnp.zeros_like(d_step)

    def pair(p):
        lanes = slice(p * LANES, (p + 1) * LANES)
        lane = lax.broadcasted_iota(jnp.int32, (count, LANES), 1)
        low_half = lane < MHDIM
        xvals = xconv[:, lanes].astype(f32)
        step_rep = jnp.where(
            low_half, column_of(stepsize[...], lane, 2 * p), column_of(stepsize[...], lane, 2 * p + 1)
        )
        weighted = (step_rep * xvals).astype(bf16)
        grads = d_ssd[:, lanes]
        columns = [column_of(cumul[...], lane, 2 * p + h) for h in range(2)]
        pieces = []
        for h in range(2):
            only = jnp.where(low_half == (h == 0), grads, jnp.zeros_like(grads))
            back_part = jnp.zeros((count, LANES), f32)
            sums = []
            col_total = jnp.zeros((1, count), f32)
            for i in range(count // BLOCK):
                lo, hi = i * BLOCK, (i + 1) * BLOCK
                differ = columns[h][lo:hi] - cumul_rows[2 * p + h : 2 * p + h + 1, :hi]
                t = lax.broadcasted_iota(jnp.int32, (BLOCK, hi), 0) + lo
                s = lax.broadcasted_iota(jnp.int32, (BLOCK, hi), 1)
                decay = jnp.exp(jnp.where(t >= s, differ, -1e30))
                mixing = inner[lo:hi, :hi] * decay
                part = left_trans(mixing.astype(bf16), only[lo:hi])
                d_mixing = right_trans(only[lo:hi], weighted[:hi])
                d_inner[lo:hi, :hi] += d_mixing * decay
                flow = d_mixing * mixing
                sums.append(jnp.sum(flow, axis=1, keepdims=True))
                down = jnp.sum(flow, axis=0, keepdims=True)
                if hi < count:
                    part = jnp.concatenate([part, jnp.zeros((count - hi, LANES), f32)], axis=0)
                    down = jnp.concatenate([down, jnp.zeros((1, count - hi), f32)], axis=1)
                back_part = back_part + part
                col_total = col_total + down
            here = lane == 2 * p + h
            row_sums[...] = jnp.where(here, jnp.concatenate(sums, axis=0), row_sums[...])
            col_sums[2 * p + h : 2 * p + h + 1, :] = col_total
            pieces.append(back_part)
        d_weighted = pieces[0] + pieces[1]
        d_xvals[:, lanes] = grads.astype(f32) * skip_rep[:, lanes] + d_weighted * step_rep
        product = d_weighted * xvals
        for h in range(2):
            value = jnp.sum(
                jnp.where(low_half == (h == 0), product, 0.0), axis=1, keepdims=True
            )
            d_step[...] = jnp.where(lane == 2 * p + h, value, d_step[...])

    for p in range(channels // LANES):
        pair(p)

    d_cumul = row_sums[...] - col_sums[...].T
    row = lax.broadcasted_iota(jnp.int32, (count, count), 0)
    col = lax.broadcasted_iota(jnp.int32, (count, count), 1)
    d_logdecay = exact_dot(jnp.where(row <= col, 1.0, 0.0), d_cumul)
    rate = rates[...]
    d_full = (d_step[...] - d_logdecay * rate) * jax.nn.sigmoid(steppre[...] + step_bias[...])
    d_steppre[...] = d_full.astype(bf16)
    g_heads[0:1, :] = jnp.sum(d_full, axis=0, keepdims=True)
    g_heads[1:2, :] = jnp.sum(-d_logdecay * stepsize[...] * rate, axis=0, keepdims=True)

    d_in = d_inner[...].astype(bf16)
    d_c = plain_dot(d_in, sconv[:, :STATE])
    d_b = left_trans(d_in, sconv[:, STATE:])
    slin = tap_sum(statepre[...], state_taps[...], state_bias[...])
    d_slin = jnp.concatenate([d_b, d_c], axis=1) * silu_slope(slin)
    back_state, tap_grads = tap_back(d_slin, statepre[...], state_taps[...])
    d_statepre[...] = back_state
    back[:, places["state"]] = back_state.astype(bf16)
    g_state[...] = jnp.concatenate([tap_grads, jnp.sum(d_slin, axis=0, keepdims=True)], axis=0)
    xlin = tap_sum(xpre[...], conv_weight[...], conv_bias[...])
    d_xlin = d_xvals[...] * silu_slope(xlin)
    back_x, tap_grads = tap_back(d_xlin, xpre[...], conv_weight[...])
    d_xpre[...] = back_x.astype(bf16)
    g_conv[...] = jnp.concatenate([tap_grads, jnp.sum(d_xlin, axis=0, keepdims=True)], axis=0)


def mixers_backward(slot, slots, held, lengths, *operands):
    count, channels = operands[0].shape
    heads_width = operands[1].shape[1]
    taps = operands[-7].shape[0]
    width = columns_of(channels, heads_width)[1]
    kernel = functools.partial(
        backward_kernel, slot=slot, places=columns_of(channels, heads_width)[0]
    )
    aliases = {}
    extra_specs, extra = [], ()
    if held is not None:
        aliases = {0: 0}
        extra_specs, extra = [pl.BlockSpec(memory_space=pl.ANY)], (held,)
        inside = kernel
        kernel = lambda _, *refs: inside(*refs)
    shapes = (
        full(count, 2 * STATE), full(count, AHDIM), full(count, AHDIM), full(taps + 1, channels),
        full(taps + 1, 2 * STATE), full(2, LANES), full(1, channels), full(1, channels),
    )
    return pl.pallas_call(
        kernel,
        grid=(1,),
        out_shape=(low(slots * count, width),) + shapes,
        in_specs=extra_specs
        + [pl.BlockSpec(memory_space=pltpu.SMEM)]
        + in_vmem(len(operands)),
        out_specs=tuple(
            [pl.BlockSpec((count, width), lambda i: (slot, 0))] + whole_blocks(shapes)
        ),
        scratch_shapes=[
            pltpu.VMEM((count, channels), bf16),
            pltpu.VMEM((count, channels), f32),
            pltpu.VMEM((LANES, count), f32),
            pltpu.VMEM((count, count), f32),
            pltpu.VMEM((count, LANES), f32),
            pltpu.VMEM((LANES, count), f32),
            pltpu.VMEM((count, LANES), f32),
        ],
        input_output_aliases=aliases,
        compiler_params=pltpu.CompilerParams(vmem_limit_bytes=56 * 2**20),
        cost_estimate=pl.CostEstimate(
            flops=10**6, bytes_accessed=10**6, transcendentals=10**3
        ),
    )(*extra, lengths, *operands)


def swap(values, axis, size, bit):
    return lax.ppermute(values, axis, [(i, i ^ bit) for i in range(size)])


def halving_order(members, bit, limit):
    if bit >= limit:
        return members
    low = halving_order([m for m in members if not m & bit], bit * 2, limit)
    high = halving_order([m for m in members if m & bit], bit * 2, limit)
    return low + high


class Order:
    def __init__(self):
        self.last = ()
        self.queue = []

    def point(self, value, skip=0):
        if len(self.queue) <= skip:
            return value
        return lax.optimization_barrier((value, self.queue.pop(skip)))[0]

    def gate(self, *values):
        return lax.optimization_barrier((values, self.last))[0]

    def mark(self, *values):
        self.last = values


def scatter_all(size, t_size, parts, halves, rests, gain, vector, shared_rows):
    rows = parts[0].shape[0]
    works = len(parts)
    share = rows // size
    chunk = min(256, rows // 4)
    levels = size.bit_length() - 1
    spans = []
    for level in range(1, levels):
        lo, hi = rows >> (level + 1), rows >> level
        step = min(chunk, hi - lo)
        spans += [(level, start, step) for start in range(hi - step, lo - 1, -step)]
    spans.append((levels, 0, share))
    pieces = [(w,) + span for w in range(works) for span in spans]
    per_work = len(spans)
    widths = [p.shape[1] for p in parts]
    wide = max(widths)
    extra = len(halves)
    half_shape = halves[0].shape
    half, width = half_shape
    slots = 1 + max(rest[0] for rest in rests)
    extras = [value for rest in rests for value in rest[1:]]
    wholes = [n for n, rest in enumerate(rests) if len(rest) == 2]

    def kernel(*refs):
        held_in, refs = refs[:works], refs[works:]
        own, refs = refs[:extra], refs[extra:]
        beside = []
        for rest in rests:
            beside.append(refs[: len(rest) - 1])
            refs = refs[len(rest) - 1 :]
        gain_ref, small, refs = refs[0], refs[1], refs[2:]
        outs, refs = refs[:works], refs[works:]
        far, refs = refs[:extra], refs[extra:]
        result, grad, small_out, wide_out, refs = refs[0], refs[1], refs[2], refs[3], refs[4:]
        loads, pair_loads, totals, low_rows, theirs, refs = (
            refs[0], refs[1], refs[2], refs[3], refs[4], refs[5:]
        )
        boxes, wide_boxes, refs = refs[0], refs[1], refs[2:]
        landed, refs = refs[:works], refs[works:]
        later, refs = refs[: works * (levels - 1)], refs[works * (levels - 1) :]
        load_sems, out_sems, x_send, x_recv, z_send, z_recv, y_sems, c_sems, pair_sems, v_sems, w_sems = refs
        me = lax.axis_index("dp")
        spot = lax.axis_index("tensor")

        def neighbour(bit):
            return spot + bit - 2 * bit * lax.rem(spot // bit, 2)


        def partner(level):
            bit = 1 << level
            return me + bit - 2 * bit * lax.rem(me // bit, 2)

        barrier = pltpu.get_barrier_semaphore()
        for other in range(1, size):
            pl.semaphore_signal(
                barrier, inc=1, device_id={"dp": lax.rem(me + other, size)}, device_id_type=MESH
            )
        for other in range(1, t_size):
            pl.semaphore_signal(
                barrier, inc=1, device_id={"tensor": lax.rem(spot + other, t_size)},
                device_id_type=MESH,
            )
        pl.semaphore_wait(barrier, size + t_size - 2)

        def small_copy(other):
            return pltpu.make_async_remote_copy(
                src_ref=small, dst_ref=boxes.at[size - other], send_sem=v_sems.at[0, other],
                recv_sem=v_sems.at[1, size - other],
                device_id={"dp": lax.rem(me + other, size)}, device_id_type=MESH,
            )

        def wide_copy(other):
            return pltpu.make_async_remote_copy(
                src_ref=small_out.at[pl.ds(0, shared_rows), :], dst_ref=wide_boxes.at[t_size - other],
                send_sem=w_sems.at[0, other], recv_sem=w_sems.at[1, t_size - other],
                device_id={"tensor": lax.rem(spot + other, t_size)}, device_id_type=MESH,
            )

        def in_turn(kept, count, place, rows):
            total = jnp.zeros((rows, LANES), f32)
            for number in range(count):
                offset = lax.rem(number - place + count, count)
                total = total + kept[offset]
            return total

        def small_sums(stage):
            if stage == 0:
                boxes[0] = small[...]
                for other in range(1, size):
                    small_copy(other).wait_recv()
                small_out[...] = in_turn(boxes, size, me, small.shape[0])
                for other in range(1, t_size):
                    wide_copy(other).start()
            else:
                wide_boxes[0] = small_out[:shared_rows, :]
                for other in range(1, t_size):
                    wide_copy(other).wait_recv()
                wide_out[...] = in_turn(wide_boxes, t_size, spot, shared_rows)


        def y_copy(e):
            return pltpu.make_async_remote_copy(
                src_ref=own[e], dst_ref=far[e], send_sem=y_sems.at[0, e], recv_sem=y_sems.at[1, e],
                device_id={"tensor": neighbour(2)}, device_id_type=MESH,
            )

        core = lax.rem(spot, 2)

        def rows_of(place):
            return pl.ds(pl.multiple_of(place * half, 8), half)

        def c_copy(e):
            slot = rests[e][0]
            if e in wholes:
                target = theirs.at[wholes.index(e)]
            else:
                target = grad.at[slot, rows_of(core), :]
            return pltpu.make_async_remote_copy(
                src_ref=totals.at[e], dst_ref=target, send_sem=c_sems.at[0, e],
                recv_sem=c_sems.at[1, e], device_id={"tensor": neighbour(1)}, device_id_type=MESH,
            )

        def fetch(source, place):
            return pltpu.make_async_copy(source, pair_loads.at[place], pair_sems.at[0, place])

        def keep(e, place):
            slot = rests[e][0]
            if e in wholes:
                n = 2 * wholes.index(e) + place
                target = result.at[slot, rows_of(core if place == 0 else 1 - core), :]
                return pltpu.make_async_copy(low_rows.at[n], target, pair_sems.at[1 + place, e])
            return pltpu.make_async_copy(
                totals.at[e], grad.at[slot, rows_of(core), :], pair_sems.at[1, e]
            )

        def exchange(e):
            y_copy(e).wait_recv()
            sources = [own[e], far[e]]
            if e in wholes:
                sources.append(beside[e][0].at[pl.ds(0, half), :])
            else:
                sources += [beside[e][0], beside[e][1]]
            for place, source in enumerate(sources):
                fetch(source, place).start()
            for place, source in enumerate(sources):
                fetch(source, place).wait()
            total = pair_loads[0] + pair_loads[1]
            if e in wholes:
                totals[e] = total
                low_rows[2 * wholes.index(e)] = (pair_loads[2] + total).astype(bf16)
            else:
                unit = pair_loads[3]
                scaled = total * gain_ref[...]
                mean = jnp.sum(scaled * unit, axis=1, keepdims=True) / width
                totals[e] = pair_loads[2] + beside[e][2][...] * (scaled - unit * mean)
            c_copy(e).start()
            keep(e, 0).start()

        def complete(e):
            fetch(beside[e][0].at[pl.ds(half, half), :], 0).start()
            c_copy(e).wait_recv()
            fetch(beside[e][0].at[pl.ds(half, half), :], 0).wait()
            n = wholes.index(e)
            low_rows[2 * n + 1] = (pair_loads[0] + theirs[n]).astype(bf16)
            keep(e, 1).start()

        def first_copy(number):
            w, _, start, step = pieces[number]
            return pltpu.make_async_remote_copy(
                src_ref=held_in[w].at[pl.ds(rows // 2 + start, step), :],
                dst_ref=landed[w].at[pl.ds(start, step), :],
                send_sem=x_send.at[number],
                recv_sem=x_recv.at[number],
                device_id={"dp": partner(0)},
                device_id_type=MESH,
            )

        def load(number):
            w, _, start, step = pieces[number]
            return pltpu.make_async_copy(
                held_in[w].at[pl.ds(start, step), :],
                loads.at[number % 2, pl.ds(0, step), pl.ds(0, widths[w])],
                load_sems.at[number % 2],
            )

        def later_copy(number):
            w, level, start, step = pieces[number]
            return pltpu.make_async_remote_copy(
                src_ref=landed[w].at[pl.ds(start, step), :],
                dst_ref=later[w * (levels - 1) + level - 1].at[pl.ds(start - (rows >> (level + 1)), step), :],
                send_sem=z_send.at[number],
                recv_sem=z_recv.at[number],
                device_id={"dp": partner(level)},
                device_id_type=MESH,
            )

        def store(w):
            return pltpu.make_async_copy(
                landed[w].at[pl.ds(0, share), :], outs[w], out_sems.at[w]
            )

        for other in range(1, size):
            small_copy(other).start()
        for e in range(extra):
            y_copy(e).start()
        for number in range(len(pieces)):
            first_copy(number).start()
        load(0).start()
        arrived = set()

        def need(w, level, start, step):
            base = rows >> (level + 1)
            for other in range(w * per_work, (w + 1) * per_work):
                _, its_level, its_start, its_step = pieces[other]
                if its_level != level or other in arrived:
                    continue
                if its_start - base < start + step and start < its_start - base + its_step:
                    later_copy(other).wait_recv()
                    arrived.add(other)

        def finish(w):
            level = levels - 1
            need(w, level, 0, share)
            landed[w][:share, :] += later[w * (levels - 1) + level - 1][:share, :]
            store(w).start()

        for number, (w, level, start, step) in enumerate(pieces):
            load(number).wait()
            if number + 1 < len(pieces):
                load(number + 1).start()
            first_copy(number).wait_recv()
            value = loads[number % 2, :step, : widths[w]] + landed[w][start : start + step, :]
            for before in range(1, min(level, levels - 1)):
                need(w, before, start, step)
                value = value + later[w * (levels - 1) + before - 1][start : start + step, :]
            landed[w][start : start + step, :] = value
            if level < levels:
                later_copy(number).start()
            if w and number == w * per_work + min(2, per_work - 1):
                finish(w - 1)
            if number in (0, 2):
                small_sums(number // 2)
            if number % 2 and number // 2 < extra:
                exchange(number // 2)
            if number % 2 == 0 and number // 2 - 2 in wholes:
                complete(number // 2 - 2)
        for e in range(len(pieces) // 2, extra):
            exchange(e)
        for e in wholes:
            if 2 * (e + 2) >= len(pieces):
                complete(e)
        finish(works - 1)
        for other in range(1, size):
            small_copy(other).wait_send()
        for other in range(1, t_size):
            wide_copy(other).wait_send()
        for e in range(extra):
            y_copy(e).wait_send()
            c_copy(e).wait_send()
            keep(e, 0).wait()
            if e in wholes:
                keep(e, 1).wait()
            else:
                c_copy(e).wait_recv()
        for number, (w, level, start, step) in enumerate(pieces):
            first_copy(number).wait_send()
            if level < levels:
                later_copy(number).wait_send()
        for w in range(works):
            store(w).wait()

    scratch = [
        pltpu.VMEM((2, chunk, wide), f32),
        pltpu.VMEM((4,) + half_shape, f32),
        pltpu.VMEM((extra,) + half_shape, f32),
        pltpu.VMEM((2 * len(wholes),) + half_shape, bf16),
        pltpu.VMEM((len(wholes),) + half_shape, f32),
        pltpu.VMEM((size,) + vector.shape, f32),
        pltpu.VMEM((t_size, shared_rows, LANES), f32),
    ]
    scratch += [pltpu.VMEM((rows // 2, n), f32) for n in widths]
    scratch += [
        pltpu.VMEM((rows >> (level + 1), n), f32) for n in widths for level in range(1, levels)
    ]
    scratch += [
        pltpu.SemaphoreType.DMA((2,)),
        pltpu.SemaphoreType.DMA((works,)),
    ] + [pltpu.SemaphoreType.DMA((len(pieces),))] * 4
    scratch += [pltpu.SemaphoreType.DMA((n, extra)) for n in (2, 2)]
    scratch += [pltpu.SemaphoreType.DMA((3, max(4, extra)))]
    scratch += [pltpu.SemaphoreType.DMA((2, size)), pltpu.SemaphoreType.DMA((2, t_size))]
    results = pl.pallas_call(
        kernel,
        out_shape=tuple(
            [full(share, n) for n in widths]
            + [full(*half_shape)] * extra
            + [low(slots, 2 * half, width), full(slots, 2 * half, width)]
            + [full(*vector.shape), full(shared_rows, LANES)]
        ),
        in_specs=[pl.BlockSpec(memory_space=pl.ANY)] * (works + extra)
        + [
            pl.BlockSpec(memory_space=pltpu.VMEM if value.shape[1] == 1 else pl.ANY)
            for value in extras
        ]
        + in_vmem(2),
        out_specs=tuple([pl.BlockSpec(memory_space=pl.ANY)] * (works + extra + 2) + in_vmem(2)),
        scratch_shapes=scratch,
        compiler_params=pltpu.CompilerParams(
            collective_id=0, has_side_effects=True, vmem_limit_bytes=60 * 2**20
        ),
        cost_estimate=pl.CostEstimate(
            flops=10**6, bytes_accessed=10**6, transcendentals=0
        ),
    )(*parts, *halves, *extras, gain, vector)
    return results[:works], *results[works + extra :]


def make_per_device(dp_size, t_size):
    def per_device(
        tokens,
        lengths,
        out_grad,
        input_gain,
        mamba_gate_weight,
        mamba_in_weight,
        state_weight,
        step_weight,
        conv_weight,
        conv_bias,
        conv_state_weight,
        conv_state_bias,
        step_bias,
        decay_log,
        skip_scale,
        mamba_gain,
        mamba_out_weight,
        query_weight,
        key_value_weight,
        attn_out_weight,
        ffn_gain,
        gate_weight,
        up_weight,
        down_weight,
    ):
        micro = tokens.shape[0]
        count = tokens.shape[1]
        width = tokens.shape[2]
        half = count // 2
        local_heads = step_weight.shape[1]
        q_local = query_weight.shape[1] // AHDIM
        kv_width = key_value_weight.shape[1] // 2
        group_size = AHEADS // KVHEADS
        me_dp = lax.axis_index("dp")
        me_t = lax.axis_index("tensor")
        core = lax.rem(me_t, 2)
        kv_head = me_t * q_local // group_size
        key_weight = lax.dynamic_slice_in_dim(key_value_weight, kv_head * AHDIM, AHDIM, 1)
        value_weight = lax.dynamic_slice_in_dim(
            key_value_weight, kv_width + kv_head * AHDIM, AHDIM, 1
        )
        rows = jnp.arange(count)
        freqs = rope_base ** (-(jnp.arange(AHDIM // 2).astype(f32) * 2.0) / AHDIM)
        angles = rows.astype(f32)[:, None] * freqs[None, :]
        cosine, sine = jnp.cos(angles), jnp.sin(angles)
        cosine = jnp.concatenate([cosine, cosine], axis=1)
        sine = jnp.concatenate([-sine, sine], axis=1)
        channels = mamba_in_weight.shape[1]
        heads_width = query_weight.shape[1]
        places, _ = columns_of(channels, heads_width)
        pad_step = LANES - local_heads

        def lane_row(vector):
            return jnp.pad(vector, (0, pad_step))[None]

        mixer_rows = (
            conv_weight, conv_bias[None], conv_state_weight, conv_state_bias[None],
            lane_row(step_bias), lane_row(jnp.exp(decay_log)), jnp.repeat(skip_scale, MHDIM)[None],
        )
        step_lanes = jnp.pad(step_weight, ((0, 0), (0, pad_step)))
        in_weights = (
            mamba_gate_weight, query_weight, mamba_in_weight, state_weight, key_weight,
            value_weight, step_lanes,
        )

        def t_swap(values, bit):
            return swap(values, "tensor", t_size, bit)

        def t_total(values):
            bit = 1
            while bit < t_size:
                values = values + t_swap(values, bit)
                bit *= 2
            return values

        def mine(values):
            return lax.dynamic_slice_in_dim(values, core * half, half, 0)

        def other(values):
            return lax.dynamic_slice_in_dim(values, (1 - core) * half, half, 0)

        def halves(values):
            values = lax.optimization_barrier(values)
            return mine(values), other(values)

        def relative(values):
            return jnp.concatenate([mine(values), other(values)], axis=0)

        def in_order(own, far):
            return jnp.where(
                core == 0,
                jnp.concatenate([own, far], axis=0),
                jnp.concatenate([far, own], axis=0),
            )

        def half_sum(own, far, pieces):
            own = own + t_swap(far, 1)
            bit = 2
            while bit < t_size // 2:
                own = own + t_swap(own, bit)
                bit *= 2
            step = -(-own.shape[0] // (8 * pieces)) * 8
            parts = []
            for start in range(0, own.shape[0], step):
                parts.append(t_swap(own[start : start + step], bit))
            order.queue += parts
            return own, parts

        def add_up(own, parts):
            for part in parts:
                order.queue = [p for p in order.queue if p is not part]
            own = order.point(own)
            own, *parts = order.gate(own, *parts)
            return own + jnp.concatenate(parts, axis=0)

        block = width // dp_size

        order = Order()

        def forward(index, slot):
            inputs = slot.astype(f32)
            inv_one = lax.rsqrt(jnp.mean(inputs * inputs, axis=-1, keepdims=True) + epsilon)
            unit_one = inputs * inv_one
            normed = (unit_one * input_gain).astype(bf16)
            pre = [plain_dot(normed, w) for w in in_weights]
            pre[0] = order.point(pre[0])
            gated, ssd, square, *kept, query, keys, values, logs, context = mixers_forward(
                index, lengths, *pre, cosine, sine, *mixer_rows
            )
            gated = order.point(gated)
            total_square = t_total(jnp.sum(square, axis=-1))
            inv_mamba = lax.rsqrt(total_square / DSSM + epsilon)[:, None]
            scaled = order.point((gated * inv_mamba * mamba_gain).astype(bf16))
            mixer = jnp.concatenate([scaled, context], axis=1)
            mixed_own, mixed_far = half_sum(
                *halves(plain_dot(scaled, mamba_out_weight) + plain_dot(context, attn_out_weight)),
                3,
            )
            order.mark(mixed_own)
            return dict(
                mixed_own=mixed_own, mixed_far=mixed_far, inputs=inputs, inv_one=inv_one,
                unit_one=unit_one, normed=normed, pre=pre, gated=gated, ssd=ssd, kept=kept,
                attention=(query, keys, values, logs), inv_mamba=inv_mamba, mixer=mixer,
            )

        def feed_forward(index, k):
            hidden_own = mine(k["inputs"]) + add_up(k["mixed_own"], k["mixed_far"])
            hidden = jnp.concatenate([hidden_own, t_swap(hidden_own, 1)], axis=0)
            inv_two = lax.rsqrt(jnp.mean(hidden * hidden, axis=-1, keepdims=True) + epsilon)
            unit_two = hidden * inv_two
            unit_two = order.point(unit_two)
            normed_two = (unit_two * ffn_gain).astype(bf16)
            gate = order.point(plain_dot(normed_two, gate_weight))
            upper = plain_dot(normed_two, up_weight)
            gsig = jax.nn.sigmoid(gate)
            gsilu = gate * gsig
            inner_ffn = (gsilu * upper).astype(bf16)
            valid = (rows < lengths[index]).astype(f32)[:, None]
            cotangent = relative(out_grad[index].astype(f32) * valid)
            cot_low = cotangent.astype(bf16)
            d_inner_ffn = order.point(right_trans(cot_low, down_weight))
            d_gate = (d_inner_ffn * upper * gsig * (1.0 + gate * (1.0 - gsig))).astype(bf16)
            d_up = (d_inner_ffn * gsilu).astype(bf16)
            back = right_trans(d_gate, gate_weight) + right_trans(d_up, up_weight)
            back_own, back_far = half_sum(back[:half], back[half:], 3)
            order.mark(back_own)
            k.update(
                back_own=back_own, back_far=back_far,
                hidden=hidden, inv_two=inv_two[:half], unit_two=unit_two[:half],
                normed_two=normed_two, inner_ffn=inner_ffn, cotangent=cotangent, cot_low=cot_low,
                d_gate=d_gate, d_up=d_up,
            )

        def output_sum(k):
            (inner_ffn,) = order.gate(k["inner_ffn"])
            ffn = plain_dot(inner_ffn, down_weight)
            k["ffn_own"] = ffn[:half] + t_swap(ffn[half:], 1)
            order.mark(k["ffn_own"])

        def back_head(k):
            unit_two = k["unit_two"]
            g_ffn_gain = jnp.sum(k["back_own"] * unit_two, axis=0)
            d_normed_two = add_up(k["back_own"], k["back_far"])
            d_unit_two = d_normed_two * ffn_gain
            d_rest = k["inv_two"] * (
                d_unit_two - unit_two * jnp.mean(d_unit_two * unit_two, axis=-1, keepdims=True)
            )
            d_both = k["cotangent"] + jnp.concatenate([d_rest, t_swap(d_rest, 1)], axis=0)
            d_mixed = in_order(d_both[:half], d_both[half:]).astype(bf16)
            d_scaled = right_trans(d_mixed, mamba_out_weight)
            d_context = right_trans(d_mixed, attn_out_weight)
            k["g_ffn_gain"] = g_ffn_gain
            k["d_hidden_own"] = d_both[:half]
            k["d_mixed"], k["d_scaled"], k["d_context"] = d_mixed, d_scaled, d_context
            k["cross"] = t_total(jnp.sum(d_scaled * mamba_gain * k["gated"], axis=-1))[:, None]
            order.mark(d_scaled, d_context)

        def back_mixers(index, k, held):
            d_scaled, cross = order.gate(k["d_scaled"], k["cross"])
            inv = k["inv_mamba"]
            inv_cross = jnp.concatenate([inv, inv**3 * cross / DSSM], axis=1)
            inv_cross = jnp.pad(inv_cross, ((0, 0), (0, LANES - 2)))
            back, d_statepre, d_keys, d_values, g_conv, g_state, g_heads, g_skip, g_gain = (
                mixers_backward(
                    index, micro, held, lengths, d_scaled, k["d_context"], k["gated"], inv_cross,
                    mamba_gain[None], k["pre"][0], k["pre"][2], k["pre"][3], k["pre"][6], k["ssd"],
                    *k["kept"], *k["attention"], cosine, sine, *mixer_rows,
                )
            )
            kv_far = jnp.where(core == 0, d_values, d_keys)
            kv_own = jnp.where(core == 0, d_keys, d_values)
            k["kv_sum"] = kv_own + t_swap(kv_far, 1)
            k["d_statepre"] = d_statepre
            k.update(
                g_conv_weight=g_conv[:-1], g_conv_bias=g_conv[-1],
                g_conv_state_weight=g_state[:-1], g_conv_state_bias=g_state[-1],
                g_step_bias=g_heads[0, :local_heads], g_decay_log=g_heads[1, :local_heads],
                g_skip=jnp.sum(g_skip.reshape(local_heads, MHDIM), axis=1),
                g_mamba_gain=g_gain[0],
            )
            order.mark(back)
            return back

        def back_inputs(index, k, back):
            back, d_statepre = order.gate(back, k["d_statepre"])
            piece = d_statepre.shape[1] // t_size
            parts = [
                lax.dynamic_slice_in_dim(d_statepre, jnp.bitwise_xor(me_t, q) * piece, piece, 1)
                for q in range(t_size)
            ]
            pieces = halving_order(list(range(0, t_size, 2)), 2, t_size)
            state_sum = jnp.concatenate([parts[q] for q in pieces], axis=1) + t_swap(
                jnp.concatenate([parts[q ^ 1] for q in pieces], axis=1), 1
            )
            bit = 2
            while bit < t_size:
                cut = state_sum.shape[1] // 2
                state_sum = state_sum[:, :cut] + t_swap(state_sum[:, cut:], bit)
                bit *= 2
            k["shared"] = jnp.concatenate([state_sum, k["kv_sum"]], axis=1).astype(bf16)
            rows_back = lax.slice_in_dim(back, index * count, (index + 1) * count, axis=0)
            norm_own, norm_other = halves(right_trans(rows_back, in_weight))
            k["norm_own"] = norm_own + t_swap(norm_other, 1)
            unit_own = mine(k["unit_one"])
            k["g_input_gain"] = jnp.sum(k["norm_own"] * unit_own, axis=0)
            order.mark(k["norm_own"])

        slots = []
        for index in range(micro):
            slot = tokens[index]
            if index:
                (slot,) = order.gate(slot)
            slots.append(forward(index, slot))
        for index in range(micro):
            feed_forward(index, slots[index])

        def joined(name):
            return jnp.concatenate([k[name] for k in slots], axis=0)

        def relative_columns(values):
            blocks = halving_order(list(range(dp_size)), 1, dp_size)
            return jnp.concatenate(
                [
                    lax.dynamic_slice_in_dim(values, jnp.bitwise_xor(me_dp, r) * block, block, 1)
                    for r in blocks
                ],
                axis=1,
            )

        def scattered(part, dimension):
            return lax.psum_scatter(part, "dp", scatter_dimension=dimension, tiled=True)

        inner_all, cot_all = order.gate(joined("inner_ffn"), joined("cot_low"))
        part_down = left_trans(inner_all, cot_all)
        order.mark(part_down)
        g_down = scattered(part_down, 1)
        first, last = slots
        back_head(first)
        in_weight = jnp.concatenate(order.gate(*in_weights), axis=1)
        (two_all,) = order.gate(joined("normed_two"))
        part_gate = order.point(left_trans(two_all, joined("d_gate")))
        order.mark(part_gate)
        g_gate = scattered(part_gate, 0)
        (two_all,) = order.gate(two_all)
        part_up = order.point(left_trans(two_all, joined("d_up")))
        order.mark(part_up)
        g_up = scattered(part_up, 0)
        back_head(last)
        back_first = back_mixers(0, first, None)
        back_inputs(0, first, back_first)
        back = back_mixers(1, last, back_first)
        back_inputs(1, last, back)
        for k in slots:
            output_sum(k)
        one_columns = relative_columns(order.gate(joined("normed"))[0])
        part_outs = left_trans(relative_columns(joined("d_mixed")), joined("mixer"))
        part_early = left_trans(one_columns, back[:, : channels + heads_width])
        part_late = left_trans(
            one_columns,
            jnp.concatenate(
                [back[:, places["xpre"]], joined("shared"), back[:, places["step"]]], axis=1
            ),
        )

        def total(name):
            value = slots[0][name]
            for k in slots[1:]:
                value = value + k[name]
            return value

        names = [
            "g_conv_state_weight", "g_conv_state_bias", "g_input_gain", "g_ffn_gain",
            "g_conv_weight", "g_conv_bias", "g_step_bias", "g_decay_log", "g_skip",
            "g_mamba_gain",
        ]
        small = {name: total(name) for name in names}
        vector = jnp.concatenate([small[name].reshape(-1) for name in names])
        vector_rows = -(-vector.size // (8 * LANES)) * 8
        vector = jnp.pad(vector, (0, vector_rows * LANES - vector.size)).reshape(-1, LANES)
        shared_size = sum(small[name].size for name in names[:4])
        shared_rows = -(-shared_size // (8 * LANES)) * 8

        sums = [first["norm_own"], first["ffn_own"], last["ffn_own"], last["norm_own"]]
        rests = [
            (0, first["d_hidden_own"], mine(first["unit_one"]), mine(first["inv_one"])),
            (0, first["hidden"]),
            (1, last["hidden"]),
            (1, last["d_hidden_own"], mine(last["unit_one"]), mine(last["inv_one"])),
        ]
        (g_outs, g_early, g_late), out, in_grad, vector, wide_vector = scatter_all(
            dp_size, t_size, [part_outs, part_early, part_late], sums, rests, input_gain[None],
            vector, shared_rows,
        )
        vector, wide_vector = vector.reshape(-1), wide_vector.reshape(-1)
        start = 0
        for name in names:
            shape, size = small[name].shape, small[name].size
            source = wide_vector if start < shared_size else vector
            small[name] = source[start : start + size].reshape(shape)
            start += size
        place = me_dp * t_size + me_t
        share = conv_state_bias.shape[0] // (dp_size * t_size)
        g_conv_state_weight = lax.dynamic_slice_in_dim(
            small["g_conv_state_weight"], place * share, share, 1
        )
        g_conv_state_bias = lax.dynamic_slice_in_dim(
            small["g_conv_state_bias"], place * share, share, 0
        )
        g_input_gain = lax.dynamic_slice_in_dim(small["g_input_gain"], me_dp * block, block, 0)
        g_ffn_gain = lax.dynamic_slice_in_dim(small["g_ffn_gain"], me_dp * block, block, 0)
        heads = [small[name] for name in names[4:]]

        shared_end = channels + joined("shared").shape[1]
        g_step = g_late[:, shared_end : shared_end + local_heads]
        g_late = g_late[:, :shared_end]
        g_outs = g_outs.T

        mamba_cols = mamba_in_weight.shape[1]
        tail = g_late[:, mamba_cols:]
        sub = block // t_size
        rowsets = []
        for q in range(t_size):
            part = lax.dynamic_slice_in_dim(tail, jnp.bitwise_xor(me_t, q) * sub, sub, 0)
            rowsets.append(part if q == 0 else t_swap(part, q))
        stacked = jnp.stack(rowsets)
        piece = state_weight.shape[1] // t_size
        sources = [
            lax.dynamic_index_in_dim(stacked, jnp.bitwise_xor(me_t, j), 0, keepdims=False)
            for j in range(t_size)
        ]
        g_state = jnp.concatenate([s[:, :piece] for s in sources], axis=1)
        pairs = t_size // 2
        g_kv = jnp.concatenate(
            [sources[(b % pairs) * 2 + b // pairs][:, piece:] for b in range(t_size)], axis=1
        )
        gate_cols = mamba_gate_weight.shape[1]
        mamba_rows = mamba_out_weight.shape[0]
        return (
            out,
            in_grad,
            g_input_gain,
            g_early[:, :gate_cols],
            g_late[:, :mamba_cols],
            g_state,
            g_step,
            heads[0],
            heads[1],
            g_conv_state_weight,
            g_conv_state_bias,
            heads[2],
            heads[3],
            heads[4],
            heads[5],
            g_outs[:mamba_rows],
            g_early[:, gate_cols:],
            g_kv,
            g_outs[mamba_rows:],
            g_ffn_gain,
            g_gate,
            g_up,
            g_down,
        )

    return per_device


def solution(mesh):
    placed = (
        P("dp", None, None),
        P("dp"),
        P("dp", None, None),
        P(),
        P(None, "tensor"),
        P(None, "tensor"),
        P(),
        P(None, "tensor"),
        P(None, "tensor"),
        P("tensor"),
        P(),
        P(),
        P("tensor"),
        P("tensor"),
        P("tensor"),
        P("tensor"),
        P("tensor", None),
        P(None, "tensor"),
        P(),
        P("tensor", None),
        P(),
        P(None, "tensor"),
        P(None, "tensor"),
        P("tensor", None),
    )
    return jax.shard_map(
        make_per_device(mesh.shape["dp"], mesh.shape["tensor"]),
        mesh=mesh,
        in_specs=placed,
        out_specs=(
            P("dp", None, None),
            P("dp", None, None),
            P("dp"),
            P("dp", "tensor"),
            P("dp", "tensor"),
            P(("dp", "tensor"), None),
            P("dp", "tensor"),
            P(None, "tensor"),
            P("tensor"),
            P(None, ("dp", "tensor")),
            P(("dp", "tensor")),
            P("tensor"),
            P("tensor"),
            P("tensor"),
            P("tensor"),
            P("tensor", "dp"),
            P("dp", "tensor"),
            P(("dp", "tensor"), None),
            P("tensor", "dp"),
            P("dp"),
            P("dp", "tensor"),
            P("dp", "tensor"),
            P("tensor", "dp"),
        ),
        check_vma=False,
    )
```

```python
import functools

import jax
import jax.numpy as jnp
from jax import lax
from jax.experimental import pallas as pl
from jax.experimental.pallas import tpu as pltpu
from jax.sharding import PartitionSpec as P

MHDIM = 64
STATE = 256
AHEADS = 8
KVHEADS = 2
AHDIM = 128
DSSM = 3072

epsilon = 1e-05
rope_base = 100000000000.0
f32 = jnp.float32
bf16 = jnp.bfloat16


def plain_dot(left, right):
    return jnp.dot(left, right, preferred_element_type=f32)


def right_trans(left, right):
    return lax.dot_general(left, right, (((1,), (1,)), ((), ())), preferred_element_type=f32)


def left_trans(left, right):
    return lax.dot_general(left, right, (((0,), (0,)), ((), ())), preferred_element_type=f32)


def silu_slope(values):
    sig = jax.nn.sigmoid(values)
    return sig * (1.0 + values * (1.0 - sig))


MESH = pl.DeviceIdType.MESH
LANES = 128
BLOCK = 128


def shifted(values, steps, row):
    if steps == 0:
        return values
    count = values.shape[0]
    moved = pltpu.roll(values, steps % count, 0)
    if steps > 0:
        return jnp.where(row >= steps, moved, 0.0)
    return jnp.where(row < count + steps, moved, 0.0)


def tap_sum(values, taps, bias):
    row = lax.broadcasted_iota(jnp.int32, values.shape, 0)
    width = taps.shape[0]
    total = jnp.zeros_like(values) + bias
    for k in range(width):
        total = total + shifted(values, width - 1 - k, row) * taps[k : k + 1, :]
    return total


def tap_back(grads, values, taps):
    row = lax.broadcasted_iota(jnp.int32, values.shape, 0)
    width = taps.shape[0]
    back = jnp.zeros_like(values)
    tap_grads = []
    for k in range(width):
        steps = width - 1 - k
        back = back + shifted(grads, -steps, row) * taps[k : k + 1, :]
        tap_grads.append(jnp.sum(grads * shifted(values, steps, row), axis=0, keepdims=True))
    return back, jnp.concatenate(tap_grads, axis=0)


def column_of(values, lane, index):
    return jnp.sum(jnp.where(lane == index, values, 0.0), axis=1, keepdims=True)


def exact_dot(left, right):
    return jnp.dot(left, right, precision=lax.Precision.HIGHEST, preferred_element_type=f32)


def turned(values, cosine, sine):
    return values * cosine + pltpu.roll(values, AHDIM // 2, 1) * sine


def scores_of(query, keys, lo, hi, length):
    scores = right_trans(query[lo:hi], keys[:hi]) * AHDIM ** (-0.5)
    t = lax.broadcasted_iota(jnp.int32, (hi - lo, hi), 0) + lo
    s = lax.broadcasted_iota(jnp.int32, (hi - lo, hi), 1)
    return scores, (t >= s) & (s < length)


def attention_forward(query_pre, key_pre, value_pre, cosine, sine, length, query, keys, values, logs, context):
    count, width = query.shape
    keys[...] = turned(key_pre, cosine, sine).astype(bf16)
    values[...] = value_pre.astype(bf16)
    lane = lax.broadcasted_iota(jnp.int32, (count, LANES), 1)
    kept = jnp.zeros((count, LANES), f32)
    for h in range(width // AHDIM):
        lanes = slice(h * AHDIM, (h + 1) * AHDIM)
        query[:, lanes] = turned(query_pre[:, lanes], cosine, sine).astype(bf16)
        found = []
        for i in range(count // BLOCK):
            lo, hi = i * BLOCK, (i + 1) * BLOCK
            scores, valid = scores_of(query[:, lanes], keys[...], lo, hi, length)
            masked = jnp.where(valid, scores, -1e30)
            peak = jnp.max(masked, axis=1, keepdims=True)
            expo = jnp.exp(masked - peak)
            total = jnp.sum(expo, axis=1, keepdims=True)
            found.append(peak + jnp.log(total))
            probs = (expo / total).astype(bf16)
            context[lo:hi, lanes] = plain_dot(probs, values[:hi, :]).astype(bf16)
        kept = jnp.where(lane == h, jnp.concatenate(found, axis=0), kept)
    logs[...] = kept


def attention_backward(d_context, query, keys, values, logs, cosine, sine, length, d_query_pre, d_keys, d_values):
    count, width = query.shape
    lane = lax.broadcasted_iota(jnp.int32, (count, LANES), 1)
    scale = AHDIM ** (-0.5)
    key_total = jnp.zeros((count, AHDIM), f32)
    value_total = jnp.zeros((count, AHDIM), f32)
    for h in range(width // AHDIM):
        lanes = slice(h * AHDIM, (h + 1) * AHDIM)
        log = column_of(logs[...], lane, h)
        pieces = []
        for i in range(count // BLOCK):
            lo, hi = i * BLOCK, (i + 1) * BLOCK
            scores, valid = scores_of(query[:, lanes], keys[...], lo, hi, length)
            probs = jnp.where(valid, jnp.exp(scores - log[lo:hi]), 0.0)
            grads = d_context[lo:hi, lanes]
            d_probs = right_trans(grads, values[:hi, :])
            delta = jnp.sum(probs * d_probs, axis=1, keepdims=True)
            d_scores = (probs * (d_probs - delta)).astype(bf16)
            pieces.append(plain_dot(d_scores, keys[:hi, :]) * scale)
            d_key = left_trans(d_scores, query[lo:hi, lanes]) * scale
            d_value = left_trans(probs.astype(bf16), grads)
            if hi < count:
                rest = jnp.zeros((count - hi, AHDIM), f32)
                d_key = jnp.concatenate([d_key, rest], axis=0)
                d_value = jnp.concatenate([d_value, rest], axis=0)
            key_total = key_total + d_key
            value_total = value_total + d_value
        d_query_pre[:, lanes] = turned(jnp.concatenate(pieces, axis=0), cosine, -sine).astype(bf16)
    d_keys[...] = turned(key_total, cosine, -sine)
    d_values[...] = value_total


def columns_of(channels, heads_width):
    places, start = {}, 0
    for name, size in (
        ("zgate", channels), ("query", heads_width), ("xpre", channels), ("state", 2 * STATE),
        ("key", AHDIM), ("value", AHDIM), ("step", LANES),
    ):
        places[name] = slice(start, start + size)
        start += size
    return places, start


def forward_kernel(
    lengths, zgate, query_pre, xpre, statepre, key_pre, value_pre, steppre, cosine, sine, conv_weight, conv_bias, state_taps, state_bias, step_bias, rates,
    skip_rep, gated, ssd, square, xconv, sconv, stepsize, cumul, inner, query, keys, values, logs,
    context, cumul_rows, *, slot,
):
    attention_forward(
        query_pre, key_pre[...], value_pre[...],
        cosine[...], sine[...], lengths[slot], query, keys, values, logs, context,
    )
    count, channels = xpre.shape
    xlin = tap_sum(xpre[...], conv_weight[...], conv_bias[...])
    xconv[...] = (xlin * jax.nn.sigmoid(xlin)).astype(bf16)
    slin = tap_sum(statepre[...], state_taps[...], state_bias[...])
    sconv[...] = (slin * jax.nn.sigmoid(slin)).astype(bf16)
    inner[...] = right_trans(sconv[:, STATE:], sconv[:, :STATE])
    step = jax.nn.softplus(steppre[...] + step_bias[...])
    stepsize[...] = step
    row = lax.broadcasted_iota(jnp.int32, (count, count), 0)
    col = lax.broadcasted_iota(jnp.int32, (count, count), 1)
    total = exact_dot(jnp.where(row >= col, 1.0, 0.0), -step * rates[...])
    cumul[...] = total
    cumul_rows[...] = total.T
    square[...] = jnp.zeros_like(square)

    def pair(p):
        lanes = slice(p * LANES, (p + 1) * LANES)
        lane = lax.broadcasted_iota(jnp.int32, (count, LANES), 1)
        xvals = xconv[:, lanes].astype(f32)
        low_half = lane < MHDIM
        step_rep = jnp.where(
            low_half, column_of(stepsize[...], lane, 2 * p), column_of(stepsize[...], lane, 2 * p + 1)
        )
        weighted = (step_rep * xvals).astype(bf16)
        columns = [column_of(cumul[...], lane, 2 * p + h) for h in range(2)]
        for i in range(count // BLOCK):
            lo, hi = i * BLOCK, (i + 1) * BLOCK
            results = []
            for h in range(2):
                differ = columns[h][lo:hi] - cumul_rows[2 * p + h : 2 * p + h + 1, :hi]
                t = lax.broadcasted_iota(jnp.int32, (BLOCK, hi), 0) + lo
                s = lax.broadcasted_iota(jnp.int32, (BLOCK, hi), 1)
                decay = jnp.exp(jnp.where(t >= s, differ, -1e30))
                mixing = (inner[lo:hi, :hi] * decay).astype(bf16)
                results.append(plain_dot(mixing, weighted[:hi]))
            half = jnp.where(low_half[lo:hi], results[0], results[1])
            half = half + skip_rep[:, lanes] * xvals[lo:hi]
            ssd[lo:hi, lanes] = half
            z = zgate[lo:hi, lanes]
            value = half * (z * jax.nn.sigmoid(z))
            gated[lo:hi, lanes] = value
            square[lo:hi, :] += value * value

    for p in range(channels // LANES):
        pair(p)


def full(*shape):
    return jax.ShapeDtypeStruct(shape, f32)


def low(*shape):
    return jax.ShapeDtypeStruct(shape, bf16)


def in_vmem(count):
    return [pl.BlockSpec(memory_space=pltpu.VMEM)] * count


def whole_blocks(shapes):
    return [pl.BlockSpec(s.shape, lambda i, n=len(s.shape): (0,) * n) for s in shapes]


def mixers_forward(slot, lengths, *operands):
    count, channels = operands[0].shape
    heads_width = operands[1].shape[1]
    shapes = (
        full(count, channels), full(count, channels), full(count, LANES), low(count, channels),
        low(count, 2 * STATE), full(count, LANES), full(count, LANES), full(count, count),
        low(count, heads_width), low(count, AHDIM), low(count, AHDIM), full(count, LANES),
        low(count, heads_width),
    )
    return pl.pallas_call(
        functools.partial(forward_kernel, slot=slot),
        grid=(1,),
        out_shape=shapes,
        in_specs=[pl.BlockSpec(memory_space=pltpu.SMEM)] + in_vmem(len(operands)),
        out_specs=tuple(whole_blocks(shapes)),
        scratch_shapes=[pltpu.VMEM((LANES, count), f32)],
        compiler_params=pltpu.CompilerParams(vmem_limit_bytes=48 * 2**20),
        cost_estimate=pl.CostEstimate(
            flops=10**6, bytes_accessed=10**6, transcendentals=10**3
        ),
    )(lengths, *operands)


def backward_kernel(
    lengths, d_scaled_in, d_context_in, gated_in, inv_cross, gain, zgate, xpre, statepre, steppre,
    ssd, xconv, sconv, stepsize, cumul, inner,
    query, keys, values, logs, cosine, sine, conv_weight, conv_bias, state_taps, state_bias,
    step_bias, rates, skip_rep,
    back, d_statepre, d_keys, d_values, g_conv, g_state, g_heads, g_skip, g_gain,
    d_ssd, d_xvals, cumul_rows, d_inner, row_sums, col_sums, d_step, *, slot, places,
):
    count, channels = ssd.shape
    attention_backward(
        d_context_in[...].astype(bf16), query, keys, values, logs, cosine[...], sine[...],
        lengths[slot], back.at[:, places["query"]], d_keys, d_values,
    )
    back[:, places["key"]] = d_keys[...].astype(bf16)
    back[:, places["value"]] = d_values[...].astype(bf16)
    d_zgate, d_xpre = back.at[:, places["zgate"]], back.at[:, places["xpre"]]
    d_steppre = back.at[:, places["step"]]
    d_scaled = d_scaled_in[...]
    g_gain[...] = jnp.sum(d_scaled * gated_in[...] * inv_cross[:, 0:1], axis=0, keepdims=True)
    inv = inv_cross[:, 0:1]
    cross = inv_cross[:, 1:2]
    d_gated = inv * (d_scaled * gain[...]) - gated_in[...] * cross
    z = zgate[...]
    sig = jax.nn.sigmoid(z)
    d_low = (d_gated * (z * sig)).astype(bf16)
    d_ssd[...] = d_low
    d_zgate[...] = (d_gated * ssd[...] * sig * (1.0 + z * (1.0 - sig))).astype(bf16)
    g_skip[...] = jnp.sum(d_low.astype(f32) * xconv[...].astype(f32), axis=0, keepdims=True)
    cumul_rows[...] = cumul[...].T
    d_inner[...] = jnp.zeros_like(d_inner)
    row_sums[...] = jnp.zeros_like(row_sums)
    col_sums[...] = jnp.zeros_like(col_sums)
    d_step[...] = jnp.zeros_like(d_step)

    def pair(p):
        lanes = slice(p * LANES, (p + 1) * LANES)
        lane = lax.broadcasted_iota(jnp.int32, (count, LANES), 1)
        low_half = lane < MHDIM
        xvals = xconv[:, lanes].astype(f32)
        step_rep = jnp.where(
            low_half, column_of(stepsize[...], lane, 2 * p), column_of(stepsize[...], lane, 2 * p + 1)
        )
        weighted = (step_rep * xvals).astype(bf16)
        grads = d_ssd[:, lanes]
        columns = [column_of(cumul[...], lane, 2 * p + h) for h in range(2)]
        pieces = []
        for h in range(2):
            only = jnp.where(low_half == (h == 0), grads, jnp.zeros_like(grads))
            back_part = jnp.zeros((count, LANES), f32)
            sums = []
            col_total = jnp.zeros((1, count), f32)
            for i in range(count // BLOCK):
                lo, hi = i * BLOCK, (i + 1) * BLOCK
                differ = columns[h][lo:hi] - cumul_rows[2 * p + h : 2 * p + h + 1, :hi]
                t = lax.broadcasted_iota(jnp.int32, (BLOCK, hi), 0) + lo
                s = lax.broadcasted_iota(jnp.int32, (BLOCK, hi), 1)
                decay = jnp.exp(jnp.where(t >= s, differ, -1e30))
                mixing = inner[lo:hi, :hi] * decay
                part = left_trans(mixing.astype(bf16), only[lo:hi])
                d_mixing = right_trans(only[lo:hi], weighted[:hi])
                d_inner[lo:hi, :hi] += d_mixing * decay
                flow = d_mixing * mixing
                sums.append(jnp.sum(flow, axis=1, keepdims=True))
                down = jnp.sum(flow, axis=0, keepdims=True)
                if hi < count:
                    part = jnp.concatenate([part, jnp.zeros((count - hi, LANES), f32)], axis=0)
                    down = jnp.concatenate([down, jnp.zeros((1, count - hi), f32)], axis=1)
                back_part = back_part + part
                col_total = col_total + down
            here = lane == 2 * p + h
            row_sums[...] = jnp.where(here, jnp.concatenate(sums, axis=0), row_sums[...])
            col_sums[2 * p + h : 2 * p + h + 1, :] = col_total
            pieces.append(back_part)
        d_weighted = pieces[0] + pieces[1]
        d_xvals[:, lanes] = grads.astype(f32) * skip_rep[:, lanes] + d_weighted * step_rep
        product = d_weighted * xvals
        for h in range(2):
            value = jnp.sum(
                jnp.where(low_half == (h == 0), product, 0.0), axis=1, keepdims=True
            )
            d_step[...] = jnp.where(lane == 2 * p + h, value, d_step[...])

    for p in range(channels // LANES):
        pair(p)

    d_cumul = row_sums[...] - col_sums[...].T
    row = lax.broadcasted_iota(jnp.int32, (count, count), 0)
    col = lax.broadcasted_iota(jnp.int32, (count, count), 1)
    d_logdecay = exact_dot(jnp.where(row <= col, 1.0, 0.0), d_cumul)
    rate = rates[...]
    d_full = (d_step[...] - d_logdecay * rate) * jax.nn.sigmoid(steppre[...] + step_bias[...])
    d_steppre[...] = d_full.astype(bf16)
    g_heads[0:1, :] = jnp.sum(d_full, axis=0, keepdims=True)
    g_heads[1:2, :] = jnp.sum(-d_logdecay * stepsize[...] * rate, axis=0, keepdims=True)

    d_in = d_inner[...].astype(bf16)
    d_c = plain_dot(d_in, sconv[:, :STATE])
    d_b = left_trans(d_in, sconv[:, STATE:])
    slin = tap_sum(statepre[...], state_taps[...], state_bias[...])
    d_slin = jnp.concatenate([d_b, d_c], axis=1) * silu_slope(slin)
    back_state, tap_grads = tap_back(d_slin, statepre[...], state_taps[...])
    d_statepre[...] = back_state
    back[:, places["state"]] = back_state.astype(bf16)
    g_state[...] = jnp.concatenate([tap_grads, jnp.sum(d_slin, axis=0, keepdims=True)], axis=0)
    xlin = tap_sum(xpre[...], conv_weight[...], conv_bias[...])
    d_xlin = d_xvals[...] * silu_slope(xlin)
    back_x, tap_grads = tap_back(d_xlin, xpre[...], conv_weight[...])
    d_xpre[...] = back_x.astype(bf16)
    g_conv[...] = jnp.concatenate([tap_grads, jnp.sum(d_xlin, axis=0, keepdims=True)], axis=0)


def mixers_backward(slot, slots, held, lengths, *operands):
    count, channels = operands[0].shape
    heads_width = operands[1].shape[1]
    taps = operands[-7].shape[0]
    width = columns_of(channels, heads_width)[1]
    kernel = functools.partial(
        backward_kernel, slot=slot, places=columns_of(channels, heads_width)[0]
    )
    aliases = {}
    extra_specs, extra = [], ()
    if held is not None:
        aliases = {0: 0}
        extra_specs, extra = [pl.BlockSpec(memory_space=pl.ANY)], (held,)
        inside = kernel
        kernel = lambda _, *refs: inside(*refs)
    shapes = (
        full(count, 2 * STATE), full(count, AHDIM), full(count, AHDIM), full(taps + 1, channels),
        full(taps + 1, 2 * STATE), full(2, LANES), full(1, channels), full(1, channels),
    )
    return pl.pallas_call(
        kernel,
        grid=(1,),
        out_shape=(low(slots * count, width),) + shapes,
        in_specs=extra_specs
        + [pl.BlockSpec(memory_space=pltpu.SMEM)]
        + in_vmem(len(operands)),
        out_specs=tuple(
            [pl.BlockSpec((count, width), lambda i: (slot, 0))] + whole_blocks(shapes)
        ),
        scratch_shapes=[
            pltpu.VMEM((count, channels), bf16),
            pltpu.VMEM((count, channels), f32),
            pltpu.VMEM((LANES, count), f32),
            pltpu.VMEM((count, count), f32),
            pltpu.VMEM((count, LANES), f32),
            pltpu.VMEM((LANES, count), f32),
            pltpu.VMEM((count, LANES), f32),
        ],
        input_output_aliases=aliases,
        compiler_params=pltpu.CompilerParams(vmem_limit_bytes=56 * 2**20),
        cost_estimate=pl.CostEstimate(
            flops=10**6, bytes_accessed=10**6, transcendentals=10**3
        ),
    )(*extra, lengths, *operands)


def feed_forward_kernel(normed, cot, gate_weight, up_weight, down_weight, *refs):
    inner, d_gate, d_up, back = refs[-4:]
    gate = plain_dot(normed[...], gate_weight[...])
    upper = plain_dot(normed[...], up_weight[...])
    d_inner = right_trans(cot[...], down_weight[...])
    sig = jax.nn.sigmoid(gate)
    silu = gate * sig
    inner[...] = (silu * upper).astype(bf16)
    d_gate[...] = (d_inner * upper * sig * (1.0 + gate * (1.0 - sig))).astype(bf16)
    d_up[...] = (d_inner * silu).astype(bf16)
    part = right_trans(d_gate[...], gate_weight[...]) + right_trans(d_up[...], up_weight[...])

    @pl.when(pl.program_id(0) == 0)
    def _():
        back[...] = part

    @pl.when(pl.program_id(0) > 0)
    def _():
        back[...] += part


def feed_forward_all(slot, slots, held, normed, cot, gate_weight, up_weight, down_weight):
    count, width = normed.shape
    hidden = gate_weight.shape[1]
    block = min(256, hidden)
    rows = pl.BlockSpec((count, width), lambda j: (0, 0))
    columns = pl.BlockSpec((width, block), lambda j: (0, j))
    joint = pl.BlockSpec((count, block), lambda j: (slot, j))
    extra = () if held is None else tuple(held)
    return pl.pallas_call(
        feed_forward_kernel,
        grid=(hidden // block,),
        out_shape=tuple([low(slots * count, hidden)] * 3 + [full(count, width)]),
        in_specs=[
            rows, rows, columns, columns, pl.BlockSpec((block, width), lambda j: (j, 0))
        ] + [pl.BlockSpec(memory_space=pl.ANY)] * len(extra),
        out_specs=(joint, joint, joint, rows),
        input_output_aliases={5 + n: n for n in range(len(extra))},
        compiler_params=pltpu.CompilerParams(vmem_limit_bytes=44 * 2**20),
        cost_estimate=pl.CostEstimate(flops=10**6, bytes_accessed=10**6, transcendentals=10**3),
    )(normed, cot, gate_weight, up_weight, down_weight, *extra)


def swap(values, axis, size, bit):
    return lax.ppermute(values, axis, [(i, i ^ bit) for i in range(size)])


def halving_order(members, bit, limit):
    if bit >= limit:
        return members
    low = halving_order([m for m in members if not m & bit], bit * 2, limit)
    high = halving_order([m for m in members if m & bit], bit * 2, limit)
    return low + high


class Order:
    def __init__(self):
        self.last = ()
        self.queue = []

    def point(self, value, skip=0):
        if len(self.queue) <= skip:
            return value
        return lax.optimization_barrier((value, self.queue.pop(skip)))[0]

    def gate(self, *values):
        return lax.optimization_barrier((values, self.last))[0]

    def mark(self, *values):
        self.last = values


def scatter_all(size, t_size, parts, halves, rests, gain, vector, shared_rows):
    rows = parts[0].shape[0]
    works = len(parts)
    share = rows // size
    chunk = min(256, rows // 4)
    levels = size.bit_length() - 1
    spans = []
    for level in range(1, levels):
        lo, hi = rows >> (level + 1), rows >> level
        step = min(chunk, hi - lo)
        spans += [(level, start, step) for start in range(hi - step, lo - 1, -step)]
    spans.append((levels, 0, share))
    pieces = [(w,) + span for w in range(works) for span in spans]
    per_work = len(spans)
    widths = [p.shape[1] for p in parts]
    wide = max(widths)
    extra = len(halves)
    half_shape = halves[0].shape
    half, width = half_shape
    slots = 1 + max(rest[0] for rest in rests)
    extras = [value for rest in rests for value in rest[1:]]
    wholes = [n for n, rest in enumerate(rests) if len(rest) == 2]

    def kernel(*refs):
        held_in, refs = refs[:works], refs[works:]
        own, refs = refs[:extra], refs[extra:]
        beside = []
        for rest in rests:
            beside.append(refs[: len(rest) - 1])
            refs = refs[len(rest) - 1 :]
        gain_ref, small, refs = refs[0], refs[1], refs[2:]
        outs, refs = refs[:works], refs[works:]
        far, refs = refs[:extra], refs[extra:]
        result, grad, small_out, wide_out, refs = refs[0], refs[1], refs[2], refs[3], refs[4:]
        loads, pair_loads, totals, low_rows, theirs, refs = (
            refs[0], refs[1], refs[2], refs[3], refs[4], refs[5:]
        )
        boxes, wide_boxes, refs = refs[0], refs[1], refs[2:]
        landed, refs = refs[:works], refs[works:]
        later, refs = refs[: works * (levels - 1)], refs[works * (levels - 1) :]
        load_sems, out_sems, x_send, x_recv, z_send, z_recv, y_sems, c_sems, pair_sems, v_sems, w_sems = refs
        me = lax.axis_index("dp")
        spot = lax.axis_index("tensor")

        def neighbour(bit):
            return spot + bit - 2 * bit * lax.rem(spot // bit, 2)


        def partner(level):
            bit = 1 << level
            return me + bit - 2 * bit * lax.rem(me // bit, 2)

        barrier = pltpu.get_barrier_semaphore()
        for other in range(1, size):
            pl.semaphore_signal(
                barrier, inc=1, device_id={"dp": lax.rem(me + other, size)}, device_id_type=MESH
            )
        for other in range(1, t_size):
            pl.semaphore_signal(
                barrier, inc=1, device_id={"tensor": lax.rem(spot + other, t_size)},
                device_id_type=MESH,
            )
        pl.semaphore_wait(barrier, size + t_size - 2)

        def small_copy(other):
            return pltpu.make_async_remote_copy(
                src_ref=small, dst_ref=boxes.at[size - other], send_sem=v_sems.at[0, other],
                recv_sem=v_sems.at[1, size - other],
                device_id={"dp": lax.rem(me + other, size)}, device_id_type=MESH,
            )

        def wide_copy(other):
            return pltpu.make_async_remote_copy(
                src_ref=small_out.at[pl.ds(0, shared_rows), :], dst_ref=wide_boxes.at[t_size - other],
                send_sem=w_sems.at[0, other], recv_sem=w_sems.at[1, t_size - other],
                device_id={"tensor": lax.rem(spot + other, t_size)}, device_id_type=MESH,
            )

        def in_turn(kept, count, place, rows):
            total = jnp.zeros((rows, LANES), f32)
            for number in range(count):
                offset = lax.rem(number - place + count, count)
                total = total + kept[offset]
            return total

        def small_sums(stage):
            if stage == 0:
                boxes[0] = small[...]
                for other in range(1, size):
                    small_copy(other).wait_recv()
                small_out[...] = in_turn(boxes, size, me, small.shape[0])
                for other in range(1, t_size):
                    wide_copy(other).start()
            else:
                wide_boxes[0] = small_out[:shared_rows, :]
                for other in range(1, t_size):
                    wide_copy(other).wait_recv()
                wide_out[...] = in_turn(wide_boxes, t_size, spot, shared_rows)


        def y_copy(e):
            return pltpu.make_async_remote_copy(
                src_ref=own[e], dst_ref=far[e], send_sem=y_sems.at[0, e], recv_sem=y_sems.at[1, e],
                device_id={"tensor": neighbour(2)}, device_id_type=MESH,
            )

        core = lax.rem(spot, 2)

        def rows_of(place):
            return pl.ds(pl.multiple_of(place * half, 8), half)

        def c_copy(e):
            slot = rests[e][0]
            if e in wholes:
                target = theirs.at[wholes.index(e)]
            else:
                target = grad.at[slot, rows_of(core), :]
            return pltpu.make_async_remote_copy(
                src_ref=totals.at[e], dst_ref=target, send_sem=c_sems.at[0, e],
                recv_sem=c_sems.at[1, e], device_id={"tensor": neighbour(1)}, device_id_type=MESH,
            )

        def fetch(source, place):
            return pltpu.make_async_copy(source, pair_loads.at[place], pair_sems.at[0, place])

        def keep(e, place):
            slot = rests[e][0]
            if e in wholes:
                n = 2 * wholes.index(e) + place
                target = result.at[slot, rows_of(core if place == 0 else 1 - core), :]
                return pltpu.make_async_copy(low_rows.at[n], target, pair_sems.at[1 + place, e])
            return pltpu.make_async_copy(
                totals.at[e], grad.at[slot, rows_of(core), :], pair_sems.at[1, e]
            )

        def exchange(e):
            y_copy(e).wait_recv()
            sources = [own[e], far[e]]
            if e in wholes:
                sources.append(beside[e][0].at[pl.ds(0, half), :])
            else:
                sources += [beside[e][0], beside[e][1]]
            for place, source in enumerate(sources):
                fetch(source, place).start()
            for place, source in enumerate(sources):
                fetch(source, place).wait()
            total = pair_loads[0] + pair_loads[1]
            if e in wholes:
                totals[e] = total
                low_rows[2 * wholes.index(e)] = (pair_loads[2] + total).astype(bf16)
            else:
                unit = pair_loads[3]
                scaled = total * gain_ref[...]
                mean = jnp.sum(scaled * unit, axis=1, keepdims=True) / width
                totals[e] = pair_loads[2] + beside[e][2][...] * (scaled - unit * mean)
            c_copy(e).start()
            keep(e, 0).start()

        def complete(e):
            fetch(beside[e][0].at[pl.ds(half, half), :], 0).start()
            c_copy(e).wait_recv()
            fetch(beside[e][0].at[pl.ds(half, half), :], 0).wait()
            n = wholes.index(e)
            low_rows[2 * n + 1] = (pair_loads[0] + theirs[n]).astype(bf16)
            keep(e, 1).start()

        def first_copy(number):
            w, _, start, step = pieces[number]
            return pltpu.make_async_remote_copy(
                src_ref=held_in[w].at[pl.ds(rows // 2 + start, step), :],
                dst_ref=landed[w].at[pl.ds(start, step), :],
                send_sem=x_send.at[number],
                recv_sem=x_recv.at[number],
                device_id={"dp": partner(0)},
                device_id_type=MESH,
            )

        def load(number):
            w, _, start, step = pieces[number]
            return pltpu.make_async_copy(
                held_in[w].at[pl.ds(start, step), :],
                loads.at[number % 2, pl.ds(0, step), pl.ds(0, widths[w])],
                load_sems.at[number % 2],
            )

        def later_copy(number):
            w, level, start, step = pieces[number]
            return pltpu.make_async_remote_copy(
                src_ref=landed[w].at[pl.ds(start, step), :],
                dst_ref=later[w * (levels - 1) + level - 1].at[pl.ds(start - (rows >> (level + 1)), step), :],
                send_sem=z_send.at[number],
                recv_sem=z_recv.at[number],
                device_id={"dp": partner(level)},
                device_id_type=MESH,
            )

        def store(w):
            return pltpu.make_async_copy(
                landed[w].at[pl.ds(0, share), :], outs[w], out_sems.at[w]
            )

        for other in range(1, size):
            small_copy(other).start()
        for e in range(extra):
            y_copy(e).start()
        for number in range(len(pieces)):
            first_copy(number).start()
        load(0).start()
        arrived = set()

        def need(w, level, start, step):
            base = rows >> (level + 1)
            for other in range(w * per_work, (w + 1) * per_work):
                _, its_level, its_start, its_step = pieces[other]
                if its_level != level or other in arrived:
                    continue
                if its_start - base < start + step and start < its_start - base + its_step:
                    later_copy(other).wait_recv()
                    arrived.add(other)

        def finish(w):
            level = levels - 1
            need(w, level, 0, share)
            landed[w][:share, :] += later[w * (levels - 1) + level - 1][:share, :]
            store(w).start()

        for number, (w, level, start, step) in enumerate(pieces):
            load(number).wait()
            if number + 1 < len(pieces):
                load(number + 1).start()
            first_copy(number).wait_recv()
            value = loads[number % 2, :step, : widths[w]] + landed[w][start : start + step, :]
            for before in range(1, min(level, levels - 1)):
                need(w, before, start, step)
                value = value + later[w * (levels - 1) + before - 1][start : start + step, :]
            landed[w][start : start + step, :] = value
            if level < levels:
                later_copy(number).start()
            if w and number == w * per_work + min(2, per_work - 1):
                finish(w - 1)
            if number in (0, 2):
                small_sums(number // 2)
            if number % 2 and number // 2 < extra:
                exchange(number // 2)
            if number % 2 == 0 and number // 2 - 2 in wholes:
                complete(number // 2 - 2)
        for e in range(len(pieces) // 2, extra):
            exchange(e)
        for e in wholes:
            if 2 * (e + 2) >= len(pieces):
                complete(e)
        finish(works - 1)
        for other in range(1, size):
            small_copy(other).wait_send()
        for other in range(1, t_size):
            wide_copy(other).wait_send()
        for e in range(extra):
            y_copy(e).wait_send()
            c_copy(e).wait_send()
            keep(e, 0).wait()
            if e in wholes:
                keep(e, 1).wait()
            else:
                c_copy(e).wait_recv()
        for number, (w, level, start, step) in enumerate(pieces):
            first_copy(number).wait_send()
            if level < levels:
                later_copy(number).wait_send()
        for w in range(works):
            store(w).wait()

    scratch = [
        pltpu.VMEM((2, chunk, wide), f32),
        pltpu.VMEM((4,) + half_shape, f32),
        pltpu.VMEM((extra,) + half_shape, f32),
        pltpu.VMEM((2 * len(wholes),) + half_shape, bf16),
        pltpu.VMEM((len(wholes),) + half_shape, f32),
        pltpu.VMEM((size,) + vector.shape, f32),
        pltpu.VMEM((t_size, shared_rows, LANES), f32),
    ]
    scratch += [pltpu.VMEM((rows // 2, n), f32) for n in widths]
    scratch += [
        pltpu.VMEM((rows >> (level + 1), n), f32) for n in widths for level in range(1, levels)
    ]
    scratch += [
        pltpu.SemaphoreType.DMA((2,)),
        pltpu.SemaphoreType.DMA((works,)),
    ] + [pltpu.SemaphoreType.DMA((len(pieces),))] * 4
    scratch += [pltpu.SemaphoreType.DMA((n, extra)) for n in (2, 2)]
    scratch += [pltpu.SemaphoreType.DMA((3, max(4, extra)))]
    scratch += [pltpu.SemaphoreType.DMA((2, size)), pltpu.SemaphoreType.DMA((2, t_size))]
    results = pl.pallas_call(
        kernel,
        out_shape=tuple(
            [full(share, n) for n in widths]
            + [full(*half_shape)] * extra
            + [low(slots, 2 * half, width), full(slots, 2 * half, width)]
            + [full(*vector.shape), full(shared_rows, LANES)]
        ),
        in_specs=[pl.BlockSpec(memory_space=pl.ANY)] * (works + extra)
        + [
            pl.BlockSpec(memory_space=pltpu.VMEM if value.shape[1] == 1 else pl.ANY)
            for value in extras
        ]
        + in_vmem(2),
        out_specs=tuple([pl.BlockSpec(memory_space=pl.ANY)] * (works + extra + 2) + in_vmem(2)),
        scratch_shapes=scratch,
        compiler_params=pltpu.CompilerParams(
            collective_id=0, has_side_effects=True, vmem_limit_bytes=60 * 2**20
        ),
        cost_estimate=pl.CostEstimate(
            flops=10**6, bytes_accessed=10**6, transcendentals=0
        ),
    )(*parts, *halves, *extras, gain, vector)
    return results[:works], *results[works + extra :]


def make_per_device(dp_size, t_size):
    def per_device(
        tokens,
        lengths,
        out_grad,
        input_gain,
        mamba_gate_weight,
        mamba_in_weight,
        state_weight,
        step_weight,
        conv_weight,
        conv_bias,
        conv_state_weight,
        conv_state_bias,
        step_bias,
        decay_log,
        skip_scale,
        mamba_gain,
        mamba_out_weight,
        query_weight,
        key_value_weight,
        attn_out_weight,
        ffn_gain,
        gate_weight,
        up_weight,
        down_weight,
    ):
        micro = tokens.shape[0]
        count = tokens.shape[1]
        width = tokens.shape[2]
        half = count // 2
        local_heads = step_weight.shape[1]
        q_local = query_weight.shape[1] // AHDIM
        kv_width = key_value_weight.shape[1] // 2
        group_size = AHEADS // KVHEADS
        me_dp = lax.axis_index("dp")
        me_t = lax.axis_index("tensor")
        core = lax.rem(me_t, 2)
        kv_head = me_t * q_local // group_size
        key_weight = lax.dynamic_slice_in_dim(key_value_weight, kv_head * AHDIM, AHDIM, 1)
        value_weight = lax.dynamic_slice_in_dim(
            key_value_weight, kv_width + kv_head * AHDIM, AHDIM, 1
        )
        rows = jnp.arange(count)
        freqs = rope_base ** (-(jnp.arange(AHDIM // 2).astype(f32) * 2.0) / AHDIM)
        angles = rows.astype(f32)[:, None] * freqs[None, :]
        cosine, sine = jnp.cos(angles), jnp.sin(angles)
        cosine = jnp.concatenate([cosine, cosine], axis=1)
        sine = jnp.concatenate([-sine, sine], axis=1)
        channels = mamba_in_weight.shape[1]
        heads_width = query_weight.shape[1]
        places, _ = columns_of(channels, heads_width)
        pad_step = LANES - local_heads

        def lane_row(vector):
            return jnp.pad(vector, (0, pad_step))[None]

        mixer_rows = (
            conv_weight, conv_bias[None], conv_state_weight, conv_state_bias[None],
            lane_row(step_bias), lane_row(jnp.exp(decay_log)), jnp.repeat(skip_scale, MHDIM)[None],
        )
        step_lanes = jnp.pad(step_weight, ((0, 0), (0, pad_step)))
        in_weights = (
            mamba_gate_weight, query_weight, mamba_in_weight, state_weight, key_weight,
            value_weight, step_lanes,
        )

        def t_swap(values, bit):
            return swap(values, "tensor", t_size, bit)

        def t_total(values):
            bit = 1
            while bit < t_size:
                values = values + t_swap(values, bit)
                bit *= 2
            return values

        def mine(values):
            return lax.dynamic_slice_in_dim(values, core * half, half, 0)

        def other(values):
            return lax.dynamic_slice_in_dim(values, (1 - core) * half, half, 0)

        def halves(values):
            values = lax.optimization_barrier(values)
            return mine(values), other(values)

        def relative(values):
            return jnp.concatenate([mine(values), other(values)], axis=0)

        def in_order(own, far):
            return jnp.where(
                core == 0,
                jnp.concatenate([own, far], axis=0),
                jnp.concatenate([far, own], axis=0),
            )

        def half_sum(own, far, pieces):
            own = own + t_swap(far, 1)
            bit = 2
            while bit < t_size // 2:
                own = own + t_swap(own, bit)
                bit *= 2
            step = -(-own.shape[0] // (8 * pieces)) * 8
            parts = []
            for start in range(0, own.shape[0], step):
                parts.append(t_swap(own[start : start + step], bit))
            order.queue += parts
            return own, parts

        def add_up(own, parts):
            for part in parts:
                order.queue = [p for p in order.queue if p is not part]
            own, *parts = order.gate(own, *parts)
            return own + jnp.concatenate(parts, axis=0)

        block = width // dp_size

        order = Order()

        def forward(index, slot):
            inputs = slot.astype(f32)
            inv_one = lax.rsqrt(jnp.mean(inputs * inputs, axis=-1, keepdims=True) + epsilon)
            unit_one = inputs * inv_one
            normed = (unit_one * input_gain).astype(bf16)
            pre = [plain_dot(normed, w) for w in in_weights]
            pre[2] = order.point(pre[2])
            pre[0] = order.point(pre[0])
            gated, ssd, square, *kept, query, keys, values, logs, context = mixers_forward(
                index, lengths, *pre, cosine, sine, *mixer_rows
            )
            gated = order.point(gated)
            total_square = t_total(jnp.sum(square, axis=-1))
            inv_mamba = lax.rsqrt(total_square / DSSM + epsilon)[:, None]
            scaled = (gated * inv_mamba * mamba_gain).astype(bf16)
            mixer = jnp.concatenate([scaled, context], axis=1)
            mixed_own, mixed_far = half_sum(
                *halves(plain_dot(scaled, mamba_out_weight) + plain_dot(context, attn_out_weight)),
                3,
            )
            order.mark(mixed_own)
            return dict(
                mixed_own=mixed_own, mixed_far=mixed_far, inputs=inputs, inv_one=inv_one,
                unit_one=unit_one, normed=normed, pre=pre, gated=gated, ssd=ssd, kept=kept,
                attention=(query, keys, values, logs), inv_mamba=inv_mamba, mixer=mixer,
            )

        def feed_forward(index, k, held):
            hidden_own = mine(k["inputs"]) + add_up(k["mixed_own"], k["mixed_far"])
            hidden = jnp.concatenate([hidden_own, t_swap(hidden_own, 1)], axis=0)
            inv_two = lax.rsqrt(jnp.mean(hidden * hidden, axis=-1, keepdims=True) + epsilon)
            unit_two = hidden * inv_two
            normed_two = (unit_two * ffn_gain).astype(bf16)
            valid = (rows < lengths[index]).astype(f32)[:, None]
            cotangent = relative(out_grad[index].astype(f32) * valid)
            cot_low = cotangent.astype(bf16)
            *held, back = feed_forward_all(
                index, micro, held, normed_two, cot_low, gate_weight, up_weight, down_weight
            )
            back = order.point(order.point(back))
            back_own, back_far = half_sum(back[:half], back[half:], 3)
            order.mark(back_own)
            k.update(
                back_own=back_own, back_far=back_far,
                hidden=hidden, inv_two=inv_two[:half], unit_two=unit_two[:half],
                normed_two=normed_two, cotangent=cotangent, cot_low=cot_low,
            )
            return held

        def output_sum(index, k):
            (inner_ffn,) = order.gate(
                lax.slice_in_dim(inner_all, index * count, (index + 1) * count, axis=0)
            )
            ffn = plain_dot(inner_ffn, down_weight)
            k["ffn_own"] = ffn[:half] + t_swap(ffn[half:], 1)
            order.mark(k["ffn_own"])

        def back_head(k):
            unit_two = k["unit_two"]
            g_ffn_gain = jnp.sum(k["back_own"] * unit_two, axis=0)
            d_normed_two = add_up(k["back_own"], k["back_far"])
            d_unit_two = d_normed_two * ffn_gain
            d_rest = k["inv_two"] * (
                d_unit_two - unit_two * jnp.mean(d_unit_two * unit_two, axis=-1, keepdims=True)
            )
            d_both = k["cotangent"] + jnp.concatenate([d_rest, t_swap(d_rest, 1)], axis=0)
            d_mixed = in_order(d_both[:half], d_both[half:]).astype(bf16)
            d_scaled = right_trans(d_mixed, mamba_out_weight)
            d_context = right_trans(d_mixed, attn_out_weight)
            k["g_ffn_gain"] = g_ffn_gain
            k["d_hidden_own"] = d_both[:half]
            k["d_mixed"], k["d_scaled"], k["d_context"] = d_mixed, d_scaled, d_context
            k["cross"] = t_total(jnp.sum(d_scaled * mamba_gain * k["gated"], axis=-1))[:, None]
            order.mark(d_scaled, d_context)

        def back_mixers(index, k, held):
            d_scaled, cross = order.gate(k["d_scaled"], k["cross"])
            inv = k["inv_mamba"]
            inv_cross = jnp.concatenate([inv, inv**3 * cross / DSSM], axis=1)
            inv_cross = jnp.pad(inv_cross, ((0, 0), (0, LANES - 2)))
            back, d_statepre, d_keys, d_values, g_conv, g_state, g_heads, g_skip, g_gain = (
                mixers_backward(
                    index, micro, held, lengths, d_scaled, k["d_context"], k["gated"], inv_cross,
                    mamba_gain[None], k["pre"][0], k["pre"][2], k["pre"][3], k["pre"][6], k["ssd"],
                    *k["kept"], *k["attention"], cosine, sine, *mixer_rows,
                )
            )
            kv_far = jnp.where(core == 0, d_values, d_keys)
            kv_own = jnp.where(core == 0, d_keys, d_values)
            k["kv_sum"] = kv_own + t_swap(kv_far, 1)
            k["d_statepre"] = d_statepre
            k.update(
                g_conv_weight=g_conv[:-1], g_conv_bias=g_conv[-1],
                g_conv_state_weight=g_state[:-1], g_conv_state_bias=g_state[-1],
                g_step_bias=g_heads[0, :local_heads], g_decay_log=g_heads[1, :local_heads],
                g_skip=jnp.sum(g_skip.reshape(local_heads, MHDIM), axis=1),
                g_mamba_gain=g_gain[0],
            )
            order.mark(back)
            return back

        def back_inputs(index, k, back):
            back, d_statepre = order.gate(back, k["d_statepre"])
            piece = d_statepre.shape[1] // t_size
            parts = [
                lax.dynamic_slice_in_dim(d_statepre, jnp.bitwise_xor(me_t, q) * piece, piece, 1)
                for q in range(t_size)
            ]
            pieces = halving_order(list(range(0, t_size, 2)), 2, t_size)
            state_sum = jnp.concatenate([parts[q] for q in pieces], axis=1) + t_swap(
                jnp.concatenate([parts[q ^ 1] for q in pieces], axis=1), 1
            )
            bit = 2
            while bit < t_size:
                cut = state_sum.shape[1] // 2
                state_sum = state_sum[:, :cut] + t_swap(state_sum[:, cut:], bit)
                bit *= 2
            k["shared"] = jnp.concatenate([state_sum, k["kv_sum"]], axis=1).astype(bf16)
            rows_back = lax.slice_in_dim(back, index * count, (index + 1) * count, axis=0)
            norm_own, norm_other = halves(right_trans(rows_back, in_weight))
            k["norm_own"] = norm_own + t_swap(norm_other, 1)
            unit_own = mine(k["unit_one"])
            k["g_input_gain"] = jnp.sum(k["norm_own"] * unit_own, axis=0)
            order.mark(k["norm_own"])

        slots = []
        for index in range(micro):
            slot = tokens[index]
            if index:
                (slot,) = order.gate(slot)
            slots.append(forward(index, slot))
        held = None
        for index in range(micro):
            held = feed_forward(index, slots[index], held)
        inner_all, d_gate_all, d_up_all = held

        def joined(name):
            return jnp.concatenate([k[name] for k in slots], axis=0)

        def relative_columns(values):
            blocks = halving_order(list(range(dp_size)), 1, dp_size)
            return jnp.concatenate(
                [
                    lax.dynamic_slice_in_dim(values, jnp.bitwise_xor(me_dp, r) * block, block, 1)
                    for r in blocks
                ],
                axis=1,
            )

        def scattered(part, dimension):
            return lax.psum_scatter(part, "dp", scatter_dimension=dimension, tiled=True)

        (cot_all,) = order.gate(joined("cot_low"))
        part_down = left_trans(inner_all, cot_all)
        order.mark(part_down)
        g_down = scattered(part_down, 1)
        first, last = slots
        back_head(first)
        in_weight = jnp.concatenate(order.gate(*in_weights), axis=1)
        (two_all,) = order.gate(joined("normed_two"))
        part_gate = order.point(left_trans(two_all, d_gate_all))
        order.mark(part_gate)
        g_gate = scattered(part_gate, 0)
        (two_all,) = order.gate(two_all)
        part_up = order.point(left_trans(two_all, d_up_all))
        order.mark(part_up)
        g_up = scattered(part_up, 0)
        back_head(last)
        back_first = back_mixers(0, first, None)
        back_inputs(0, first, back_first)
        back = back_mixers(1, last, back_first)
        back_inputs(1, last, back)
        for index, k in enumerate(slots):
            output_sum(index, k)
        one_columns = relative_columns(order.gate(joined("normed"))[0])
        part_outs = left_trans(relative_columns(joined("d_mixed")), joined("mixer"))
        part_early = left_trans(one_columns, back[:, : channels + heads_width])
        part_late = left_trans(
            one_columns,
            jnp.concatenate(
                [back[:, places["xpre"]], joined("shared"), back[:, places["step"]]], axis=1
            ),
        )

        def total(name):
            value = slots[0][name]
            for k in slots[1:]:
                value = value + k[name]
            return value

        names = [
            "g_conv_state_weight", "g_conv_state_bias", "g_input_gain", "g_ffn_gain",
            "g_conv_weight", "g_conv_bias", "g_step_bias", "g_decay_log", "g_skip",
            "g_mamba_gain",
        ]
        small = {name: total(name) for name in names}
        vector = jnp.concatenate([small[name].reshape(-1) for name in names])
        vector_rows = -(-vector.size // (8 * LANES)) * 8
        vector = jnp.pad(vector, (0, vector_rows * LANES - vector.size)).reshape(-1, LANES)
        shared_size = sum(small[name].size for name in names[:4])
        shared_rows = -(-shared_size // (8 * LANES)) * 8

        sums = [first["norm_own"], first["ffn_own"], last["ffn_own"], last["norm_own"]]
        rests = [
            (0, first["d_hidden_own"], mine(first["unit_one"]), mine(first["inv_one"])),
            (0, first["hidden"]),
            (1, last["hidden"]),
            (1, last["d_hidden_own"], mine(last["unit_one"]), mine(last["inv_one"])),
        ]
        (g_outs, g_early, g_late), out, in_grad, vector, wide_vector = scatter_all(
            dp_size, t_size, [part_outs, part_early, part_late], sums, rests, input_gain[None],
            vector, shared_rows,
        )
        vector, wide_vector = vector.reshape(-1), wide_vector.reshape(-1)
        start = 0
        for name in names:
            shape, size = small[name].shape, small[name].size
            source = wide_vector if start < shared_size else vector
            small[name] = source[start : start + size].reshape(shape)
            start += size
        place = me_dp * t_size + me_t
        share = conv_state_bias.shape[0] // (dp_size * t_size)
        g_conv_state_weight = lax.dynamic_slice_in_dim(
            small["g_conv_state_weight"], place * share, share, 1
        )
        g_conv_state_bias = lax.dynamic_slice_in_dim(
            small["g_conv_state_bias"], place * share, share, 0
        )
        g_input_gain = lax.dynamic_slice_in_dim(small["g_input_gain"], me_dp * block, block, 0)
        g_ffn_gain = lax.dynamic_slice_in_dim(small["g_ffn_gain"], me_dp * block, block, 0)
        heads = [small[name] for name in names[4:]]

        shared_end = channels + joined("shared").shape[1]
        g_step = g_late[:, shared_end : shared_end + local_heads]
        g_late = g_late[:, :shared_end]
        g_outs = g_outs.T

        mamba_cols = mamba_in_weight.shape[1]
        tail = g_late[:, mamba_cols:]
        sub = block // t_size
        rowsets = []
        for q in range(t_size):
            part = lax.dynamic_slice_in_dim(tail, jnp.bitwise_xor(me_t, q) * sub, sub, 0)
            rowsets.append(part if q == 0 else t_swap(part, q))
        stacked = jnp.stack(rowsets)
        piece = state_weight.shape[1] // t_size
        sources = [
            lax.dynamic_index_in_dim(stacked, jnp.bitwise_xor(me_t, j), 0, keepdims=False)
            for j in range(t_size)
        ]
        g_state = jnp.concatenate([s[:, :piece] for s in sources], axis=1)
        pairs = t_size // 2
        g_kv = jnp.concatenate(
            [sources[(b % pairs) * 2 + b // pairs][:, piece:] for b in range(t_size)], axis=1
        )
        gate_cols = mamba_gate_weight.shape[1]
        mamba_rows = mamba_out_weight.shape[0]
        return (
            out,
            in_grad,
            g_input_gain,
            g_early[:, :gate_cols],
            g_late[:, :mamba_cols],
            g_state,
            g_step,
            heads[0],
            heads[1],
            g_conv_state_weight,
            g_conv_state_bias,
            heads[2],
            heads[3],
            heads[4],
            heads[5],
            g_outs[:mamba_rows],
            g_early[:, gate_cols:],
            g_kv,
            g_outs[mamba_rows:],
            g_ffn_gain,
            g_gate,
            g_up,
            g_down,
        )

    return per_device


def solution(mesh):
    placed = (
        P("dp", None, None),
        P("dp"),
        P("dp", None, None),
        P(),
        P(None, "tensor"),
        P(None, "tensor"),
        P(),
        P(None, "tensor"),
        P(None, "tensor"),
        P("tensor"),
        P(),
        P(),
        P("tensor"),
        P("tensor"),
        P("tensor"),
        P("tensor"),
        P("tensor", None),
        P(None, "tensor"),
        P(),
        P("tensor", None),
        P(),
        P(None, "tensor"),
        P(None, "tensor"),
        P("tensor", None),
    )
    return jax.shard_map(
        make_per_device(mesh.shape["dp"], mesh.shape["tensor"]),
        mesh=mesh,
        in_specs=placed,
        out_specs=(
            P("dp", None, None),
            P("dp", None, None),
            P("dp"),
            P("dp", "tensor"),
            P("dp", "tensor"),
            P(("dp", "tensor"), None),
            P("dp", "tensor"),
            P(None, "tensor"),
            P("tensor"),
            P(None, ("dp", "tensor")),
            P(("dp", "tensor")),
            P("tensor"),
            P("tensor"),
            P("tensor"),
            P("tensor"),
            P("tensor", "dp"),
            P("dp", "tensor"),
            P(("dp", "tensor"), None),
            P("tensor", "dp"),
            P("dp"),
            P("dp", "tensor"),
            P("dp", "tensor"),
            P("tensor", "dp"),
        ),
        check_vma=False,
    )
```

```python
import functools

import jax
import jax.numpy as jnp
from jax import lax
from jax.experimental import pallas as pl
from jax.experimental.pallas import tpu as pltpu
from jax.sharding import PartitionSpec as P

MHDIM = 64
STATE = 256
AHEADS = 8
KVHEADS = 2
AHDIM = 128
DSSM = 3072

epsilon = 1e-05
rope_base = 100000000000.0
f32 = jnp.float32
bf16 = jnp.bfloat16


def plain_dot(left, right):
    return jnp.dot(left, right, preferred_element_type=f32)


def right_trans(left, right):
    return lax.dot_general(left, right, (((1,), (1,)), ((), ())), preferred_element_type=f32)


def left_trans(left, right):
    return lax.dot_general(left, right, (((0,), (0,)), ((), ())), preferred_element_type=f32)


def silu_slope(values):
    sig = jax.nn.sigmoid(values)
    return sig * (1.0 + values * (1.0 - sig))


MESH = pl.DeviceIdType.MESH
LANES = 128
BLOCK = 128


def shifted(values, steps, row):
    if steps == 0:
        return values
    count = values.shape[0]
    moved = pltpu.roll(values, steps % count, 0)
    if steps > 0:
        return jnp.where(row >= steps, moved, 0.0)
    return jnp.where(row < count + steps, moved, 0.0)


def tap_sum(values, taps, bias):
    row = lax.broadcasted_iota(jnp.int32, values.shape, 0)
    width = taps.shape[0]
    total = jnp.zeros_like(values) + bias
    for k in range(width):
        total = total + shifted(values, width - 1 - k, row) * taps[k : k + 1, :]
    return total


def tap_back(grads, values, taps):
    row = lax.broadcasted_iota(jnp.int32, values.shape, 0)
    width = taps.shape[0]
    back = jnp.zeros_like(values)
    tap_grads = []
    for k in range(width):
        steps = width - 1 - k
        back = back + shifted(grads, -steps, row) * taps[k : k + 1, :]
        tap_grads.append(jnp.sum(grads * shifted(values, steps, row), axis=0, keepdims=True))
    return back, jnp.concatenate(tap_grads, axis=0)


def column_of(values, lane, index):
    return jnp.sum(jnp.where(lane == index, values, 0.0), axis=1, keepdims=True)


def exact_dot(left, right):
    return jnp.dot(left, right, precision=lax.Precision.HIGHEST, preferred_element_type=f32)


def turned(values, cosine, sine):
    return values * cosine + pltpu.roll(values, AHDIM // 2, 1) * sine


def scores_of(query, keys, lo, hi, length):
    scores = right_trans(query[lo:hi], keys[:hi]) * AHDIM ** (-0.5)
    t = lax.broadcasted_iota(jnp.int32, (hi - lo, hi), 0) + lo
    s = lax.broadcasted_iota(jnp.int32, (hi - lo, hi), 1)
    return scores, (t >= s) & (s < length)


def attention_forward(query_pre, key_pre, value_pre, cosine, sine, length, query, keys, values, logs, context):
    count, width = query.shape
    keys[...] = turned(key_pre, cosine, sine).astype(bf16)
    values[...] = value_pre.astype(bf16)
    lane = lax.broadcasted_iota(jnp.int32, (count, LANES), 1)
    kept = jnp.zeros((count, LANES), f32)
    for h in range(width // AHDIM):
        lanes = slice(h * AHDIM, (h + 1) * AHDIM)
        query[:, lanes] = turned(query_pre[:, lanes], cosine, sine).astype(bf16)
        found = []
        for i in range(count // BLOCK):
            lo, hi = i * BLOCK, (i + 1) * BLOCK
            scores, valid = scores_of(query[:, lanes], keys[...], lo, hi, length)
            masked = jnp.where(valid, scores, -1e30)
            peak = jnp.max(masked, axis=1, keepdims=True)
            expo = jnp.exp(masked - peak)
            total = jnp.sum(expo, axis=1, keepdims=True)
            found.append(peak + jnp.log(total))
            probs = (expo / total).astype(bf16)
            context[lo:hi, lanes] = plain_dot(probs, values[:hi, :]).astype(bf16)
        kept = jnp.where(lane == h, jnp.concatenate(found, axis=0), kept)
    logs[...] = kept


def attention_backward(d_context, query, keys, values, logs, cosine, sine, length, d_query_pre, d_keys, d_values):
    count, width = query.shape
    lane = lax.broadcasted_iota(jnp.int32, (count, LANES), 1)
    scale = AHDIM ** (-0.5)
    key_total = jnp.zeros((count, AHDIM), f32)
    value_total = jnp.zeros((count, AHDIM), f32)
    for h in range(width // AHDIM):
        lanes = slice(h * AHDIM, (h + 1) * AHDIM)
        log = column_of(logs[...], lane, h)
        pieces = []
        for i in range(count // BLOCK):
            lo, hi = i * BLOCK, (i + 1) * BLOCK
            scores, valid = scores_of(query[:, lanes], keys[...], lo, hi, length)
            probs = jnp.where(valid, jnp.exp(scores - log[lo:hi]), 0.0)
            grads = d_context[lo:hi, lanes]
            d_probs = right_trans(grads, values[:hi, :])
            delta = jnp.sum(probs * d_probs, axis=1, keepdims=True)
            d_scores = (probs * (d_probs - delta)).astype(bf16)
            pieces.append(plain_dot(d_scores, keys[:hi, :]) * scale)
            d_key = left_trans(d_scores, query[lo:hi, lanes]) * scale
            d_value = left_trans(probs.astype(bf16), grads)
            if hi < count:
                rest = jnp.zeros((count - hi, AHDIM), f32)
                d_key = jnp.concatenate([d_key, rest], axis=0)
                d_value = jnp.concatenate([d_value, rest], axis=0)
            key_total = key_total + d_key
            value_total = value_total + d_value
        d_query_pre[:, lanes] = turned(jnp.concatenate(pieces, axis=0), cosine, -sine).astype(bf16)
    d_keys[...] = turned(key_total, cosine, -sine)
    d_values[...] = value_total


def columns_of(channels, heads_width):
    places, start = {}, 0
    for name, size in (
        ("zgate", channels), ("query", heads_width), ("xpre", channels), ("state", 2 * STATE),
        ("key", AHDIM), ("value", AHDIM), ("step", LANES),
    ):
        places[name] = slice(start, start + size)
        start += size
    return places, start


def forward_kernel(
    lengths, zgate, query_pre, xpre, statepre, key_pre, value_pre, steppre, cosine, sine, conv_weight, conv_bias, state_taps, state_bias, step_bias, rates,
    skip_rep, gated, ssd, square, xconv, sconv, stepsize, cumul, inner, query, keys, values, logs,
    context, cumul_rows, *, slot,
):
    attention_forward(
        query_pre, key_pre[...], value_pre[...],
        cosine[...], sine[...], lengths[slot], query, keys, values, logs, context,
    )
    count, channels = xpre.shape
    xlin = tap_sum(xpre[...], conv_weight[...], conv_bias[...])
    xconv[...] = (xlin * jax.nn.sigmoid(xlin)).astype(bf16)
    slin = tap_sum(statepre[...], state_taps[...], state_bias[...])
    sconv[...] = (slin * jax.nn.sigmoid(slin)).astype(bf16)
    inner[...] = right_trans(sconv[:, STATE:], sconv[:, :STATE])
    step = jax.nn.softplus(steppre[...] + step_bias[...])
    stepsize[...] = step
    row = lax.broadcasted_iota(jnp.int32, (count, count), 0)
    col = lax.broadcasted_iota(jnp.int32, (count, count), 1)
    total = exact_dot(jnp.where(row >= col, 1.0, 0.0), -step * rates[...])
    cumul[...] = total
    cumul_rows[...] = total.T
    square[...] = jnp.zeros_like(square)

    def pair(p):
        lanes = slice(p * LANES, (p + 1) * LANES)
        lane = lax.broadcasted_iota(jnp.int32, (count, LANES), 1)
        xvals = xconv[:, lanes].astype(f32)
        low_half = lane < MHDIM
        step_rep = jnp.where(
            low_half, column_of(stepsize[...], lane, 2 * p), column_of(stepsize[...], lane, 2 * p + 1)
        )
        weighted = (step_rep * xvals).astype(bf16)
        columns = [column_of(cumul[...], lane, 2 * p + h) for h in range(2)]
        for i in range(count // BLOCK):
            lo, hi = i * BLOCK, (i + 1) * BLOCK
            results = []
            for h in range(2):
                differ = columns[h][lo:hi] - cumul_rows[2 * p + h : 2 * p + h + 1, :hi]
                t = lax.broadcasted_iota(jnp.int32, (BLOCK, hi), 0) + lo
                s = lax.broadcasted_iota(jnp.int32, (BLOCK, hi), 1)
                decay = jnp.exp(jnp.where(t >= s, differ, -1e30))
                mixing = (inner[lo:hi, :hi] * decay).astype(bf16)
                results.append(plain_dot(mixing, weighted[:hi]))
            half = jnp.where(low_half[lo:hi], results[0], results[1])
            half = half + skip_rep[:, lanes] * xvals[lo:hi]
            ssd[lo:hi, lanes] = half
            z = zgate[lo:hi, lanes]
            value = half * (z * jax.nn.sigmoid(z))
            gated[lo:hi, lanes] = value
            square[lo:hi, :] += value * value

    for p in range(channels // LANES):
        pair(p)


def full(*shape):
    return jax.ShapeDtypeStruct(shape, f32)


def low(*shape):
    return jax.ShapeDtypeStruct(shape, bf16)


def in_vmem(count):
    return [pl.BlockSpec(memory_space=pltpu.VMEM)] * count


def whole_blocks(shapes):
    return [pl.BlockSpec(s.shape, lambda i, n=len(s.shape): (0,) * n) for s in shapes]


def mixers_forward(slot, lengths, *operands):
    count, channels = operands[0].shape
    heads_width = operands[1].shape[1]
    shapes = (
        full(count, channels), full(count, channels), full(count, LANES), low(count, channels),
        low(count, 2 * STATE), full(count, LANES), full(count, LANES), full(count, count),
        low(count, heads_width), low(count, AHDIM), low(count, AHDIM), full(count, LANES),
        low(count, heads_width),
    )
    return pl.pallas_call(
        functools.partial(forward_kernel, slot=slot),
        grid=(1,),
        out_shape=shapes,
        in_specs=[pl.BlockSpec(memory_space=pltpu.SMEM)] + in_vmem(len(operands)),
        out_specs=tuple(whole_blocks(shapes)),
        scratch_shapes=[pltpu.VMEM((LANES, count), f32)],
        compiler_params=pltpu.CompilerParams(vmem_limit_bytes=48 * 2**20),
        cost_estimate=pl.CostEstimate(
            flops=10**6, bytes_accessed=10**6, transcendentals=10**3
        ),
    )(lengths, *operands)


def backward_kernel(
    lengths, d_scaled_in, d_context_in, gated_in, inv_cross, gain, zgate, xpre, statepre, steppre,
    ssd, xconv, sconv, stepsize, cumul, inner,
    query, keys, values, logs, cosine, sine, conv_weight, conv_bias, state_taps, state_bias,
    step_bias, rates, skip_rep,
    back, d_statepre, d_keys, d_values, g_conv, g_state, g_heads, g_skip, g_gain,
    d_ssd, d_xvals, cumul_rows, d_inner, row_sums, col_sums, d_step, *, slot, places,
):
    count, channels = ssd.shape
    attention_backward(
        d_context_in[...].astype(bf16), query, keys, values, logs, cosine[...], sine[...],
        lengths[slot], back.at[:, places["query"]], d_keys, d_values,
    )
    back[:, places["key"]] = d_keys[...].astype(bf16)
    back[:, places["value"]] = d_values[...].astype(bf16)
    d_zgate, d_xpre = back.at[:, places["zgate"]], back.at[:, places["xpre"]]
    d_steppre = back.at[:, places["step"]]
    d_scaled = d_scaled_in[...]
    g_gain[...] = jnp.sum(d_scaled * gated_in[...] * inv_cross[:, 0:1], axis=0, keepdims=True)
    inv = inv_cross[:, 0:1]
    cross = inv_cross[:, 1:2]
    d_gated = inv * (d_scaled * gain[...]) - gated_in[...] * cross
    z = zgate[...]
    sig = jax.nn.sigmoid(z)
    d_low = (d_gated * (z * sig)).astype(bf16)
    d_ssd[...] = d_low
    d_zgate[...] = (d_gated * ssd[...] * sig * (1.0 + z * (1.0 - sig))).astype(bf16)
    g_skip[...] = jnp.sum(d_low.astype(f32) * xconv[...].astype(f32), axis=0, keepdims=True)
    cumul_rows[...] = cumul[...].T
    d_inner[...] = jnp.zeros_like(d_inner)
    row_sums[...] = jnp.zeros_like(row_sums)
    col_sums[...] = jnp.zeros_like(col_sums)
    d_step[...] = jnp.zeros_like(d_step)

    def pair(p):
        lanes = slice(p * LANES, (p + 1) * LANES)
        lane = lax.broadcasted_iota(jnp.int32, (count, LANES), 1)
        low_half = lane < MHDIM
        xvals = xconv[:, lanes].astype(f32)
        step_rep = jnp.where(
            low_half, column_of(stepsize[...], lane, 2 * p), column_of(stepsize[...], lane, 2 * p + 1)
        )
        weighted = (step_rep * xvals).astype(bf16)
        grads = d_ssd[:, lanes]
        columns = [column_of(cumul[...], lane, 2 * p + h) for h in range(2)]
        pieces = []
        for h in range(2):
            only = jnp.where(low_half == (h == 0), grads, jnp.zeros_like(grads))
            back_part = jnp.zeros((count, LANES), f32)
            sums = []
            col_total = jnp.zeros((1, count), f32)
            for i in range(count // BLOCK):
                lo, hi = i * BLOCK, (i + 1) * BLOCK
                differ = columns[h][lo:hi] - cumul_rows[2 * p + h : 2 * p + h + 1, :hi]
                t = lax.broadcasted_iota(jnp.int32, (BLOCK, hi), 0) + lo
                s = lax.broadcasted_iota(jnp.int32, (BLOCK, hi), 1)
                decay = jnp.exp(jnp.where(t >= s, differ, -1e30))
                mixing = inner[lo:hi, :hi] * decay
                part = left_trans(mixing.astype(bf16), only[lo:hi])
                d_mixing = right_trans(only[lo:hi], weighted[:hi])
                d_inner[lo:hi, :hi] += d_mixing * decay
                flow = d_mixing * mixing
                sums.append(jnp.sum(flow, axis=1, keepdims=True))
                down = jnp.sum(flow, axis=0, keepdims=True)
                if hi < count:
                    part = jnp.concatenate([part, jnp.zeros((count - hi, LANES), f32)], axis=0)
                    down = jnp.concatenate([down, jnp.zeros((1, count - hi), f32)], axis=1)
                back_part = back_part + part
                col_total = col_total + down
            here = lane == 2 * p + h
            row_sums[...] = jnp.where(here, jnp.concatenate(sums, axis=0), row_sums[...])
            col_sums[2 * p + h : 2 * p + h + 1, :] = col_total
            pieces.append(back_part)
        d_weighted = pieces[0] + pieces[1]
        d_xvals[:, lanes] = grads.astype(f32) * skip_rep[:, lanes] + d_weighted * step_rep
        product = d_weighted * xvals
        for h in range(2):
            value = jnp.sum(
                jnp.where(low_half == (h == 0), product, 0.0), axis=1, keepdims=True
            )
            d_step[...] = jnp.where(lane == 2 * p + h, value, d_step[...])

    for p in range(channels // LANES):
        pair(p)

    d_cumul = row_sums[...] - col_sums[...].T
    row = lax.broadcasted_iota(jnp.int32, (count, count), 0)
    col = lax.broadcasted_iota(jnp.int32, (count, count), 1)
    d_logdecay = exact_dot(jnp.where(row <= col, 1.0, 0.0), d_cumul)
    rate = rates[...]
    d_full = (d_step[...] - d_logdecay * rate) * jax.nn.sigmoid(steppre[...] + step_bias[...])
    d_steppre[...] = d_full.astype(bf16)
    g_heads[0:1, :] = jnp.sum(d_full, axis=0, keepdims=True)
    g_heads[1:2, :] = jnp.sum(-d_logdecay * stepsize[...] * rate, axis=0, keepdims=True)

    d_in = d_inner[...].astype(bf16)
    d_c = plain_dot(d_in, sconv[:, :STATE])
    d_b = left_trans(d_in, sconv[:, STATE:])
    slin = tap_sum(statepre[...], state_taps[...], state_bias[...])
    d_slin = jnp.concatenate([d_b, d_c], axis=1) * silu_slope(slin)
    back_state, tap_grads = tap_back(d_slin, statepre[...], state_taps[...])
    d_statepre[...] = back_state
    back[:, places["state"]] = back_state.astype(bf16)
    g_state[...] = jnp.concatenate([tap_grads, jnp.sum(d_slin, axis=0, keepdims=True)], axis=0)
    xlin = tap_sum(xpre[...], conv_weight[...], conv_bias[...])
    d_xlin = d_xvals[...] * silu_slope(xlin)
    back_x, tap_grads = tap_back(d_xlin, xpre[...], conv_weight[...])
    d_xpre[...] = back_x.astype(bf16)
    g_conv[...] = jnp.concatenate([tap_grads, jnp.sum(d_xlin, axis=0, keepdims=True)], axis=0)


def mixers_backward(slot, slots, held, lengths, *operands):
    count, channels = operands[0].shape
    heads_width = operands[1].shape[1]
    taps = operands[-7].shape[0]
    width = columns_of(channels, heads_width)[1]
    kernel = functools.partial(
        backward_kernel, slot=slot, places=columns_of(channels, heads_width)[0]
    )
    aliases = {}
    extra_specs, extra = [], ()
    if held is not None:
        aliases = {0: 0}
        extra_specs, extra = [pl.BlockSpec(memory_space=pl.ANY)], (held,)
        inside = kernel
        kernel = lambda _, *refs: inside(*refs)
    shapes = (
        full(count, 2 * STATE), full(count, AHDIM), full(count, AHDIM), full(taps + 1, channels),
        full(taps + 1, 2 * STATE), full(2, LANES), full(1, channels), full(1, channels),
    )
    return pl.pallas_call(
        kernel,
        grid=(1,),
        out_shape=(low(slots * count, width),) + shapes,
        in_specs=extra_specs
        + [pl.BlockSpec(memory_space=pltpu.SMEM)]
        + in_vmem(len(operands)),
        out_specs=tuple(
            [pl.BlockSpec((count, width), lambda i: (slot, 0))] + whole_blocks(shapes)
        ),
        scratch_shapes=[
            pltpu.VMEM((count, channels), bf16),
            pltpu.VMEM((count, channels), f32),
            pltpu.VMEM((LANES, count), f32),
            pltpu.VMEM((count, count), f32),
            pltpu.VMEM((count, LANES), f32),
            pltpu.VMEM((LANES, count), f32),
            pltpu.VMEM((count, LANES), f32),
        ],
        input_output_aliases=aliases,
        compiler_params=pltpu.CompilerParams(vmem_limit_bytes=56 * 2**20),
        cost_estimate=pl.CostEstimate(
            flops=10**6, bytes_accessed=10**6, transcendentals=10**3
        ),
    )(*extra, lengths, *operands)


def feed_forward_kernel(normed, cot, gate_weight, up_weight, down_weight, *refs):
    inner, d_gate, d_up, back = refs[-4:]
    gate = plain_dot(normed[...], gate_weight[...])
    upper = plain_dot(normed[...], up_weight[...])
    d_inner = right_trans(cot[...], down_weight[...])
    sig = jax.nn.sigmoid(gate)
    silu = gate * sig
    inner[...] = (silu * upper).astype(bf16)
    d_gate[...] = (d_inner * upper * sig * (1.0 + gate * (1.0 - sig))).astype(bf16)
    d_up[...] = (d_inner * silu).astype(bf16)
    part = right_trans(d_gate[...], gate_weight[...]) + right_trans(d_up[...], up_weight[...])

    @pl.when(pl.program_id(0) == 0)
    def _():
        back[...] = part

    @pl.when(pl.program_id(0) > 0)
    def _():
        back[...] += part


def feed_forward_all(slot, slots, held, normed, cot, gate_weight, up_weight, down_weight):
    count, width = normed.shape
    hidden = gate_weight.shape[1]
    block = min(512, hidden)
    rows = pl.BlockSpec((count, width), lambda j: (0, 0))
    columns = pl.BlockSpec((width, block), lambda j: (0, j))
    joint = pl.BlockSpec((count, block), lambda j: (slot, j))
    extra = () if held is None else tuple(held)
    return pl.pallas_call(
        feed_forward_kernel,
        grid=(hidden // block,),
        out_shape=tuple([low(slots * count, hidden)] * 3 + [full(count, width)]),
        in_specs=[
            rows, rows, columns, columns, pl.BlockSpec((block, width), lambda j: (j, 0))
        ] + [pl.BlockSpec(memory_space=pl.ANY)] * len(extra),
        out_specs=(joint, joint, joint, rows),
        input_output_aliases={5 + n: n for n in range(len(extra))},
        compiler_params=pltpu.CompilerParams(vmem_limit_bytes=56 * 2**20),
        cost_estimate=pl.CostEstimate(flops=10**6, bytes_accessed=10**6, transcendentals=10**3),
    )(normed, cot, gate_weight, up_weight, down_weight, *extra)


def swap(values, axis, size, bit):
    return lax.ppermute(values, axis, [(i, i ^ bit) for i in range(size)])


def halving_order(members, bit, limit):
    if bit >= limit:
        return members
    low = halving_order([m for m in members if not m & bit], bit * 2, limit)
    high = halving_order([m for m in members if m & bit], bit * 2, limit)
    return low + high


class Order:
    def __init__(self):
        self.last = ()
        self.queue = []

    def point(self, value, skip=0):
        if len(self.queue) <= skip:
            return value
        return lax.optimization_barrier((value, self.queue.pop(skip)))[0]

    def gate(self, *values):
        return lax.optimization_barrier((values, self.last))[0]

    def mark(self, *values):
        self.last = values


def scatter_all(size, t_size, parts, halves, rests, gain, vector, shared_rows):
    rows = parts[0].shape[0]
    works = len(parts)
    share = rows // size
    chunk = min(256, rows // 4)
    levels = size.bit_length() - 1
    spans = []
    for level in range(1, levels):
        lo, hi = rows >> (level + 1), rows >> level
        step = min(chunk, hi - lo)
        spans += [(level, start, step) for start in range(hi - step, lo - 1, -step)]
    spans.append((levels, 0, share))
    pieces = [(w,) + span for w in range(works) for span in spans]
    per_work = len(spans)
    widths = [p.shape[1] for p in parts]
    wide = max(widths)
    extra = len(halves)
    half_shape = halves[0].shape
    half, width = half_shape
    slots = 1 + max(rest[0] for rest in rests)
    extras = [value for rest in rests for value in rest[1:]]
    wholes = [n for n, rest in enumerate(rests) if len(rest) == 2]

    def kernel(*refs):
        held_in, refs = refs[:works], refs[works:]
        own, refs = refs[:extra], refs[extra:]
        beside = []
        for rest in rests:
            beside.append(refs[: len(rest) - 1])
            refs = refs[len(rest) - 1 :]
        gain_ref, small, refs = refs[0], refs[1], refs[2:]
        outs, refs = refs[:works], refs[works:]
        far, refs = refs[:extra], refs[extra:]
        result, grad, small_out, wide_out, refs = refs[0], refs[1], refs[2], refs[3], refs[4:]
        loads, pair_loads, totals, low_rows, theirs, refs = (
            refs[0], refs[1], refs[2], refs[3], refs[4], refs[5:]
        )
        boxes, wide_boxes, refs = refs[0], refs[1], refs[2:]
        landed, refs = refs[:works], refs[works:]
        later, refs = refs[: works * (levels - 1)], refs[works * (levels - 1) :]
        load_sems, out_sems, x_send, x_recv, z_send, z_recv, y_sems, c_sems, pair_sems, v_sems, w_sems = refs
        me = lax.axis_index("dp")
        spot = lax.axis_index("tensor")

        def neighbour(bit):
            return spot + bit - 2 * bit * lax.rem(spot // bit, 2)


        def partner(level):
            bit = 1 << level
            return me + bit - 2 * bit * lax.rem(me // bit, 2)

        barrier = pltpu.get_barrier_semaphore()
        for other in range(1, size):
            pl.semaphore_signal(
                barrier, inc=1, device_id={"dp": lax.rem(me + other, size)}, device_id_type=MESH
            )
        for other in range(1, t_size):
            pl.semaphore_signal(
                barrier, inc=1, device_id={"tensor": lax.rem(spot + other, t_size)},
                device_id_type=MESH,
            )
        pl.semaphore_wait(barrier, size + t_size - 2)

        def small_copy(other):
            return pltpu.make_async_remote_copy(
                src_ref=small, dst_ref=boxes.at[size - other], send_sem=v_sems.at[0, other],
                recv_sem=v_sems.at[1, size - other],
                device_id={"dp": lax.rem(me + other, size)}, device_id_type=MESH,
            )

        def wide_copy(other):
            return pltpu.make_async_remote_copy(
                src_ref=small_out.at[pl.ds(0, shared_rows), :], dst_ref=wide_boxes.at[t_size - other],
                send_sem=w_sems.at[0, other], recv_sem=w_sems.at[1, t_size - other],
                device_id={"tensor": lax.rem(spot + other, t_size)}, device_id_type=MESH,
            )

        def in_turn(kept, count, place, rows):
            total = jnp.zeros((rows, LANES), f32)
            for number in range(count):
                offset = lax.rem(number - place + count, count)
                total = total + kept[offset]
            return total

        def small_sums(stage):
            if stage == 0:
                boxes[0] = small[...]
                for other in range(1, size):
                    small_copy(other).wait_recv()
                small_out[...] = in_turn(boxes, size, me, small.shape[0])
                for other in range(1, t_size):
                    wide_copy(other).start()
            else:
                wide_boxes[0] = small_out[:shared_rows, :]
                for other in range(1, t_size):
                    wide_copy(other).wait_recv()
                wide_out[...] = in_turn(wide_boxes, t_size, spot, shared_rows)


        def y_copy(e):
            return pltpu.make_async_remote_copy(
                src_ref=own[e], dst_ref=far[e], send_sem=y_sems.at[0, e], recv_sem=y_sems.at[1, e],
                device_id={"tensor": neighbour(2)}, device_id_type=MESH,
            )

        core = lax.rem(spot, 2)

        def rows_of(place):
            return pl.ds(pl.multiple_of(place * half, 8), half)

        def c_copy(e):
            slot = rests[e][0]
            if e in wholes:
                target = theirs.at[wholes.index(e)]
            else:
                target = grad.at[slot, rows_of(core), :]
            return pltpu.make_async_remote_copy(
                src_ref=totals.at[e], dst_ref=target, send_sem=c_sems.at[0, e],
                recv_sem=c_sems.at[1, e], device_id={"tensor": neighbour(1)}, device_id_type=MESH,
            )

        def fetch(source, place):
            return pltpu.make_async_copy(source, pair_loads.at[place], pair_sems.at[0, place])

        def keep(e, place):
            slot = rests[e][0]
            if e in wholes:
                n = 2 * wholes.index(e) + place
                target = result.at[slot, rows_of(core if place == 0 else 1 - core), :]
                return pltpu.make_async_copy(low_rows.at[n], target, pair_sems.at[1 + place, e])
            return pltpu.make_async_copy(
                totals.at[e], grad.at[slot, rows_of(core), :], pair_sems.at[1, e]
            )

        def exchange(e):
            y_copy(e).wait_recv()
            sources = [own[e], far[e]]
            if e in wholes:
                sources.append(beside[e][0].at[pl.ds(0, half), :])
            else:
                sources += [beside[e][0], beside[e][1]]
            for place, source in enumerate(sources):
                fetch(source, place).start()
            for place, source in enumerate(sources):
                fetch(source, place).wait()
            total = pair_loads[0] + pair_loads[1]
            if e in wholes:
                totals[e] = total
                low_rows[2 * wholes.index(e)] = (pair_loads[2] + total).astype(bf16)
            else:
                unit = pair_loads[3]
                scaled = total * gain_ref[...]
                mean = jnp.sum(scaled * unit, axis=1, keepdims=True) / width
                totals[e] = pair_loads[2] + beside[e][2][...] * (scaled - unit * mean)
            c_copy(e).start()
            keep(e, 0).start()

        def complete(e):
            fetch(beside[e][0].at[pl.ds(half, half), :], 0).start()
            c_copy(e).wait_recv()
            fetch(beside[e][0].at[pl.ds(half, half), :], 0).wait()
            n = wholes.index(e)
            low_rows[2 * n + 1] = (pair_loads[0] + theirs[n]).astype(bf16)
            keep(e, 1).start()

        def first_copy(number):
            w, _, start, step = pieces[number]
            return pltpu.make_async_remote_copy(
                src_ref=held_in[w].at[pl.ds(rows // 2 + start, step), :],
                dst_ref=landed[w].at[pl.ds(start, step), :],
                send_sem=x_send.at[number],
                recv_sem=x_recv.at[number],
                device_id={"dp": partner(0)},
                device_id_type=MESH,
            )

        def load(number):
            w, _, start, step = pieces[number]
            return pltpu.make_async_copy(
                held_in[w].at[pl.ds(start, step), :],
                loads.at[number % 2, pl.ds(0, step), pl.ds(0, widths[w])],
                load_sems.at[number % 2],
            )

        def later_copy(number):
            w, level, start, step = pieces[number]
            return pltpu.make_async_remote_copy(
                src_ref=landed[w].at[pl.ds(start, step), :],
                dst_ref=later[w * (levels - 1) + level - 1].at[pl.ds(start - (rows >> (level + 1)), step), :],
                send_sem=z_send.at[number],
                recv_sem=z_recv.at[number],
                device_id={"dp": partner(level)},
                device_id_type=MESH,
            )

        def store(w):
            return pltpu.make_async_copy(
                landed[w].at[pl.ds(0, share), :], outs[w], out_sems.at[w]
            )

        for other in range(1, size):
            small_copy(other).start()
        for e in range(extra):
            y_copy(e).start()
        for number in range(len(pieces)):
            first_copy(number).start()
        load(0).start()
        arrived = set()

        def need(w, level, start, step):
            base = rows >> (level + 1)
            for other in range(w * per_work, (w + 1) * per_work):
                _, its_level, its_start, its_step = pieces[other]
                if its_level != level or other in arrived:
                    continue
                if its_start - base < start + step and start < its_start - base + its_step:
                    later_copy(other).wait_recv()
                    arrived.add(other)

        def finish(w):
            level = levels - 1
            need(w, level, 0, share)
            landed[w][:share, :] += later[w * (levels - 1) + level - 1][:share, :]
            store(w).start()

        for number, (w, level, start, step) in enumerate(pieces):
            load(number).wait()
            if number + 1 < len(pieces):
                load(number + 1).start()
            first_copy(number).wait_recv()
            value = loads[number % 2, :step, : widths[w]] + landed[w][start : start + step, :]
            for before in range(1, min(level, levels - 1)):
                need(w, before, start, step)
                value = value + later[w * (levels - 1) + before - 1][start : start + step, :]
            landed[w][start : start + step, :] = value
            if level < levels:
                later_copy(number).start()
            if w and number == w * per_work + min(2, per_work - 1):
                finish(w - 1)
            if number in (0, 2):
                small_sums(number // 2)
            if number % 2 and number // 2 < extra:
                exchange(number // 2)
            if number % 2 == 0 and number // 2 - 2 in wholes:
                complete(number // 2 - 2)
        for e in range(len(pieces) // 2, extra):
            exchange(e)
        for e in wholes:
            if 2 * (e + 2) >= len(pieces):
                complete(e)
        finish(works - 1)
        for other in range(1, size):
            small_copy(other).wait_send()
        for other in range(1, t_size):
            wide_copy(other).wait_send()
        for e in range(extra):
            y_copy(e).wait_send()
            c_copy(e).wait_send()
            keep(e, 0).wait()
            if e in wholes:
                keep(e, 1).wait()
            else:
                c_copy(e).wait_recv()
        for number, (w, level, start, step) in enumerate(pieces):
            first_copy(number).wait_send()
            if level < levels:
                later_copy(number).wait_send()
        for w in range(works):
            store(w).wait()

    scratch = [
        pltpu.VMEM((2, chunk, wide), f32),
        pltpu.VMEM((4,) + half_shape, f32),
        pltpu.VMEM((extra,) + half_shape, f32),
        pltpu.VMEM((2 * len(wholes),) + half_shape, bf16),
        pltpu.VMEM((len(wholes),) + half_shape, f32),
        pltpu.VMEM((size,) + vector.shape, f32),
        pltpu.VMEM((t_size, shared_rows, LANES), f32),
    ]
    scratch += [pltpu.VMEM((rows // 2, n), f32) for n in widths]
    scratch += [
        pltpu.VMEM((rows >> (level + 1), n), f32) for n in widths for level in range(1, levels)
    ]
    scratch += [
        pltpu.SemaphoreType.DMA((2,)),
        pltpu.SemaphoreType.DMA((works,)),
    ] + [pltpu.SemaphoreType.DMA((len(pieces),))] * 4
    scratch += [pltpu.SemaphoreType.DMA((n, extra)) for n in (2, 2)]
    scratch += [pltpu.SemaphoreType.DMA((3, max(4, extra)))]
    scratch += [pltpu.SemaphoreType.DMA((2, size)), pltpu.SemaphoreType.DMA((2, t_size))]
    results = pl.pallas_call(
        kernel,
        out_shape=tuple(
            [full(share, n) for n in widths]
            + [full(*half_shape)] * extra
            + [low(slots, 2 * half, width), full(slots, 2 * half, width)]
            + [full(*vector.shape), full(shared_rows, LANES)]
        ),
        in_specs=[pl.BlockSpec(memory_space=pl.ANY)] * (works + extra)
        + [
            pl.BlockSpec(memory_space=pltpu.VMEM if value.shape[1] == 1 else pl.ANY)
            for value in extras
        ]
        + in_vmem(2),
        out_specs=tuple([pl.BlockSpec(memory_space=pl.ANY)] * (works + extra + 2) + in_vmem(2)),
        scratch_shapes=scratch,
        compiler_params=pltpu.CompilerParams(
            collective_id=0, has_side_effects=True, vmem_limit_bytes=60 * 2**20
        ),
        cost_estimate=pl.CostEstimate(
            flops=10**6, bytes_accessed=10**6, transcendentals=0
        ),
    )(*parts, *halves, *extras, gain, vector)
    return results[:works], *results[works + extra :]


def make_per_device(dp_size, t_size):
    def per_device(
        tokens,
        lengths,
        out_grad,
        input_gain,
        mamba_gate_weight,
        mamba_in_weight,
        state_weight,
        step_weight,
        conv_weight,
        conv_bias,
        conv_state_weight,
        conv_state_bias,
        step_bias,
        decay_log,
        skip_scale,
        mamba_gain,
        mamba_out_weight,
        query_weight,
        key_value_weight,
        attn_out_weight,
        ffn_gain,
        gate_weight,
        up_weight,
        down_weight,
    ):
        micro = tokens.shape[0]
        count = tokens.shape[1]
        width = tokens.shape[2]
        half = count // 2
        local_heads = step_weight.shape[1]
        q_local = query_weight.shape[1] // AHDIM
        kv_width = key_value_weight.shape[1] // 2
        group_size = AHEADS // KVHEADS
        me_dp = lax.axis_index("dp")
        me_t = lax.axis_index("tensor")
        core = lax.rem(me_t, 2)
        kv_head = me_t * q_local // group_size
        key_weight = lax.dynamic_slice_in_dim(key_value_weight, kv_head * AHDIM, AHDIM, 1)
        value_weight = lax.dynamic_slice_in_dim(
            key_value_weight, kv_width + kv_head * AHDIM, AHDIM, 1
        )
        rows = jnp.arange(count)
        freqs = rope_base ** (-(jnp.arange(AHDIM // 2).astype(f32) * 2.0) / AHDIM)
        angles = rows.astype(f32)[:, None] * freqs[None, :]
        cosine, sine = jnp.cos(angles), jnp.sin(angles)
        cosine = jnp.concatenate([cosine, cosine], axis=1)
        sine = jnp.concatenate([-sine, sine], axis=1)
        channels = mamba_in_weight.shape[1]
        heads_width = query_weight.shape[1]
        places, _ = columns_of(channels, heads_width)
        pad_step = LANES - local_heads

        def lane_row(vector):
            return jnp.pad(vector, (0, pad_step))[None]

        mixer_rows = (
            conv_weight, conv_bias[None], conv_state_weight, conv_state_bias[None],
            lane_row(step_bias), lane_row(jnp.exp(decay_log)), jnp.repeat(skip_scale, MHDIM)[None],
        )
        step_lanes = jnp.pad(step_weight, ((0, 0), (0, pad_step)))
        in_weights = (
            mamba_gate_weight, query_weight, mamba_in_weight, state_weight, key_weight,
            value_weight, step_lanes,
        )

        def t_swap(values, bit):
            return swap(values, "tensor", t_size, bit)

        def t_total(values):
            bit = 1
            while bit < t_size:
                values = values + t_swap(values, bit)
                bit *= 2
            return values

        def mine(values):
            return lax.dynamic_slice_in_dim(values, core * half, half, 0)

        def other(values):
            return lax.dynamic_slice_in_dim(values, (1 - core) * half, half, 0)

        def halves(values):
            values = lax.optimization_barrier(values)
            return mine(values), other(values)

        def relative(values):
            return jnp.concatenate([mine(values), other(values)], axis=0)

        def in_order(own, far):
            return jnp.where(
                core == 0,
                jnp.concatenate([own, far], axis=0),
                jnp.concatenate([far, own], axis=0),
            )

        def half_sum(own, far, pieces):
            own = own + t_swap(far, 1)
            bit = 2
            while bit < t_size // 2:
                own = own + t_swap(own, bit)
                bit *= 2
            step = -(-own.shape[0] // (8 * pieces)) * 8
            parts = []
            for start in range(0, own.shape[0], step):
                parts.append(t_swap(own[start : start + step], bit))
            order.queue += parts
            return own, parts

        def add_up(own, parts):
            for part in parts:
                order.queue = [p for p in order.queue if p is not part]
            own, *parts = order.gate(own, *parts)
            return own + jnp.concatenate(parts, axis=0)

        block = width // dp_size

        order = Order()

        def forward(index, slot):
            inputs = slot.astype(f32)
            inv_one = lax.rsqrt(jnp.mean(inputs * inputs, axis=-1, keepdims=True) + epsilon)
            unit_one = inputs * inv_one
            normed = (unit_one * input_gain).astype(bf16)
            normed = order.point(normed)
            pre = [plain_dot(normed, w) for w in in_weights]
            gated, ssd, square, *kept, query, keys, values, logs, context = mixers_forward(
                index, lengths, *pre, cosine, sine, *mixer_rows
            )
            gated = order.point(order.point(gated))
            total_square = t_total(jnp.sum(square, axis=-1))
            inv_mamba = lax.rsqrt(total_square / DSSM + epsilon)[:, None]
            scaled = (gated * inv_mamba * mamba_gain).astype(bf16)
            mixer = jnp.concatenate([scaled, context], axis=1)
            mixed_own, mixed_far = half_sum(
                *halves(plain_dot(scaled, mamba_out_weight) + plain_dot(context, attn_out_weight)),
                3,
            )
            order.mark(mixed_own)
            return dict(
                mixed_own=mixed_own, mixed_far=mixed_far, inputs=inputs, inv_one=inv_one,
                unit_one=unit_one, normed=normed, pre=pre, gated=gated, ssd=ssd, kept=kept,
                attention=(query, keys, values, logs), inv_mamba=inv_mamba, mixer=mixer,
            )

        def feed_forward(index, k, held):
            hidden_own = mine(k["inputs"]) + add_up(k["mixed_own"], k["mixed_far"])
            hidden = jnp.concatenate([hidden_own, t_swap(hidden_own, 1)], axis=0)
            inv_two = lax.rsqrt(jnp.mean(hidden * hidden, axis=-1, keepdims=True) + epsilon)
            unit_two = hidden * inv_two
            normed_two = (unit_two * ffn_gain).astype(bf16)
            valid = (rows < lengths[index]).astype(f32)[:, None]
            cotangent = relative(out_grad[index].astype(f32) * valid)
            cot_low = cotangent.astype(bf16)
            *held, back = feed_forward_all(
                index, micro, held, normed_two, cot_low, gate_weight, up_weight, down_weight
            )
            back = order.point(order.point(back))
            back_own, back_far = half_sum(back[:half], back[half:], 3)
            order.mark(back_own)
            k.update(
                back_own=back_own, back_far=back_far,
                hidden=hidden, inv_two=inv_two[:half], unit_two=unit_two[:half],
                normed_two=normed_two, cotangent=cotangent, cot_low=cot_low,
            )
            return held

        def output_sum(index, k):
            (inner_ffn,) = order.gate(
                lax.slice_in_dim(inner_all, index * count, (index + 1) * count, axis=0)
            )
            ffn = plain_dot(inner_ffn, down_weight)
            k["ffn_own"] = ffn[:half] + t_swap(ffn[half:], 1)
            order.mark(k["ffn_own"])

        def back_head(k):
            unit_two = k["unit_two"]
            g_ffn_gain = jnp.sum(k["back_own"] * unit_two, axis=0)
            d_normed_two = add_up(k["back_own"], k["back_far"])
            d_unit_two = d_normed_two * ffn_gain
            d_rest = k["inv_two"] * (
                d_unit_two - unit_two * jnp.mean(d_unit_two * unit_two, axis=-1, keepdims=True)
            )
            d_both = k["cotangent"] + jnp.concatenate([d_rest, t_swap(d_rest, 1)], axis=0)
            d_mixed = in_order(d_both[:half], d_both[half:]).astype(bf16)
            d_scaled = right_trans(d_mixed, mamba_out_weight)
            d_context = right_trans(d_mixed, attn_out_weight)
            k["g_ffn_gain"] = g_ffn_gain
            k["d_hidden_own"] = d_both[:half]
            k["d_mixed"], k["d_scaled"], k["d_context"] = d_mixed, d_scaled, d_context
            k["cross"] = t_total(jnp.sum(d_scaled * mamba_gain * k["gated"], axis=-1))[:, None]
            order.mark(d_scaled, d_context)

        def back_mixers(index, k, held):
            d_scaled, cross = order.gate(k["d_scaled"], k["cross"])
            inv = k["inv_mamba"]
            inv_cross = jnp.concatenate([inv, inv**3 * cross / DSSM], axis=1)
            inv_cross = jnp.pad(inv_cross, ((0, 0), (0, LANES - 2)))
            back, d_statepre, d_keys, d_values, g_conv, g_state, g_heads, g_skip, g_gain = (
                mixers_backward(
                    index, micro, held, lengths, d_scaled, k["d_context"], k["gated"], inv_cross,
                    mamba_gain[None], k["pre"][0], k["pre"][2], k["pre"][3], k["pre"][6], k["ssd"],
                    *k["kept"], *k["attention"], cosine, sine, *mixer_rows,
                )
            )
            kv_far = jnp.where(core == 0, d_values, d_keys)
            kv_own = jnp.where(core == 0, d_keys, d_values)
            k["kv_sum"] = kv_own + t_swap(kv_far, 1)
            k["d_statepre"] = d_statepre
            k.update(
                g_conv_weight=g_conv[:-1], g_conv_bias=g_conv[-1],
                g_conv_state_weight=g_state[:-1], g_conv_state_bias=g_state[-1],
                g_step_bias=g_heads[0, :local_heads], g_decay_log=g_heads[1, :local_heads],
                g_skip=jnp.sum(g_skip.reshape(local_heads, MHDIM), axis=1),
                g_mamba_gain=g_gain[0],
            )
            order.mark(back)
            return back

        def back_inputs(index, k, back):
            back, d_statepre = order.gate(back, k["d_statepre"])
            piece = d_statepre.shape[1] // t_size
            parts = [
                lax.dynamic_slice_in_dim(d_statepre, jnp.bitwise_xor(me_t, q) * piece, piece, 1)
                for q in range(t_size)
            ]
            pieces = halving_order(list(range(0, t_size, 2)), 2, t_size)
            state_sum = jnp.concatenate([parts[q] for q in pieces], axis=1) + t_swap(
                jnp.concatenate([parts[q ^ 1] for q in pieces], axis=1), 1
            )
            bit = 2
            while bit < t_size:
                cut = state_sum.shape[1] // 2
                state_sum = state_sum[:, :cut] + t_swap(state_sum[:, cut:], bit)
                bit *= 2
            k["shared"] = jnp.concatenate([state_sum, k["kv_sum"]], axis=1).astype(bf16)
            rows_back = lax.slice_in_dim(back, index * count, (index + 1) * count, axis=0)
            norm_own, norm_other = halves(right_trans(rows_back, in_weight))
            k["norm_own"] = norm_own + t_swap(norm_other, 1)
            unit_own = mine(k["unit_one"])
            k["g_input_gain"] = jnp.sum(k["norm_own"] * unit_own, axis=0)
            order.mark(k["norm_own"])

        slots = []
        for index in range(micro):
            slot = tokens[index]
            if index:
                (slot,) = order.gate(slot)
            slots.append(forward(index, slot))
        held = None
        for index in range(micro):
            held = feed_forward(index, slots[index], held)
        inner_all, d_gate_all, d_up_all = held

        def joined(name):
            return jnp.concatenate([k[name] for k in slots], axis=0)

        def relative_columns(values):
            blocks = halving_order(list(range(dp_size)), 1, dp_size)
            return jnp.concatenate(
                [
                    lax.dynamic_slice_in_dim(values, jnp.bitwise_xor(me_dp, r) * block, block, 1)
                    for r in blocks
                ],
                axis=1,
            )

        def scattered(part, dimension):
            return lax.psum_scatter(part, "dp", scatter_dimension=dimension, tiled=True)

        (cot_all,) = order.gate(joined("cot_low"))
        part_down = left_trans(inner_all, cot_all)
        order.mark(part_down)
        g_down = scattered(part_down, 1)
        first, last = slots
        in_weight = jnp.concatenate(order.gate(*in_weights), axis=1)
        order.mark(in_weight)
        back_head(first)
        (two_all,) = order.gate(joined("normed_two"))
        part_gate = order.point(left_trans(two_all, d_gate_all))
        order.mark(part_gate)
        g_gate = scattered(part_gate, 0)
        (two_all,) = order.gate(two_all)
        part_up = order.point(left_trans(two_all, d_up_all))
        order.mark(part_up)
        g_up = scattered(part_up, 0)
        for index, k in enumerate(slots):
            output_sum(index, k)
        back_head(last)
        back_first = back_mixers(0, first, None)
        back_inputs(0, first, back_first)
        back = back_mixers(1, last, back_first)
        back_inputs(1, last, back)
        one_columns = relative_columns(order.gate(joined("normed"))[0])
        part_outs = left_trans(relative_columns(joined("d_mixed")), joined("mixer"))
        part_early = left_trans(one_columns, back[:, : channels + heads_width])
        part_late = left_trans(
            one_columns,
            jnp.concatenate(
                [back[:, places["xpre"]], joined("shared"), back[:, places["step"]]], axis=1
            ),
        )

        def total(name):
            value = slots[0][name]
            for k in slots[1:]:
                value = value + k[name]
            return value

        names = [
            "g_conv_state_weight", "g_conv_state_bias", "g_input_gain", "g_ffn_gain",
            "g_conv_weight", "g_conv_bias", "g_step_bias", "g_decay_log", "g_skip",
            "g_mamba_gain",
        ]
        small = {name: total(name) for name in names}
        vector = jnp.concatenate([small[name].reshape(-1) for name in names])
        vector_rows = -(-vector.size // (8 * LANES)) * 8
        vector = jnp.pad(vector, (0, vector_rows * LANES - vector.size)).reshape(-1, LANES)
        shared_size = sum(small[name].size for name in names[:4])
        shared_rows = -(-shared_size // (8 * LANES)) * 8

        sums = [first["norm_own"], first["ffn_own"], last["ffn_own"], last["norm_own"]]
        rests = [
            (0, first["d_hidden_own"], mine(first["unit_one"]), mine(first["inv_one"])),
            (0, first["hidden"]),
            (1, last["hidden"]),
            (1, last["d_hidden_own"], mine(last["unit_one"]), mine(last["inv_one"])),
        ]
        (g_outs, g_early, g_late), out, in_grad, vector, wide_vector = scatter_all(
            dp_size, t_size, [part_outs, part_early, part_late], sums, rests, input_gain[None],
            vector, shared_rows,
        )
        vector, wide_vector = vector.reshape(-1), wide_vector.reshape(-1)
        start = 0
        for name in names:
            shape, size = small[name].shape, small[name].size
            source = wide_vector if start < shared_size else vector
            small[name] = source[start : start + size].reshape(shape)
            start += size
        place = me_dp * t_size + me_t
        share = conv_state_bias.shape[0] // (dp_size * t_size)
        g_conv_state_weight = lax.dynamic_slice_in_dim(
            small["g_conv_state_weight"], place * share, share, 1
        )
        g_conv_state_bias = lax.dynamic_slice_in_dim(
            small["g_conv_state_bias"], place * share, share, 0
        )
        g_input_gain = lax.dynamic_slice_in_dim(small["g_input_gain"], me_dp * block, block, 0)
        g_ffn_gain = lax.dynamic_slice_in_dim(small["g_ffn_gain"], me_dp * block, block, 0)
        heads = [small[name] for name in names[4:]]

        shared_end = channels + joined("shared").shape[1]
        g_step = g_late[:, shared_end : shared_end + local_heads]
        g_late = g_late[:, :shared_end]
        g_outs = g_outs.T

        mamba_cols = mamba_in_weight.shape[1]
        tail = g_late[:, mamba_cols:]
        sub = block // t_size
        rowsets = []
        for q in range(t_size):
            part = lax.dynamic_slice_in_dim(tail, jnp.bitwise_xor(me_t, q) * sub, sub, 0)
            rowsets.append(part if q == 0 else t_swap(part, q))
        stacked = jnp.stack(rowsets)
        piece = state_weight.shape[1] // t_size
        sources = [
            lax.dynamic_index_in_dim(stacked, jnp.bitwise_xor(me_t, j), 0, keepdims=False)
            for j in range(t_size)
        ]
        g_state = jnp.concatenate([s[:, :piece] for s in sources], axis=1)
        pairs = t_size // 2
        g_kv = jnp.concatenate(
            [sources[(b % pairs) * 2 + b // pairs][:, piece:] for b in range(t_size)], axis=1
        )
        gate_cols = mamba_gate_weight.shape[1]
        mamba_rows = mamba_out_weight.shape[0]
        return (
            out,
            in_grad,
            g_input_gain,
            g_early[:, :gate_cols],
            g_late[:, :mamba_cols],
            g_state,
            g_step,
            heads[0],
            heads[1],
            g_conv_state_weight,
            g_conv_state_bias,
            heads[2],
            heads[3],
            heads[4],
            heads[5],
            g_outs[:mamba_rows],
            g_early[:, gate_cols:],
            g_kv,
            g_outs[mamba_rows:],
            g_ffn_gain,
            g_gate,
            g_up,
            g_down,
        )

    return per_device


def solution(mesh):
    placed = (
        P("dp", None, None),
        P("dp"),
        P("dp", None, None),
        P(),
        P(None, "tensor"),
        P(None, "tensor"),
        P(),
        P(None, "tensor"),
        P(None, "tensor"),
        P("tensor"),
        P(),
        P(),
        P("tensor"),
        P("tensor"),
        P("tensor"),
        P("tensor"),
        P("tensor", None),
        P(None, "tensor"),
        P(),
        P("tensor", None),
        P(),
        P(None, "tensor"),
        P(None, "tensor"),
        P("tensor", None),
    )
    return jax.shard_map(
        make_per_device(mesh.shape["dp"], mesh.shape["tensor"]),
        mesh=mesh,
        in_specs=placed,
        out_specs=(
            P("dp", None, None),
            P("dp", None, None),
            P("dp"),
            P("dp", "tensor"),
            P("dp", "tensor"),
            P(("dp", "tensor"), None),
            P("dp", "tensor"),
            P(None, "tensor"),
            P("tensor"),
            P(None, ("dp", "tensor")),
            P(("dp", "tensor")),
            P("tensor"),
            P("tensor"),
            P("tensor"),
            P("tensor"),
            P("tensor", "dp"),
            P("dp", "tensor"),
            P(("dp", "tensor"), None),
            P("tensor", "dp"),
            P("dp"),
            P("dp", "tensor"),
            P("dp", "tensor"),
            P("tensor", "dp"),
        ),
        check_vma=False,
    )
```

```python
import functools

import jax
import jax.numpy as jnp
from jax import lax
from jax.experimental import pallas as pl
from jax.experimental.pallas import tpu as pltpu
from jax.sharding import PartitionSpec as P

MHDIM = 64
STATE = 256
AHEADS = 8
KVHEADS = 2
AHDIM = 128
DSSM = 3072

epsilon = 1e-05
rope_base = 100000000000.0
f32 = jnp.float32
bf16 = jnp.bfloat16


def plain_dot(left, right):
    return jnp.dot(left, right, preferred_element_type=f32)


def right_trans(left, right):
    return lax.dot_general(left, right, (((1,), (1,)), ((), ())), preferred_element_type=f32)


def left_trans(left, right):
    return lax.dot_general(left, right, (((0,), (0,)), ((), ())), preferred_element_type=f32)


def silu_slope(values):
    sig = jax.nn.sigmoid(values)
    return sig * (1.0 + values * (1.0 - sig))


MESH = pl.DeviceIdType.MESH
LANES = 128
BLOCK = 128


def shifted(values, steps, row):
    if steps == 0:
        return values
    count = values.shape[0]
    moved = pltpu.roll(values, steps % count, 0)
    if steps > 0:
        return jnp.where(row >= steps, moved, 0.0)
    return jnp.where(row < count + steps, moved, 0.0)


def tap_sum(values, taps, bias):
    row = lax.broadcasted_iota(jnp.int32, values.shape, 0)
    width = taps.shape[0]
    total = jnp.zeros_like(values) + bias
    for k in range(width):
        total = total + shifted(values, width - 1 - k, row) * taps[k : k + 1, :]
    return total


def tap_back(grads, values, taps):
    row = lax.broadcasted_iota(jnp.int32, values.shape, 0)
    width = taps.shape[0]
    back = jnp.zeros_like(values)
    tap_grads = []
    for k in range(width):
        steps = width - 1 - k
        back = back + shifted(grads, -steps, row) * taps[k : k + 1, :]
        tap_grads.append(jnp.sum(grads * shifted(values, steps, row), axis=0, keepdims=True))
    return back, jnp.concatenate(tap_grads, axis=0)


def column_of(values, lane, index):
    return jnp.sum(jnp.where(lane == index, values, 0.0), axis=1, keepdims=True)


def exact_dot(left, right):
    return jnp.dot(left, right, precision=lax.Precision.HIGHEST, preferred_element_type=f32)


def turned(values, cosine, sine):
    return values * cosine + pltpu.roll(values, AHDIM // 2, 1) * sine


def scores_of(query, keys, lo, hi, length):
    scores = right_trans(query[lo:hi], keys[:hi]) * AHDIM ** (-0.5)
    t = lax.broadcasted_iota(jnp.int32, (hi - lo, hi), 0) + lo
    s = lax.broadcasted_iota(jnp.int32, (hi - lo, hi), 1)
    return scores, (t >= s) & (s < length)


def attention_forward(query_pre, key_pre, value_pre, cosine, sine, length, query, keys, values, logs, context):
    count, width = query.shape
    keys[...] = turned(key_pre, cosine, sine).astype(bf16)
    values[...] = value_pre.astype(bf16)
    lane = lax.broadcasted_iota(jnp.int32, (count, LANES), 1)
    kept = jnp.zeros((count, LANES), f32)
    for h in range(width // AHDIM):
        lanes = slice(h * AHDIM, (h + 1) * AHDIM)
        query[:, lanes] = turned(query_pre[:, lanes], cosine, sine).astype(bf16)
        found = []
        for i in range(count // BLOCK):
            lo, hi = i * BLOCK, (i + 1) * BLOCK
            scores, valid = scores_of(query[:, lanes], keys[...], lo, hi, length)
            masked = jnp.where(valid, scores, -1e30)
            peak = jnp.max(masked, axis=1, keepdims=True)
            expo = jnp.exp(masked - peak)
            total = jnp.sum(expo, axis=1, keepdims=True)
            found.append(peak + jnp.log(total))
            probs = (expo / total).astype(bf16)
            context[lo:hi, lanes] = plain_dot(probs, values[:hi, :]).astype(bf16)
        kept = jnp.where(lane == h, jnp.concatenate(found, axis=0), kept)
    logs[...] = kept


def attention_backward(d_context, query, keys, values, logs, cosine, sine, length, d_query_pre, d_keys, d_values):
    count, width = query.shape
    lane = lax.broadcasted_iota(jnp.int32, (count, LANES), 1)
    scale = AHDIM ** (-0.5)
    key_total = jnp.zeros((count, AHDIM), f32)
    value_total = jnp.zeros((count, AHDIM), f32)
    for h in range(width // AHDIM):
        lanes = slice(h * AHDIM, (h + 1) * AHDIM)
        log = column_of(logs[...], lane, h)
        pieces = []
        for i in range(count // BLOCK):
            lo, hi = i * BLOCK, (i + 1) * BLOCK
            scores, valid = scores_of(query[:, lanes], keys[...], lo, hi, length)
            probs = jnp.where(valid, jnp.exp(scores - log[lo:hi]), 0.0)
            grads = d_context[lo:hi, lanes]
            d_probs = right_trans(grads, values[:hi, :])
            delta = jnp.sum(probs * d_probs, axis=1, keepdims=True)
            d_scores = (probs * (d_probs - delta)).astype(bf16)
            pieces.append(plain_dot(d_scores, keys[:hi, :]) * scale)
            d_key = left_trans(d_scores, query[lo:hi, lanes]) * scale
            d_value = left_trans(probs.astype(bf16), grads)
            if hi < count:
                rest = jnp.zeros((count - hi, AHDIM), f32)
                d_key = jnp.concatenate([d_key, rest], axis=0)
                d_value = jnp.concatenate([d_value, rest], axis=0)
            key_total = key_total + d_key
            value_total = value_total + d_value
        d_query_pre[:, lanes] = turned(jnp.concatenate(pieces, axis=0), cosine, -sine).astype(bf16)
    d_keys[...] = turned(key_total, cosine, -sine)
    d_values[...] = value_total


def columns_of(channels, heads_width):
    places, start = {}, 0
    for name, size in (
        ("zgate", channels), ("query", heads_width), ("xpre", channels), ("state", 2 * STATE),
        ("key", AHDIM), ("value", AHDIM), ("step", LANES),
    ):
        places[name] = slice(start, start + size)
        start += size
    return places, start


def forward_kernel(
    lengths, zgate, query_pre, xpre, statepre, key_pre, value_pre, steppre, cosine, sine, conv_weight, conv_bias, state_taps, state_bias, step_bias, rates,
    skip_rep, gated, ssd, square, xconv, sconv, stepsize, cumul, inner, query, keys, values, logs,
    context, cumul_rows, *, slot,
):
    attention_forward(
        query_pre, key_pre[...], value_pre[...],
        cosine[...], sine[...], lengths[slot], query, keys, values, logs, context,
    )
    count, channels = xpre.shape
    xlin = tap_sum(xpre[...], conv_weight[...], conv_bias[...])
    xconv[...] = (xlin * jax.nn.sigmoid(xlin)).astype(bf16)
    slin = tap_sum(statepre[...], state_taps[...], state_bias[...])
    sconv[...] = (slin * jax.nn.sigmoid(slin)).astype(bf16)
    inner[...] = right_trans(sconv[:, STATE:], sconv[:, :STATE])
    step = jax.nn.softplus(steppre[...] + step_bias[...])
    stepsize[...] = step
    row = lax.broadcasted_iota(jnp.int32, (count, count), 0)
    col = lax.broadcasted_iota(jnp.int32, (count, count), 1)
    total = exact_dot(jnp.where(row >= col, 1.0, 0.0), -step * rates[...])
    cumul[...] = total
    cumul_rows[...] = total.T
    square[...] = jnp.zeros_like(square)

    def pair(p):
        lanes = slice(p * LANES, (p + 1) * LANES)
        lane = lax.broadcasted_iota(jnp.int32, (count, LANES), 1)
        xvals = xconv[:, lanes].astype(f32)
        low_half = lane < MHDIM
        step_rep = jnp.where(
            low_half, column_of(stepsize[...], lane, 2 * p), column_of(stepsize[...], lane, 2 * p + 1)
        )
        weighted = (step_rep * xvals).astype(bf16)
        columns = [column_of(cumul[...], lane, 2 * p + h) for h in range(2)]
        for i in range(count // BLOCK):
            lo, hi = i * BLOCK, (i + 1) * BLOCK
            results = []
            for h in range(2):
                differ = columns[h][lo:hi] - cumul_rows[2 * p + h : 2 * p + h + 1, :hi]
                t = lax.broadcasted_iota(jnp.int32, (BLOCK, hi), 0) + lo
                s = lax.broadcasted_iota(jnp.int32, (BLOCK, hi), 1)
                decay = jnp.exp(jnp.where(t >= s, differ, -1e30))
                mixing = (inner[lo:hi, :hi] * decay).astype(bf16)
                results.append(plain_dot(mixing, weighted[:hi]))
            half = jnp.where(low_half[lo:hi], results[0], results[1])
            half = half + skip_rep[:, lanes] * xvals[lo:hi]
            ssd[lo:hi, lanes] = half
            z = zgate[lo:hi, lanes]
            value = half * (z * jax.nn.sigmoid(z))
            gated[lo:hi, lanes] = value
            square[lo:hi, :] += value * value

    for p in range(channels // LANES):
        pair(p)


def full(*shape):
    return jax.ShapeDtypeStruct(shape, f32)


def low(*shape):
    return jax.ShapeDtypeStruct(shape, bf16)


def in_vmem(count):
    return [pl.BlockSpec(memory_space=pltpu.VMEM)] * count


def in_hbm(shapes):
    return tuple(pltpu.HBM(s.shape, s.dtype) for s in shapes)


def whole_blocks(shapes):
    return [pl.BlockSpec(s.shape, lambda i, n=len(s.shape): (0,) * n) for s in shapes]


def mixers_forward(slot, lengths, *operands):
    count, channels = operands[0].shape
    heads_width = operands[1].shape[1]
    shapes = (
        full(count, channels), full(count, channels), full(count, LANES), low(count, channels),
        low(count, 2 * STATE), full(count, LANES), full(count, LANES), full(count, count),
        low(count, heads_width), low(count, AHDIM), low(count, AHDIM), full(count, LANES),
        low(count, heads_width),
    )
    return pl.pallas_call(
        functools.partial(forward_kernel, slot=slot),
        grid=(1,),
        out_shape=in_hbm(shapes),
        in_specs=[pl.BlockSpec(memory_space=pltpu.SMEM)] + in_vmem(len(operands)),
        out_specs=tuple(whole_blocks(shapes)),
        scratch_shapes=[pltpu.VMEM((LANES, count), f32)],
        compiler_params=pltpu.CompilerParams(vmem_limit_bytes=48 * 2**20),
        cost_estimate=pl.CostEstimate(
            flops=10**6, bytes_accessed=10**6, transcendentals=10**3
        ),
    )(lengths, *operands)


def backward_kernel(
    lengths, d_scaled_in, d_context_in, gated_in, inv_cross, gain, zgate, xpre, statepre, steppre,
    ssd, xconv, sconv, stepsize, cumul, inner,
    query, keys, values, logs, cosine, sine, conv_weight, conv_bias, state_taps, state_bias,
    step_bias, rates, skip_rep,
    back, d_statepre, d_keys, d_values, g_conv, g_state, g_heads, g_skip, g_gain,
    d_ssd, d_xvals, cumul_rows, d_inner, row_sums, col_sums, d_step, *, slot, places,
):
    count, channels = ssd.shape
    attention_backward(
        d_context_in[...].astype(bf16), query, keys, values, logs, cosine[...], sine[...],
        lengths[slot], back.at[:, places["query"]], d_keys, d_values,
    )
    back[:, places["key"]] = d_keys[...].astype(bf16)
    back[:, places["value"]] = d_values[...].astype(bf16)
    d_zgate, d_xpre = back.at[:, places["zgate"]], back.at[:, places["xpre"]]
    d_steppre = back.at[:, places["step"]]
    d_scaled = d_scaled_in[...]
    g_gain[...] = jnp.sum(d_scaled * gated_in[...] * inv_cross[:, 0:1], axis=0, keepdims=True)
    inv = inv_cross[:, 0:1]
    cross = inv_cross[:, 1:2]
    d_gated = inv * (d_scaled * gain[...]) - gated_in[...] * cross
    z = zgate[...]
    sig = jax.nn.sigmoid(z)
    d_low = (d_gated * (z * sig)).astype(bf16)
    d_ssd[...] = d_low
    d_zgate[...] = (d_gated * ssd[...] * sig * (1.0 + z * (1.0 - sig))).astype(bf16)
    g_skip[...] = jnp.sum(d_low.astype(f32) * xconv[...].astype(f32), axis=0, keepdims=True)
    cumul_rows[...] = cumul[...].T
    d_inner[...] = jnp.zeros_like(d_inner)
    row_sums[...] = jnp.zeros_like(row_sums)
    col_sums[...] = jnp.zeros_like(col_sums)
    d_step[...] = jnp.zeros_like(d_step)

    def pair(p):
        lanes = slice(p * LANES, (p + 1) * LANES)
        lane = lax.broadcasted_iota(jnp.int32, (count, LANES), 1)
        low_half = lane < MHDIM
        xvals = xconv[:, lanes].astype(f32)
        step_rep = jnp.where(
            low_half, column_of(stepsize[...], lane, 2 * p), column_of(stepsize[...], lane, 2 * p + 1)
        )
        weighted = (step_rep * xvals).astype(bf16)
        grads = d_ssd[:, lanes]
        columns = [column_of(cumul[...], lane, 2 * p + h) for h in range(2)]
        pieces = []
        for h in range(2):
            only = jnp.where(low_half == (h == 0), grads, jnp.zeros_like(grads))
            back_part = jnp.zeros((count, LANES), f32)
            sums = []
            col_total = jnp.zeros((1, count), f32)
            for i in range(count // BLOCK):
                lo, hi = i * BLOCK, (i + 1) * BLOCK
                differ = columns[h][lo:hi] - cumul_rows[2 * p + h : 2 * p + h + 1, :hi]
                t = lax.broadcasted_iota(jnp.int32, (BLOCK, hi), 0) + lo
                s = lax.broadcasted_iota(jnp.int32, (BLOCK, hi), 1)
                decay = jnp.exp(jnp.where(t >= s, differ, -1e30))
                mixing = inner[lo:hi, :hi] * decay
                part = left_trans(mixing.astype(bf16), only[lo:hi])
                d_mixing = right_trans(only[lo:hi], weighted[:hi])
                d_inner[lo:hi, :hi] += d_mixing * decay
                flow = d_mixing * mixing
                sums.append(jnp.sum(flow, axis=1, keepdims=True))
                down = jnp.sum(flow, axis=0, keepdims=True)
                if hi < count:
                    part = jnp.concatenate([part, jnp.zeros((count - hi, LANES), f32)], axis=0)
                    down = jnp.concatenate([down, jnp.zeros((1, count - hi), f32)], axis=1)
                back_part = back_part + part
                col_total = col_total + down
            here = lane == 2 * p + h
            row_sums[...] = jnp.where(here, jnp.concatenate(sums, axis=0), row_sums[...])
            col_sums[2 * p + h : 2 * p + h + 1, :] = col_total
            pieces.append(back_part)
        d_weighted = pieces[0] + pieces[1]
        d_xvals[:, lanes] = grads.astype(f32) * skip_rep[:, lanes] + d_weighted * step_rep
        product = d_weighted * xvals
        for h in range(2):
            value = jnp.sum(
                jnp.where(low_half == (h == 0), product, 0.0), axis=1, keepdims=True
            )
            d_step[...] = jnp.where(lane == 2 * p + h, value, d_step[...])

    for p in range(channels // LANES):
        pair(p)

    d_cumul = row_sums[...] - col_sums[...].T
    row = lax.broadcasted_iota(jnp.int32, (count, count), 0)
    col = lax.broadcasted_iota(jnp.int32, (count, count), 1)
    d_logdecay = exact_dot(jnp.where(row <= col, 1.0, 0.0), d_cumul)
    rate = rates[...]
    d_full = (d_step[...] - d_logdecay * rate) * jax.nn.sigmoid(steppre[...] + step_bias[...])
    d_steppre[...] = d_full.astype(bf16)
    g_heads[0:1, :] = jnp.sum(d_full, axis=0, keepdims=True)
    g_heads[1:2, :] = jnp.sum(-d_logdecay * stepsize[...] * rate, axis=0, keepdims=True)

    d_in = d_inner[...].astype(bf16)
    d_c = plain_dot(d_in, sconv[:, :STATE])
    d_b = left_trans(d_in, sconv[:, STATE:])
    slin = tap_sum(statepre[...], state_taps[...], state_bias[...])
    d_slin = jnp.concatenate([d_b, d_c], axis=1) * silu_slope(slin)
    back_state, tap_grads = tap_back(d_slin, statepre[...], state_taps[...])
    d_statepre[...] = back_state
    back[:, places["state"]] = back_state.astype(bf16)
    g_state[...] = jnp.concatenate([tap_grads, jnp.sum(d_slin, axis=0, keepdims=True)], axis=0)
    xlin = tap_sum(xpre[...], conv_weight[...], conv_bias[...])
    d_xlin = d_xvals[...] * silu_slope(xlin)
    back_x, tap_grads = tap_back(d_xlin, xpre[...], conv_weight[...])
    d_xpre[...] = back_x.astype(bf16)
    g_conv[...] = jnp.concatenate([tap_grads, jnp.sum(d_xlin, axis=0, keepdims=True)], axis=0)


def mixers_backward(slot, slots, held, lengths, *operands):
    count, channels = operands[0].shape
    heads_width = operands[1].shape[1]
    taps = operands[-7].shape[0]
    width = columns_of(channels, heads_width)[1]
    kernel = functools.partial(
        backward_kernel, slot=slot, places=columns_of(channels, heads_width)[0]
    )
    aliases = {}
    extra_specs, extra = [], ()
    if held is not None:
        aliases = {0: 0}
        extra_specs, extra = [pl.BlockSpec(memory_space=pl.ANY)], (held,)
        inside = kernel
        kernel = lambda _, *refs: inside(*refs)
    shapes = (
        full(count, 2 * STATE), full(count, AHDIM), full(count, AHDIM), full(taps + 1, channels),
        full(taps + 1, 2 * STATE), full(2, LANES), full(1, channels), full(1, channels),
    )
    return pl.pallas_call(
        kernel,
        grid=(1,),
        out_shape=in_hbm((low(slots * count, width),) + shapes),
        in_specs=extra_specs
        + [pl.BlockSpec(memory_space=pltpu.SMEM)]
        + in_vmem(len(operands)),
        out_specs=tuple(
            [pl.BlockSpec((count, width), lambda i: (slot, 0))] + whole_blocks(shapes)
        ),
        scratch_shapes=[
            pltpu.VMEM((count, channels), bf16),
            pltpu.VMEM((count, channels), f32),
            pltpu.VMEM((LANES, count), f32),
            pltpu.VMEM((count, count), f32),
            pltpu.VMEM((count, LANES), f32),
            pltpu.VMEM((LANES, count), f32),
            pltpu.VMEM((count, LANES), f32),
        ],
        input_output_aliases=aliases,
        compiler_params=pltpu.CompilerParams(vmem_limit_bytes=56 * 2**20),
        cost_estimate=pl.CostEstimate(
            flops=10**6, bytes_accessed=10**6, transcendentals=10**3
        ),
    )(*extra, lengths, *operands)


def feed_forward_kernel(normed, cot, gate_weight, up_weight, down_weight, *refs):
    inner, d_gate, d_up, back = refs[-4:]
    gate = plain_dot(normed[...], gate_weight[...])
    upper = plain_dot(normed[...], up_weight[...])
    d_inner = right_trans(cot[...], down_weight[...])
    sig = jax.nn.sigmoid(gate)
    silu = gate * sig
    inner[...] = (silu * upper).astype(bf16)
    d_gate[...] = (d_inner * upper * sig * (1.0 + gate * (1.0 - sig))).astype(bf16)
    d_up[...] = (d_inner * silu).astype(bf16)
    part = right_trans(d_gate[...], gate_weight[...]) + right_trans(d_up[...], up_weight[...])

    @pl.when(pl.program_id(0) == 0)
    def _():
        back[...] = part

    @pl.when(pl.program_id(0) > 0)
    def _():
        back[...] += part


def feed_forward_all(slot, slots, held, normed, cot, gate_weight, up_weight, down_weight):
    count, width = normed.shape
    hidden = gate_weight.shape[1]
    block = min(512, hidden)
    rows = pl.BlockSpec((count, width), lambda j: (0, 0))
    columns = pl.BlockSpec((width, block), lambda j: (0, j))
    joint = pl.BlockSpec((count, block), lambda j: (slot, j))
    extra = () if held is None else tuple(held)
    return pl.pallas_call(
        feed_forward_kernel,
        grid=(hidden // block,),
        out_shape=tuple([low(slots * count, hidden)] * 3 + [full(count, width)]),
        in_specs=[
            rows, rows, columns, columns, pl.BlockSpec((block, width), lambda j: (j, 0))
        ] + [pl.BlockSpec(memory_space=pl.ANY)] * len(extra),
        out_specs=(joint, joint, joint, rows),
        input_output_aliases={5 + n: n for n in range(len(extra))},
        compiler_params=pltpu.CompilerParams(vmem_limit_bytes=56 * 2**20),
        cost_estimate=pl.CostEstimate(flops=10**6, bytes_accessed=10**6, transcendentals=10**3),
    )(normed, cot, gate_weight, up_weight, down_weight, *extra)


def swap(values, axis, size, bit):
    return lax.ppermute(values, axis, [(i, i ^ bit) for i in range(size)])


def halving_order(members, bit, limit):
    if bit >= limit:
        return members
    low = halving_order([m for m in members if not m & bit], bit * 2, limit)
    high = halving_order([m for m in members if m & bit], bit * 2, limit)
    return low + high


class Order:
    def __init__(self):
        self.last = ()
        self.queue = []

    def point(self, value, skip=0):
        if len(self.queue) <= skip:
            return value
        return lax.optimization_barrier((value, self.queue.pop(skip)))[0]

    def gate(self, *values):
        return lax.optimization_barrier((values, self.last))[0]

    def mark(self, *values):
        self.last = values


def scatter_all(size, t_size, parts, cuts, halves, rests, gain, vector, shared_rows):
    rows = parts[0].shape[0]
    works = len(parts)
    share = rows // size
    chunk = min(256, rows // 4)
    levels = size.bit_length() - 1
    spans = []
    for level in range(1, levels):
        lo, hi = rows >> (level + 1), rows >> level
        step = min(chunk, hi - lo)
        spans += [(level, start, step) for start in range(hi - step, lo - 1, -step)]
    spans.append((levels, 0, share))
    pieces = [(w,) + span for w in range(works) for span in spans]
    per_work = len(spans)
    widths = [p.shape[1] for p in parts]
    ranges = []
    for cut in cuts:
        stops = [sum(cut[: n + 1]) for n in range(len(cut))]
        ranges.append([(stop - size_, size_) for stop, size_ in zip(stops, cut)])
    outputs = sum(len(cut) for cut in cuts)
    wide = max(widths)
    extra = len(halves)
    half_shape = halves[0].shape
    half, width = half_shape
    slots = 1 + max(rest[0] for rest in rests)
    extras = [value for rest in rests for value in rest[1:]]
    wholes = [n for n, rest in enumerate(rests) if len(rest) == 2]

    def kernel(*refs):
        held_in, refs = refs[:works], refs[works:]
        own, refs = refs[:extra], refs[extra:]
        beside = []
        for rest in rests:
            beside.append(refs[: len(rest) - 1])
            refs = refs[len(rest) - 1 :]
        gain_ref, small, refs = refs[0], refs[1], refs[2:]
        outs = []
        for cut in cuts:
            outs.append(refs[: len(cut)])
            refs = refs[len(cut) :]
        far, refs = refs[:extra], refs[extra:]
        result, grad, small_out, wide_out, refs = refs[0], refs[1], refs[2], refs[3], refs[4:]
        loads, pair_loads, totals, low_rows, theirs, refs = (
            refs[0], refs[1], refs[2], refs[3], refs[4], refs[5:]
        )
        boxes, wide_boxes, turned_rows, refs = refs[0], refs[1], refs[2], refs[3:]
        landed, refs = refs[:works], refs[works:]
        later, refs = refs[: works * (levels - 1)], refs[works * (levels - 1) :]
        load_sems, out_sems, x_send, x_recv, z_send, z_recv, y_sems, c_sems, pair_sems, v_sems, w_sems = refs
        me = lax.axis_index("dp")
        spot = lax.axis_index("tensor")

        def neighbour(bit):
            return spot + bit - 2 * bit * lax.rem(spot // bit, 2)


        def partner(level):
            bit = 1 << level
            return me + bit - 2 * bit * lax.rem(me // bit, 2)

        barrier = pltpu.get_barrier_semaphore()
        for other in range(1, size):
            pl.semaphore_signal(
                barrier, inc=1, device_id={"dp": lax.rem(me + other, size)}, device_id_type=MESH
            )
        for other in range(1, t_size):
            pl.semaphore_signal(
                barrier, inc=1, device_id={"tensor": lax.rem(spot + other, t_size)},
                device_id_type=MESH,
            )
        pl.semaphore_wait(barrier, size + t_size - 2)

        def small_copy(other):
            return pltpu.make_async_remote_copy(
                src_ref=small, dst_ref=boxes.at[size - other], send_sem=v_sems.at[0, other],
                recv_sem=v_sems.at[1, size - other],
                device_id={"dp": lax.rem(me + other, size)}, device_id_type=MESH,
            )

        def wide_copy(other):
            return pltpu.make_async_remote_copy(
                src_ref=small_out.at[pl.ds(0, shared_rows), :], dst_ref=wide_boxes.at[t_size - other],
                send_sem=w_sems.at[0, other], recv_sem=w_sems.at[1, t_size - other],
                device_id={"tensor": lax.rem(spot + other, t_size)}, device_id_type=MESH,
            )

        def in_turn(kept, count, place, rows):
            total = jnp.zeros((rows, LANES), f32)
            for number in range(count):
                offset = lax.rem(number - place + count, count)
                total = total + kept[offset]
            return total

        def small_sums(stage):
            if stage == 0:
                boxes[0] = small[...]
                for other in range(1, size):
                    small_copy(other).wait_recv()
                small_out[...] = in_turn(boxes, size, me, small.shape[0])
                for other in range(1, t_size):
                    wide_copy(other).start()
            else:
                wide_boxes[0] = small_out[:shared_rows, :]
                for other in range(1, t_size):
                    wide_copy(other).wait_recv()
                wide_out[...] = in_turn(wide_boxes, t_size, spot, shared_rows)


        def y_copy(e):
            return pltpu.make_async_remote_copy(
                src_ref=own[e], dst_ref=far[e], send_sem=y_sems.at[0, e], recv_sem=y_sems.at[1, e],
                device_id={"tensor": neighbour(2)}, device_id_type=MESH,
            )

        core = lax.rem(spot, 2)

        def rows_of(place):
            return pl.ds(pl.multiple_of(place * half, 8), half)

        def c_copy(e):
            slot = rests[e][0]
            if e in wholes:
                target = theirs.at[wholes.index(e)]
            else:
                target = grad.at[slot, rows_of(core), :]
            return pltpu.make_async_remote_copy(
                src_ref=totals.at[e], dst_ref=target, send_sem=c_sems.at[0, e],
                recv_sem=c_sems.at[1, e], device_id={"tensor": neighbour(1)}, device_id_type=MESH,
            )

        def fetch(source, place):
            return pltpu.make_async_copy(source, pair_loads.at[place], pair_sems.at[0, place])

        def keep(e, place):
            slot = rests[e][0]
            if e in wholes:
                n = 2 * wholes.index(e) + place
                target = result.at[slot, rows_of(core if place == 0 else 1 - core), :]
                return pltpu.make_async_copy(low_rows.at[n], target, pair_sems.at[1 + place, e])
            return pltpu.make_async_copy(
                totals.at[e], grad.at[slot, rows_of(core), :], pair_sems.at[1, e]
            )

        def exchange(e):
            y_copy(e).wait_recv()
            sources = [own[e], far[e]]
            if e in wholes:
                sources.append(beside[e][0].at[pl.ds(0, half), :])
            else:
                sources += [beside[e][0], beside[e][1]]
            for place, source in enumerate(sources):
                fetch(source, place).start()
            for place, source in enumerate(sources):
                fetch(source, place).wait()
            total = pair_loads[0] + pair_loads[1]
            if e in wholes:
                totals[e] = total
                low_rows[2 * wholes.index(e)] = (pair_loads[2] + total).astype(bf16)
            else:
                unit = pair_loads[3]
                scaled = total * gain_ref[...]
                mean = jnp.sum(scaled * unit, axis=1, keepdims=True) / width
                totals[e] = pair_loads[2] + beside[e][2][...] * (scaled - unit * mean)
            c_copy(e).start()
            keep(e, 0).start()

        def complete(e):
            fetch(beside[e][0].at[pl.ds(half, half), :], 0).start()
            c_copy(e).wait_recv()
            fetch(beside[e][0].at[pl.ds(half, half), :], 0).wait()
            n = wholes.index(e)
            low_rows[2 * n + 1] = (pair_loads[0] + theirs[n]).astype(bf16)
            keep(e, 1).start()

        def first_copy(number):
            w, _, start, step = pieces[number]
            return pltpu.make_async_remote_copy(
                src_ref=held_in[w].at[pl.ds(rows // 2 + start, step), :],
                dst_ref=landed[w].at[pl.ds(start, step), :],
                send_sem=x_send.at[number],
                recv_sem=x_recv.at[number],
                device_id={"dp": partner(0)},
                device_id_type=MESH,
            )

        def load(number):
            w, _, start, step = pieces[number]
            return pltpu.make_async_copy(
                held_in[w].at[pl.ds(start, step), :],
                loads.at[number % 2, pl.ds(0, step), pl.ds(0, widths[w])],
                load_sems.at[number % 2],
            )

        def later_copy(number):
            w, level, start, step = pieces[number]
            return pltpu.make_async_remote_copy(
                src_ref=landed[w].at[pl.ds(start, step), :],
                dst_ref=later[w * (levels - 1) + level - 1].at[pl.ds(start - (rows >> (level + 1)), step), :],
                send_sem=z_send.at[number],
                recv_sem=z_recv.at[number],
                device_id={"dp": partner(level)},
                device_id_type=MESH,
            )

        def stores(w):
            copies = []
            for n, (lo, length) in enumerate(ranges[w]):
                if w == 0:
                    source = turned_rows.at[pl.ds(lo, length), :]
                else:
                    source = landed[w].at[pl.ds(0, share), pl.ds(lo, length)]
                copies.append(pltpu.make_async_copy(source, outs[w][n], out_sems.at[w, n]))
            return copies

        for other in range(1, size):
            small_copy(other).start()
        for e in range(extra):
            y_copy(e).start()
        for number in range(len(pieces)):
            first_copy(number).start()
        load(0).start()
        arrived = set()

        def need(w, level, start, step):
            base = rows >> (level + 1)
            for other in range(w * per_work, (w + 1) * per_work):
                _, its_level, its_start, its_step = pieces[other]
                if its_level != level or other in arrived:
                    continue
                if its_start - base < start + step and start < its_start - base + its_step:
                    later_copy(other).wait_recv()
                    arrived.add(other)

        def finish(w):
            level = levels - 1
            need(w, level, 0, share)
            landed[w][:share, :] += later[w * (levels - 1) + level - 1][:share, :]
            if w == 0:
                turned_rows[...] = landed[w][:share, :].T
            for copy in stores(w):
                copy.start()

        for number, (w, level, start, step) in enumerate(pieces):
            load(number).wait()
            if number + 1 < len(pieces):
                load(number + 1).start()
            first_copy(number).wait_recv()
            value = loads[number % 2, :step, : widths[w]] + landed[w][start : start + step, :]
            for before in range(1, min(level, levels - 1)):
                need(w, before, start, step)
                value = value + later[w * (levels - 1) + before - 1][start : start + step, :]
            landed[w][start : start + step, :] = value
            if level < levels:
                later_copy(number).start()
            if w and number == w * per_work + min(2, per_work - 1):
                finish(w - 1)
            if number in (0, 2):
                small_sums(number // 2)
            if number % 2 and number // 2 < extra:
                exchange(number // 2)
            if number % 2 == 0 and number // 2 - 2 in wholes:
                complete(number // 2 - 2)
        for e in range(len(pieces) // 2, extra):
            exchange(e)
        for e in wholes:
            if 2 * (e + 2) >= len(pieces):
                complete(e)
        finish(works - 1)
        for other in range(1, size):
            small_copy(other).wait_send()
        for other in range(1, t_size):
            wide_copy(other).wait_send()
        for e in range(extra):
            y_copy(e).wait_send()
            c_copy(e).wait_send()
            keep(e, 0).wait()
            if e in wholes:
                keep(e, 1).wait()
            else:
                c_copy(e).wait_recv()
        for number, (w, level, start, step) in enumerate(pieces):
            first_copy(number).wait_send()
            if level < levels:
                later_copy(number).wait_send()
        for w in range(works):
            for copy in stores(w):
                copy.wait()

    scratch = [
        pltpu.VMEM((2, chunk, wide), f32),
        pltpu.VMEM((4,) + half_shape, f32),
        pltpu.VMEM((extra,) + half_shape, f32),
        pltpu.VMEM((2 * len(wholes),) + half_shape, bf16),
        pltpu.VMEM((len(wholes),) + half_shape, f32),
        pltpu.VMEM((size,) + vector.shape, f32),
        pltpu.VMEM((t_size, shared_rows, LANES), f32),
        pltpu.VMEM((widths[0], share), f32),
    ]
    scratch += [pltpu.VMEM((rows // 2, n), f32) for n in widths]
    scratch += [
        pltpu.VMEM((rows >> (level + 1), n), f32) for n in widths for level in range(1, levels)
    ]
    scratch += [
        pltpu.SemaphoreType.DMA((2,)),
        pltpu.SemaphoreType.DMA((works, max(len(cut) for cut in cuts))),
    ] + [pltpu.SemaphoreType.DMA((len(pieces),))] * 4
    scratch += [pltpu.SemaphoreType.DMA((n, extra)) for n in (2, 2)]
    scratch += [pltpu.SemaphoreType.DMA((3, max(4, extra)))]
    scratch += [pltpu.SemaphoreType.DMA((2, size)), pltpu.SemaphoreType.DMA((2, t_size))]
    results = pl.pallas_call(
        kernel,
        out_shape=tuple(
            [full(n, share) for n in cuts[0]]
            + [full(share, n) for cut in cuts[1:] for n in cut]
            + [full(*half_shape)] * extra
            + [low(slots, 2 * half, width), full(slots, 2 * half, width)]
            + [full(*vector.shape), full(shared_rows, LANES)]
        ),
        in_specs=[pl.BlockSpec(memory_space=pl.ANY)] * (works + extra)
        + [
            pl.BlockSpec(memory_space=pltpu.VMEM if value.shape[1] == 1 else pl.ANY)
            for value in extras
        ]
        + in_vmem(2),
        out_specs=tuple([pl.BlockSpec(memory_space=pl.ANY)] * (outputs + extra + 2) + in_vmem(2)),
        scratch_shapes=scratch,
        compiler_params=pltpu.CompilerParams(
            collective_id=0, has_side_effects=True, vmem_limit_bytes=60 * 2**20
        ),
        cost_estimate=pl.CostEstimate(
            flops=10**6, bytes_accessed=10**6, transcendentals=0
        ),
    )(*parts, *halves, *extras, gain, vector)
    return results[:outputs], *results[outputs + extra :]


def make_per_device(dp_size, t_size):
    def per_device(
        tokens,
        lengths,
        out_grad,
        input_gain,
        mamba_gate_weight,
        mamba_in_weight,
        state_weight,
        step_weight,
        conv_weight,
        conv_bias,
        conv_state_weight,
        conv_state_bias,
        step_bias,
        decay_log,
        skip_scale,
        mamba_gain,
        mamba_out_weight,
        query_weight,
        key_value_weight,
        attn_out_weight,
        ffn_gain,
        gate_weight,
        up_weight,
        down_weight,
    ):
        micro = tokens.shape[0]
        count = tokens.shape[1]
        width = tokens.shape[2]
        half = count // 2
        local_heads = step_weight.shape[1]
        q_local = query_weight.shape[1] // AHDIM
        kv_width = key_value_weight.shape[1] // 2
        group_size = AHEADS // KVHEADS
        me_dp = lax.axis_index("dp")
        me_t = lax.axis_index("tensor")
        core = lax.rem(me_t, 2)
        kv_head = me_t * q_local // group_size
        key_weight = lax.dynamic_slice_in_dim(key_value_weight, kv_head * AHDIM, AHDIM, 1)
        value_weight = lax.dynamic_slice_in_dim(
            key_value_weight, kv_width + kv_head * AHDIM, AHDIM, 1
        )
        rows = jnp.arange(count)
        freqs = rope_base ** (-(jnp.arange(AHDIM // 2).astype(f32) * 2.0) / AHDIM)
        angles = rows.astype(f32)[:, None] * freqs[None, :]
        cosine, sine = jnp.cos(angles), jnp.sin(angles)
        cosine = jnp.concatenate([cosine, cosine], axis=1)
        sine = jnp.concatenate([-sine, sine], axis=1)
        channels = mamba_in_weight.shape[1]
        heads_width = query_weight.shape[1]
        places, _ = columns_of(channels, heads_width)
        pad_step = LANES - local_heads

        def lane_row(vector):
            return jnp.pad(vector, (0, pad_step))[None]

        mixer_rows = (
            conv_weight, conv_bias[None], conv_state_weight, conv_state_bias[None],
            lane_row(step_bias), lane_row(jnp.exp(decay_log)), jnp.repeat(skip_scale, MHDIM)[None],
        )
        step_lanes = jnp.pad(step_weight, ((0, 0), (0, pad_step)))
        in_weights = (
            mamba_gate_weight, query_weight, mamba_in_weight, state_weight, key_weight,
            value_weight, step_lanes,
        )

        def t_swap(values, bit):
            return swap(values, "tensor", t_size, bit)

        def t_total(values):
            bit = 1
            while bit < t_size:
                values = values + t_swap(values, bit)
                bit *= 2
            return values

        def mine(values):
            return lax.dynamic_slice_in_dim(values, core * half, half, 0)

        def other(values):
            return lax.dynamic_slice_in_dim(values, (1 - core) * half, half, 0)

        def halves(values):
            values = lax.optimization_barrier(values)
            return mine(values), other(values)

        def relative(values):
            return jnp.concatenate([mine(values), other(values)], axis=0)

        def in_order(own, far):
            return jnp.where(
                core == 0,
                jnp.concatenate([own, far], axis=0),
                jnp.concatenate([far, own], axis=0),
            )

        def half_sum(own, far, pieces):
            own = own + t_swap(far, 1)
            bit = 2
            while bit < t_size // 2:
                own = own + t_swap(own, bit)
                bit *= 2
            step = -(-own.shape[0] // (8 * pieces)) * 8
            parts = []
            for start in range(0, own.shape[0], step):
                parts.append(t_swap(own[start : start + step], bit))
            order.queue += parts
            return own, parts

        def add_up(own, parts):
            for part in parts:
                order.queue = [p for p in order.queue if p is not part]
            own, *parts = order.gate(own, *parts)
            return own + jnp.concatenate(parts, axis=0)

        block = width // dp_size

        order = Order()

        def forward(index, slot):
            inputs = slot.astype(f32)
            inv_one = lax.rsqrt(jnp.mean(inputs * inputs, axis=-1, keepdims=True) + epsilon)
            unit_one = inputs * inv_one
            normed = (unit_one * input_gain).astype(bf16)
            normed = order.point(normed)
            pre = [plain_dot(normed, w) for w in in_weights]
            gated, ssd, square, *kept, query, keys, values, logs, context = mixers_forward(
                index, lengths, *pre, cosine, sine, *mixer_rows
            )
            gated = order.point(order.point(gated))
            total_square = t_total(jnp.sum(square, axis=-1))
            inv_mamba = lax.rsqrt(total_square / DSSM + epsilon)[:, None]
            scaled = (gated * inv_mamba * mamba_gain).astype(bf16)
            mixer = jnp.concatenate([scaled, context], axis=1)
            mixed_own, mixed_far = half_sum(
                *halves(plain_dot(scaled, mamba_out_weight) + plain_dot(context, attn_out_weight)),
                3,
            )
            order.mark(mixed_own)
            return dict(
                mixed_own=mixed_own, mixed_far=mixed_far, inputs=inputs, inv_one=inv_one,
                unit_one=unit_one, normed=normed, pre=pre, gated=gated, ssd=ssd, kept=kept,
                attention=(query, keys, values, logs), inv_mamba=inv_mamba, mixer=mixer,
            )

        def feed_forward(index, k, held):
            hidden_own = mine(k["inputs"]) + add_up(k["mixed_own"], k["mixed_far"])
            hidden = order.point(jnp.concatenate([hidden_own, t_swap(hidden_own, 1)], axis=0))
            inv_two = lax.rsqrt(jnp.mean(hidden * hidden, axis=-1, keepdims=True) + epsilon)
            unit_two = hidden * inv_two
            normed_two = (unit_two * ffn_gain).astype(bf16)
            valid = (rows < lengths[index]).astype(f32)[:, None]
            cotangent = relative(out_grad[index].astype(f32) * valid)
            cot_low = cotangent.astype(bf16)
            *held, back = feed_forward_all(
                index, micro, held, normed_two, cot_low, gate_weight, up_weight, down_weight
            )
            back = order.point(order.point(back))
            back_own, back_far = half_sum(back[:half], back[half:], 3)
            order.mark(back_own)
            k.update(
                back_own=back_own, back_far=back_far,
                hidden=hidden, inv_two=inv_two[:half], unit_two=unit_two[:half],
                normed_two=normed_two, cotangent=cotangent, cot_low=cot_low,
            )
            return held

        def output_sum(index, k):
            (inner_ffn,) = order.gate(
                lax.slice_in_dim(inner_all, index * count, (index + 1) * count, axis=0)
            )
            ffn = plain_dot(inner_ffn, down_weight)
            k["ffn_own"] = ffn[:half] + t_swap(ffn[half:], 1)
            order.mark(k["ffn_own"])

        def back_head(k):
            unit_two = k["unit_two"]
            g_ffn_gain = jnp.sum(k["back_own"] * unit_two, axis=0)
            d_normed_two = add_up(k["back_own"], k["back_far"])
            d_unit_two = d_normed_two * ffn_gain
            d_rest = k["inv_two"] * (
                d_unit_two - unit_two * jnp.mean(d_unit_two * unit_two, axis=-1, keepdims=True)
            )
            d_both = k["cotangent"] + jnp.concatenate([d_rest, t_swap(d_rest, 1)], axis=0)
            d_mixed = in_order(d_both[:half], d_both[half:]).astype(bf16)
            d_scaled = right_trans(d_mixed, mamba_out_weight)
            d_context = right_trans(d_mixed, attn_out_weight)
            k["g_ffn_gain"] = g_ffn_gain
            k["d_hidden_own"] = d_both[:half]
            k["d_mixed"], k["d_scaled"], k["d_context"] = d_mixed, d_scaled, d_context
            k["cross"] = t_total(jnp.sum(d_scaled * mamba_gain * k["gated"], axis=-1))[:, None]
            order.mark(d_scaled, d_context)

        def back_mixers(index, k, held):
            d_scaled, cross = order.gate(k["d_scaled"], k["cross"])
            inv = k["inv_mamba"]
            inv_cross = jnp.concatenate([inv, inv**3 * cross / DSSM], axis=1)
            inv_cross = jnp.pad(inv_cross, ((0, 0), (0, LANES - 2)))
            back, d_statepre, d_keys, d_values, g_conv, g_state, g_heads, g_skip, g_gain = (
                mixers_backward(
                    index, micro, held, lengths, d_scaled, k["d_context"], k["gated"], inv_cross,
                    mamba_gain[None], k["pre"][0], k["pre"][2], k["pre"][3], k["pre"][6], k["ssd"],
                    *k["kept"], *k["attention"], cosine, sine, *mixer_rows,
                )
            )
            kv_far = jnp.where(core == 0, d_values, d_keys)
            kv_own = jnp.where(core == 0, d_keys, d_values)
            k["kv_sum"] = kv_own + t_swap(kv_far, 1)
            k["d_statepre"] = d_statepre
            k.update(
                g_conv_weight=g_conv[:-1], g_conv_bias=g_conv[-1],
                g_conv_state_weight=g_state[:-1], g_conv_state_bias=g_state[-1],
                g_step_bias=g_heads[0, :local_heads], g_decay_log=g_heads[1, :local_heads],
                g_skip=jnp.sum(g_skip.reshape(local_heads, MHDIM), axis=1),
                g_mamba_gain=g_gain[0],
            )
            order.mark(back)
            return back

        def back_inputs(index, k, back):
            back, d_statepre = order.gate(back, k["d_statepre"])
            piece = d_statepre.shape[1] // t_size
            parts = [
                lax.dynamic_slice_in_dim(d_statepre, jnp.bitwise_xor(me_t, q) * piece, piece, 1)
                for q in range(t_size)
            ]
            pieces = halving_order(list(range(0, t_size, 2)), 2, t_size)
            state_sum = jnp.concatenate([parts[q] for q in pieces], axis=1) + t_swap(
                jnp.concatenate([parts[q ^ 1] for q in pieces], axis=1), 1
            )
            bit = 2
            while bit < t_size:
                cut = state_sum.shape[1] // 2
                state_sum = state_sum[:, :cut] + t_swap(state_sum[:, cut:], bit)
                bit *= 2
            k["shared"] = jnp.concatenate([state_sum, k["kv_sum"]], axis=1).astype(bf16)
            rows_back = lax.slice_in_dim(back, index * count, (index + 1) * count, axis=0)
            norm_own, norm_other = halves(right_trans(rows_back, in_weight))
            k["norm_own"] = norm_own + t_swap(norm_other, 1)
            unit_own = mine(k["unit_one"])
            k["g_input_gain"] = jnp.sum(k["norm_own"] * unit_own, axis=0)
            order.mark(k["norm_own"])

        slots = []
        for index in range(micro):
            slot = tokens[index]
            if index:
                (slot,) = order.gate(slot)
            slots.append(forward(index, slot))
        held = None
        for index in range(micro):
            held = feed_forward(index, slots[index], held)
        inner_all, d_gate_all, d_up_all = held

        def joined(name):
            return jnp.concatenate([k[name] for k in slots], axis=0)

        def relative_columns(values):
            blocks = halving_order(list(range(dp_size)), 1, dp_size)
            return jnp.concatenate(
                [
                    lax.dynamic_slice_in_dim(values, jnp.bitwise_xor(me_dp, r) * block, block, 1)
                    for r in blocks
                ],
                axis=1,
            )

        def scattered(part, dimension):
            return lax.psum_scatter(part, "dp", scatter_dimension=dimension, tiled=True)

        (cot_all,) = order.gate(joined("cot_low"))
        part_down = left_trans(inner_all, cot_all)
        order.mark(part_down)
        g_down = scattered(part_down, 1)
        first, last = slots
        in_weight = jnp.concatenate(order.gate(*in_weights), axis=1)
        order.mark(in_weight)
        back_head(first)
        (two_all,) = order.gate(joined("normed_two"))
        part_gate = order.point(left_trans(two_all, d_gate_all))
        order.mark(part_gate)
        g_gate = scattered(part_gate, 0)
        (two_all,) = order.gate(two_all)
        part_up = order.point(left_trans(two_all, d_up_all))
        order.mark(part_up)
        g_up = scattered(part_up, 0)
        for index, k in enumerate(slots):
            output_sum(index, k)
        back_head(last)
        back_first = back_mixers(0, first, None)
        back_inputs(0, first, back_first)
        back = back_mixers(1, last, back_first)
        back_inputs(1, last, back)
        one_columns = relative_columns(order.gate(joined("normed"))[0])
        part_outs = left_trans(relative_columns(joined("d_mixed")), joined("mixer"))
        part_early = left_trans(one_columns, back[:, : channels + heads_width])
        part_late = left_trans(
            one_columns,
            jnp.concatenate(
                [back[:, places["xpre"]], joined("shared"), back[:, places["step"]]], axis=1
            ),
        )

        def total(name):
            value = slots[0][name]
            for k in slots[1:]:
                value = value + k[name]
            return value

        names = [
            "g_conv_state_weight", "g_conv_state_bias", "g_input_gain", "g_ffn_gain",
            "g_conv_weight", "g_conv_bias", "g_step_bias", "g_decay_log", "g_skip",
            "g_mamba_gain",
        ]
        small = {name: total(name) for name in names}
        vector = jnp.concatenate([small[name].reshape(-1) for name in names])
        vector_rows = -(-vector.size // (8 * LANES)) * 8
        vector = jnp.pad(vector, (0, vector_rows * LANES - vector.size)).reshape(-1, LANES)
        shared_size = sum(small[name].size for name in names[:4])
        shared_rows = -(-shared_size // (8 * LANES)) * 8

        sums = [first["norm_own"], first["ffn_own"], last["ffn_own"], last["norm_own"]]
        rests = [
            (0, first["d_hidden_own"], mine(first["unit_one"]), mine(first["inv_one"])),
            (0, first["hidden"]),
            (1, last["hidden"]),
            (1, last["d_hidden_own"], mine(last["unit_one"]), mine(last["inv_one"])),
        ]
        shared_width = joined("shared").shape[1]
        cuts = [
            [mamba_out_weight.shape[0], attn_out_weight.shape[0]],
            [channels, heads_width],
            [channels, shared_width, LANES],
        ]
        grads, out, in_grad, vector, wide_vector = scatter_all(
            dp_size, t_size, [part_outs, part_early, part_late], cuts, sums, rests,
            input_gain[None], vector, shared_rows,
        )
        g_mamba_out, g_attn_out, g_mamba_gate, g_query, g_mamba_in, tail, g_step = grads
        g_step = g_step[:, :local_heads]
        vector, wide_vector = vector.reshape(-1), wide_vector.reshape(-1)
        start = 0
        for name in names:
            shape, size = small[name].shape, small[name].size
            source = wide_vector if start < shared_size else vector
            small[name] = source[start : start + size].reshape(shape)
            start += size
        place = me_dp * t_size + me_t
        share = conv_state_bias.shape[0] // (dp_size * t_size)
        g_conv_state_weight = lax.dynamic_slice_in_dim(
            small["g_conv_state_weight"], place * share, share, 1
        )
        g_conv_state_bias = lax.dynamic_slice_in_dim(
            small["g_conv_state_bias"], place * share, share, 0
        )
        g_input_gain = lax.dynamic_slice_in_dim(small["g_input_gain"], me_dp * block, block, 0)
        g_ffn_gain = lax.dynamic_slice_in_dim(small["g_ffn_gain"], me_dp * block, block, 0)
        heads = [small[name] for name in names[4:]]

        sub = block // t_size
        rowsets = []
        for q in range(t_size):
            part = lax.dynamic_slice_in_dim(tail, jnp.bitwise_xor(me_t, q) * sub, sub, 0)
            rowsets.append(part if q == 0 else t_swap(part, q))
        stacked = jnp.stack(rowsets)
        piece = state_weight.shape[1] // t_size
        sources = [
            lax.dynamic_index_in_dim(stacked, jnp.bitwise_xor(me_t, j), 0, keepdims=False)
            for j in range(t_size)
        ]
        g_state = jnp.concatenate([s[:, :piece] for s in sources], axis=1)
        pairs = t_size // 2
        g_kv = jnp.concatenate(
            [sources[(b % pairs) * 2 + b // pairs][:, piece:] for b in range(t_size)], axis=1
        )
        return (
            out,
            in_grad,
            g_input_gain,
            g_mamba_gate,
            g_mamba_in,
            g_state,
            g_step,
            heads[0],
            heads[1],
            g_conv_state_weight,
            g_conv_state_bias,
            heads[2],
            heads[3],
            heads[4],
            heads[5],
            g_mamba_out,
            g_query,
            g_kv,
            g_attn_out,
            g_ffn_gain,
            g_gate,
            g_up,
            g_down,
        )

    return per_device


def solution(mesh):
    placed = (
        P("dp", None, None),
        P("dp"),
        P("dp", None, None),
        P(),
        P(None, "tensor"),
        P(None, "tensor"),
        P(),
        P(None, "tensor"),
        P(None, "tensor"),
        P("tensor"),
        P(),
        P(),
        P("tensor"),
        P("tensor"),
        P("tensor"),
        P("tensor"),
        P("tensor", None),
        P(None, "tensor"),
        P(),
        P("tensor", None),
        P(),
        P(None, "tensor"),
        P(None, "tensor"),
        P("tensor", None),
    )
    return jax.shard_map(
        make_per_device(mesh.shape["dp"], mesh.shape["tensor"]),
        mesh=mesh,
        in_specs=placed,
        out_specs=(
            P("dp", None, None),
            P("dp", None, None),
            P("dp"),
            P("dp", "tensor"),
            P("dp", "tensor"),
            P(("dp", "tensor"), None),
            P("dp", "tensor"),
            P(None, "tensor"),
            P("tensor"),
            P(None, ("dp", "tensor")),
            P(("dp", "tensor")),
            P("tensor"),
            P("tensor"),
            P("tensor"),
            P("tensor"),
            P("tensor", "dp"),
            P("dp", "tensor"),
            P(("dp", "tensor"), None),
            P("tensor", "dp"),
            P("dp"),
            P("dp", "tensor"),
            P("dp", "tensor"),
            P("tensor", "dp"),
        ),
        check_vma=False,
    )
```

```python
import functools

import jax
import jax.numpy as jnp
from jax import lax
from jax.experimental import pallas as pl
from jax.experimental.pallas import tpu as pltpu
from jax.sharding import PartitionSpec as P

MHDIM = 64
STATE = 256
AHEADS = 8
KVHEADS = 2
AHDIM = 128
DSSM = 3072

epsilon = 1e-05
rope_base = 100000000000.0
f32 = jnp.float32
bf16 = jnp.bfloat16


def plain_dot(left, right):
    return jnp.dot(left, right, preferred_element_type=f32)


def right_trans(left, right):
    return lax.dot_general(left, right, (((1,), (1,)), ((), ())), preferred_element_type=f32)


def left_trans(left, right):
    return lax.dot_general(left, right, (((0,), (0,)), ((), ())), preferred_element_type=f32)


def silu_slope(values):
    sig = jax.nn.sigmoid(values)
    return sig * (1.0 + values * (1.0 - sig))


MESH = pl.DeviceIdType.MESH
LANES = 128
BLOCK = 128


def shifted(values, steps, row):
    if steps == 0:
        return values
    count = values.shape[0]
    moved = pltpu.roll(values, steps % count, 0)
    if steps > 0:
        return jnp.where(row >= steps, moved, 0.0)
    return jnp.where(row < count + steps, moved, 0.0)


def tap_sum(values, taps, bias):
    row = lax.broadcasted_iota(jnp.int32, values.shape, 0)
    width = taps.shape[0]
    total = jnp.zeros_like(values) + bias
    for k in range(width):
        total = total + shifted(values, width - 1 - k, row) * taps[k : k + 1, :]
    return total


def tap_back(grads, values, taps):
    row = lax.broadcasted_iota(jnp.int32, values.shape, 0)
    width = taps.shape[0]
    back = jnp.zeros_like(values)
    tap_grads = []
    for k in range(width):
        steps = width - 1 - k
        back = back + shifted(grads, -steps, row) * taps[k : k + 1, :]
        tap_grads.append(jnp.sum(grads * shifted(values, steps, row), axis=0, keepdims=True))
    return back, jnp.concatenate(tap_grads, axis=0)


def column_of(values, lane, index):
    return jnp.sum(jnp.where(lane == index, values, 0.0), axis=1, keepdims=True)


def exact_dot(left, right):
    return jnp.dot(left, right, precision=lax.Precision.HIGHEST, preferred_element_type=f32)


def turned(values, cosine, sine):
    return values * cosine + pltpu.roll(values, AHDIM // 2, 1) * sine


def scores_of(query, keys, lo, hi, length):
    scores = right_trans(query[lo:hi], keys[:hi]) * AHDIM ** (-0.5)
    t = lax.broadcasted_iota(jnp.int32, (hi - lo, hi), 0) + lo
    s = lax.broadcasted_iota(jnp.int32, (hi - lo, hi), 1)
    return scores, (t >= s) & (s < length)


def attention_forward(query_pre, key_pre, value_pre, cosine, sine, length, query, keys, values, logs, context):
    count, width = query.shape
    keys[...] = turned(key_pre, cosine, sine).astype(bf16)
    values[...] = value_pre.astype(bf16)
    lane = lax.broadcasted_iota(jnp.int32, (count, LANES), 1)
    kept = jnp.zeros((count, LANES), f32)
    for h in range(width // AHDIM):
        lanes = slice(h * AHDIM, (h + 1) * AHDIM)
        query[:, lanes] = turned(query_pre[:, lanes], cosine, sine).astype(bf16)
        found = []
        for i in range(count // BLOCK):
            lo, hi = i * BLOCK, (i + 1) * BLOCK
            scores, valid = scores_of(query[:, lanes], keys[...], lo, hi, length)
            masked = jnp.where(valid, scores, -1e30)
            peak = jnp.max(masked, axis=1, keepdims=True)
            expo = jnp.exp(masked - peak)
            total = jnp.sum(expo, axis=1, keepdims=True)
            found.append(peak + jnp.log(total))
            probs = (expo / total).astype(bf16)
            context[lo:hi, lanes] = plain_dot(probs, values[:hi, :]).astype(bf16)
        kept = jnp.where(lane == h, jnp.concatenate(found, axis=0), kept)
    logs[...] = kept


def attention_backward(d_context, query, keys, values, logs, cosine, sine, length, d_query_pre, d_keys, d_values):
    count, width = query.shape
    lane = lax.broadcasted_iota(jnp.int32, (count, LANES), 1)
    scale = AHDIM ** (-0.5)
    key_total = jnp.zeros((count, AHDIM), f32)
    value_total = jnp.zeros((count, AHDIM), f32)
    for h in range(width // AHDIM):
        lanes = slice(h * AHDIM, (h + 1) * AHDIM)
        log = column_of(logs[...], lane, h)
        pieces = []
        for i in range(count // BLOCK):
            lo, hi = i * BLOCK, (i + 1) * BLOCK
            scores, valid = scores_of(query[:, lanes], keys[...], lo, hi, length)
            probs = jnp.where(valid, jnp.exp(scores - log[lo:hi]), 0.0)
            grads = d_context[lo:hi, lanes]
            d_probs = right_trans(grads, values[:hi, :])
            delta = jnp.sum(probs * d_probs, axis=1, keepdims=True)
            d_scores = (probs * (d_probs - delta)).astype(bf16)
            pieces.append(plain_dot(d_scores, keys[:hi, :]) * scale)
            d_key = left_trans(d_scores, query[lo:hi, lanes]) * scale
            d_value = left_trans(probs.astype(bf16), grads)
            if hi < count:
                rest = jnp.zeros((count - hi, AHDIM), f32)
                d_key = jnp.concatenate([d_key, rest], axis=0)
                d_value = jnp.concatenate([d_value, rest], axis=0)
            key_total = key_total + d_key
            value_total = value_total + d_value
        d_query_pre[:, lanes] = turned(jnp.concatenate(pieces, axis=0), cosine, -sine).astype(bf16)
    d_keys[...] = turned(key_total, cosine, -sine)
    d_values[...] = value_total


def columns_of(channels, heads_width):
    places, start = {}, 0
    for name, size in (
        ("zgate", channels), ("query", heads_width), ("xpre", channels), ("state", 2 * STATE),
        ("key", AHDIM), ("value", AHDIM), ("step", LANES),
    ):
        places[name] = slice(start, start + size)
        start += size
    return places, start


def forward_kernel(
    lengths, zgate, query_pre, xpre, statepre, key_pre, value_pre, steppre, cosine, sine, conv_weight, conv_bias, state_taps, state_bias, step_bias, rates,
    skip_rep, gated, ssd, square, xconv, sconv, stepsize, cumul, inner, query, keys, values, logs,
    context, cumul_rows, *, slot,
):
    attention_forward(
        query_pre, key_pre[...], value_pre[...],
        cosine[...], sine[...], lengths[slot], query, keys, values, logs, context,
    )
    count, channels = xpre.shape
    xlin = tap_sum(xpre[...], conv_weight[...], conv_bias[...])
    xconv[...] = (xlin * jax.nn.sigmoid(xlin)).astype(bf16)
    slin = tap_sum(statepre[...], state_taps[...], state_bias[...])
    sconv[...] = (slin * jax.nn.sigmoid(slin)).astype(bf16)
    inner[...] = right_trans(sconv[:, STATE:], sconv[:, :STATE])
    step = jax.nn.softplus(steppre[...] + step_bias[...])
    stepsize[...] = step
    row = lax.broadcasted_iota(jnp.int32, (count, count), 0)
    col = lax.broadcasted_iota(jnp.int32, (count, count), 1)
    total = exact_dot(jnp.where(row >= col, 1.0, 0.0), -step * rates[...])
    cumul[...] = total
    cumul_rows[...] = total.T
    square[...] = jnp.zeros_like(square)

    def pair(p):
        lanes = slice(p * LANES, (p + 1) * LANES)
        lane = lax.broadcasted_iota(jnp.int32, (count, LANES), 1)
        xvals = xconv[:, lanes].astype(f32)
        low_half = lane < MHDIM
        step_rep = jnp.where(
            low_half, column_of(stepsize[...], lane, 2 * p), column_of(stepsize[...], lane, 2 * p + 1)
        )
        weighted = (step_rep * xvals).astype(bf16)
        columns = [column_of(cumul[...], lane, 2 * p + h) for h in range(2)]
        for i in range(count // BLOCK):
            lo, hi = i * BLOCK, (i + 1) * BLOCK
            results = []
            for h in range(2):
                differ = columns[h][lo:hi] - cumul_rows[2 * p + h : 2 * p + h + 1, :hi]
                t = lax.broadcasted_iota(jnp.int32, (BLOCK, hi), 0) + lo
                s = lax.broadcasted_iota(jnp.int32, (BLOCK, hi), 1)
                decay = jnp.exp(jnp.where(t >= s, differ, -1e30))
                mixing = (inner[lo:hi, :hi] * decay).astype(bf16)
                results.append(plain_dot(mixing, weighted[:hi]))
            half = jnp.where(low_half[lo:hi], results[0], results[1])
            half = half + skip_rep[:, lanes] * xvals[lo:hi]
            ssd[lo:hi, lanes] = half
            z = zgate[lo:hi, lanes]
            value = half * (z * jax.nn.sigmoid(z))
            gated[lo:hi, lanes] = value
            square[lo:hi, :] += value * value

    for p in range(channels // LANES):
        pair(p)


def full(*shape):
    return jax.ShapeDtypeStruct(shape, f32)


def low(*shape):
    return jax.ShapeDtypeStruct(shape, bf16)


def in_vmem(count):
    return [pl.BlockSpec(memory_space=pltpu.VMEM)] * count


def in_hbm(shapes):
    return tuple(pltpu.HBM(s.shape, s.dtype) for s in shapes)


def whole_blocks(shapes):
    return [pl.BlockSpec(s.shape, lambda i, n=len(s.shape): (0,) * n) for s in shapes]


def mixers_forward(slot, lengths, *operands):
    count, channels = operands[0].shape
    heads_width = operands[1].shape[1]
    shapes = (
        full(count, channels), full(count, channels), full(count, LANES), low(count, channels),
        low(count, 2 * STATE), full(count, LANES), full(count, LANES), full(count, count),
        low(count, heads_width), low(count, AHDIM), low(count, AHDIM), full(count, LANES),
        low(count, heads_width),
    )
    return pl.pallas_call(
        functools.partial(forward_kernel, slot=slot),
        grid=(1,),
        out_shape=in_hbm(shapes),
        in_specs=[pl.BlockSpec(memory_space=pltpu.SMEM)] + in_vmem(len(operands)),
        out_specs=tuple(whole_blocks(shapes)),
        scratch_shapes=[pltpu.VMEM((LANES, count), f32)],
        compiler_params=pltpu.CompilerParams(vmem_limit_bytes=48 * 2**20),
        cost_estimate=pl.CostEstimate(
            flops=10**6, bytes_accessed=10**6, transcendentals=10**3
        ),
    )(lengths, *operands)


def backward_kernel(
    lengths, d_scaled_in, d_context_in, gated_in, inv_cross, gain, zgate, xpre, statepre, steppre,
    ssd, xconv, sconv, stepsize, cumul, inner,
    query, keys, values, logs, cosine, sine, conv_weight, conv_bias, state_taps, state_bias,
    step_bias, rates, skip_rep,
    back, d_statepre, d_keys, d_values, g_conv, g_state, g_heads, g_skip, g_gain,
    d_ssd, d_xvals, cumul_rows, d_inner, row_sums, col_sums, d_step, *, slot, places,
):
    count, channels = ssd.shape
    attention_backward(
        d_context_in[...].astype(bf16), query, keys, values, logs, cosine[...], sine[...],
        lengths[slot], back.at[:, places["query"]], d_keys, d_values,
    )
    back[:, places["key"]] = d_keys[...].astype(bf16)
    back[:, places["value"]] = d_values[...].astype(bf16)
    d_zgate, d_xpre = back.at[:, places["zgate"]], back.at[:, places["xpre"]]
    d_steppre = back.at[:, places["step"]]
    d_scaled = d_scaled_in[...]
    g_gain[...] = jnp.sum(d_scaled * gated_in[...] * inv_cross[:, 0:1], axis=0, keepdims=True)
    inv = inv_cross[:, 0:1]
    cross = inv_cross[:, 1:2]
    d_gated = inv * (d_scaled * gain[...]) - gated_in[...] * cross
    z = zgate[...]
    sig = jax.nn.sigmoid(z)
    d_low = (d_gated * (z * sig)).astype(bf16)
    d_ssd[...] = d_low
    d_zgate[...] = (d_gated * ssd[...] * sig * (1.0 + z * (1.0 - sig))).astype(bf16)
    g_skip[...] = jnp.sum(d_low.astype(f32) * xconv[...].astype(f32), axis=0, keepdims=True)
    cumul_rows[...] = cumul[...].T
    d_inner[...] = jnp.zeros_like(d_inner)
    row_sums[...] = jnp.zeros_like(row_sums)
    col_sums[...] = jnp.zeros_like(col_sums)
    d_step[...] = jnp.zeros_like(d_step)

    def pair(p):
        lanes = slice(p * LANES, (p + 1) * LANES)
        lane = lax.broadcasted_iota(jnp.int32, (count, LANES), 1)
        low_half = lane < MHDIM
        xvals = xconv[:, lanes].astype(f32)
        step_rep = jnp.where(
            low_half, column_of(stepsize[...], lane, 2 * p), column_of(stepsize[...], lane, 2 * p + 1)
        )
        weighted = (step_rep * xvals).astype(bf16)
        grads = d_ssd[:, lanes]
        columns = [column_of(cumul[...], lane, 2 * p + h) for h in range(2)]
        pieces = []
        for h in range(2):
            only = jnp.where(low_half == (h == 0), grads, jnp.zeros_like(grads))
            back_part = jnp.zeros((count, LANES), f32)
            sums = []
            col_total = jnp.zeros((1, count), f32)
            for i in range(count // BLOCK):
                lo, hi = i * BLOCK, (i + 1) * BLOCK
                differ = columns[h][lo:hi] - cumul_rows[2 * p + h : 2 * p + h + 1, :hi]
                t = lax.broadcasted_iota(jnp.int32, (BLOCK, hi), 0) + lo
                s = lax.broadcasted_iota(jnp.int32, (BLOCK, hi), 1)
                decay = jnp.exp(jnp.where(t >= s, differ, -1e30))
                mixing = inner[lo:hi, :hi] * decay
                part = left_trans(mixing.astype(bf16), only[lo:hi])
                d_mixing = right_trans(only[lo:hi], weighted[:hi])
                d_inner[lo:hi, :hi] += d_mixing * decay
                flow = d_mixing * mixing
                sums.append(jnp.sum(flow, axis=1, keepdims=True))
                down = jnp.sum(flow, axis=0, keepdims=True)
                if hi < count:
                    part = jnp.concatenate([part, jnp.zeros((count - hi, LANES), f32)], axis=0)
                    down = jnp.concatenate([down, jnp.zeros((1, count - hi), f32)], axis=1)
                back_part = back_part + part
                col_total = col_total + down
            here = lane == 2 * p + h
            row_sums[...] = jnp.where(here, jnp.concatenate(sums, axis=0), row_sums[...])
            col_sums[2 * p + h : 2 * p + h + 1, :] = col_total
            pieces.append(back_part)
        d_weighted = pieces[0] + pieces[1]
        d_xvals[:, lanes] = grads.astype(f32) * skip_rep[:, lanes] + d_weighted * step_rep
        product = d_weighted * xvals
        for h in range(2):
            value = jnp.sum(
                jnp.where(low_half == (h == 0), product, 0.0), axis=1, keepdims=True
            )
            d_step[...] = jnp.where(lane == 2 * p + h, value, d_step[...])

    for p in range(channels // LANES):
        pair(p)

    d_cumul = row_sums[...] - col_sums[...].T
    row = lax.broadcasted_iota(jnp.int32, (count, count), 0)
    col = lax.broadcasted_iota(jnp.int32, (count, count), 1)
    d_logdecay = exact_dot(jnp.where(row <= col, 1.0, 0.0), d_cumul)
    rate = rates[...]
    d_full = (d_step[...] - d_logdecay * rate) * jax.nn.sigmoid(steppre[...] + step_bias[...])
    d_steppre[...] = d_full.astype(bf16)
    g_heads[0:1, :] = jnp.sum(d_full, axis=0, keepdims=True)
    g_heads[1:2, :] = jnp.sum(-d_logdecay * stepsize[...] * rate, axis=0, keepdims=True)

    d_in = d_inner[...].astype(bf16)
    d_c = plain_dot(d_in, sconv[:, :STATE])
    d_b = left_trans(d_in, sconv[:, STATE:])
    slin = tap_sum(statepre[...], state_taps[...], state_bias[...])
    d_slin = jnp.concatenate([d_b, d_c], axis=1) * silu_slope(slin)
    back_state, tap_grads = tap_back(d_slin, statepre[...], state_taps[...])
    d_statepre[...] = back_state
    back[:, places["state"]] = back_state.astype(bf16)
    g_state[...] = jnp.concatenate([tap_grads, jnp.sum(d_slin, axis=0, keepdims=True)], axis=0)
    xlin = tap_sum(xpre[...], conv_weight[...], conv_bias[...])
    d_xlin = d_xvals[...] * silu_slope(xlin)
    back_x, tap_grads = tap_back(d_xlin, xpre[...], conv_weight[...])
    d_xpre[...] = back_x.astype(bf16)
    g_conv[...] = jnp.concatenate([tap_grads, jnp.sum(d_xlin, axis=0, keepdims=True)], axis=0)


def mixers_backward(slot, slots, held, lengths, *operands):
    count, channels = operands[0].shape
    heads_width = operands[1].shape[1]
    taps = operands[-7].shape[0]
    width = columns_of(channels, heads_width)[1]
    kernel = functools.partial(
        backward_kernel, slot=slot, places=columns_of(channels, heads_width)[0]
    )
    aliases = {}
    extra_specs, extra = [], ()
    if held is not None:
        aliases = {0: 0}
        extra_specs, extra = [pl.BlockSpec(memory_space=pl.ANY)], (held,)
        inside = kernel
        kernel = lambda _, *refs: inside(*refs)
    shapes = (
        full(count, 2 * STATE), full(count, AHDIM), full(count, AHDIM), full(taps + 1, channels),
        full(taps + 1, 2 * STATE), full(2, LANES), full(1, channels), full(1, channels),
    )
    return pl.pallas_call(
        kernel,
        grid=(1,),
        out_shape=in_hbm((low(slots * count, width),) + shapes),
        in_specs=extra_specs
        + [pl.BlockSpec(memory_space=pltpu.SMEM)]
        + in_vmem(len(operands)),
        out_specs=tuple(
            [pl.BlockSpec((count, width), lambda i: (slot, 0))] + whole_blocks(shapes)
        ),
        scratch_shapes=[
            pltpu.VMEM((count, channels), bf16),
            pltpu.VMEM((count, channels), f32),
            pltpu.VMEM((LANES, count), f32),
            pltpu.VMEM((count, count), f32),
            pltpu.VMEM((count, LANES), f32),
            pltpu.VMEM((LANES, count), f32),
            pltpu.VMEM((count, LANES), f32),
        ],
        input_output_aliases=aliases,
        compiler_params=pltpu.CompilerParams(vmem_limit_bytes=56 * 2**20),
        cost_estimate=pl.CostEstimate(
            flops=10**6, bytes_accessed=10**6, transcendentals=10**3
        ),
    )(*extra, lengths, *operands)


def feed_forward_kernel(normed, cot, gate_weight, up_weight, down_weight, *refs):
    inner, d_gate, d_up, back = refs[-4:]
    gate = plain_dot(normed[...], gate_weight[...])
    upper = plain_dot(normed[...], up_weight[...])
    d_inner = right_trans(cot[...], down_weight[...])
    sig = jax.nn.sigmoid(gate)
    silu = gate * sig
    inner[...] = (silu * upper).astype(bf16)
    d_gate[...] = (d_inner * upper * sig * (1.0 + gate * (1.0 - sig))).astype(bf16)
    d_up[...] = (d_inner * silu).astype(bf16)
    part = right_trans(d_gate[...], gate_weight[...]) + right_trans(d_up[...], up_weight[...])

    @pl.when(pl.program_id(0) == 0)
    def _():
        back[...] = part

    @pl.when(pl.program_id(0) > 0)
    def _():
        back[...] += part


def feed_forward_all(slot, slots, held, normed, cot, gate_weight, up_weight, down_weight):
    count, width = normed.shape
    hidden = gate_weight.shape[1]
    block = min(512, hidden)
    rows = pl.BlockSpec((count, width), lambda j: (0, 0))
    columns = pl.BlockSpec((width, block), lambda j: (0, j))
    joint = pl.BlockSpec((count, block), lambda j: (slot, j))
    extra = () if held is None else tuple(held)
    return pl.pallas_call(
        feed_forward_kernel,
        grid=(hidden // block,),
        out_shape=tuple([low(slots * count, hidden)] * 3 + [full(count, width)]),
        in_specs=[
            rows, rows, columns, columns, pl.BlockSpec((block, width), lambda j: (j, 0))
        ] + [pl.BlockSpec(memory_space=pl.ANY)] * len(extra),
        out_specs=(joint, joint, joint, rows),
        input_output_aliases={5 + n: n for n in range(len(extra))},
        compiler_params=pltpu.CompilerParams(vmem_limit_bytes=56 * 2**20),
        cost_estimate=pl.CostEstimate(flops=10**6, bytes_accessed=10**6, transcendentals=10**3),
    )(normed, cot, gate_weight, up_weight, down_weight, *extra)


def swap(values, axis, size, bit):
    return lax.ppermute(values, axis, [(i, i ^ bit) for i in range(size)])


def halving_order(members, bit, limit):
    if bit >= limit:
        return members
    low = halving_order([m for m in members if not m & bit], bit * 2, limit)
    high = halving_order([m for m in members if m & bit], bit * 2, limit)
    return low + high


class Order:
    def __init__(self):
        self.last = ()
        self.queue = []

    def point(self, value, skip=0):
        if len(self.queue) <= skip:
            return value
        return lax.optimization_barrier((value, self.queue.pop(skip)))[0]

    def gate(self, *values):
        return lax.optimization_barrier((values, self.last))[0]

    def mark(self, *values):
        self.last = values


def scatter_all(size, t_size, parts, cuts, halves, rests, gain, vector, shared_rows, blocks):
    rows = parts[0].shape[0]
    works = len(parts)
    share = rows // size
    chunk = min(256, rows // 4)
    levels = size.bit_length() - 1
    spans = []
    for level in range(1, levels):
        lo, hi = rows >> (level + 1), rows >> level
        step = min(chunk, hi - lo)
        spans += [(level, start, step) for start in range(hi - step, lo - 1, -step)]
    spans.append((levels, 0, share))
    pieces = [(w,) + span for w in range(works) for span in spans]
    per_work = len(spans)
    widths = [p.shape[1] for p in parts]
    ranges = []
    for cut in cuts:
        stops = [sum(cut[: n + 1]) for n in range(len(cut))]
        ranges.append([(stop - size_, size_) for stop, size_ in zip(stops, cut)])
    outputs = sum(len(cut) for cut in cuts)
    wide = max(widths)
    extra = len(halves)
    half_shape = halves[0].shape
    half, width = half_shape
    slots = 1 + max(rest[0] for rest in rests)
    extras = [value for rest in rests for value in rest[1:]]
    wholes = [n for n, rest in enumerate(rests) if len(rest) == 2]

    def kernel(*refs):
        held_in, refs = refs[:works], refs[works:]
        own, refs = refs[:extra], refs[extra:]
        beside = []
        for rest in rests:
            beside.append(refs[: len(rest) - 1])
            refs = refs[len(rest) - 1 :]
        gain_ref, small, block_ref, refs = refs[0], refs[1], refs[2], refs[3:]
        outs = []
        for cut in cuts:
            outs.append(refs[: len(cut)])
            refs = refs[len(cut) :]
        far, refs = refs[:extra], refs[extra:]
        result, grad, small_out, wide_out, block_out, refs = (
            refs[0], refs[1], refs[2], refs[3], refs[4], refs[5:]
        )
        loads, pair_loads, totals, low_rows, theirs, refs = (
            refs[0], refs[1], refs[2], refs[3], refs[4], refs[5:]
        )
        boxes, wide_boxes, turned_rows, block_boxes, refs = (
            refs[0], refs[1], refs[2], refs[3], refs[4:]
        )
        landed, refs = refs[:works], refs[works:]
        later, refs = refs[: works * (levels - 1)], refs[works * (levels - 1) :]
        load_sems, out_sems, x_send, x_recv, z_send, z_recv, y_sems, c_sems, pair_sems, v_sems, w_sems, b_sems = refs
        me = lax.axis_index("dp")
        spot = lax.axis_index("tensor")

        def neighbour(bit):
            return spot + bit - 2 * bit * lax.rem(spot // bit, 2)


        def partner(level):
            bit = 1 << level
            return me + bit - 2 * bit * lax.rem(me // bit, 2)

        barrier = pltpu.get_barrier_semaphore()
        for other in range(1, size):
            pl.semaphore_signal(
                barrier, inc=1, device_id={"dp": lax.rem(me + other, size)}, device_id_type=MESH
            )
        for other in range(1, t_size):
            pl.semaphore_signal(
                barrier, inc=1, device_id={"tensor": lax.rem(spot + other, t_size)},
                device_id_type=MESH,
            )
        pl.semaphore_wait(barrier, size + t_size - 2)

        def small_copy(other):
            return pltpu.make_async_remote_copy(
                src_ref=small, dst_ref=boxes.at[size - other], send_sem=v_sems.at[0, other],
                recv_sem=v_sems.at[1, size - other],
                device_id={"dp": lax.rem(me + other, size)}, device_id_type=MESH,
            )

        def block_copy(other):
            return pltpu.make_async_remote_copy(
                src_ref=block_ref.at[other], dst_ref=block_boxes.at[size - other],
                send_sem=b_sems.at[0, other], recv_sem=b_sems.at[1, size - other],
                device_id={"dp": lax.rem(me + other, size)}, device_id_type=MESH,
            )

        def wide_copy(other):
            return pltpu.make_async_remote_copy(
                src_ref=small_out.at[pl.ds(0, shared_rows), :], dst_ref=wide_boxes.at[t_size - other],
                send_sem=w_sems.at[0, other], recv_sem=w_sems.at[1, t_size - other],
                device_id={"tensor": lax.rem(spot + other, t_size)}, device_id_type=MESH,
            )

        def in_turn(kept, count, place, rows):
            total = jnp.zeros((rows, LANES), f32)
            for number in range(count):
                offset = lax.rem(number - place + count, count)
                total = total + kept[offset]
            return total

        def small_sums(stage):
            if stage == 0:
                boxes[0] = small[...]
                for other in range(1, size):
                    small_copy(other).wait_recv()
                small_out[...] = in_turn(boxes, size, me, small.shape[0])
                for other in range(1, t_size):
                    wide_copy(other).start()
                block_boxes[0] = block_ref[0]
                for other in range(1, size):
                    block_copy(other).wait_recv()
                block_out[...] = in_turn(block_boxes, size, me, blocks.shape[1])
            else:
                wide_boxes[0] = small_out[:shared_rows, :]
                for other in range(1, t_size):
                    wide_copy(other).wait_recv()
                wide_out[...] = in_turn(wide_boxes, t_size, spot, shared_rows)


        def y_copy(e):
            return pltpu.make_async_remote_copy(
                src_ref=own[e], dst_ref=far[e], send_sem=y_sems.at[0, e], recv_sem=y_sems.at[1, e],
                device_id={"tensor": neighbour(2)}, device_id_type=MESH,
            )

        core = lax.rem(spot, 2)

        def rows_of(place):
            return pl.ds(pl.multiple_of(place * half, 8), half)

        def c_copy(e):
            slot = rests[e][0]
            if e in wholes:
                target = theirs.at[wholes.index(e)]
            else:
                target = grad.at[slot, rows_of(core), :]
            return pltpu.make_async_remote_copy(
                src_ref=totals.at[e], dst_ref=target, send_sem=c_sems.at[0, e],
                recv_sem=c_sems.at[1, e], device_id={"tensor": neighbour(1)}, device_id_type=MESH,
            )

        def fetch(source, place):
            return pltpu.make_async_copy(source, pair_loads.at[place], pair_sems.at[0, place])

        def keep(e, place):
            slot = rests[e][0]
            if e in wholes:
                n = 2 * wholes.index(e) + place
                target = result.at[slot, rows_of(core if place == 0 else 1 - core), :]
                return pltpu.make_async_copy(low_rows.at[n], target, pair_sems.at[1 + place, e])
            return pltpu.make_async_copy(
                totals.at[e], grad.at[slot, rows_of(core), :], pair_sems.at[1, e]
            )

        def exchange(e):
            y_copy(e).wait_recv()
            sources = [own[e], far[e]]
            if e in wholes:
                sources.append(beside[e][0].at[pl.ds(0, half), :])
            else:
                sources += [beside[e][0], beside[e][1]]
            for place, source in enumerate(sources):
                fetch(source, place).start()
            for place, source in enumerate(sources):
                fetch(source, place).wait()
            total = pair_loads[0] + pair_loads[1]
            if e in wholes:
                totals[e] = total
                low_rows[2 * wholes.index(e)] = (pair_loads[2] + total).astype(bf16)
            else:
                unit = pair_loads[3]
                scaled = total * gain_ref[...]
                mean = jnp.sum(scaled * unit, axis=1, keepdims=True) / width
                totals[e] = pair_loads[2] + beside[e][2][...] * (scaled - unit * mean)
            c_copy(e).start()
            keep(e, 0).start()

        def complete(e):
            fetch(beside[e][0].at[pl.ds(half, half), :], 0).start()
            c_copy(e).wait_recv()
            fetch(beside[e][0].at[pl.ds(half, half), :], 0).wait()
            n = wholes.index(e)
            low_rows[2 * n + 1] = (pair_loads[0] + theirs[n]).astype(bf16)
            keep(e, 1).start()

        def first_copy(number):
            w, _, start, step = pieces[number]
            return pltpu.make_async_remote_copy(
                src_ref=held_in[w].at[pl.ds(rows // 2 + start, step), :],
                dst_ref=landed[w].at[pl.ds(start, step), :],
                send_sem=x_send.at[number],
                recv_sem=x_recv.at[number],
                device_id={"dp": partner(0)},
                device_id_type=MESH,
            )

        def load(number):
            w, _, start, step = pieces[number]
            return pltpu.make_async_copy(
                held_in[w].at[pl.ds(start, step), :],
                loads.at[number % 2, pl.ds(0, step), pl.ds(0, widths[w])],
                load_sems.at[number % 2],
            )

        def later_copy(number):
            w, level, start, step = pieces[number]
            return pltpu.make_async_remote_copy(
                src_ref=landed[w].at[pl.ds(start, step), :],
                dst_ref=later[w * (levels - 1) + level - 1].at[pl.ds(start - (rows >> (level + 1)), step), :],
                send_sem=z_send.at[number],
                recv_sem=z_recv.at[number],
                device_id={"dp": partner(level)},
                device_id_type=MESH,
            )

        def stores(w):
            copies = []
            for n, (lo, length) in enumerate(ranges[w]):
                if w == 0:
                    source = turned_rows.at[pl.ds(lo, length), :]
                else:
                    source = landed[w].at[pl.ds(0, share), pl.ds(lo, length)]
                copies.append(pltpu.make_async_copy(source, outs[w][n], out_sems.at[w, n]))
            return copies

        for other in range(1, size):
            small_copy(other).start()
            block_copy(other).start()
        for e in range(extra):
            y_copy(e).start()
        for number in range(len(pieces)):
            first_copy(number).start()
        load(0).start()
        arrived = set()

        def need(w, level, start, step):
            base = rows >> (level + 1)
            for other in range(w * per_work, (w + 1) * per_work):
                _, its_level, its_start, its_step = pieces[other]
                if its_level != level or other in arrived:
                    continue
                if its_start - base < start + step and start < its_start - base + its_step:
                    later_copy(other).wait_recv()
                    arrived.add(other)

        def finish(w):
            level = levels - 1
            need(w, level, 0, share)
            landed[w][:share, :] += later[w * (levels - 1) + level - 1][:share, :]
            if w == 0:
                turned_rows[...] = landed[w][:share, :].T
            for copy in stores(w):
                copy.start()

        for number, (w, level, start, step) in enumerate(pieces):
            load(number).wait()
            if number + 1 < len(pieces):
                load(number + 1).start()
            first_copy(number).wait_recv()
            value = loads[number % 2, :step, : widths[w]] + landed[w][start : start + step, :]
            for before in range(1, min(level, levels - 1)):
                need(w, before, start, step)
                value = value + later[w * (levels - 1) + before - 1][start : start + step, :]
            landed[w][start : start + step, :] = value
            if level < levels:
                later_copy(number).start()
            if w and number == w * per_work + min(2, per_work - 1):
                finish(w - 1)
            if number in (0, 2):
                small_sums(number // 2)
            if number % 2 and number // 2 < extra:
                exchange(number // 2)
            if number % 2 == 0 and number // 2 - 2 in wholes:
                complete(number // 2 - 2)
        for e in range(len(pieces) // 2, extra):
            exchange(e)
        for e in wholes:
            if 2 * (e + 2) >= len(pieces):
                complete(e)
        finish(works - 1)
        for other in range(1, size):
            small_copy(other).wait_send()
            block_copy(other).wait_send()
        for other in range(1, t_size):
            wide_copy(other).wait_send()
        for e in range(extra):
            y_copy(e).wait_send()
            c_copy(e).wait_send()
            keep(e, 0).wait()
            if e in wholes:
                keep(e, 1).wait()
            else:
                c_copy(e).wait_recv()
        for number, (w, level, start, step) in enumerate(pieces):
            first_copy(number).wait_send()
            if level < levels:
                later_copy(number).wait_send()
        for w in range(works):
            for copy in stores(w):
                copy.wait()

    scratch = [
        pltpu.VMEM((2, chunk, wide), f32),
        pltpu.VMEM((4,) + half_shape, f32),
        pltpu.VMEM((extra,) + half_shape, f32),
        pltpu.VMEM((2 * len(wholes),) + half_shape, bf16),
        pltpu.VMEM((len(wholes),) + half_shape, f32),
        pltpu.VMEM((size,) + vector.shape, f32),
        pltpu.VMEM((t_size, shared_rows, LANES), f32),
        pltpu.VMEM((widths[0], share), f32),
        pltpu.VMEM(blocks.shape, f32),
    ]
    scratch += [pltpu.VMEM((rows // 2, n), f32) for n in widths]
    scratch += [
        pltpu.VMEM((rows >> (level + 1), n), f32) for n in widths for level in range(1, levels)
    ]
    scratch += [
        pltpu.SemaphoreType.DMA((2,)),
        pltpu.SemaphoreType.DMA((works, max(len(cut) for cut in cuts))),
    ] + [pltpu.SemaphoreType.DMA((len(pieces),))] * 4
    scratch += [pltpu.SemaphoreType.DMA((n, extra)) for n in (2, 2)]
    scratch += [pltpu.SemaphoreType.DMA((3, max(4, extra)))]
    scratch += [pltpu.SemaphoreType.DMA((2, n)) for n in (size, t_size, size)]
    results = pl.pallas_call(
        kernel,
        out_shape=tuple(
            [full(n, share) for n in cuts[0]]
            + [full(share, n) for cut in cuts[1:] for n in cut]
            + [full(*half_shape)] * extra
            + [low(slots, 2 * half, width), full(slots, 2 * half, width)]
            + [full(*vector.shape), full(shared_rows, LANES), full(*blocks.shape[1:])]
        ),
        in_specs=[pl.BlockSpec(memory_space=pl.ANY)] * (works + extra)
        + [
            pl.BlockSpec(memory_space=pltpu.VMEM if value.shape[1] == 1 else pl.ANY)
            for value in extras
        ]
        + in_vmem(3),
        out_specs=tuple([pl.BlockSpec(memory_space=pl.ANY)] * (outputs + extra + 2) + in_vmem(3)),
        scratch_shapes=scratch,
        compiler_params=pltpu.CompilerParams(
            collective_id=0, has_side_effects=True, vmem_limit_bytes=60 * 2**20
        ),
        cost_estimate=pl.CostEstimate(
            flops=10**6, bytes_accessed=10**6, transcendentals=0
        ),
    )(*parts, *halves, *extras, gain, vector, blocks)
    return results[:outputs], *results[outputs + extra :]


def make_per_device(dp_size, t_size):
    def per_device(
        tokens,
        lengths,
        out_grad,
        input_gain,
        mamba_gate_weight,
        mamba_in_weight,
        state_weight,
        step_weight,
        conv_weight,
        conv_bias,
        conv_state_weight,
        conv_state_bias,
        step_bias,
        decay_log,
        skip_scale,
        mamba_gain,
        mamba_out_weight,
        query_weight,
        key_value_weight,
        attn_out_weight,
        ffn_gain,
        gate_weight,
        up_weight,
        down_weight,
    ):
        micro = tokens.shape[0]
        count = tokens.shape[1]
        width = tokens.shape[2]
        half = count // 2
        local_heads = step_weight.shape[1]
        q_local = query_weight.shape[1] // AHDIM
        kv_width = key_value_weight.shape[1] // 2
        group_size = AHEADS // KVHEADS
        me_dp = lax.axis_index("dp")
        me_t = lax.axis_index("tensor")
        core = lax.rem(me_t, 2)
        kv_head = me_t * q_local // group_size
        key_weight = lax.dynamic_slice_in_dim(key_value_weight, kv_head * AHDIM, AHDIM, 1)
        value_weight = lax.dynamic_slice_in_dim(
            key_value_weight, kv_width + kv_head * AHDIM, AHDIM, 1
        )
        rows = jnp.arange(count)
        freqs = rope_base ** (-(jnp.arange(AHDIM // 2).astype(f32) * 2.0) / AHDIM)
        angles = rows.astype(f32)[:, None] * freqs[None, :]
        cosine, sine = jnp.cos(angles), jnp.sin(angles)
        cosine = jnp.concatenate([cosine, cosine], axis=1)
        sine = jnp.concatenate([-sine, sine], axis=1)
        channels = mamba_in_weight.shape[1]
        heads_width = query_weight.shape[1]
        places, _ = columns_of(channels, heads_width)
        pad_step = LANES - local_heads

        def lane_row(vector):
            return jnp.pad(vector, (0, pad_step))[None]

        mixer_rows = (
            conv_weight, conv_bias[None], conv_state_weight, conv_state_bias[None],
            lane_row(step_bias), lane_row(jnp.exp(decay_log)), jnp.repeat(skip_scale, MHDIM)[None],
        )
        step_lanes = jnp.pad(step_weight, ((0, 0), (0, pad_step)))
        in_weights = (
            mamba_gate_weight, query_weight, mamba_in_weight, state_weight, key_weight,
            value_weight, step_lanes,
        )

        def t_swap(values, bit):
            return swap(values, "tensor", t_size, bit)

        def t_total(values):
            bit = 1
            while bit < t_size:
                values = values + t_swap(values, bit)
                bit *= 2
            return values

        def mine(values):
            return lax.dynamic_slice_in_dim(values, core * half, half, 0)

        def other(values):
            return lax.dynamic_slice_in_dim(values, (1 - core) * half, half, 0)

        def halves(values):
            values = lax.optimization_barrier(values)
            return mine(values), other(values)

        def relative(values):
            return jnp.concatenate([mine(values), other(values)], axis=0)

        def in_order(own, far):
            return jnp.where(
                core == 0,
                jnp.concatenate([own, far], axis=0),
                jnp.concatenate([far, own], axis=0),
            )

        def half_sum(own, far, pieces):
            own = own + t_swap(far, 1)
            bit = 2
            while bit < t_size // 2:
                own = own + t_swap(own, bit)
                bit *= 2
            count = own.shape[0]
            head = count // 8
            step = -(-(count - head) // (8 * (pieces - 1))) * 8
            parts = [t_swap(own[:head], bit)]
            for start in range(head, count, step):
                parts.append(t_swap(own[start : start + step], bit))
            order.queue += parts
            return own, parts

        def add_up(own, parts):
            for part in parts:
                order.queue = [p for p in order.queue if p is not part]
            own, *parts = order.gate(own, *parts)
            return own + jnp.concatenate(parts, axis=0)

        block = width // dp_size

        order = Order()

        def forward(index, slot):
            inputs = slot.astype(f32)
            inv_one = lax.rsqrt(jnp.mean(inputs * inputs, axis=-1, keepdims=True) + epsilon)
            unit_one = inputs * inv_one
            normed = (unit_one * input_gain).astype(bf16)
            normed = order.point(normed)
            pre = [plain_dot(normed, w) for w in in_weights]
            gated, ssd, square, *kept, query, keys, values, logs, context = mixers_forward(
                index, lengths, *pre, cosine, sine, *mixer_rows
            )
            gated = order.point(order.point(gated))
            total_square = t_total(jnp.sum(square, axis=-1))
            inv_mamba = lax.rsqrt(total_square / DSSM + epsilon)[:, None]
            scaled = (gated * inv_mamba * mamba_gain).astype(bf16)
            mixer = jnp.concatenate([scaled, context], axis=1)
            mixed_own, mixed_far = half_sum(
                *halves(plain_dot(scaled, mamba_out_weight) + plain_dot(context, attn_out_weight)),
                3,
            )
            order.mark(mixed_own)
            return dict(
                mixed_own=mixed_own, mixed_far=mixed_far, inputs=inputs, inv_one=inv_one,
                unit_one=unit_one, normed=normed, pre=pre, gated=gated, ssd=ssd, kept=kept,
                attention=(query, keys, values, logs), inv_mamba=inv_mamba, mixer=mixer,
            )

        def feed_forward(index, k, held):
            hidden_own = mine(k["inputs"]) + add_up(k["mixed_own"], k["mixed_far"])
            hidden = order.point(jnp.concatenate([hidden_own, t_swap(hidden_own, 1)], axis=0))
            inv_two = lax.rsqrt(jnp.mean(hidden * hidden, axis=-1, keepdims=True) + epsilon)
            unit_two = hidden * inv_two
            normed_two = (unit_two * ffn_gain).astype(bf16)
            valid = (rows < lengths[index]).astype(f32)[:, None]
            cotangent = relative(out_grad[index].astype(f32) * valid)
            cot_low = cotangent.astype(bf16)
            *held, back = feed_forward_all(
                index, micro, held, normed_two, cot_low, gate_weight, up_weight, down_weight
            )
            back = order.point(order.point(back))
            back_own, back_far = half_sum(back[:half], back[half:], 3)
            order.mark(back_own)
            k.update(
                back_own=back_own, back_far=back_far,
                hidden=hidden, inv_two=inv_two[:half], unit_two=unit_two[:half],
                normed_two=normed_two, cotangent=cotangent, cot_low=cot_low,
            )
            return held

        def output_sum(index, k):
            (inner_ffn,) = order.gate(
                lax.slice_in_dim(inner_all, index * count, (index + 1) * count, axis=0)
            )
            ffn = plain_dot(inner_ffn, down_weight)
            k["ffn_own"] = ffn[:half] + t_swap(ffn[half:], 1)
            order.mark(k["ffn_own"])

        def back_head(k):
            unit_two = k["unit_two"]
            g_ffn_gain = jnp.sum(k["back_own"] * unit_two, axis=0)
            d_normed_two = add_up(k["back_own"], k["back_far"])
            d_unit_two = d_normed_two * ffn_gain
            d_rest = k["inv_two"] * (
                d_unit_two - unit_two * jnp.mean(d_unit_two * unit_two, axis=-1, keepdims=True)
            )
            d_both = k["cotangent"] + jnp.concatenate([d_rest, t_swap(d_rest, 1)], axis=0)
            d_mixed = in_order(d_both[:half], d_both[half:]).astype(bf16)
            d_scaled = right_trans(d_mixed, mamba_out_weight)
            d_context = right_trans(d_mixed, attn_out_weight)
            k["g_ffn_gain"] = g_ffn_gain
            k["d_hidden_own"] = d_both[:half]
            k["d_mixed"], k["d_scaled"], k["d_context"] = d_mixed, d_scaled, d_context
            k["cross"] = t_total(jnp.sum(d_scaled * mamba_gain * k["gated"], axis=-1))[:, None]
            order.mark(d_scaled, d_context)

        def back_mixers(index, k, held):
            d_scaled, cross = order.gate(k["d_scaled"], k["cross"])
            inv = k["inv_mamba"]
            inv_cross = jnp.concatenate([inv, inv**3 * cross / DSSM], axis=1)
            inv_cross = jnp.pad(inv_cross, ((0, 0), (0, LANES - 2)))
            back, d_statepre, d_keys, d_values, g_conv, g_state, g_heads, g_skip, g_gain = (
                mixers_backward(
                    index, micro, held, lengths, d_scaled, k["d_context"], k["gated"], inv_cross,
                    mamba_gain[None], k["pre"][0], k["pre"][2], k["pre"][3], k["pre"][6], k["ssd"],
                    *k["kept"], *k["attention"], cosine, sine, *mixer_rows,
                )
            )
            kv_far = jnp.where(core == 0, d_values, d_keys)
            kv_own = jnp.where(core == 0, d_keys, d_values)
            k["kv_sum"] = kv_own + t_swap(kv_far, 1)
            k["d_statepre"] = d_statepre
            k.update(
                g_conv_weight=g_conv[:-1], g_conv_bias=g_conv[-1],
                g_conv_state_weight=g_state[:-1], g_conv_state_bias=g_state[-1],
                g_step_bias=g_heads[0, :local_heads], g_decay_log=g_heads[1, :local_heads],
                g_skip=jnp.sum(g_skip.reshape(local_heads, MHDIM), axis=1),
                g_mamba_gain=g_gain[0],
            )
            order.mark(back)
            return back

        def back_inputs(index, k, back):
            back, d_statepre = order.gate(back, k["d_statepre"])
            piece = d_statepre.shape[1] // t_size
            parts = [
                lax.dynamic_slice_in_dim(d_statepre, jnp.bitwise_xor(me_t, q) * piece, piece, 1)
                for q in range(t_size)
            ]
            pieces = halving_order(list(range(0, t_size, 2)), 2, t_size)
            state_sum = jnp.concatenate([parts[q] for q in pieces], axis=1) + t_swap(
                jnp.concatenate([parts[q ^ 1] for q in pieces], axis=1), 1
            )
            bit = 2
            while bit < t_size:
                cut = state_sum.shape[1] // 2
                state_sum = state_sum[:, :cut] + t_swap(state_sum[:, cut:], bit)
                bit *= 2
            k["shared"] = jnp.concatenate([state_sum, k["kv_sum"]], axis=1).astype(bf16)
            rows_back = lax.slice_in_dim(back, index * count, (index + 1) * count, axis=0)
            norm_own, norm_other = halves(right_trans(rows_back, in_weight))
            k["norm_own"] = norm_own + t_swap(norm_other, 1)
            unit_own = mine(k["unit_one"])
            k["g_input_gain"] = jnp.sum(k["norm_own"] * unit_own, axis=0)
            order.mark(k["norm_own"])

        slots = []
        for index in range(micro):
            slot = tokens[index]
            if index:
                (slot,) = order.gate(slot)
            slots.append(forward(index, slot))
        held = None
        for index in range(micro):
            held = feed_forward(index, slots[index], held)
        inner_all, d_gate_all, d_up_all = held

        def joined(name):
            return jnp.concatenate([k[name] for k in slots], axis=0)

        def relative_columns(values):
            blocks = halving_order(list(range(dp_size)), 1, dp_size)
            return jnp.concatenate(
                [
                    lax.dynamic_slice_in_dim(values, jnp.bitwise_xor(me_dp, r) * block, block, 1)
                    for r in blocks
                ],
                axis=1,
            )

        def scattered(part, dimension):
            return lax.psum_scatter(part, "dp", scatter_dimension=dimension, tiled=True)

        (cot_all,) = order.gate(joined("cot_low"))
        part_down = left_trans(inner_all, cot_all)
        order.mark(part_down)
        g_down = scattered(part_down, 1)
        first, last = slots
        in_weight = jnp.concatenate(order.gate(*in_weights), axis=1)
        order.mark(in_weight)
        back_head(first)
        (two_all,) = order.gate(joined("normed_two"))
        part_gate = order.point(left_trans(two_all, d_gate_all))
        order.mark(part_gate)
        g_gate = scattered(part_gate, 0)
        (two_all,) = order.gate(two_all)
        part_up = order.point(left_trans(two_all, d_up_all))
        order.mark(part_up)
        g_up = scattered(part_up, 0)
        for index, k in enumerate(slots):
            output_sum(index, k)
        back_head(last)
        back_first = back_mixers(0, first, None)
        back_inputs(0, first, back_first)
        back = back_mixers(1, last, back_first)
        back_inputs(1, last, back)
        one_columns = relative_columns(order.gate(joined("normed"))[0])
        part_outs = left_trans(relative_columns(joined("d_mixed")), joined("mixer"))
        part_early = left_trans(one_columns, back[:, : channels + heads_width])
        part_late = left_trans(
            one_columns,
            jnp.concatenate([back[:, places["xpre"]], joined("shared")], axis=1),
        )
        part_step = left_trans(joined("normed"), back[:, places["step"]])[:, :local_heads]
        step_size = block * local_heads
        step_rows = -(-step_size // (8 * LANES)) * 8
        step_blocks = jnp.pad(
            part_step.reshape(dp_size, step_size), ((0, 0), (0, step_rows * LANES - step_size))
        ).reshape(dp_size, step_rows, LANES)
        step_blocks = lax.dynamic_slice_in_dim(
            jnp.concatenate([step_blocks, step_blocks], axis=0), me_dp, dp_size, 0
        )

        def total(name):
            value = slots[0][name]
            for k in slots[1:]:
                value = value + k[name]
            return value

        names = [
            "g_conv_state_weight", "g_conv_state_bias", "g_input_gain", "g_ffn_gain",
            "g_conv_weight", "g_conv_bias", "g_step_bias", "g_decay_log", "g_skip",
            "g_mamba_gain",
        ]
        small = {name: total(name) for name in names}
        vector = jnp.concatenate([small[name].reshape(-1) for name in names])
        vector_rows = -(-vector.size // (8 * LANES)) * 8
        vector = jnp.pad(vector, (0, vector_rows * LANES - vector.size)).reshape(-1, LANES)
        shared_size = sum(small[name].size for name in names[:4])
        shared_rows = -(-shared_size // (8 * LANES)) * 8

        sums = [first["norm_own"], first["ffn_own"], last["ffn_own"], last["norm_own"]]
        rests = [
            (0, first["d_hidden_own"], mine(first["unit_one"]), mine(first["inv_one"])),
            (0, first["hidden"]),
            (1, last["hidden"]),
            (1, last["d_hidden_own"], mine(last["unit_one"]), mine(last["inv_one"])),
        ]
        shared_width = joined("shared").shape[1]
        cuts = [
            [mamba_out_weight.shape[0], attn_out_weight.shape[0]],
            [channels, heads_width],
            [channels, shared_width],
        ]
        grads, out, in_grad, vector, wide_vector, g_step = scatter_all(
            dp_size, t_size, [part_outs, part_early, part_late], cuts, sums, rests,
            input_gain[None], vector, shared_rows, step_blocks,
        )
        g_mamba_out, g_attn_out, g_mamba_gate, g_query, g_mamba_in, tail = grads
        g_step = g_step.reshape(-1)[:step_size].reshape(block, local_heads)
        vector, wide_vector = vector.reshape(-1), wide_vector.reshape(-1)
        start = 0
        for name in names:
            shape, size = small[name].shape, small[name].size
            source = wide_vector if start < shared_size else vector
            small[name] = source[start : start + size].reshape(shape)
            start += size
        place = me_dp * t_size + me_t
        share = conv_state_bias.shape[0] // (dp_size * t_size)
        g_conv_state_weight = lax.dynamic_slice_in_dim(
            small["g_conv_state_weight"], place * share, share, 1
        )
        g_conv_state_bias = lax.dynamic_slice_in_dim(
            small["g_conv_state_bias"], place * share, share, 0
        )
        g_input_gain = lax.dynamic_slice_in_dim(small["g_input_gain"], me_dp * block, block, 0)
        g_ffn_gain = lax.dynamic_slice_in_dim(small["g_ffn_gain"], me_dp * block, block, 0)
        heads = [small[name] for name in names[4:]]

        sub = block // t_size
        rowsets = []
        for q in range(t_size):
            part = lax.dynamic_slice_in_dim(tail, jnp.bitwise_xor(me_t, q) * sub, sub, 0)
            rowsets.append(part if q == 0 else t_swap(part, q))
        stacked = jnp.stack(rowsets)
        piece = state_weight.shape[1] // t_size
        sources = [
            lax.dynamic_index_in_dim(stacked, jnp.bitwise_xor(me_t, j), 0, keepdims=False)
            for j in range(t_size)
        ]
        g_state = jnp.concatenate([s[:, :piece] for s in sources], axis=1)
        pairs = t_size // 2
        g_kv = jnp.concatenate(
            [sources[(b % pairs) * 2 + b // pairs][:, piece:] for b in range(t_size)], axis=1
        )
        return (
            out,
            in_grad,
            g_input_gain,
            g_mamba_gate,
            g_mamba_in,
            g_state,
            g_step,
            heads[0],
            heads[1],
            g_conv_state_weight,
            g_conv_state_bias,
            heads[2],
            heads[3],
            heads[4],
            heads[5],
            g_mamba_out,
            g_query,
            g_kv,
            g_attn_out,
            g_ffn_gain,
            g_gate,
            g_up,
            g_down,
        )

    return per_device


def solution(mesh):
    placed = (
        P("dp", None, None),
        P("dp"),
        P("dp", None, None),
        P(),
        P(None, "tensor"),
        P(None, "tensor"),
        P(),
        P(None, "tensor"),
        P(None, "tensor"),
        P("tensor"),
        P(),
        P(),
        P("tensor"),
        P("tensor"),
        P("tensor"),
        P("tensor"),
        P("tensor", None),
        P(None, "tensor"),
        P(),
        P("tensor", None),
        P(),
        P(None, "tensor"),
        P(None, "tensor"),
        P("tensor", None),
    )
    return jax.shard_map(
        make_per_device(mesh.shape["dp"], mesh.shape["tensor"]),
        mesh=mesh,
        in_specs=placed,
        out_specs=(
            P("dp", None, None),
            P("dp", None, None),
            P("dp"),
            P("dp", "tensor"),
            P("dp", "tensor"),
            P(("dp", "tensor"), None),
            P("dp", "tensor"),
            P(None, "tensor"),
            P("tensor"),
            P(None, ("dp", "tensor")),
            P(("dp", "tensor")),
            P("tensor"),
            P("tensor"),
            P("tensor"),
            P("tensor"),
            P("tensor", "dp"),
            P("dp", "tensor"),
            P(("dp", "tensor"), None),
            P("tensor", "dp"),
            P("dp"),
            P("dp", "tensor"),
            P("dp", "tensor"),
            P("tensor", "dp"),
        ),
        check_vma=False,
    )
```

```python
import functools

import jax
import jax.numpy as jnp
from jax import lax
from jax.experimental import pallas as pl
from jax.experimental.pallas import tpu as pltpu
from jax.sharding import PartitionSpec as P

MHDIM = 64
STATE = 256
AHEADS = 8
KVHEADS = 2
AHDIM = 128
DSSM = 3072

epsilon = 1e-05
rope_base = 100000000000.0
f32 = jnp.float32
bf16 = jnp.bfloat16


def plain_dot(left, right):
    return jnp.dot(left, right, preferred_element_type=f32)


def right_trans(left, right):
    return lax.dot_general(left, right, (((1,), (1,)), ((), ())), preferred_element_type=f32)


def left_trans(left, right):
    return lax.dot_general(left, right, (((0,), (0,)), ((), ())), preferred_element_type=f32)


def silu_slope(values):
    sig = jax.nn.sigmoid(values)
    return sig * (1.0 + values * (1.0 - sig))


MESH = pl.DeviceIdType.MESH
LANES = 128
BLOCK = 128


def shifted(values, steps, row):
    if steps == 0:
        return values
    count = values.shape[0]
    moved = pltpu.roll(values, steps % count, 0)
    if steps > 0:
        return jnp.where(row >= steps, moved, 0.0)
    return jnp.where(row < count + steps, moved, 0.0)


def tap_sum(values, taps, bias):
    row = lax.broadcasted_iota(jnp.int32, values.shape, 0)
    width = taps.shape[0]
    total = jnp.zeros_like(values) + bias
    for k in range(width):
        total = total + shifted(values, width - 1 - k, row) * taps[k : k + 1, :]
    return total


def tap_back(grads, values, taps):
    row = lax.broadcasted_iota(jnp.int32, values.shape, 0)
    width = taps.shape[0]
    back = jnp.zeros_like(values)
    tap_grads = []
    for k in range(width):
        steps = width - 1 - k
        back = back + shifted(grads, -steps, row) * taps[k : k + 1, :]
        tap_grads.append(jnp.sum(grads * shifted(values, steps, row), axis=0, keepdims=True))
    return back, jnp.concatenate(tap_grads, axis=0)


def column_of(values, lane, index):
    return jnp.sum(jnp.where(lane == index, values, 0.0), axis=1, keepdims=True)


def exact_dot(left, right):
    return jnp.dot(left, right, precision=lax.Precision.HIGHEST, preferred_element_type=f32)


def turned(values, cosine, sine):
    return values * cosine + pltpu.roll(values, AHDIM // 2, 1) * sine


def scores_of(query, keys, lo, hi, length):
    scores = right_trans(query[lo:hi], keys[:hi]) * AHDIM ** (-0.5)
    t = lax.broadcasted_iota(jnp.int32, (hi - lo, hi), 0) + lo
    s = lax.broadcasted_iota(jnp.int32, (hi - lo, hi), 1)
    return scores, (t >= s) & (s < length)


def attention_forward(query_pre, key_pre, value_pre, cosine, sine, length, query, keys, values, logs, context):
    count, width = query.shape
    keys[...] = turned(key_pre, cosine, sine).astype(bf16)
    values[...] = value_pre.astype(bf16)
    lane = lax.broadcasted_iota(jnp.int32, (count, LANES), 1)
    kept = jnp.zeros((count, LANES), f32)
    for h in range(width // AHDIM):
        lanes = slice(h * AHDIM, (h + 1) * AHDIM)
        query[:, lanes] = turned(query_pre[:, lanes], cosine, sine).astype(bf16)
        found = []
        for i in range(count // BLOCK):
            lo, hi = i * BLOCK, (i + 1) * BLOCK
            scores, valid = scores_of(query[:, lanes], keys[...], lo, hi, length)
            masked = jnp.where(valid, scores, -1e30)
            peak = jnp.max(masked, axis=1, keepdims=True)
            expo = jnp.exp(masked - peak)
            total = jnp.sum(expo, axis=1, keepdims=True)
            found.append(peak + jnp.log(total))
            probs = (expo / total).astype(bf16)
            context[lo:hi, lanes] = plain_dot(probs, values[:hi, :]).astype(bf16)
        kept = jnp.where(lane == h, jnp.concatenate(found, axis=0), kept)
    logs[...] = kept


def attention_backward(d_context, query, keys, values, logs, cosine, sine, length, d_query_pre, d_keys, d_values):
    count, width = query.shape
    lane = lax.broadcasted_iota(jnp.int32, (count, LANES), 1)
    scale = AHDIM ** (-0.5)
    key_total = jnp.zeros((count, AHDIM), f32)
    value_total = jnp.zeros((count, AHDIM), f32)
    for h in range(width // AHDIM):
        lanes = slice(h * AHDIM, (h + 1) * AHDIM)
        log = column_of(logs[...], lane, h)
        pieces = []
        for i in range(count // BLOCK):
            lo, hi = i * BLOCK, (i + 1) * BLOCK
            scores, valid = scores_of(query[:, lanes], keys[...], lo, hi, length)
            probs = jnp.where(valid, jnp.exp(scores - log[lo:hi]), 0.0)
            grads = d_context[lo:hi, lanes]
            d_probs = right_trans(grads, values[:hi, :])
            delta = jnp.sum(probs * d_probs, axis=1, keepdims=True)
            d_scores = (probs * (d_probs - delta)).astype(bf16)
            pieces.append(plain_dot(d_scores, keys[:hi, :]) * scale)
            d_key = left_trans(d_scores, query[lo:hi, lanes]) * scale
            d_value = left_trans(probs.astype(bf16), grads)
            if hi < count:
                rest = jnp.zeros((count - hi, AHDIM), f32)
                d_key = jnp.concatenate([d_key, rest], axis=0)
                d_value = jnp.concatenate([d_value, rest], axis=0)
            key_total = key_total + d_key
            value_total = value_total + d_value
        d_query_pre[:, lanes] = turned(jnp.concatenate(pieces, axis=0), cosine, -sine).astype(bf16)
    d_keys[...] = turned(key_total, cosine, -sine)
    d_values[...] = value_total


def columns_of(channels, heads_width):
    places, start = {}, 0
    for name, size in (
        ("zgate", channels), ("query", heads_width), ("xpre", channels), ("state", 2 * STATE),
        ("key", AHDIM), ("value", AHDIM), ("step", LANES),
    ):
        places[name] = slice(start, start + size)
        start += size
    return places, start


def forward_kernel(
    lengths, zgate, query_pre, xpre, statepre, key_pre, value_pre, steppre, cosine, sine, conv_weight, conv_bias, state_taps, state_bias, step_bias, rates,
    skip_rep, gated, ssd, square, xconv, sconv, stepsize, cumul, inner, query, keys, values, logs,
    context, cumul_rows, *, slot,
):
    attention_forward(
        query_pre, key_pre[...], value_pre[...],
        cosine[...], sine[...], lengths[slot], query, keys, values, logs, context,
    )
    count, channels = xpre.shape
    xlin = tap_sum(xpre[...], conv_weight[...], conv_bias[...])
    xconv[...] = (xlin * jax.nn.sigmoid(xlin)).astype(bf16)
    slin = tap_sum(statepre[...], state_taps[...], state_bias[...])
    sconv[...] = (slin * jax.nn.sigmoid(slin)).astype(bf16)
    inner[...] = right_trans(sconv[:, STATE:], sconv[:, :STATE])
    step = jax.nn.softplus(steppre[...] + step_bias[...])
    stepsize[...] = step
    row = lax.broadcasted_iota(jnp.int32, (count, count), 0)
    col = lax.broadcasted_iota(jnp.int32, (count, count), 1)
    total = exact_dot(jnp.where(row >= col, 1.0, 0.0), -step * rates[...])
    cumul[...] = total
    cumul_rows[...] = total.T
    square[...] = jnp.zeros_like(square)

    def pair(p):
        lanes = slice(p * LANES, (p + 1) * LANES)
        lane = lax.broadcasted_iota(jnp.int32, (count, LANES), 1)
        xvals = xconv[:, lanes].astype(f32)
        low_half = lane < MHDIM
        step_rep = jnp.where(
            low_half, column_of(stepsize[...], lane, 2 * p), column_of(stepsize[...], lane, 2 * p + 1)
        )
        weighted = (step_rep * xvals).astype(bf16)
        columns = [column_of(cumul[...], lane, 2 * p + h) for h in range(2)]
        for i in range(count // BLOCK):
            lo, hi = i * BLOCK, (i + 1) * BLOCK
            results = []
            for h in range(2):
                differ = columns[h][lo:hi] - cumul_rows[2 * p + h : 2 * p + h + 1, :hi]
                t = lax.broadcasted_iota(jnp.int32, (BLOCK, hi), 0) + lo
                s = lax.broadcasted_iota(jnp.int32, (BLOCK, hi), 1)
                decay = jnp.exp(jnp.where(t >= s, differ, -1e30))
                mixing = (inner[lo:hi, :hi] * decay).astype(bf16)
                results.append(plain_dot(mixing, weighted[:hi]))
            half = jnp.where(low_half[lo:hi], results[0], results[1])
            half = half + skip_rep[:, lanes] * xvals[lo:hi]
            ssd[lo:hi, lanes] = half
            z = zgate[lo:hi, lanes]
            value = half * (z * jax.nn.sigmoid(z))
            gated[lo:hi, lanes] = value
            square[lo:hi, :] += value * value

    for p in range(channels // LANES):
        pair(p)


def full(*shape):
    return jax.ShapeDtypeStruct(shape, f32)


def low(*shape):
    return jax.ShapeDtypeStruct(shape, bf16)


def in_vmem(count):
    return [pl.BlockSpec(memory_space=pltpu.VMEM)] * count


def in_hbm(shapes):
    return tuple(pltpu.HBM(s.shape, s.dtype) for s in shapes)


def whole_blocks(shapes):
    return [pl.BlockSpec(s.shape, lambda i, n=len(s.shape): (0,) * n) for s in shapes]


def mixers_forward(slot, lengths, *operands):
    count, channels = operands[0].shape
    heads_width = operands[1].shape[1]
    shapes = (
        full(count, channels), full(count, channels), full(count, LANES), low(count, channels),
        low(count, 2 * STATE), full(count, LANES), full(count, LANES), full(count, count),
        low(count, heads_width), low(count, AHDIM), low(count, AHDIM), full(count, LANES),
        low(count, heads_width),
    )
    return pl.pallas_call(
        functools.partial(forward_kernel, slot=slot),
        grid=(1,),
        out_shape=in_hbm(shapes),
        in_specs=[pl.BlockSpec(memory_space=pltpu.SMEM)] + in_vmem(len(operands)),
        out_specs=tuple(whole_blocks(shapes)),
        scratch_shapes=[pltpu.VMEM((LANES, count), f32)],
        compiler_params=pltpu.CompilerParams(vmem_limit_bytes=48 * 2**20),
        cost_estimate=pl.CostEstimate(
            flops=10**6, bytes_accessed=10**6, transcendentals=10**3
        ),
    )(lengths, *operands)


def backward_kernel(
    lengths, d_scaled_in, d_context_in, gated_in, inv_cross, gain, zgate, xpre, statepre, steppre,
    ssd, xconv, sconv, stepsize, cumul, inner,
    query, keys, values, logs, cosine, sine, conv_weight, conv_bias, state_taps, state_bias,
    step_bias, rates, skip_rep,
    back, d_statepre, d_keys, d_values, g_conv, g_state, g_heads, g_skip, g_gain,
    d_ssd, d_xvals, cumul_rows, d_inner, row_sums, col_sums, d_step, *, slot, places,
):
    count, channels = ssd.shape
    attention_backward(
        d_context_in[...].astype(bf16), query, keys, values, logs, cosine[...], sine[...],
        lengths[slot], back.at[:, places["query"]], d_keys, d_values,
    )
    back[:, places["key"]] = d_keys[...].astype(bf16)
    back[:, places["value"]] = d_values[...].astype(bf16)
    d_zgate, d_xpre = back.at[:, places["zgate"]], back.at[:, places["xpre"]]
    d_steppre = back.at[:, places["step"]]
    d_scaled = d_scaled_in[...]
    g_gain[...] = jnp.sum(d_scaled * gated_in[...] * inv_cross[:, 0:1], axis=0, keepdims=True)
    inv = inv_cross[:, 0:1]
    cross = inv_cross[:, 1:2]
    d_gated = inv * (d_scaled * gain[...]) - gated_in[...] * cross
    z = zgate[...]
    sig = jax.nn.sigmoid(z)
    d_low = (d_gated * (z * sig)).astype(bf16)
    d_ssd[...] = d_low
    d_zgate[...] = (d_gated * ssd[...] * sig * (1.0 + z * (1.0 - sig))).astype(bf16)
    g_skip[...] = jnp.sum(d_low.astype(f32) * xconv[...].astype(f32), axis=0, keepdims=True)
    cumul_rows[...] = cumul[...].T
    d_inner[...] = jnp.zeros_like(d_inner)
    row_sums[...] = jnp.zeros_like(row_sums)
    col_sums[...] = jnp.zeros_like(col_sums)
    d_step[...] = jnp.zeros_like(d_step)

    def pair(p):
        lanes = slice(p * LANES, (p + 1) * LANES)
        lane = lax.broadcasted_iota(jnp.int32, (count, LANES), 1)
        low_half = lane < MHDIM
        xvals = xconv[:, lanes].astype(f32)
        step_rep = jnp.where(
            low_half, column_of(stepsize[...], lane, 2 * p), column_of(stepsize[...], lane, 2 * p + 1)
        )
        weighted = (step_rep * xvals).astype(bf16)
        grads = d_ssd[:, lanes]
        columns = [column_of(cumul[...], lane, 2 * p + h) for h in range(2)]
        pieces = []
        for h in range(2):
            only = jnp.where(low_half == (h == 0), grads, jnp.zeros_like(grads))
            back_part = jnp.zeros((count, LANES), f32)
            sums = []
            col_total = jnp.zeros((1, count), f32)
            for i in range(count // BLOCK):
                lo, hi = i * BLOCK, (i + 1) * BLOCK
                differ = columns[h][lo:hi] - cumul_rows[2 * p + h : 2 * p + h + 1, :hi]
                t = lax.broadcasted_iota(jnp.int32, (BLOCK, hi), 0) + lo
                s = lax.broadcasted_iota(jnp.int32, (BLOCK, hi), 1)
                decay = jnp.exp(jnp.where(t >= s, differ, -1e30))
                mixing = inner[lo:hi, :hi] * decay
                part = left_trans(mixing.astype(bf16), only[lo:hi])
                d_mixing = right_trans(only[lo:hi], weighted[:hi])
                d_inner[lo:hi, :hi] += d_mixing * decay
                flow = d_mixing * mixing
                sums.append(jnp.sum(flow, axis=1, keepdims=True))
                down = jnp.sum(flow, axis=0, keepdims=True)
                if hi < count:
                    part = jnp.concatenate([part, jnp.zeros((count - hi, LANES), f32)], axis=0)
                    down = jnp.concatenate([down, jnp.zeros((1, count - hi), f32)], axis=1)
                back_part = back_part + part
                col_total = col_total + down
            here = lane == 2 * p + h
            row_sums[...] = jnp.where(here, jnp.concatenate(sums, axis=0), row_sums[...])
            col_sums[2 * p + h : 2 * p + h + 1, :] = col_total
            pieces.append(back_part)
        d_weighted = pieces[0] + pieces[1]
        d_xvals[:, lanes] = grads.astype(f32) * skip_rep[:, lanes] + d_weighted * step_rep
        product = d_weighted * xvals
        for h in range(2):
            value = jnp.sum(
                jnp.where(low_half == (h == 0), product, 0.0), axis=1, keepdims=True
            )
            d_step[...] = jnp.where(lane == 2 * p + h, value, d_step[...])

    for p in range(channels // LANES):
        pair(p)

    d_cumul = row_sums[...] - col_sums[...].T
    row = lax.broadcasted_iota(jnp.int32, (count, count), 0)
    col = lax.broadcasted_iota(jnp.int32, (count, count), 1)
    d_logdecay = exact_dot(jnp.where(row <= col, 1.0, 0.0), d_cumul)
    rate = rates[...]
    d_full = (d_step[...] - d_logdecay * rate) * jax.nn.sigmoid(steppre[...] + step_bias[...])
    d_steppre[...] = d_full.astype(bf16)
    g_heads[0:1, :] = jnp.sum(d_full, axis=0, keepdims=True)
    g_heads[1:2, :] = jnp.sum(-d_logdecay * stepsize[...] * rate, axis=0, keepdims=True)

    d_in = d_inner[...].astype(bf16)
    d_c = plain_dot(d_in, sconv[:, :STATE])
    d_b = left_trans(d_in, sconv[:, STATE:])
    slin = tap_sum(statepre[...], state_taps[...], state_bias[...])
    d_slin = jnp.concatenate([d_b, d_c], axis=1) * silu_slope(slin)
    back_state, tap_grads = tap_back(d_slin, statepre[...], state_taps[...])
    d_statepre[...] = back_state
    back[:, places["state"]] = back_state.astype(bf16)
    g_state[...] = jnp.concatenate([tap_grads, jnp.sum(d_slin, axis=0, keepdims=True)], axis=0)
    xlin = tap_sum(xpre[...], conv_weight[...], conv_bias[...])
    d_xlin = d_xvals[...] * silu_slope(xlin)
    back_x, tap_grads = tap_back(d_xlin, xpre[...], conv_weight[...])
    d_xpre[...] = back_x.astype(bf16)
    g_conv[...] = jnp.concatenate([tap_grads, jnp.sum(d_xlin, axis=0, keepdims=True)], axis=0)


def mixers_backward(slot, slots, held, lengths, *operands):
    count, channels = operands[0].shape
    heads_width = operands[1].shape[1]
    taps = operands[-7].shape[0]
    width = columns_of(channels, heads_width)[1]
    kernel = functools.partial(
        backward_kernel, slot=slot, places=columns_of(channels, heads_width)[0]
    )
    aliases = {}
    extra_specs, extra = [], ()
    if held is not None:
        aliases = {0: 0}
        extra_specs, extra = [pl.BlockSpec(memory_space=pl.ANY)], (held,)
        inside = kernel
        kernel = lambda _, *refs: inside(*refs)
    shapes = (
        full(count, 2 * STATE), full(count, AHDIM), full(count, AHDIM), full(taps + 1, channels),
        full(taps + 1, 2 * STATE), full(2, LANES), full(1, channels), full(1, channels),
    )
    return pl.pallas_call(
        kernel,
        grid=(1,),
        out_shape=in_hbm((low(slots * count, width),) + shapes),
        in_specs=extra_specs
        + [pl.BlockSpec(memory_space=pltpu.SMEM)]
        + in_vmem(len(operands)),
        out_specs=tuple(
            [pl.BlockSpec((count, width), lambda i: (slot, 0))] + whole_blocks(shapes)
        ),
        scratch_shapes=[
            pltpu.VMEM((count, channels), bf16),
            pltpu.VMEM((count, channels), f32),
            pltpu.VMEM((LANES, count), f32),
            pltpu.VMEM((count, count), f32),
            pltpu.VMEM((count, LANES), f32),
            pltpu.VMEM((LANES, count), f32),
            pltpu.VMEM((count, LANES), f32),
        ],
        input_output_aliases=aliases,
        compiler_params=pltpu.CompilerParams(vmem_limit_bytes=56 * 2**20),
        cost_estimate=pl.CostEstimate(
            flops=10**6, bytes_accessed=10**6, transcendentals=10**3
        ),
    )(*extra, lengths, *operands)


def feed_forward_kernel(normed, cot, gate_weight, up_weight, down_weight, *refs):
    inner, d_gate, d_up, back = refs[-4:]
    gate = plain_dot(normed[...], gate_weight[...])
    upper = plain_dot(normed[...], up_weight[...])
    d_inner = right_trans(cot[...], down_weight[...])
    sig = jax.nn.sigmoid(gate)
    silu = gate * sig
    inner[...] = (silu * upper).astype(bf16)
    d_gate[...] = (d_inner * upper * sig * (1.0 + gate * (1.0 - sig))).astype(bf16)
    d_up[...] = (d_inner * silu).astype(bf16)
    part = right_trans(d_gate[...], gate_weight[...]) + right_trans(d_up[...], up_weight[...])

    @pl.when(pl.program_id(0) == 0)
    def _():
        back[...] = part

    @pl.when(pl.program_id(0) > 0)
    def _():
        back[...] += part


def feed_forward_all(slot, slots, held, normed, cot, gate_weight, up_weight, down_weight):
    count, width = normed.shape
    hidden = gate_weight.shape[1]
    block = min(512, hidden)
    rows = pl.BlockSpec((count, width), lambda j: (0, 0))
    columns = pl.BlockSpec((width, block), lambda j: (0, j))
    joint = pl.BlockSpec((count, block), lambda j: (slot, j))
    extra = () if held is None else tuple(held)
    return pl.pallas_call(
        feed_forward_kernel,
        grid=(hidden // block,),
        out_shape=tuple([low(slots * count, hidden)] * 3 + [full(count, width)]),
        in_specs=[
            rows, rows, columns, columns, pl.BlockSpec((block, width), lambda j: (j, 0))
        ] + [pl.BlockSpec(memory_space=pl.ANY)] * len(extra),
        out_specs=(joint, joint, joint, rows),
        input_output_aliases={5 + n: n for n in range(len(extra))},
        compiler_params=pltpu.CompilerParams(vmem_limit_bytes=56 * 2**20),
        cost_estimate=pl.CostEstimate(flops=10**6, bytes_accessed=10**6, transcendentals=10**3),
    )(normed, cot, gate_weight, up_weight, down_weight, *extra)


def swap(values, axis, size, bit):
    return lax.ppermute(values, axis, [(i, i ^ bit) for i in range(size)])


def halving_order(members, bit, limit):
    if bit >= limit:
        return members
    low = halving_order([m for m in members if not m & bit], bit * 2, limit)
    high = halving_order([m for m in members if m & bit], bit * 2, limit)
    return low + high


class Order:
    def __init__(self):
        self.last = ()
        self.queue = []

    def point(self, value, skip=0):
        if len(self.queue) <= skip:
            return value
        return lax.optimization_barrier((value, self.queue.pop(skip)))[0]

    def gate(self, *values):
        return lax.optimization_barrier((values, self.last))[0]

    def mark(self, *values):
        self.last = values


def scatter_all(size, t_size, parts, cuts, halves, rests, gain, vector, shared_rows, blocks):
    rows = parts[0].shape[0]
    works = len(parts)
    share = rows // size
    chunk = min(256, rows // 4)
    levels = size.bit_length() - 1
    spans = []
    for level in range(1, levels):
        lo, hi = rows >> (level + 1), rows >> level
        step = min(chunk, hi - lo)
        spans += [(level, start, step) for start in range(hi - step, lo - 1, -step)]
    spans.append((levels, 0, share))
    pieces = [(w,) + span for w in range(works) for span in spans]
    per_work = len(spans)
    widths = [p.shape[1] for p in parts]
    ranges = []
    for cut in cuts:
        stops = [sum(cut[: n + 1]) for n in range(len(cut))]
        ranges.append([(stop - size_, size_) for stop, size_ in zip(stops, cut)])
    outputs = sum(len(cut) for cut in cuts)
    wide = max(widths)
    extra = len(halves)
    half_shape = halves[0].shape
    half, width = half_shape
    slots = 1 + max(rest[0] for rest in rests)
    extras = [value for rest in rests for value in rest[1:]]
    wholes = [n for n, rest in enumerate(rests) if len(rest) == 2]

    def kernel(*refs):
        held_in, refs = refs[:works], refs[works:]
        own, refs = refs[:extra], refs[extra:]
        beside = []
        for rest in rests:
            beside.append(refs[: len(rest) - 1])
            refs = refs[len(rest) - 1 :]
        gain_ref, small, block_ref, refs = refs[0], refs[1], refs[2], refs[3:]
        outs = []
        for cut in cuts:
            outs.append(refs[: len(cut)])
            refs = refs[len(cut) :]
        far, refs = refs[:extra], refs[extra:]
        result, grad, small_out, wide_out, block_out, refs = (
            refs[0], refs[1], refs[2], refs[3], refs[4], refs[5:]
        )
        loads, pair_loads, totals, low_rows, theirs, refs = (
            refs[0], refs[1], refs[2], refs[3], refs[4], refs[5:]
        )
        boxes, wide_boxes, turned_rows, block_boxes, refs = (
            refs[0], refs[1], refs[2], refs[3], refs[4:]
        )
        landed, refs = refs[:works], refs[works:]
        later, refs = refs[: works * (levels - 1)], refs[works * (levels - 1) :]
        load_sems, out_sems, x_send, x_recv, z_send, z_recv, y_sems, c_sems, pair_sems, v_sems, w_sems, b_sems = refs
        me = lax.axis_index("dp")
        spot = lax.axis_index("tensor")

        def neighbour(bit):
            return spot + bit - 2 * bit * lax.rem(spot // bit, 2)


        def partner(level):
            bit = 1 << level
            return me + bit - 2 * bit * lax.rem(me // bit, 2)

        barrier = pltpu.get_barrier_semaphore()
        for other in range(1, size):
            pl.semaphore_signal(
                barrier, inc=1, device_id={"dp": lax.rem(me + other, size)}, device_id_type=MESH
            )
        for other in range(1, t_size):
            pl.semaphore_signal(
                barrier, inc=1, device_id={"tensor": lax.rem(spot + other, t_size)},
                device_id_type=MESH,
            )
        pl.semaphore_wait(barrier, size + t_size - 2)

        def small_copy(other):
            return pltpu.make_async_remote_copy(
                src_ref=small, dst_ref=boxes.at[size - other], send_sem=v_sems.at[0, other],
                recv_sem=v_sems.at[1, size - other],
                device_id={"dp": lax.rem(me + other, size)}, device_id_type=MESH,
            )

        def block_copy(other):
            return pltpu.make_async_remote_copy(
                src_ref=block_ref.at[other], dst_ref=block_boxes.at[size - other],
                send_sem=b_sems.at[0, other], recv_sem=b_sems.at[1, size - other],
                device_id={"dp": lax.rem(me + other, size)}, device_id_type=MESH,
            )

        def wide_copy(other):
            return pltpu.make_async_remote_copy(
                src_ref=small_out.at[pl.ds(0, shared_rows), :], dst_ref=wide_boxes.at[t_size - other],
                send_sem=w_sems.at[0, other], recv_sem=w_sems.at[1, t_size - other],
                device_id={"tensor": lax.rem(spot + other, t_size)}, device_id_type=MESH,
            )

        def in_turn(kept, count, place, rows):
            total = jnp.zeros((rows, LANES), f32)
            for number in range(count):
                offset = lax.rem(number - place + count, count)
                total = total + kept[offset]
            return total

        def small_sums(stage):
            if stage == 0:
                boxes[0] = small[...]
                for other in range(1, size):
                    small_copy(other).wait_recv()
                small_out[...] = in_turn(boxes, size, me, small.shape[0])
                for other in range(1, t_size):
                    wide_copy(other).start()
                block_boxes[0] = block_ref[0]
                for other in range(1, size):
                    block_copy(other).wait_recv()
                block_out[...] = in_turn(block_boxes, size, me, blocks.shape[1])
            else:
                wide_boxes[0] = small_out[:shared_rows, :]
                for other in range(1, t_size):
                    wide_copy(other).wait_recv()
                wide_out[...] = in_turn(wide_boxes, t_size, spot, shared_rows)


        def y_copy(e):
            return pltpu.make_async_remote_copy(
                src_ref=own[e], dst_ref=far[e], send_sem=y_sems.at[0, e], recv_sem=y_sems.at[1, e],
                device_id={"tensor": neighbour(2)}, device_id_type=MESH,
            )

        core = lax.rem(spot, 2)

        def rows_of(place):
            return pl.ds(pl.multiple_of(place * half, 8), half)

        def c_copy(e):
            slot = rests[e][0]
            if e in wholes:
                target = theirs.at[wholes.index(e)]
            else:
                target = grad.at[slot, rows_of(core), :]
            return pltpu.make_async_remote_copy(
                src_ref=totals.at[e], dst_ref=target, send_sem=c_sems.at[0, e],
                recv_sem=c_sems.at[1, e], device_id={"tensor": neighbour(1)}, device_id_type=MESH,
            )

        def fetch(source, place):
            return pltpu.make_async_copy(source, pair_loads.at[place], pair_sems.at[0, place])

        def keep(e, place):
            slot = rests[e][0]
            if e in wholes:
                n = 2 * wholes.index(e) + place
                target = result.at[slot, rows_of(core if place == 0 else 1 - core), :]
                return pltpu.make_async_copy(low_rows.at[n], target, pair_sems.at[1 + place, e])
            return pltpu.make_async_copy(
                totals.at[e], grad.at[slot, rows_of(core), :], pair_sems.at[1, e]
            )

        def exchange(e):
            y_copy(e).wait_recv()
            sources = [own[e], far[e]]
            if e in wholes:
                sources.append(beside[e][0].at[pl.ds(0, half), :])
            else:
                sources += [beside[e][0], beside[e][1]]
            for place, source in enumerate(sources):
                fetch(source, place).start()
            for place, source in enumerate(sources):
                fetch(source, place).wait()
            total = pair_loads[0] + pair_loads[1]
            if e in wholes:
                totals[e] = total
                low_rows[2 * wholes.index(e)] = (pair_loads[2] + total).astype(bf16)
            else:
                unit = pair_loads[3]
                scaled = total * gain_ref[...]
                mean = jnp.sum(scaled * unit, axis=1, keepdims=True) / width
                totals[e] = pair_loads[2] + beside[e][2][...] * (scaled - unit * mean)
            c_copy(e).start()
            keep(e, 0).start()

        def complete(e):
            fetch(beside[e][0].at[pl.ds(half, half), :], 0).start()
            c_copy(e).wait_recv()
            fetch(beside[e][0].at[pl.ds(half, half), :], 0).wait()
            n = wholes.index(e)
            low_rows[2 * n + 1] = (pair_loads[0] + theirs[n]).astype(bf16)
            keep(e, 1).start()

        def first_copy(number):
            w, _, start, step = pieces[number]
            return pltpu.make_async_remote_copy(
                src_ref=held_in[w].at[pl.ds(rows // 2 + start, step), :],
                dst_ref=landed[w].at[pl.ds(start, step), :],
                send_sem=x_send.at[number],
                recv_sem=x_recv.at[number],
                device_id={"dp": partner(0)},
                device_id_type=MESH,
            )

        def load(number):
            w, _, start, step = pieces[number]
            return pltpu.make_async_copy(
                held_in[w].at[pl.ds(start, step), :],
                loads.at[number % 2, pl.ds(0, step), pl.ds(0, widths[w])],
                load_sems.at[number % 2],
            )

        def later_copy(number):
            w, level, start, step = pieces[number]
            return pltpu.make_async_remote_copy(
                src_ref=landed[w].at[pl.ds(start, step), :],
                dst_ref=later[w * (levels - 1) + level - 1].at[pl.ds(start - (rows >> (level + 1)), step), :],
                send_sem=z_send.at[number],
                recv_sem=z_recv.at[number],
                device_id={"dp": partner(level)},
                device_id_type=MESH,
            )

        def stores(w):
            copies = []
            for n, (lo, length) in enumerate(ranges[w]):
                if w == 0:
                    source = turned_rows.at[pl.ds(lo, length), :]
                else:
                    source = landed[w].at[pl.ds(0, share), pl.ds(lo, length)]
                copies.append(pltpu.make_async_copy(source, outs[w][n], out_sems.at[w, n]))
            return copies

        for other in range(1, size):
            small_copy(other).start()
            block_copy(other).start()
        for e in range(extra):
            y_copy(e).start()
        for number in range(len(pieces)):
            first_copy(number).start()
        load(0).start()
        arrived = set()

        def need(w, level, start, step):
            base = rows >> (level + 1)
            for other in range(w * per_work, (w + 1) * per_work):
                _, its_level, its_start, its_step = pieces[other]
                if its_level != level or other in arrived:
                    continue
                if its_start - base < start + step and start < its_start - base + its_step:
                    later_copy(other).wait_recv()
                    arrived.add(other)

        def finish(w):
            level = levels - 1
            need(w, level, 0, share)
            landed[w][:share, :] += later[w * (levels - 1) + level - 1][:share, :]
            if w == 0:
                turned_rows[...] = landed[w][:share, :].T
            for copy in stores(w):
                copy.start()

        for number, (w, level, start, step) in enumerate(pieces):
            load(number).wait()
            if number + 1 < len(pieces):
                load(number + 1).start()
            first_copy(number).wait_recv()
            value = loads[number % 2, :step, : widths[w]] + landed[w][start : start + step, :]
            for before in range(1, min(level, levels - 1)):
                need(w, before, start, step)
                value = value + later[w * (levels - 1) + before - 1][start : start + step, :]
            landed[w][start : start + step, :] = value
            if level < levels:
                later_copy(number).start()
            if w and number == w * per_work + min(2, per_work - 1):
                finish(w - 1)
            if number in (0, 2):
                small_sums(number // 2)
            if number % 2 and number // 2 < extra:
                exchange(number // 2)
            if number % 2 == 0 and number // 2 - 2 in wholes:
                complete(number // 2 - 2)
        for e in range(len(pieces) // 2, extra):
            exchange(e)
        for e in wholes:
            if 2 * (e + 2) >= len(pieces):
                complete(e)
        finish(works - 1)
        for other in range(1, size):
            small_copy(other).wait_send()
            block_copy(other).wait_send()
        for other in range(1, t_size):
            wide_copy(other).wait_send()
        for e in range(extra):
            y_copy(e).wait_send()
            c_copy(e).wait_send()
            keep(e, 0).wait()
            if e in wholes:
                keep(e, 1).wait()
            else:
                c_copy(e).wait_recv()
        for number, (w, level, start, step) in enumerate(pieces):
            first_copy(number).wait_send()
            if level < levels:
                later_copy(number).wait_send()
        for w in range(works):
            for copy in stores(w):
                copy.wait()

    scratch = [
        pltpu.VMEM((2, chunk, wide), f32),
        pltpu.VMEM((4,) + half_shape, f32),
        pltpu.VMEM((extra,) + half_shape, f32),
        pltpu.VMEM((2 * len(wholes),) + half_shape, bf16),
        pltpu.VMEM((len(wholes),) + half_shape, f32),
        pltpu.VMEM((size,) + vector.shape, f32),
        pltpu.VMEM((t_size, shared_rows, LANES), f32),
        pltpu.VMEM((widths[0], share), f32),
        pltpu.VMEM(blocks.shape, f32),
    ]
    scratch += [pltpu.VMEM((rows // 2, n), f32) for n in widths]
    scratch += [
        pltpu.VMEM((rows >> (level + 1), n), f32) for n in widths for level in range(1, levels)
    ]
    scratch += [
        pltpu.SemaphoreType.DMA((2,)),
        pltpu.SemaphoreType.DMA((works, max(len(cut) for cut in cuts))),
    ] + [pltpu.SemaphoreType.DMA((len(pieces),))] * 4
    scratch += [pltpu.SemaphoreType.DMA((n, extra)) for n in (2, 2)]
    scratch += [pltpu.SemaphoreType.DMA((3, max(4, extra)))]
    scratch += [pltpu.SemaphoreType.DMA((2, n)) for n in (size, t_size, size)]
    results = pl.pallas_call(
        kernel,
        out_shape=tuple(
            [full(n, share) for n in cuts[0]]
            + [full(share, n) for cut in cuts[1:] for n in cut]
            + [full(*half_shape)] * extra
            + [low(slots, 2 * half, width), full(slots, 2 * half, width)]
            + [full(*vector.shape), full(shared_rows, LANES), full(*blocks.shape[1:])]
        ),
        in_specs=[pl.BlockSpec(memory_space=pl.ANY)] * (works + extra)
        + [
            pl.BlockSpec(memory_space=pltpu.VMEM if value.shape[1] == 1 else pl.ANY)
            for value in extras
        ]
        + in_vmem(3),
        out_specs=tuple([pl.BlockSpec(memory_space=pl.ANY)] * (outputs + extra + 2) + in_vmem(3)),
        scratch_shapes=scratch,
        compiler_params=pltpu.CompilerParams(
            collective_id=0, has_side_effects=True, vmem_limit_bytes=60 * 2**20
        ),
        cost_estimate=pl.CostEstimate(
            flops=10**6, bytes_accessed=10**6, transcendentals=0
        ),
    )(*parts, *halves, *extras, gain, vector, blocks)
    return results[:outputs], *results[outputs + extra :]


def make_per_device(dp_size, t_size):
    def per_device(
        tokens,
        lengths,
        out_grad,
        input_gain,
        mamba_gate_weight,
        mamba_in_weight,
        state_weight,
        step_weight,
        conv_weight,
        conv_bias,
        conv_state_weight,
        conv_state_bias,
        step_bias,
        decay_log,
        skip_scale,
        mamba_gain,
        mamba_out_weight,
        query_weight,
        key_value_weight,
        attn_out_weight,
        ffn_gain,
        gate_weight,
        up_weight,
        down_weight,
    ):
        micro = tokens.shape[0]
        count = tokens.shape[1]
        width = tokens.shape[2]
        half = count // 2
        local_heads = step_weight.shape[1]
        q_local = query_weight.shape[1] // AHDIM
        kv_width = key_value_weight.shape[1] // 2
        group_size = AHEADS // KVHEADS
        me_dp = lax.axis_index("dp")
        me_t = lax.axis_index("tensor")
        core = lax.rem(me_t, 2)
        kv_head = me_t * q_local // group_size
        key_weight = lax.dynamic_slice_in_dim(key_value_weight, kv_head * AHDIM, AHDIM, 1)
        value_weight = lax.dynamic_slice_in_dim(
            key_value_weight, kv_width + kv_head * AHDIM, AHDIM, 1
        )
        rows = jnp.arange(count)
        freqs = rope_base ** (-(jnp.arange(AHDIM // 2).astype(f32) * 2.0) / AHDIM)
        angles = rows.astype(f32)[:, None] * freqs[None, :]
        cosine, sine = jnp.cos(angles), jnp.sin(angles)
        cosine = jnp.concatenate([cosine, cosine], axis=1)
        sine = jnp.concatenate([-sine, sine], axis=1)
        channels = mamba_in_weight.shape[1]
        heads_width = query_weight.shape[1]
        places, _ = columns_of(channels, heads_width)
        pad_step = LANES - local_heads

        def lane_row(vector):
            return jnp.pad(vector, (0, pad_step))[None]

        mixer_rows = (
            conv_weight, conv_bias[None], conv_state_weight, conv_state_bias[None],
            lane_row(step_bias), lane_row(jnp.exp(decay_log)), jnp.repeat(skip_scale, MHDIM)[None],
        )
        step_lanes = jnp.pad(step_weight, ((0, 0), (0, pad_step)))
        in_weights = (
            mamba_gate_weight, query_weight, mamba_in_weight, state_weight, key_weight,
            value_weight, step_lanes,
        )

        def t_swap(values, bit):
            return swap(values, "tensor", t_size, bit)

        def t_total(values):
            bit = 1
            while bit < t_size:
                values = values + t_swap(values, bit)
                bit *= 2
            return values

        def mine(values):
            return lax.dynamic_slice_in_dim(values, core * half, half, 0)

        def other(values):
            return lax.dynamic_slice_in_dim(values, (1 - core) * half, half, 0)

        def halves(values):
            values = lax.optimization_barrier(values)
            return mine(values), other(values)

        def relative(values):
            return jnp.concatenate([mine(values), other(values)], axis=0)

        def in_order(own, far):
            return jnp.where(
                core == 0,
                jnp.concatenate([own, far], axis=0),
                jnp.concatenate([far, own], axis=0),
            )

        def half_sum(own, far, pieces):
            own = own + t_swap(far, 1)
            bit = 2
            while bit < t_size // 2:
                own = own + t_swap(own, bit)
                bit *= 2
            step = -(-own.shape[0] // (8 * pieces)) * 8
            parts = []
            for start in range(0, own.shape[0], step):
                parts.append(t_swap(own[start : start + step], bit))
            order.queue += parts
            return own, parts

        def add_up(own, parts):
            for part in parts:
                order.queue = [p for p in order.queue if p is not part]
            own, *parts = order.gate(own, *parts)
            return own + jnp.concatenate(parts, axis=0)

        block = width // dp_size

        order = Order()

        def forward(index, slot):
            inputs = slot.astype(f32)
            inv_one = lax.rsqrt(jnp.mean(inputs * inputs, axis=-1, keepdims=True) + epsilon)
            unit_one = inputs * inv_one
            normed = (unit_one * input_gain).astype(bf16)
            normed = order.point(normed)
            pre = [plain_dot(normed, w) for w in in_weights]
            gated, ssd, square, *kept, query, keys, values, logs, context = mixers_forward(
                index, lengths, *pre, cosine, sine, *mixer_rows
            )
            gated = order.point(order.point(gated))
            total_square = t_total(jnp.sum(square, axis=-1))
            inv_mamba = lax.rsqrt(total_square / DSSM + epsilon)[:, None]
            scaled = (gated * inv_mamba * mamba_gain).astype(bf16)
            mixer = jnp.concatenate([scaled, context], axis=1)
            mixed_own, mixed_far = half_sum(
                *halves(plain_dot(scaled, mamba_out_weight) + plain_dot(context, attn_out_weight)),
                3,
            )
            order.mark(mixed_own)
            return dict(
                mixed_own=mixed_own, mixed_far=mixed_far, inputs=inputs, inv_one=inv_one,
                unit_one=unit_one, normed=normed, pre=pre, gated=gated, ssd=ssd, kept=kept,
                attention=(query, keys, values, logs), inv_mamba=inv_mamba, mixer=mixer,
            )

        def feed_forward(index, k, held):
            hidden_own = mine(k["inputs"]) + add_up(k["mixed_own"], k["mixed_far"])
            hidden = order.point(jnp.concatenate([hidden_own, t_swap(hidden_own, 1)], axis=0))
            inv_two = lax.rsqrt(jnp.mean(hidden * hidden, axis=-1, keepdims=True) + epsilon)
            unit_two = hidden * inv_two
            normed_two = (unit_two * ffn_gain).astype(bf16)
            valid = (rows < lengths[index]).astype(f32)[:, None]
            cotangent = relative(out_grad[index].astype(f32) * valid)
            cot_low = cotangent.astype(bf16)
            *held, back = feed_forward_all(
                index, micro, held, normed_two, cot_low, gate_weight, up_weight, down_weight
            )
            if index == micro - 1:
                cot_all = jnp.concatenate([p["cot_low"] for p in slots[:index]] + [cot_low], axis=0)
                k["part_down"] = left_trans(order.point(held[0]), cot_all)
                back = order.point(back)
                back = lax.optimization_barrier((back, k["part_down"]))[0]
            else:
                back = order.point(order.point(back))
            back_own, back_far = half_sum(back[:half], back[half:], 3)
            order.mark(back_own)
            k.update(
                back_own=back_own, back_far=back_far,
                hidden=hidden, inv_two=inv_two[:half], unit_two=unit_two[:half],
                normed_two=normed_two, cotangent=cotangent, cot_low=cot_low,
            )
            return held

        def output_sum(index, k):
            (inner_ffn,) = order.gate(
                lax.slice_in_dim(inner_all, index * count, (index + 1) * count, axis=0)
            )
            ffn = plain_dot(inner_ffn, down_weight)
            k["ffn_own"] = ffn[:half] + t_swap(ffn[half:], 1)
            order.mark(k["ffn_own"])

        def back_head(k):
            unit_two = k["unit_two"]
            g_ffn_gain = jnp.sum(k["back_own"] * unit_two, axis=0)
            d_normed_two = add_up(k["back_own"], k["back_far"])
            d_unit_two = d_normed_two * ffn_gain
            d_rest = k["inv_two"] * (
                d_unit_two - unit_two * jnp.mean(d_unit_two * unit_two, axis=-1, keepdims=True)
            )
            d_both = k["cotangent"] + jnp.concatenate([d_rest, t_swap(d_rest, 1)], axis=0)
            d_mixed = in_order(d_both[:half], d_both[half:]).astype(bf16)
            d_scaled = right_trans(d_mixed, mamba_out_weight)
            d_context = right_trans(d_mixed, attn_out_weight)
            k["g_ffn_gain"] = g_ffn_gain
            k["d_hidden_own"] = d_both[:half]
            k["d_mixed"], k["d_scaled"], k["d_context"] = d_mixed, d_scaled, d_context
            k["cross"] = t_total(jnp.sum(d_scaled * mamba_gain * k["gated"], axis=-1))[:, None]
            order.mark(d_scaled, d_context)

        def back_mixers(index, k, held):
            d_scaled, cross = order.gate(k["d_scaled"], k["cross"])
            inv = k["inv_mamba"]
            inv_cross = jnp.concatenate([inv, inv**3 * cross / DSSM], axis=1)
            inv_cross = jnp.pad(inv_cross, ((0, 0), (0, LANES - 2)))
            back, d_statepre, d_keys, d_values, g_conv, g_state, g_heads, g_skip, g_gain = (
                mixers_backward(
                    index, micro, held, lengths, d_scaled, k["d_context"], k["gated"], inv_cross,
                    mamba_gain[None], k["pre"][0], k["pre"][2], k["pre"][3], k["pre"][6], k["ssd"],
                    *k["kept"], *k["attention"], cosine, sine, *mixer_rows,
                )
            )
            kv_far = jnp.where(core == 0, d_values, d_keys)
            kv_own = jnp.where(core == 0, d_keys, d_values)
            k["kv_sum"] = kv_own + t_swap(kv_far, 1)
            k["d_statepre"] = d_statepre
            k.update(
                g_conv_weight=g_conv[:-1], g_conv_bias=g_conv[-1],
                g_conv_state_weight=g_state[:-1], g_conv_state_bias=g_state[-1],
                g_step_bias=g_heads[0, :local_heads], g_decay_log=g_heads[1, :local_heads],
                g_skip=jnp.sum(g_skip.reshape(local_heads, MHDIM), axis=1),
                g_mamba_gain=g_gain[0],
            )
            order.mark(back)
            return back

        def back_inputs(index, k, back):
            back, d_statepre = order.gate(back, k["d_statepre"])
            piece = d_statepre.shape[1] // t_size
            parts = [
                lax.dynamic_slice_in_dim(d_statepre, jnp.bitwise_xor(me_t, q) * piece, piece, 1)
                for q in range(t_size)
            ]
            pieces = halving_order(list(range(0, t_size, 2)), 2, t_size)
            state_sum = jnp.concatenate([parts[q] for q in pieces], axis=1) + t_swap(
                jnp.concatenate([parts[q ^ 1] for q in pieces], axis=1), 1
            )
            bit = 2
            while bit < t_size:
                cut = state_sum.shape[1] // 2
                state_sum = state_sum[:, :cut] + t_swap(state_sum[:, cut:], bit)
                bit *= 2
            k["shared"] = jnp.concatenate([state_sum, k["kv_sum"]], axis=1).astype(bf16)
            rows_back = lax.slice_in_dim(back, index * count, (index + 1) * count, axis=0)
            norm_own, norm_other = halves(right_trans(rows_back, in_weight))
            k["norm_own"] = norm_own + t_swap(norm_other, 1)
            unit_own = mine(k["unit_one"])
            k["g_input_gain"] = jnp.sum(k["norm_own"] * unit_own, axis=0)
            order.mark(k["norm_own"])

        slots = []
        for index in range(micro):
            slot = tokens[index]
            if index:
                (slot,) = order.gate(slot)
            slots.append(forward(index, slot))
        held = None
        for index in range(micro):
            held = feed_forward(index, slots[index], held)
        inner_all, d_gate_all, d_up_all = held

        def joined(name):
            return jnp.concatenate([k[name] for k in slots], axis=0)

        def relative_columns(values):
            blocks = halving_order(list(range(dp_size)), 1, dp_size)
            return jnp.concatenate(
                [
                    lax.dynamic_slice_in_dim(values, jnp.bitwise_xor(me_dp, r) * block, block, 1)
                    for r in blocks
                ],
                axis=1,
            )

        def scattered(part, dimension):
            return lax.psum_scatter(part, "dp", scatter_dimension=dimension, tiled=True)

        g_down = scattered(slots[-1]["part_down"], 1)
        first, last = slots
        in_weight = jnp.concatenate(order.gate(*in_weights), axis=1)
        order.mark(in_weight)
        back_head(first)
        (two_all,) = order.gate(joined("normed_two"))
        part_gate = order.point(left_trans(two_all, d_gate_all))
        order.mark(part_gate)
        g_gate = scattered(part_gate, 0)
        (two_all,) = order.gate(two_all)
        part_up = order.point(left_trans(two_all, d_up_all))
        order.mark(part_up)
        g_up = scattered(part_up, 0)
        for index, k in enumerate(slots):
            output_sum(index, k)
        back_head(last)
        back_first = back_mixers(0, first, None)
        back_inputs(0, first, back_first)
        back = back_mixers(1, last, back_first)
        back_inputs(1, last, back)
        one_columns = relative_columns(order.gate(joined("normed"))[0])
        part_outs = left_trans(relative_columns(joined("d_mixed")), joined("mixer"))
        part_early = left_trans(one_columns, back[:, : channels + heads_width])
        part_late = left_trans(
            one_columns,
            jnp.concatenate([back[:, places["xpre"]], joined("shared")], axis=1),
        )
        part_step = left_trans(joined("normed"), back[:, places["step"]])[:, :local_heads]
        step_size = block * local_heads
        step_rows = -(-step_size // (8 * LANES)) * 8
        step_blocks = jnp.pad(
            part_step.reshape(dp_size, step_size), ((0, 0), (0, step_rows * LANES - step_size))
        ).reshape(dp_size, step_rows, LANES)
        step_blocks = lax.dynamic_slice_in_dim(
            jnp.concatenate([step_blocks, step_blocks], axis=0), me_dp, dp_size, 0
        )

        def total(name):
            value = slots[0][name]
            for k in slots[1:]:
                value = value + k[name]
            return value

        names = [
            "g_conv_state_weight", "g_conv_state_bias", "g_input_gain", "g_ffn_gain",
            "g_conv_weight", "g_conv_bias", "g_step_bias", "g_decay_log", "g_skip",
            "g_mamba_gain",
        ]
        small = {name: total(name) for name in names}
        vector = jnp.concatenate([small[name].reshape(-1) for name in names])
        vector_rows = -(-vector.size // (8 * LANES)) * 8
        vector = jnp.pad(vector, (0, vector_rows * LANES - vector.size)).reshape(-1, LANES)
        shared_size = sum(small[name].size for name in names[:4])
        shared_rows = -(-shared_size // (8 * LANES)) * 8

        sums = [first["norm_own"], first["ffn_own"], last["ffn_own"], last["norm_own"]]
        rests = [
            (0, first["d_hidden_own"], mine(first["unit_one"]), mine(first["inv_one"])),
            (0, first["hidden"]),
            (1, last["hidden"]),
            (1, last["d_hidden_own"], mine(last["unit_one"]), mine(last["inv_one"])),
        ]
        shared_width = joined("shared").shape[1]
        cuts = [
            [mamba_out_weight.shape[0], attn_out_weight.shape[0]],
            [channels, heads_width],
            [channels, shared_width],
        ]
        grads, out, in_grad, vector, wide_vector, g_step = scatter_all(
            dp_size, t_size, [part_outs, part_early, part_late], cuts, sums, rests,
            input_gain[None], vector, shared_rows, step_blocks,
        )
        g_mamba_out, g_attn_out, g_mamba_gate, g_query, g_mamba_in, tail = grads
        g_step = g_step.reshape(-1)[:step_size].reshape(block, local_heads)
        vector, wide_vector = vector.reshape(-1), wide_vector.reshape(-1)
        start = 0
        for name in names:
            shape, size = small[name].shape, small[name].size
            source = wide_vector if start < shared_size else vector
            small[name] = source[start : start + size].reshape(shape)
            start += size
        place = me_dp * t_size + me_t
        share = conv_state_bias.shape[0] // (dp_size * t_size)
        g_conv_state_weight = lax.dynamic_slice_in_dim(
            small["g_conv_state_weight"], place * share, share, 1
        )
        g_conv_state_bias = lax.dynamic_slice_in_dim(
            small["g_conv_state_bias"], place * share, share, 0
        )
        g_input_gain = lax.dynamic_slice_in_dim(small["g_input_gain"], me_dp * block, block, 0)
        g_ffn_gain = lax.dynamic_slice_in_dim(small["g_ffn_gain"], me_dp * block, block, 0)
        heads = [small[name] for name in names[4:]]

        sub = block // t_size
        rowsets = []
        for q in range(t_size):
            part = lax.dynamic_slice_in_dim(tail, jnp.bitwise_xor(me_t, q) * sub, sub, 0)
            rowsets.append(part if q == 0 else t_swap(part, q))
        stacked = jnp.stack(rowsets)
        piece = state_weight.shape[1] // t_size
        sources = [
            lax.dynamic_index_in_dim(stacked, jnp.bitwise_xor(me_t, j), 0, keepdims=False)
            for j in range(t_size)
        ]
        g_state = jnp.concatenate([s[:, :piece] for s in sources], axis=1)
        pairs = t_size // 2
        g_kv = jnp.concatenate(
            [sources[(b % pairs) * 2 + b // pairs][:, piece:] for b in range(t_size)], axis=1
        )
        return (
            out,
            in_grad,
            g_input_gain,
            g_mamba_gate,
            g_mamba_in,
            g_state,
            g_step,
            heads[0],
            heads[1],
            g_conv_state_weight,
            g_conv_state_bias,
            heads[2],
            heads[3],
            heads[4],
            heads[5],
            g_mamba_out,
            g_query,
            g_kv,
            g_attn_out,
            g_ffn_gain,
            g_gate,
            g_up,
            g_down,
        )

    return per_device


def solution(mesh):
    placed = (
        P("dp", None, None),
        P("dp"),
        P("dp", None, None),
        P(),
        P(None, "tensor"),
        P(None, "tensor"),
        P(),
        P(None, "tensor"),
        P(None, "tensor"),
        P("tensor"),
        P(),
        P(),
        P("tensor"),
        P("tensor"),
        P("tensor"),
        P("tensor"),
        P("tensor", None),
        P(None, "tensor"),
        P(),
        P("tensor", None),
        P(),
        P(None, "tensor"),
        P(None, "tensor"),
        P("tensor", None),
    )
    return jax.shard_map(
        make_per_device(mesh.shape["dp"], mesh.shape["tensor"]),
        mesh=mesh,
        in_specs=placed,
        out_specs=(
            P("dp", None, None),
            P("dp", None, None),
            P("dp"),
            P("dp", "tensor"),
            P("dp", "tensor"),
            P(("dp", "tensor"), None),
            P("dp", "tensor"),
            P(None, "tensor"),
            P("tensor"),
            P(None, ("dp", "tensor")),
            P(("dp", "tensor")),
            P("tensor"),
            P("tensor"),
            P("tensor"),
            P("tensor"),
            P("tensor", "dp"),
            P("dp", "tensor"),
            P(("dp", "tensor"), None),
            P("tensor", "dp"),
            P("dp"),
            P("dp", "tensor"),
            P("dp", "tensor"),
            P("tensor", "dp"),
        ),
        check_vma=False,
    )
```
